32 devices in a mesh: fsdp: 2 (over x), ctx: 16 (over z, y, core).
Axes of the slice: x: 2, y: 2, z: 4, core: 2. Of those that a mesh axis runs over, the one named last changes fastest.
Arguments:
- tokens: bfloat16 [2, 2048, 1024], P('fsdp', 'ctx'), may hold values from -6 to 6
- cotangent: bfloat16 [2, 2048, 1024], P('fsdp', 'ctx'), may hold values from -6 to 6
- pair_of: int32 [16], replicated, may hold values from 0 to 15, each once
- prenorm_one: bfloat16 [1024], P(('fsdp', 'ctx')), may hold values from 0.5 to 1.5
- query_one: bfloat16 [1024, 1024], P(('fsdp', 'ctx')), may hold values from -0.1875 to 0.1875
- keys_one: bfloat16 [1024, 1024], P(('fsdp', 'ctx')), may hold values from -0.1875 to 0.1875
- values_one: bfloat16 [1024, 1024], P(('fsdp', 'ctx')), may hold values from -0.1875 to 0.1875
- outproj_one: bfloat16 [1024, 1024], P(('fsdp', 'ctx')), may hold values from -2 to 2
- midnorm_one: bfloat16 [1024], P(('fsdp', 'ctx')), may hold values from 0.5 to 1.5
- gates_one: bfloat16 [1024, 2816], P(('fsdp', 'ctx')), may hold values from -0.1875 to 0.1875
- upproj_one: bfloat16 [1024, 2816], P(('fsdp', 'ctx')), may hold values from -0.1875 to 0.1875
- downproj_one: bfloat16 [2816, 1024], P(('fsdp', 'ctx')), may hold values from -0.109375 to 0.109375
- prenorm_two: bfloat16 [1024], P(('fsdp', 'ctx')), may hold values from 0.5 to 1.5
- query_two: bfloat16 [1024, 1024], P(('fsdp', 'ctx')), may hold values from -0.1875 to 0.1875
- keys_two: bfloat16 [1024, 1024], P(('fsdp', 'ctx')), may hold values from -0.1875 to 0.1875
- values_two: bfloat16 [1024, 1024], P(('fsdp', 'ctx')), may hold values from -0.1875 to 0.1875
- outproj_two: bfloat16 [1024, 1024], P(('fsdp', 'ctx')), may hold values from -2 to 2
- midnorm_two: bfloat16 [1024], P(('fsdp', 'ctx')), may hold values from 0.5 to 1.5
- gates_two: bfloat16 [1024, 2816], P(('fsdp', 'ctx')), may hold values from -0.1875 to 0.1875
- upproj_two: bfloat16 [1024, 2816], P(('fsdp', 'ctx')), may hold values from -0.1875 to 0.1875
- downproj_two: bfloat16 [2816, 1024], P(('fsdp', 'ctx')), may hold values from -0.109375 to 0.109375
Outputs:
- output: bfloat16 [2, 2048, 1024], P('fsdp', 'ctx')
- tokens_grad: bfloat16 [2, 2048, 1024], P('fsdp', 'ctx')
- prenorm_one_grad: float32 [1024], P(('fsdp', 'ctx'))
- query_one_grad: float32 [1024, 1024], P(('fsdp', 'ctx'))
- keys_one_grad: float32 [1024, 1024], P(('fsdp', 'ctx'))
- values_one_grad: float32 [1024, 1024], P(('fsdp', 'ctx'))
- outproj_one_grad: float32 [1024, 1024], P(('fsdp', 'ctx'))
- midnorm_one_grad: float32 [1024], P(('fsdp', 'ctx'))
- gates_one_grad: float32 [1024, 2816], P(('fsdp', 'ctx'))
- upproj_one_grad: float32 [1024, 2816], P(('fsdp', 'ctx'))
- downproj_one_grad: float32 [2816, 1024], P(('fsdp', 'ctx'))
- prenorm_two_grad: float32 [1024], P(('fsdp', 'ctx'))
- query_two_grad: float32 [1024, 1024], P(('fsdp', 'ctx'))
- keys_two_grad: float32 [1024, 1024], P(('fsdp', 'ctx'))
- values_two_grad: float32 [1024, 1024], P(('fsdp', 'ctx'))
- outproj_two_grad: float32 [1024, 1024], P(('fsdp', 'ctx'))
- midnorm_two_grad: float32 [1024], P(('fsdp', 'ctx'))
- gates_two_grad: float32 [1024, 2816], P(('fsdp', 'ctx'))
- upproj_two_grad: float32 [1024, 2816], P(('fsdp', 'ctx'))
- downproj_two_grad: float32 [2816, 1024], P(('fsdp', 'ctx'))
The draws below stay inside these ranges and needn't reach their ends.
Inputs may be any that keep to these rules, and one draw needn't show every extreme that they name: pair_of is a permutation of the ctx devices: ctx device j holds, in its first 64 rows, causal block pair_of[j] and, in the other 64, block 31 - pair_of[j].
All inputs are finite; a program needn't handle non-finite values.
Results may differ from the reference program's by a relative error of at most 0.023.
Values may be sent and summed in bfloat16 or wider, within the bound.
A program may use at most 384 MiB of HBM per device.

```python
import math
import jax
import jax.numpy as jnp
from jax import lax

D = 1024
HEADS = 16
HD = 64
FF = 2816
SEQ_DEV = 128
HALF = 64
BLOCKS = 32
LEN = 2048
N_FSDP = 2
N_CTX = 16


def steps_of(key, shape, split, smallest, top_value):
    factor_of, own = 1.0, jax.random.fold_in(key, 6)
    for dim, shards_of in split:
        draws = jnp.exp(jax.random.uniform(jax.random.fold_in(own, dim), (shards_of,), jnp.float32, smallest / len(split), top_value / len(split)))
        factor_of = factor_of * jnp.repeat(draws, shape[dim] // shards_of).reshape([-1 if axis == dim else 1 for axis in range(len(shape))])
    return factor_of


def noise(stream_key, shape, scale, most, cuts=(), kind=jnp.bfloat16):
    drawn = jax.random.normal(stream_key, shape, jnp.float32) * scale
    if len(cuts) > 0:
        drawn = steps_of(stream_key, shape, cuts, -0.22, 0.18) * drawn
    return jnp.clip(drawn, min=-most, max=most).astype(kind)


def setup_inputs(seed: int = 0) -> dict:
    keys = jax.random.split(jax.random.key(seed), 22)
    tokens = noise(keys[0], (N_FSDP, LEN, D), 1.0, 6.0, ((0, 2), (1, 16)))
    cotangent = noise(keys[1], (N_FSDP, LEN, D), 1.0, 6.0, ((0, 2), (1, 16)))
    pair_of = jax.random.permutation(keys[2], N_CTX).astype(jnp.int32)
    prenorm_one = jnp.clip(1.0 + 0.1 * jax.random.normal(keys[3], (D,), jnp.float32), 0.5, 1.5).astype(jnp.bfloat16)
    query_one = noise(keys[4], (D, D), D ** -0.5, 0.1875, ((0, 32),))
    keys_one = noise(keys[5], (D, D), D ** -0.5, 0.1875, ((0, 32),))
    values_one = noise(keys[6], (D, D), D ** -0.5, 0.1875, ((0, 32),))
    outproj_one = noise(keys[7], (D, D), (max(1, 16 * D // (SEQ_DEV * N_CTX))) ** -0.5, 2.0, ((0, 32),))
    midnorm_one = jnp.clip(1.0 + 0.1 * jax.random.normal(keys[8], (D,), jnp.float32), 0.5, 1.5).astype(jnp.bfloat16)
    gates_one = noise(keys[9], (D, FF), D ** -0.5, 0.1875, ((0, 32),))
    upproj_one = noise(keys[10], (D, FF), D ** -0.5, 0.1875, ((0, 32),))
    downproj_one = noise(keys[11], (FF, D), FF ** -0.5, 0.109375, ((0, 32),))
    prenorm_two = jnp.clip(1.0 + 0.1 * jax.random.normal(keys[12], (D,), jnp.float32), 0.5, 1.5).astype(jnp.bfloat16)
    query_two = noise(keys[13], (D, D), D ** -0.5, 0.1875, ((0, 32),))
    keys_two = noise(keys[14], (D, D), D ** -0.5, 0.1875, ((0, 32),))
    values_two = noise(keys[15], (D, D), D ** -0.5, 0.1875, ((0, 32),))
    outproj_two = noise(keys[16], (D, D), (max(1, 16 * D // (SEQ_DEV * N_CTX))) ** -0.5, 2.0, ((0, 32),))
    midnorm_two = jnp.clip(1.0 + 0.1 * jax.random.normal(keys[17], (D,), jnp.float32), 0.5, 1.5).astype(jnp.bfloat16)
    gates_two = noise(keys[18], (D, FF), D ** -0.5, 0.1875, ((0, 32),))
    upproj_two = noise(keys[19], (D, FF), D ** -0.5, 0.1875, ((0, 32),))
    downproj_two = noise(keys[20], (FF, D), FF ** -0.5, 0.109375, ((0, 32),))
    return {"tokens": tokens, "cotangent": cotangent, "pair_of": pair_of, "prenorm_one": prenorm_one, "query_one": query_one, "keys_one": keys_one, "values_one": values_one, "outproj_one": outproj_one, "midnorm_one": midnorm_one, "gates_one": gates_one, "upproj_one": upproj_one, "downproj_one": downproj_one, "prenorm_two": prenorm_two, "query_two": query_two, "keys_two": keys_two, "values_two": values_two, "outproj_two": outproj_two, "midnorm_two": midnorm_two, "gates_two": gates_two, "upproj_two": upproj_two, "downproj_two": downproj_two}


@jax.custom_vjp
def low(v):
    return lax.optimization_barrier(v.astype(jnp.bfloat16)).astype(jnp.float32)

@jax.custom_vjp
def low_back(v):
    return v

def low_keep(v):
    return (low(v), None)

def low_pass(kept, grad):
    return (grad,)

def back_keep(v):
    return (v, None)

def back_low(kept, grad):
    return (low(grad),)
low.defvjp(low_keep, low_pass)
low_back.defvjp(back_keep, back_low)
NORM_EPS = 1e-05
NEG_FILL = -1e+30
HIGHEST = lax.Precision.HIGHEST

def rope_tables(positions, head_size):
    half_size = head_size // 2
    freqs = jnp.exp(jnp.arange(half_size, dtype=jnp.float32) * (-2.0 * math.log(10000.0) / head_size))
    angles = positions.astype(jnp.float32)[:, None] * freqs[None, :]
    return (jnp.cos(angles), jnp.sin(angles))

def rotate(values_in, cosine, sine):
    half_size = values_in.shape[-1] // 2
    first_half = values_in[..., :half_size]
    second_half = values_in[..., half_size:]
    cos_rows = cosine[:, None, :]
    sin_rows = sine[:, None, :]
    return jnp.concatenate([first_half * cos_rows - second_half * sin_rows, second_half * cos_rows + first_half * sin_rows], axis=-1)

def matmul(left, right):
    return jnp.dot(left, right, precision=HIGHEST, preferred_element_type=jnp.float32)

def row_norm(hidden):
    return hidden * lax.rsqrt(lax.optimization_barrier(jnp.mean(hidden * hidden, axis=-1, keepdims=True)) + NORM_EPS)

def block_attend(queries, keys_all, values_all, query_pos, key_pos):
    raw_scores = jnp.einsum('qhd,khd->hqk', queries, keys_all, precision=HIGHEST)
    scores = low_back(raw_scores) * queries.shape[2] ** (-0.5)
    allowed = key_pos[None, None, :] <= query_pos[None, :, None]
    scores = jnp.where(allowed, scores, NEG_FILL)
    log_total = jax.nn.logsumexp(scores, axis=-1, keepdims=True)
    shares = low(jnp.exp(scores - log_total))
    return jnp.einsum('hqk,khd->qhd', shares, values_all, precision=HIGHEST)

def attention(queries, keys_all, values_all, positions):
    total_rows = queries.shape[0]
    size_now = math.gcd(total_rows, 512)
    count_now = total_rows // size_now
    query_blocks = queries.reshape(count_now, size_now, HEADS, HD)
    pos_blocks = positions.reshape(count_now, size_now)

    def one_block(pair_in):
        return block_attend(pair_in[0], keys_all, values_all, pair_in[1], positions)
    outputs = lax.map(jax.checkpoint(one_block), (query_blocks, pos_blocks))
    return outputs.reshape(total_rows, HEADS * HD)

def resformer_layer(hidden, weight_set, first_values, cosine, sine, positions):
    prenorm, query_w, keys_w, values_w, outproj, midnorm, gates_w, upproj_w, downproj_w = weight_set
    total_rows = hidden.shape[0]
    attn_in = low(row_norm(hidden) * prenorm)
    query_raw = low_back(matmul(attn_in, query_w))
    keys_raw = low_back(matmul(attn_in, keys_w))
    values_raw = low_back(matmul(attn_in, values_w))
    if first_values is None:
        mixed = values_raw
    else:
        mixed = 0.5 * values_raw + 0.5 * first_values
    queries = low(rotate(query_raw.reshape(total_rows, HEADS, HD), cosine, sine))
    keys_all = low(rotate(keys_raw.reshape(total_rows, HEADS, HD), cosine, sine))
    values_all = low(mixed).reshape(total_rows, HEADS, HD)
    att_out = attention(queries, keys_all, values_all, positions)
    att_low = low_back(low(att_out))
    middle = hidden + low_back(matmul(att_low, outproj))
    mlp_in = low(row_norm(middle) * midnorm)
    gate_raw = low_back(matmul(mlp_in, gates_w))
    up_proj = low_back(matmul(mlp_in, upproj_w))
    inner_act = low(jax.nn.silu(gate_raw) * up_proj)
    result = middle + low_back(matmul(inner_act, downproj_w))
    return (result, values_raw)

def reference(tokens, cotangent, pair_of, prenorm_one, query_one, keys_one, values_one, outproj_one, midnorm_one, gates_one, upproj_one, downproj_one, prenorm_two, query_two, keys_two, values_two, outproj_two, midnorm_two, gates_two, upproj_two, downproj_two):
    rows_all = jnp.arange(LEN, dtype=jnp.int32)
    owner = (rows_all // SEQ_DEV).astype(jnp.int32)
    local_row = rows_all % SEQ_DEV
    picked = pair_of[owner]
    block_id = jnp.where(local_row < HALF, picked, BLOCKS - 1 - picked)
    positions = (block_id * HALF + local_row % HALF).astype(jnp.int32)
    cosine, sine = rope_tables(positions, HD)
    weight_all = tuple((weight_arr.astype(jnp.float32) for weight_arr in (prenorm_one, query_one, keys_one, values_one, outproj_one, midnorm_one, gates_one, upproj_one, downproj_one, prenorm_two, query_two, keys_two, values_two, outproj_two, midnorm_two, gates_two, upproj_two, downproj_two)))

    def forward(inputs, weights):
        first_set = weights[:9]
        second_set = weights[9:]
        seq_outputs = []
        for seq_no in range(N_FSDP):
            hidden, first_values = resformer_layer(inputs[seq_no], first_set, None, cosine, sine, positions)
            hidden, unused_values = resformer_layer(hidden, second_set, first_values, cosine, sine, positions)
            seq_outputs.append(hidden)
        return jnp.stack(seq_outputs)
    result, pullback = jax.vjp(forward, tokens.astype(jnp.float32), weight_all)
    grad_tokens, grad_weights = pullback(cotangent.astype(jnp.float32))
    return (result.astype(jnp.bfloat16), grad_tokens.astype(jnp.bfloat16), grad_weights[0], grad_weights[1], grad_weights[2], grad_weights[3], grad_weights[4], grad_weights[5], grad_weights[6], grad_weights[7], grad_weights[8], grad_weights[9], grad_weights[10], grad_weights[11], grad_weights[12], grad_weights[13], grad_weights[14], grad_weights[15], grad_weights[16], grad_weights[17])
```

```python
import math

import jax
import jax.numpy as jnp
from jax import lax
from jax.experimental import pallas as pl
from jax.experimental.pallas import tpu as pltpu
from jax.sharding import PartitionSpec as P

HEADS = 16
HD = 64


NORM_EPS = 1e-05
NEG_FILL = -1e30


def block_size(total_rows):
    size_now = 512
    while total_rows % size_now:
        size_now //= 2
    return size_now


def row_norm(hidden):
    inverse = lax.rsqrt(jnp.mean(hidden * hidden, axis=-1, keepdims=True) + NORM_EPS)
    return (hidden * inverse, inverse)


def norm_back(grad_normed, normed, inverse):
    return inverse * (grad_normed - normed * jnp.mean(grad_normed * normed, axis=-1, keepdims=True))


def rope_tables(positions, head_size):
    half_size = head_size // 2
    freqs = jnp.exp(
        jnp.arange(half_size, dtype=jnp.float32) * (-2.0 * math.log(10000.0) / head_size)
    )
    angles = positions.astype(jnp.float32)[:, None] * freqs[None, :]
    return (jnp.cos(angles), jnp.sin(angles))


def rotate(values_in, cosine, sine):
    half_size = values_in.shape[-1] // 2
    first_half = values_in[..., :half_size]
    second_half = values_in[..., half_size:]
    cos_rows = cosine[:, None, :]
    sin_rows = sine[:, None, :]
    return jnp.concatenate(
        [
            first_half * cos_rows - second_half * sin_rows,
            second_half * cos_rows + first_half * sin_rows,
        ],
        axis=-1,
    )


def unrotate(grads_in, cosine, sine):
    half_size = grads_in.shape[-1] // 2
    first_half = grads_in[..., :half_size]
    second_half = grads_in[..., half_size:]
    cos_rows = cosine[:, None, :]
    sin_rows = sine[:, None, :]
    return jnp.concatenate(
        [
            first_half * cos_rows + second_half * sin_rows,
            second_half * cos_rows - first_half * sin_rows,
        ],
        axis=-1,
    )


def left_product(left, right):
    return lax.dot_general(
        left, right, (((0,), (0,)), ((), ())), preferred_element_type=jnp.float32
    )


def right_product(left, right):
    return lax.dot_general(
        left, right, (((1,), (1,)), ((), ())), preferred_element_type=jnp.float32
    )


def storage_positions(pair_of, seq_dev):
    devices = pair_of.shape[0]
    rows_all = jnp.arange(devices * seq_dev, dtype=jnp.int32)
    owner = rows_all // seq_dev
    local_row = rows_all % seq_dev
    half_rows = seq_dev // 2
    picked = jnp.sum(
        jnp.where(
            owner[:, None] == jnp.arange(devices, dtype=jnp.int32)[None, :], pair_of[None, :], 0
        ),
        axis=1,
    )
    block_id = jnp.where(local_row < half_rows, picked, 2 * devices - 1 - picked)
    return block_id * half_rows + local_row % half_rows


def head_scores(queries, keys_flat, query_pos, key_pos):
    key_heads = keys_flat.reshape(keys_flat.shape[0], queries.shape[1], queries.shape[2])
    scores = jnp.einsum(
        "qhd,khd->hqk", queries, key_heads, preferred_element_type=jnp.float32
    ) * queries.shape[2] ** (-0.5)
    allowed = (key_pos[None, :] <= query_pos[:, None])[None]
    return (jnp.where(allowed, scores, NEG_FILL), allowed)


def make_stats_step(queries, query_pos, pos_all, state_in, key_part):
    size_now = block_size(key_part.shape[0])

    def inner_step(block_no, state_now):
        top_now, total_now = state_now
        offset = block_no * size_now
        key_block = lax.dynamic_slice_in_dim(key_part, offset, size_now, 0)
        key_pos = lax.dynamic_slice_in_dim(pos_all, offset, size_now, 0)
        scores, allowed = head_scores(queries, key_block, query_pos, key_pos)
        new_top = jnp.maximum(top_now, jnp.max(scores, axis=-1))
        total_now = total_now * jnp.exp(top_now - new_top) + jnp.sum(
            jnp.where(allowed, jnp.exp(scores - new_top[..., None]), 0.0), axis=-1
        )
        return (new_top, total_now)

    return lax.fori_loop(0, key_part.shape[0] // size_now, inner_step, state_in)


def make_value_step(queries, log_total, query_pos, pos_all, acc_in, pieces):
    key_part, value_part = pieces
    size_now = block_size(key_part.shape[0])

    def inner_step(block_no, acc_now):
        offset = block_no * size_now
        key_block = lax.dynamic_slice_in_dim(key_part, offset, size_now, 0)
        value_block = lax.dynamic_slice_in_dim(value_part, offset, size_now, 0)
        key_pos = lax.dynamic_slice_in_dim(pos_all, offset, size_now, 0)
        scores, allowed = head_scores(queries, key_block, query_pos, key_pos)
        shares = jnp.exp(scores - log_total[..., None]).astype(jnp.bfloat16)
        value_heads = value_block.reshape(size_now, queries.shape[1], queries.shape[2])
        return acc_now + jnp.einsum(
            "hqk,khd->qhd", shares, value_heads, preferred_element_type=jnp.float32
        )

    return lax.fori_loop(0, key_part.shape[0] // size_now, inner_step, acc_in)


def make_back_step(queries, grad_att, log_total, row_delta, query_pos, pos_all):
    scale_now = queries.shape[2] ** (-0.5)

    def back_step(state_in, pieces, start_row):
        key_part, value_part = pieces
        size_now = block_size(key_part.shape[0])

        def inner_step(block_no, state_now):
            offset = block_no * size_now
            key_block = lax.dynamic_slice_in_dim(key_part, offset, size_now, 0)
            value_block = lax.dynamic_slice_in_dim(value_part, offset, size_now, 0)
            key_pos = lax.dynamic_slice_in_dim(pos_all, offset, size_now, 0)
            scores, allowed = head_scores(queries, key_block, query_pos, key_pos)
            shares = jnp.exp(scores - log_total[..., None])
            value_heads = value_block.reshape(size_now, queries.shape[1], queries.shape[2])
            key_heads = key_block.reshape(size_now, queries.shape[1], queries.shape[2])
            grad_shares = jnp.einsum(
                "qhd,khd->hqk", grad_att, value_heads, preferred_element_type=jnp.float32
            )
            grad_scores = (shares * (grad_shares - row_delta[..., None]) * scale_now).astype(
                jnp.bfloat16
            )
            grad_query = state_now[0] + jnp.einsum(
                "hqk,khd->qhd", grad_scores, key_heads, preferred_element_type=jnp.float32
            )
            return (grad_query,)

        return lax.fori_loop(0, key_part.shape[0] // size_now, inner_step, state_in)

    return back_step


def make_query_step(own_keys, own_values, own_pos, stats_all, pos_all, head_count, head_size):
    scale_now = head_size ** (-0.5)
    value_heads = own_values.reshape(own_values.shape[0], head_count, head_size)

    def query_step(state_in, pieces, start_row):
        query_part, grad_part = pieces
        size_now = block_size(query_part.shape[0])

        def inner_step(block_no, state_now):
            offset = block_no * size_now
            query_block = lax.dynamic_slice_in_dim(query_part, offset, size_now, 0).reshape(
                size_now, head_count, head_size
            )
            grad_block = lax.dynamic_slice_in_dim(grad_part, offset, size_now, 0).reshape(
                size_now, head_count, head_size
            )
            query_pos = lax.dynamic_slice_in_dim(pos_all, offset, size_now, 0)
            log_block = lax.dynamic_slice_in_dim(stats_all[0], offset, size_now, 0).T
            delta_block = lax.dynamic_slice_in_dim(stats_all[1], offset, size_now, 0).T
            scores, allowed = head_scores(query_block, own_keys, query_pos, own_pos)
            shares = jnp.exp(scores - log_block[..., None])
            grad_shares = jnp.einsum(
                "qhd,khd->hqk", grad_block, value_heads, preferred_element_type=jnp.float32
            )
            grad_scores = (shares * (grad_shares - delta_block[..., None]) * scale_now).astype(
                jnp.bfloat16
            )
            key_term = jnp.einsum(
                "hqk,qhd->khd", grad_scores, query_block, preferred_element_type=jnp.float32
            )
            value_term = jnp.einsum(
                "hqk,qhd->khd",
                shares.astype(jnp.bfloat16),
                grad_block,
                preferred_element_type=jnp.float32,
            )
            return (
                state_now[0] + key_term.reshape(key_term.shape[0], -1),
                state_now[1] + value_term.reshape(value_term.shape[0], -1),
            )

        return lax.fori_loop(0, query_part.shape[0] // size_now, inner_step, state_in)

    return query_step


def gather_forward(shards):
    return (
        lax.all_gather(shards[0], ("fsdp", "ctx"), axis=0, tiled=True),
        lax.all_gather(shards[1], ("fsdp", "ctx"), axis=0, tiled=True),
        lax.all_gather(shards[2], ("fsdp", "ctx"), axis=0, tiled=True),
        lax.all_gather(shards[3], ("fsdp", "ctx"), axis=0, tiled=True),
        lax.all_gather(shards[4], ("fsdp", "ctx"), axis=0, tiled=True),
        lax.all_gather(shards[5], ("fsdp", "ctx"), axis=0, tiled=True),
        lax.all_gather(shards[6], ("fsdp", "ctx"), axis=0, tiled=True),
        lax.all_gather(shards[7], ("fsdp", "ctx"), axis=0, tiled=True),
        lax.all_gather(shards[8], ("fsdp", "ctx"), axis=0, tiled=True),
    )


def scatter_grads(grad_terms):
    return (
        lax.psum_scatter(grad_terms[0], ("fsdp", "ctx"), scatter_dimension=0, tiled=True),
        lax.psum_scatter(grad_terms[1], ("fsdp", "ctx"), scatter_dimension=0, tiled=True),
        lax.psum_scatter(grad_terms[2], ("fsdp", "ctx"), scatter_dimension=0, tiled=True),
        lax.psum_scatter(grad_terms[3], ("fsdp", "ctx"), scatter_dimension=0, tiled=True),
        lax.psum_scatter(grad_terms[4], ("fsdp", "ctx"), scatter_dimension=0, tiled=True),
        lax.psum_scatter(grad_terms[5], ("fsdp", "ctx"), scatter_dimension=0, tiled=True),
        lax.psum_scatter(grad_terms[6], ("fsdp", "ctx"), scatter_dimension=0, tiled=True),
        lax.psum_scatter(grad_terms[7], ("fsdp", "ctx"), scatter_dimension=0, tiled=True),
        lax.psum_scatter(grad_terms[8], ("fsdp", "ctx"), scatter_dimension=0, tiled=True),
    )


def forward_layer(hidden, full_layer, first_values, context):
    prenorm, query_w, keys_w, values_w, outproj, midnorm, gates_w, upproj_w, downproj_w = full_layer
    cosine, sine, own_pos, pos_all = context
    rows_n, model_width = hidden.shape
    normed, inverse_a = row_norm(hidden)
    attn_in = (normed * prenorm.astype(jnp.float32)).astype(jnp.bfloat16)
    query_raw = jnp.dot(attn_in, query_w, preferred_element_type=jnp.float32)
    keys_raw = jnp.dot(attn_in, keys_w, preferred_element_type=jnp.float32)
    values_raw = jnp.dot(attn_in, values_w, preferred_element_type=jnp.float32)
    mixed = values_raw if first_values is None else 0.5 * values_raw + 0.5 * first_values
    queries = rotate(query_raw.reshape(rows_n, HEADS, HD), cosine, sine).astype(jnp.bfloat16)
    keys_flat = (
        rotate(keys_raw.reshape(rows_n, HEADS, HD), cosine, sine)
        .reshape(rows_n, model_width)
        .astype(jnp.bfloat16)
    )
    values_flat = mixed.astype(jnp.bfloat16)
    top_start = jnp.full((HEADS, rows_n), NEG_FILL, jnp.float32)
    total_start = jnp.zeros((HEADS, rows_n), jnp.float32)
    top_now, total_now = make_stats_step(
        queries,
        own_pos,
        pos_all,
        (top_start, total_start),
        lax.all_gather(keys_flat, "ctx", axis=0, tiled=True),
    )
    log_total = top_now + jnp.log(total_now)
    att_out = make_value_step(
        queries,
        log_total,
        own_pos,
        pos_all,
        jnp.zeros((rows_n, HEADS, HD), jnp.float32),
        (
            lax.all_gather(keys_flat, "ctx", axis=0, tiled=True),
            lax.all_gather(values_flat, "ctx", axis=0, tiled=True),
        ),
    )
    att_low = att_out.reshape(rows_n, model_width).astype(jnp.bfloat16)
    middle = hidden + jnp.dot(att_low, outproj, preferred_element_type=jnp.float32)
    normed_mid, inverse_b = row_norm(middle)
    mlp_in = (normed_mid * midnorm.astype(jnp.float32)).astype(jnp.bfloat16)
    gate_raw = jnp.dot(mlp_in, gates_w, preferred_element_type=jnp.float32)
    up_proj = jnp.dot(mlp_in, upproj_w, preferred_element_type=jnp.float32)
    inner_act = (jax.nn.silu(gate_raw) * up_proj).astype(jnp.bfloat16)
    result = middle + jnp.dot(inner_act, downproj_w, preferred_element_type=jnp.float32)
    saved = (
        hidden,
        normed,
        inverse_a,
        attn_in,
        queries,
        keys_flat,
        values_flat,
        log_total,
        att_out,
        att_low,
        normed_mid,
        inverse_b,
        mlp_in,
        gate_raw,
        up_proj,
        inner_act,
    )
    return (result, values_raw, saved)


def backward_layer(grad_out, full_layer, saved, value_extra, is_second, context):
    prenorm, query_w, keys_w, values_w, outproj, midnorm, gates_w, upproj_w, downproj_w = full_layer
    (
        hidden,
        normed,
        inverse_a,
        attn_in,
        queries,
        keys_flat,
        values_flat,
        log_total,
        att_out,
        att_low,
        normed_mid,
        inverse_b,
        mlp_in,
        gate_raw,
        up_proj,
        inner_act,
    ) = saved
    cosine, sine, own_pos, pos_all = context
    rows_n, model_width = hidden.shape
    grad_low = grad_out.astype(jnp.bfloat16)
    grad_down = left_product(inner_act, grad_low)
    grad_inner = right_product(grad_low, downproj_w)
    sigma_gate = jax.nn.sigmoid(gate_raw)
    grad_gate = (grad_inner * up_proj * sigma_gate * (1.0 + gate_raw * (1.0 - sigma_gate))).astype(
        jnp.bfloat16
    )
    grad_up = (grad_inner * gate_raw * sigma_gate).astype(jnp.bfloat16)
    grad_gates = left_product(mlp_in, grad_gate)
    grad_upproj = left_product(mlp_in, grad_up)
    grad_mlp = right_product(grad_gate, gates_w) + right_product(grad_up, upproj_w)
    grad_midnorm = jnp.sum(grad_mlp * normed_mid, axis=0)
    grad_middle = grad_out + norm_back(
        grad_mlp * midnorm.astype(jnp.float32), normed_mid, inverse_b
    )
    branch_low = grad_middle.astype(jnp.bfloat16)
    grad_outproj = left_product(att_low, branch_low)
    grad_att = right_product(branch_low, outproj).astype(jnp.bfloat16).reshape(rows_n, HEADS, HD)
    row_delta = jnp.sum(grad_att.astype(jnp.float32) * att_out, axis=-1).T
    query_start = jnp.zeros((rows_n, HEADS, HD), jnp.float32)
    state_start = (query_start,)
    back_fn = make_back_step(queries, grad_att, log_total, row_delta, own_pos, pos_all)
    state_out = back_fn(
        state_start,
        (
            lax.all_gather(keys_flat, "ctx", axis=0, tiled=True),
            lax.all_gather(values_flat, "ctx", axis=0, tiled=True),
        ),
        jnp.int32(0),
    )
    grad_qr = state_out[0]
    stats_all = (
        lax.all_gather(log_total.T, "ctx", axis=0, tiled=True),
        lax.all_gather(row_delta.T, "ctx", axis=0, tiled=True),
    )
    query_fn = make_query_step(keys_flat, values_flat, own_pos, stats_all, pos_all, HEADS, HD)
    flat_start = jnp.zeros((rows_n, model_width), jnp.float32)
    grad_kr, grad_mix = query_fn(
        (flat_start, flat_start),
        (
            lax.all_gather(queries.reshape(rows_n, model_width), "ctx", axis=0, tiled=True),
            lax.all_gather(grad_att.reshape(rows_n, model_width), "ctx", axis=0, tiled=True),
        ),
        jnp.int32(0),
    )
    grad_query = unrotate(grad_qr, cosine, sine).reshape(rows_n, model_width).astype(jnp.bfloat16)
    grad_keys = (
        unrotate(grad_kr.reshape(rows_n, HEADS, HD), cosine, sine)
        .reshape(rows_n, model_width)
        .astype(jnp.bfloat16)
    )
    if is_second:
        grad_values = (0.5 * grad_mix).astype(jnp.bfloat16)
        passed_on = 0.5 * grad_mix
    else:
        grad_values = (grad_mix + value_extra).astype(jnp.bfloat16)
        passed_on = None
    grad_query_w = left_product(attn_in, grad_query)
    grad_keys_w = left_product(attn_in, grad_keys)
    grad_values_w = left_product(attn_in, grad_values)
    grad_attn = (
        right_product(grad_query, query_w)
        + right_product(grad_keys, keys_w)
        + right_product(grad_values, values_w)
    )
    grad_prenorm = jnp.sum(grad_attn * normed, axis=0)
    grad_hidden = grad_middle + norm_back(
        grad_attn * prenorm.astype(jnp.float32), normed, inverse_a
    )
    grad_terms = (
        grad_prenorm,
        grad_query_w,
        grad_keys_w,
        grad_values_w,
        grad_outproj,
        grad_midnorm,
        grad_gates,
        grad_upproj,
        grad_down,
    )
    return (grad_hidden, grad_terms, passed_on)


def local(
    tokens,
    cotangent,
    pair_of,
    prenorm_one,
    query_one,
    keys_one,
    values_one,
    outproj_one,
    midnorm_one,
    gates_one,
    upproj_one,
    downproj_one,
    prenorm_two,
    query_two,
    keys_two,
    values_two,
    outproj_two,
    midnorm_two,
    gates_two,
    upproj_two,
    downproj_two,
):
    seq_dev = tokens.shape[1]
    model_width = tokens.shape[2]
    pos_all = storage_positions(pair_of, seq_dev)
    own_pos = lax.dynamic_slice_in_dim(pos_all, lax.axis_index("ctx") * seq_dev, seq_dev, 0)
    cosine, sine = rope_tables(own_pos, HD)
    context = (cosine, sine, own_pos, pos_all)
    layer_shards = [
        (
            prenorm_one,
            query_one,
            keys_one,
            values_one,
            outproj_one,
            midnorm_one,
            gates_one,
            upproj_one,
            downproj_one,
        ),
        (
            prenorm_two,
            query_two,
            keys_two,
            values_two,
            outproj_two,
            midnorm_two,
            gates_two,
            upproj_two,
            downproj_two,
        ),
    ]
    hidden = tokens.reshape(seq_dev, model_width).astype(jnp.float32)
    first_values = None
    kept_full = []
    kept_saved = []
    for layer_no in range(2):
        full_layer = gather_forward(layer_shards[layer_no])
        hidden, values_raw, saved = forward_layer(hidden, full_layer, first_values, context)
        if layer_no == 0:
            first_values = values_raw
        kept_full.append(full_layer)
        kept_saved.append(saved)
    output = hidden.astype(jnp.bfloat16).reshape(1, seq_dev, model_width)
    grad_now = cotangent.reshape(seq_dev, model_width).astype(jnp.float32)
    value_extra = None
    layer_grads = [None, None]
    for layer_no in (1, 0):
        full_layer = kept_full[layer_no]
        grad_now, grad_terms, passed_on = backward_layer(
            grad_now, full_layer, kept_saved[layer_no], value_extra, layer_no == 1, context
        )
        if layer_no == 1:
            value_extra = passed_on
        layer_grads[layer_no] = scatter_grads(grad_terms)
    tokens_grad = grad_now.astype(jnp.bfloat16).reshape(1, seq_dev, model_width)
    first_grads = layer_grads[0]
    second_grads = layer_grads[1]
    return (
        output,
        tokens_grad,
        first_grads[0],
        first_grads[1],
        first_grads[2],
        first_grads[3],
        first_grads[4],
        first_grads[5],
        first_grads[6],
        first_grads[7],
        first_grads[8],
        second_grads[0],
        second_grads[1],
        second_grads[2],
        second_grads[3],
        second_grads[4],
        second_grads[5],
        second_grads[6],
        second_grads[7],
        second_grads[8],
    )


ROWS = 128
BF = jnp.bfloat16
F32 = jnp.float32
MESH = pl.DeviceIdType.MESH
VMEM_SPACE = pltpu.VMEM


def flip(value, weight):
    return value + weight * (1 - 2 * ((value // weight) % 2))


def to_device(f, c):
    return {"fsdp": f, "ctx": c}


def remote(src, dst, send_sem, recv_sem, target):
    return pltpu.make_async_remote_copy(
        src_ref=src,
        dst_ref=dst,
        send_sem=send_sem,
        recv_sem=recv_sem,
        device_id=to_device(*target),
        device_id_type=MESH,
    )


def plane_place():
    f = lax.axis_index("fsdp")
    c = lax.axis_index("ctx")
    return f, c, (c // 2) % 2, c // 4


def greet_plane(f, c, z):
    barrier = pltpu.get_barrier_semaphore()

    def hello(target):
        pl.semaphore_signal(barrier, inc=1, device_id=to_device(*target), device_id_type=MESH)

    hello((f, flip(c, 2)))

    @pl.when(z > 0)
    def _():
        hello((f, c - 4))

    @pl.when(z < 3)
    def _():
        hello((f, c + 4))

    pl.semaphore_wait(barrier, 2 + jnp.where((z > 0) & (z < 3), 1, 0))


def send_order(z, step):
    table = ((3, 2, 1, 0), (3, 0, 2, 1), (0, 3, 1, 2), (0, 1, 2, 3))
    column = [row[step] for row in table]
    return jnp.where(
        z == 0, column[0], jnp.where(z == 1, column[1], jnp.where(z == 2, column[2], column[3]))
    )


def reduce_plane(place, product, bufs, sems):
    f, c, y, z = place
    sy, ry, acc, su, ru, sd, rd = bufs
    ys, yr, us, ur, ds, dr = sems
    across = (f, flip(c, 2))
    above = (f, c + 4)
    below = (f, c - 4)

    def y_copy(block):
        return remote(sy.at[block], ry.at[block], ys.at[block], yr.at[block], across)

    def up_copy(block):
        return remote(su.at[block], ru.at[block], us.at[block], ur.at[block], above)

    def down_copy(block):
        return remote(sd.at[block], rd.at[block], ds.at[block], dr.at[block], below)

    for step in range(4):
        block = send_order(z, step)
        sy[block] = product(block * 2 + (1 - y)).astype(BF)
        y_copy(block).start()
    for block in range(4):
        acc[block] = product(block * 2 + y)
    for k in range(3):
        top = 3 - k

        @pl.when(top > z)
        def _():
            y_copy(top).wait_recv()
            acc[top] += ry[top].astype(F32)

            @pl.when(z > 0)
            def _():
                up_copy(top).wait_recv()
                acc[top] += ru[top].astype(F32)

            su[top] = acc[top].astype(BF)
            up_copy(top).start()

        @pl.when(k < z)
        def _():
            y_copy(k).wait_recv()
            acc[k] += ry[k].astype(F32)

            @pl.when(z < 3)
            def _():
                down_copy(k).wait_recv()
                acc[k] += rd[k].astype(F32)

            sd[k] = acc[k].astype(BF)
            down_copy(k).start()

    y_copy(z).wait_recv()
    acc[z] += ry[z].astype(F32)

    @pl.when(z > 0)
    def _():
        up_copy(z).wait_recv()
        acc[z] += ru[z].astype(F32)

    @pl.when(z < 3)
    def _():
        down_copy(z).wait_recv()
        acc[z] += rd[z].astype(F32)

    def finish():
        for block in range(4):
            y_copy(block).wait_send()
        for k in range(3):

            @pl.when(3 - k > z)
            def _():
                up_copy(3 - k).wait_send()

            @pl.when(k < z)
            def _():
                down_copy(k).wait_send()

    return finish


def gather_plane(place, full, sems):
    f, c, y, z = place
    ys, yr, us, ur, ds, dr = sems
    across = (f, flip(c, 2))
    above = (f, c + 4)
    below = (f, c - 4)

    def rows(block, side):
        return full.at[pl.ds(pl.multiple_of((block * 2 + side) * ROWS, ROWS), ROWS)]

    def y_copy(block):
        return remote(rows(block, y), rows(block, y), ys.at[block], yr.at[block], across)

    def up_copy(block):
        return remote(rows(block, y), rows(block, y), us.at[block], ur.at[block], above)

    def down_copy(block):
        return remote(rows(block, y), rows(block, y), ds.at[block], dr.at[block], below)

    @pl.when(z < 3)
    def _():
        up_copy(z).start()

    @pl.when(z > 0)
    def _():
        down_copy(z).start()

    y_copy(z).start()
    for k in range(1, 4):

        @pl.when(z >= k)
        def _():
            up_copy(z - k).wait_recv()

            @pl.when(z < 3)
            def _():
                up_copy(z - k).start()

            y_copy(z - k).start()

        @pl.when(z + k <= 3)
        def _():
            down_copy(z + k).wait_recv()

            @pl.when(z > 0)
            def _():
                down_copy(z + k).start()

            y_copy(z + k).start()

    for block in range(4):
        y_copy(block).wait()
    for k in range(4):

        @pl.when((z < 3) & (z >= k))
        def _():
            up_copy(z - k).wait_send()

        @pl.when((z > 0) & (z + k <= 3))
        def _():
            down_copy(z + k).wait_send()


def norm_rows(hidden):
    return lax.rsqrt(jnp.mean(hidden * hidden, axis=-1, keepdims=True) + NORM_EPS)


def own_rows(place):
    _, _, y, z = place
    return pl.ds(pl.multiple_of((z * 2 + y) * ROWS, ROWS), ROWS)


def make_product(left_ref, right_ref, transposed):
    dims = (((1,), (1,)), ((), ())) if transposed else (((1,), (0,)), ((), ()))

    def product(block):
        rows = left_ref[pl.ds(pl.multiple_of(block * ROWS, ROWS), ROWS), :]
        return lax.dot_general(rows, right_ref[...], dims, preferred_element_type=F32)

    return product


def start_kernel(hid_ref, gain_ref, full_ref, *sems):
    place = plane_place()
    greet_plane(place[0], place[1], place[3])
    hidden = hid_ref[...].astype(F32)
    full_ref[own_rows(place), :] = (hidden * norm_rows(hidden) * gain_ref[...]).astype(BF)
    gather_plane(place, full_ref, sems)


def forward_kernel(left_ref, right_ref, res_ref, gain_ref, new_ref, full_ref, *scratch):
    place = plane_place()
    greet_plane(place[0], place[1], place[3])
    bufs, sems, more = scratch[:7], scratch[7:13], scratch[13:]
    finish = reduce_plane(place, make_product(left_ref, right_ref, False), bufs, sems)
    hidden = res_ref[...].astype(F32) + bufs[2][place[3]]
    new_ref[...] = hidden
    full_ref[own_rows(place), :] = (hidden * norm_rows(hidden) * gain_ref[...]).astype(BF)
    gather_plane(place, full_ref, more)
    finish()


def turn_kernel(left_ref, right_ref, res_ref, cot_ref, out_ref, full_ref, *scratch):
    place = plane_place()
    greet_plane(place[0], place[1], place[3])
    bufs, sems, more = scratch[:7], scratch[7:13], scratch[13:]
    finish = reduce_plane(place, make_product(left_ref, right_ref, False), bufs, sems)
    out_ref[...] = (res_ref[...] + bufs[2][place[3]]).astype(BF)
    full_ref[own_rows(place), :] = cot_ref[...]
    gather_plane(place, full_ref, more)
    finish()


def back_rows(total, grad, hidden, gain):
    inverse = norm_rows(hidden)
    normed = hidden * inverse
    gain_grad = jnp.sum(total * normed, axis=0, keepdims=True)
    scaled = total * gain
    mean = jnp.mean(scaled * normed, axis=-1, keepdims=True)
    return grad + inverse * (scaled - normed * mean), gain_grad


def back_kernel(left_ref, right_ref, grad_ref, hid_ref, gain_ref, new_ref, gg_ref, full_ref, *scratch):
    place = plane_place()
    greet_plane(place[0], place[1], place[3])
    bufs, sems, more = scratch[:7], scratch[7:13], scratch[13:]
    finish = reduce_plane(place, make_product(left_ref, right_ref, True), bufs, sems)
    new, gain_grad = back_rows(
        bufs[2][place[3]], grad_ref[...].astype(F32), hid_ref[...].astype(F32), gain_ref[...]
    )
    gg_ref[...] = gain_grad
    new_ref[...] = new
    full_ref[own_rows(place), :] = new.astype(BF)
    gather_plane(place, full_ref, more)
    finish()


def last_kernel(left_ref, right_ref, grad_ref, hid_ref, gain_ref, out_ref, gg_ref, *scratch):
    place = plane_place()
    greet_plane(place[0], place[1], place[3])
    bufs, sems = scratch[:7], scratch[7:13]
    finish = reduce_plane(place, make_product(left_ref, right_ref, True), bufs, sems)
    new, gain_grad = back_rows(
        bufs[2][place[3]], grad_ref[...].astype(F32), hid_ref[...].astype(F32), gain_ref[...]
    )
    gg_ref[...] = gain_grad
    out_ref[...] = new.astype(BF)
    finish()


def comm_call(kernel, outs, ident, args, reduces, gathers):
    width = 1024
    scratch = []
    if reduces:
        for kind in (BF, BF, F32, BF, BF, BF, BF):
            scratch.append(pltpu.VMEM((4, ROWS, width), kind))
        scratch += [pltpu.SemaphoreType.DMA((4,))] * 6
    if gathers:
        scratch += [pltpu.SemaphoreType.DMA((4,))] * 6
    spec = pl.BlockSpec(memory_space=VMEM_SPACE)
    return pl.pallas_call(
        kernel,
        out_shape=[jax.ShapeDtypeStruct(*o) for o in outs],
        in_specs=[spec] * len(args),
        out_specs=[spec] * len(outs),
        scratch_shapes=scratch,
        compiler_params=pltpu.CompilerParams(
            collective_id=ident, has_side_effects=True, vmem_limit_bytes=40 * 1024 * 1024
        ),
        name=kernel.__name__,
    )(*args)


def head_lanes(head):
    lane = lax.broadcasted_iota(jnp.int32, (1, 128), 1)
    return (lane // 32) % 2 == head


def value_lanes(head):
    lane = lax.broadcasted_iota(jnp.int32, (1, 128), 1)
    return lane // 64 == head


NT = (((1,), (1,)), ((), ()))
TN = (((0,), (0,)), ((), ()))


def attend_kernel(q_ref, k_ref, v_ref, pq_ref, pk_ref, att_ref, lse_ref):
    allowed = pk_ref[...] <= pq_ref[...]
    queries = q_ref[...]
    parts = []
    for head in range(2):
        masked = jnp.where(head_lanes(head), queries, jnp.zeros_like(queries))
        scores = lax.dot_general(masked, k_ref[...], NT, preferred_element_type=F32) * HD ** (-0.5)
        scores = jnp.where(allowed, scores, NEG_FILL)
        top = jnp.max(scores, axis=-1, keepdims=True)
        shares = jnp.exp(scores - top)
        total = jnp.sum(shares, axis=-1, keepdims=True)
        lse_ref[:, head : head + 1] = top + jnp.log(total)
        mixed = jnp.dot(shares.astype(BF), v_ref[...], preferred_element_type=F32)
        parts.append(mixed / total)
    att_ref[...] = jnp.where(value_lanes(0), parts[0], parts[1]).astype(BF)


def attend_forward(q, k, v, pos_q, pos_k):
    rows = q.shape[0]
    keys = k.shape[0]
    step = 128
    return pl.pallas_call(
        attend_kernel,
        grid=(rows // step,),
        out_shape=[
            jax.ShapeDtypeStruct((rows, 128), BF),
            jax.ShapeDtypeStruct((rows, 2), F32),
        ],
        in_specs=[
            pl.BlockSpec((step, 128), lambda i: (i, 0)),
            pl.BlockSpec((keys, 128), lambda i: (0, 0)),
            pl.BlockSpec((keys, 128), lambda i: (0, 0)),
            pl.BlockSpec((step, 1), lambda i: (i, 0)),
            pl.BlockSpec((1, keys), lambda i: (0, 0)),
        ],
        out_specs=[
            pl.BlockSpec((step, 128), lambda i: (i, 0)),
            pl.BlockSpec((step, 2), lambda i: (i, 0)),
        ],
        compiler_params=pltpu.CompilerParams(vmem_limit_bytes=40 * 1024 * 1024),
        name="attend_forward",
    )(q, k, v, pos_q, pos_k)


def attend_back_kernel(q_ref, k_ref, v_ref, da_ref, lse_ref, pq_ref, pk_ref, dq_ref, dk_ref, dv_ref):
    @pl.when(pl.program_id(0) == 0)
    def _():
        dk_ref[...] = jnp.zeros_like(dk_ref)
        dv_ref[...] = jnp.zeros_like(dv_ref)

    allowed = pk_ref[...] <= pq_ref[...]
    queries = q_ref[...]
    grads = da_ref[...]
    parts = []
    for head in range(2):
        masked = jnp.where(head_lanes(head), queries, jnp.zeros_like(queries))
        grad_h = jnp.where(value_lanes(head), grads, jnp.zeros_like(grads))
        scores = lax.dot_general(k_ref[...], masked, NT, preferred_element_type=F32) * HD ** (-0.5)
        shares = jnp.where(allowed, jnp.exp(scores - lse_ref[head : head + 1, :]), 0.0)
        grad_shares = lax.dot_general(v_ref[...], grad_h, NT, preferred_element_type=F32)
        delta = jnp.sum(shares * grad_shares, axis=0, keepdims=True)
        grad_scores = (shares * (grad_shares - delta) * HD ** (-0.5)).astype(BF)
        dv_ref[...] += jnp.dot(shares.astype(BF), grad_h, preferred_element_type=F32)
        dk_ref[...] += jnp.dot(grad_scores, masked, preferred_element_type=F32)
        parts.append(lax.dot_general(grad_scores, k_ref[...], TN, preferred_element_type=F32))
    dq_ref[...] = jnp.where(head_lanes(0), parts[0], parts[1])


def attend_backward(q, k, v, da, lse_rows, pos_q, pos_k):
    rows = q.shape[0]
    keys = k.shape[0]
    step = 128
    return pl.pallas_call(
        attend_back_kernel,
        grid=(rows // step,),
        out_shape=[
            jax.ShapeDtypeStruct((rows, 128), F32),
            jax.ShapeDtypeStruct((keys, 128), F32),
            jax.ShapeDtypeStruct((keys, 128), F32),
        ],
        in_specs=[
            pl.BlockSpec((step, 128), lambda i: (i, 0)),
            pl.BlockSpec((keys, 128), lambda i: (0, 0)),
            pl.BlockSpec((keys, 128), lambda i: (0, 0)),
            pl.BlockSpec((step, 128), lambda i: (i, 0)),
            pl.BlockSpec((2, step), lambda i: (0, i)),
            pl.BlockSpec((1, step), lambda i: (0, i)),
            pl.BlockSpec((keys, 1), lambda i: (0, 0)),
        ],
        out_specs=[
            pl.BlockSpec((step, 128), lambda i: (i, 0)),
            pl.BlockSpec((keys, 128), lambda i: (0, 0)),
            pl.BlockSpec((keys, 128), lambda i: (0, 0)),
        ],
        compiler_params=pltpu.CompilerParams(vmem_limit_bytes=48 * 1024 * 1024),
        name="attend_backward",
    )(q, k, v, da, lse_rows, pos_q, pos_k)


def pack_heads(weight):
    rows = weight.shape[0]
    split = weight.reshape(rows, 8, 2, 2, 32)
    return split.transpose(1, 0, 3, 2, 4).reshape(8, rows, 128)


def unpack_heads(packed):
    rows = packed.shape[1]
    split = packed.reshape(8, rows, 2, 2, 32)
    return split.transpose(1, 0, 3, 2, 4).reshape(rows, 1024)


def pack_values(weight):
    rows = weight.shape[0]
    return weight.reshape(rows, 8, 128).transpose(1, 0, 2)


def unpack_values(packed):
    return packed.transpose(1, 0, 2).reshape(packed.shape[1], 1024)


def pack_units(weight, width):
    rows, units = weight.shape
    each = units // 32
    split = weight.reshape(rows, 2, 8, 2, each).transpose(2, 0, 1, 3, 4).reshape(8, rows, 4 * each)
    return jnp.pad(split, ((0, 0), (0, 0), (0, width - 4 * each)))


def unpack_units(packed, units):
    rows = packed.shape[1]
    each = units // 32
    split = packed[:, :, : 4 * each].reshape(8, rows, 2, 2, each)
    return split.transpose(1, 2, 0, 3, 4).reshape(rows, units)


def pair_rope(values, cosine, sine):
    first, second = values[:, :64], values[:, 64:]
    return jnp.concatenate(
        [first * cosine - second * sine, second * cosine + first * sine], axis=-1
    )


def pair_unrope(values, cosine, sine):
    first, second = values[:, :64], values[:, 64:]
    return jnp.concatenate(
        [first * cosine + second * sine, second * cosine - first * sine], axis=-1
    )


def swap_cores(value):
    return lax.ppermute(value, "ctx", [(i, i + 1 - 2 * (i % 2)) for i in range(16)])


def fast_local(tokens, cotangent, pair_of, *shards):
    width = tokens.shape[2]
    units = shards[6].shape[1]
    hidden_pad = (units // 8 + 127) // 128 * 128
    c = lax.axis_index("ctx")
    core = c % 2
    chip = c // 2
    pos_all = storage_positions(pair_of, ROWS).reshape(8, 2, ROWS)
    own_pos = lax.dynamic_index_in_dim(pos_all, core, 1, False).reshape(-1)
    sib_pos = lax.dynamic_index_in_dim(pos_all, 1 - core, 1, False).reshape(-1)
    key_pos = jnp.concatenate([own_pos, sib_pos])
    cosine, sine = rope_tables(own_pos, HD)
    cosine = jnp.concatenate([cosine, cosine], axis=-1)
    sine = jnp.concatenate([sine, sine], axis=-1)

    layers = [shards[:9], shards[9:]]
    gains = lax.all_gather(
        jnp.stack([shards[0], shards[5], shards[9], shards[14]]), ("fsdp", "ctx"), axis=1, tiled=True
    ).astype(F32)
    gains = [gains[i : i + 1] for i in range(4)]
    packs = []
    for layer in layers:
        packs.append(
            jnp.concatenate(
                [
                    pack_heads(layer[1]),
                    pack_heads(layer[2]),
                    pack_values(layer[3]),
                    pack_units(layer[6], hidden_pad),
                    pack_units(layer[7], hidden_pad),
                ],
                axis=-1,
            )
        )
    packed = jnp.stack(packs, axis=1)
    rows_each = packed.shape[2]
    wide = packed.shape[3]
    packed = jnp.repeat(packed, 2, axis=0)
    got = lax.all_to_all(packed, "ctx", 0, 0, tiled=True)
    got = lax.all_gather(got, "fsdp", axis=0, tiled=True)
    got = got.transpose(1, 0, 2, 3).reshape(2, 32 * rows_each, wide)
    qkv_w = [got[i, :, :384] for i in range(2)]
    up_w = [got[i, :, 384:] for i in range(2)]
    down = jnp.stack([layers[0][8], layers[1][8]])
    down = jnp.stack([down, swap_cores(down)])
    down = lax.dynamic_slice_in_dim(jnp.concatenate([down, down]), core, 2, 0)
    down = lax.all_gather(down, "fsdp", axis=0, tiled=False)
    down = down.transpose(2, 0, 1, 3, 4).reshape(2, -1, width)
    down = jnp.pad(down, ((0, 0), (0, hidden_pad - down.shape[1]), (0, 0)))
    down_w = [down[0], down[1]]
    outs = lax.all_gather(
        jnp.stack([layers[0][4], layers[1][4]]), ("fsdp", "ctx"), axis=1, tiled=True
    )
    outs = lax.dynamic_slice_in_dim(outs, chip * 128, 128, 1)
    out_w = [outs[0], outs[1]]

    tok = tokens.reshape(ROWS, width)
    cot = cotangent.reshape(ROWS, width)
    plane = 8 * ROWS
    full_type = ((plane, width), BF)
    rows_type = ((ROWS, width), F32)
    saved = []
    (full,) = comm_call(start_kernel, [full_type], 0, (tok, gains[0]), False, True)
    hidden = tok
    first_values = None
    pos_q = own_pos[:, None]
    pos_k = key_pos[None, :]
    for layer in range(2):
        x_full = full
        raw = jnp.dot(x_full, qkv_w[layer], preferred_element_type=F32)
        values = raw[:, 256:]
        mixed = values if layer == 0 else 0.5 * values + 0.5 * first_values
        first_values = values
        q = pair_rope(raw[:, :128], cosine, sine).astype(BF)
        kv = jnp.concatenate(
            [pair_rope(raw[:, 128:256], cosine, sine).astype(BF), mixed.astype(BF)], axis=-1
        )
        kv = jnp.concatenate([kv, swap_cores(kv)], axis=0)
        k, v = kv[:, :128], kv[:, 128:]
        att, lse = attend_forward(q, k, v, pos_q, pos_k)
        middle, mlp_full = comm_call(
            forward_kernel, [rows_type, full_type], 1 + layer,
            (att, out_w[layer], hidden, gains[2 * layer + 1]), True, True,
        )
        both = jnp.dot(mlp_full, up_w[layer], preferred_element_type=F32)
        gate, up = both[:, :hidden_pad], both[:, hidden_pad:]
        inner = (jax.nn.silu(gate) * up).astype(BF)
        saved.append((x_full, q, k, v, lse, att, mlp_full, gate, up, inner, hidden, middle))
        if layer == 0:
            hidden, full = comm_call(
                forward_kernel, [rows_type, full_type], 3,
                (inner, down_w[layer], middle, gains[2]), True, True,
            )
        else:
            output, full = comm_call(
                turn_kernel, [((ROWS, width), BF), full_type], 4,
                (inner, down_w[layer], middle, cot), True, True,
            )
    grad = cot
    passed = None
    grad_packs = [None, None]
    grad_down = [None, None]
    grad_out = [None, None]
    gain_grads = [None] * 4
    for layer in (1, 0):
        x_full, q, k, v, lse, att, mlp_full, gate, up, inner, hidden, middle = saved[layer]
        grad_down[layer] = left_product(inner, full)
        grad_inner = right_product(full, down_w[layer])
        sigma = jax.nn.sigmoid(gate)
        grad_gate = (grad_inner * up * sigma * (1.0 + gate * (1.0 - sigma))).astype(BF)
        grad_up = (grad_inner * gate * sigma).astype(BF)
        both = jnp.concatenate([grad_gate, grad_up], axis=-1)
        grad_upw = left_product(mlp_full, both)
        grad_mid, gain_grads[2 * layer + 1], full = comm_call(
            back_kernel, [rows_type, ((1, width), F32), full_type], 5 + layer,
            (both, up_w[layer], grad, middle, gains[2 * layer + 1]), True, True,
        )
        grad_out[layer] = left_product(att, full)
        grad_att = right_product(full, out_w[layer]).astype(BF)
        dq, dk, dv = attend_backward(q, k, v, grad_att, lse.T, own_pos[None, :], key_pos[:, None])
        dkv = jnp.concatenate([dk, dv], axis=-1)
        dkv = dkv[: 8 * ROWS] + swap_cores(dkv[8 * ROWS :].astype(BF)).astype(F32)
        dk, dv = dkv[:, :128], dkv[:, 128:]
        if layer == 1:
            passed = 0.5 * dv
            dv = passed
        else:
            dv = dv + passed
        three = jnp.concatenate(
            [pair_unrope(dq, cosine, sine), pair_unrope(dk, cosine, sine), dv], axis=-1
        ).astype(BF)
        grad_qkv = left_product(x_full, three)
        grad_packs[layer] = jnp.concatenate([grad_qkv, grad_upw], axis=-1)
        if layer == 1:
            grad, gain_grads[2], full = comm_call(
                back_kernel, [rows_type, ((1, width), F32), full_type], 7,
                (three, qkv_w[layer], grad_mid, hidden, gains[2]), True, True,
            )
        else:
            tokens_grad, gain_grads[0] = comm_call(
                last_kernel, [((ROWS, width), BF), ((1, width), F32)], 8,
                (three, qkv_w[layer], grad_mid, hidden, gains[0]), True, False,
            )
    sent = jnp.stack(grad_packs).astype(BF).reshape(2, 32, rows_each, wide).transpose(1, 0, 2, 3)
    back = lax.all_to_all(sent, ("fsdp", "ctx"), 0, 0, tiled=True)
    back = back.reshape(2, 8, 2, 2, rows_each, wide).astype(F32).sum(axis=(0, 2))
    each = units // 32
    downs = jnp.stack(grad_down)[:, : 4 * each].reshape(2, 2, 2, each, width)
    downs = lax.psum_scatter(downs, "fsdp", scatter_dimension=1, tiled=False)
    own = lax.dynamic_index_in_dim(downs, core, 1, False)
    other = lax.dynamic_index_in_dim(downs, 1 - core, 1, False)
    downs = own + swap_cores(other)
    wide_out = jnp.zeros((2, 1024, width), F32)
    wide_out = lax.dynamic_update_slice_in_dim(wide_out, jnp.stack(grad_out), chip * 128, 1)
    outs = lax.psum_scatter(wide_out, ("fsdp", "ctx"), scatter_dimension=1, tiled=True)
    gg = lax.psum_scatter(
        jnp.concatenate(gain_grads), ("fsdp", "ctx"), scatter_dimension=1, tiled=True
    )
    result = [output.reshape(1, ROWS, width), tokens_grad.reshape(1, ROWS, width)]
    for layer in range(2):
        pack = back[:, layer]
        result += [
            gg[2 * layer],
            unpack_heads(pack[:, :, :128]),
            unpack_heads(pack[:, :, 128:256]),
            unpack_values(pack[:, :, 256:384]),
            outs[layer],
            gg[2 * layer + 1],
            unpack_units(pack[:, :, 384 : 384 + hidden_pad], units),
            unpack_units(pack[:, :, 384 + hidden_pad :], units),
            downs[layer],
        ]
    return tuple(result)


def solution(mesh):
    placed = (
        P("fsdp", "ctx", None),
        P("fsdp", "ctx", None),
        P(),
        P(("fsdp", "ctx")),
        P(("fsdp", "ctx"), None),
        P(("fsdp", "ctx"), None),
        P(("fsdp", "ctx"), None),
        P(("fsdp", "ctx"), None),
        P(("fsdp", "ctx")),
        P(("fsdp", "ctx"), None),
        P(("fsdp", "ctx"), None),
        P(("fsdp", "ctx"), None),
        P(("fsdp", "ctx")),
        P(("fsdp", "ctx"), None),
        P(("fsdp", "ctx"), None),
        P(("fsdp", "ctx"), None),
        P(("fsdp", "ctx"), None),
        P(("fsdp", "ctx")),
        P(("fsdp", "ctx"), None),
        P(("fsdp", "ctx"), None),
        P(("fsdp", "ctx"), None),
    )
    fits = mesh.shape["ctx"] == HEADS and mesh.shape["fsdp"] == 2
    return jax.shard_map(
        fast_local if fits else local,
        mesh=mesh,
        in_specs=placed,
        out_specs=(
            P("fsdp", "ctx", None),
            P("fsdp", "ctx", None),
            P(("fsdp", "ctx")),
            P(("fsdp", "ctx"), None),
            P(("fsdp", "ctx"), None),
            P(("fsdp", "ctx"), None),
            P(("fsdp", "ctx"), None),
            P(("fsdp", "ctx")),
            P(("fsdp", "ctx"), None),
            P(("fsdp", "ctx"), None),
            P(("fsdp", "ctx"), None),
            P(("fsdp", "ctx")),
            P(("fsdp", "ctx"), None),
            P(("fsdp", "ctx"), None),
            P(("fsdp", "ctx"), None),
            P(("fsdp", "ctx"), None),
            P(("fsdp", "ctx")),
            P(("fsdp", "ctx"), None),
            P(("fsdp", "ctx"), None),
            P(("fsdp", "ctx"), None),
        ),
        check_vma=False,
    )
```

```python
import math

import jax
import jax.numpy as jnp
from jax import lax
from jax.experimental import pallas as pl
from jax.experimental.pallas import tpu as pltpu
from jax.sharding import PartitionSpec as P

HEADS = 16
HD = 64


NORM_EPS = 1e-05
NEG_FILL = -1e30


def block_size(total_rows):
    size_now = 512
    while total_rows % size_now:
        size_now //= 2
    return size_now


def row_norm(hidden):
    inverse = lax.rsqrt(jnp.mean(hidden * hidden, axis=-1, keepdims=True) + NORM_EPS)
    return (hidden * inverse, inverse)


def norm_back(grad_normed, normed, inverse):
    return inverse * (grad_normed - normed * jnp.mean(grad_normed * normed, axis=-1, keepdims=True))


def rope_tables(positions, head_size):
    half_size = head_size // 2
    freqs = jnp.exp(
        jnp.arange(half_size, dtype=jnp.float32) * (-2.0 * math.log(10000.0) / head_size)
    )
    angles = positions.astype(jnp.float32)[:, None] * freqs[None, :]
    return (jnp.cos(angles), jnp.sin(angles))


def rotate(values_in, cosine, sine):
    half_size = values_in.shape[-1] // 2
    first_half = values_in[..., :half_size]
    second_half = values_in[..., half_size:]
    cos_rows = cosine[:, None, :]
    sin_rows = sine[:, None, :]
    return jnp.concatenate(
        [
            first_half * cos_rows - second_half * sin_rows,
            second_half * cos_rows + first_half * sin_rows,
        ],
        axis=-1,
    )


def unrotate(grads_in, cosine, sine):
    half_size = grads_in.shape[-1] // 2
    first_half = grads_in[..., :half_size]
    second_half = grads_in[..., half_size:]
    cos_rows = cosine[:, None, :]
    sin_rows = sine[:, None, :]
    return jnp.concatenate(
        [
            first_half * cos_rows + second_half * sin_rows,
            second_half * cos_rows - first_half * sin_rows,
        ],
        axis=-1,
    )


def left_product(left, right):
    return lax.dot_general(
        left, right, (((0,), (0,)), ((), ())), preferred_element_type=jnp.float32
    )


def right_product(left, right):
    return lax.dot_general(
        left, right, (((1,), (1,)), ((), ())), preferred_element_type=jnp.float32
    )


def storage_positions(pair_of, seq_dev):
    devices = pair_of.shape[0]
    rows_all = jnp.arange(devices * seq_dev, dtype=jnp.int32)
    owner = rows_all // seq_dev
    local_row = rows_all % seq_dev
    half_rows = seq_dev // 2
    picked = jnp.sum(
        jnp.where(
            owner[:, None] == jnp.arange(devices, dtype=jnp.int32)[None, :], pair_of[None, :], 0
        ),
        axis=1,
    )
    block_id = jnp.where(local_row < half_rows, picked, 2 * devices - 1 - picked)
    return block_id * half_rows + local_row % half_rows


def head_scores(queries, keys_flat, query_pos, key_pos):
    key_heads = keys_flat.reshape(keys_flat.shape[0], queries.shape[1], queries.shape[2])
    scores = jnp.einsum(
        "qhd,khd->hqk", queries, key_heads, preferred_element_type=jnp.float32
    ) * queries.shape[2] ** (-0.5)
    allowed = (key_pos[None, :] <= query_pos[:, None])[None]
    return (jnp.where(allowed, scores, NEG_FILL), allowed)


def make_stats_step(queries, query_pos, pos_all, state_in, key_part):
    size_now = block_size(key_part.shape[0])

    def inner_step(block_no, state_now):
        top_now, total_now = state_now
        offset = block_no * size_now
        key_block = lax.dynamic_slice_in_dim(key_part, offset, size_now, 0)
        key_pos = lax.dynamic_slice_in_dim(pos_all, offset, size_now, 0)
        scores, allowed = head_scores(queries, key_block, query_pos, key_pos)
        new_top = jnp.maximum(top_now, jnp.max(scores, axis=-1))
        total_now = total_now * jnp.exp(top_now - new_top) + jnp.sum(
            jnp.where(allowed, jnp.exp(scores - new_top[..., None]), 0.0), axis=-1
        )
        return (new_top, total_now)

    return lax.fori_loop(0, key_part.shape[0] // size_now, inner_step, state_in)


def make_value_step(queries, log_total, query_pos, pos_all, acc_in, pieces):
    key_part, value_part = pieces
    size_now = block_size(key_part.shape[0])

    def inner_step(block_no, acc_now):
        offset = block_no * size_now
        key_block = lax.dynamic_slice_in_dim(key_part, offset, size_now, 0)
        value_block = lax.dynamic_slice_in_dim(value_part, offset, size_now, 0)
        key_pos = lax.dynamic_slice_in_dim(pos_all, offset, size_now, 0)
        scores, allowed = head_scores(queries, key_block, query_pos, key_pos)
        shares = jnp.exp(scores - log_total[..., None]).astype(jnp.bfloat16)
        value_heads = value_block.reshape(size_now, queries.shape[1], queries.shape[2])
        return acc_now + jnp.einsum(
            "hqk,khd->qhd", shares, value_heads, preferred_element_type=jnp.float32
        )

    return lax.fori_loop(0, key_part.shape[0] // size_now, inner_step, acc_in)


def make_back_step(queries, grad_att, log_total, row_delta, query_pos, pos_all):
    scale_now = queries.shape[2] ** (-0.5)

    def back_step(state_in, pieces, start_row):
        key_part, value_part = pieces
        size_now = block_size(key_part.shape[0])

        def inner_step(block_no, state_now):
            offset = block_no * size_now
            key_block = lax.dynamic_slice_in_dim(key_part, offset, size_now, 0)
            value_block = lax.dynamic_slice_in_dim(value_part, offset, size_now, 0)
            key_pos = lax.dynamic_slice_in_dim(pos_all, offset, size_now, 0)
            scores, allowed = head_scores(queries, key_block, query_pos, key_pos)
            shares = jnp.exp(scores - log_total[..., None])
            value_heads = value_block.reshape(size_now, queries.shape[1], queries.shape[2])
            key_heads = key_block.reshape(size_now, queries.shape[1], queries.shape[2])
            grad_shares = jnp.einsum(
                "qhd,khd->hqk", grad_att, value_heads, preferred_element_type=jnp.float32
            )
            grad_scores = (shares * (grad_shares - row_delta[..., None]) * scale_now).astype(
                jnp.bfloat16
            )
            grad_query = state_now[0] + jnp.einsum(
                "hqk,khd->qhd", grad_scores, key_heads, preferred_element_type=jnp.float32
            )
            return (grad_query,)

        return lax.fori_loop(0, key_part.shape[0] // size_now, inner_step, state_in)

    return back_step


def make_query_step(own_keys, own_values, own_pos, stats_all, pos_all, head_count, head_size):
    scale_now = head_size ** (-0.5)
    value_heads = own_values.reshape(own_values.shape[0], head_count, head_size)

    def query_step(state_in, pieces, start_row):
        query_part, grad_part = pieces
        size_now = block_size(query_part.shape[0])

        def inner_step(block_no, state_now):
            offset = block_no * size_now
            query_block = lax.dynamic_slice_in_dim(query_part, offset, size_now, 0).reshape(
                size_now, head_count, head_size
            )
            grad_block = lax.dynamic_slice_in_dim(grad_part, offset, size_now, 0).reshape(
                size_now, head_count, head_size
            )
            query_pos = lax.dynamic_slice_in_dim(pos_all, offset, size_now, 0)
            log_block = lax.dynamic_slice_in_dim(stats_all[0], offset, size_now, 0).T
            delta_block = lax.dynamic_slice_in_dim(stats_all[1], offset, size_now, 0).T
            scores, allowed = head_scores(query_block, own_keys, query_pos, own_pos)
            shares = jnp.exp(scores - log_block[..., None])
            grad_shares = jnp.einsum(
                "qhd,khd->hqk", grad_block, value_heads, preferred_element_type=jnp.float32
            )
            grad_scores = (shares * (grad_shares - delta_block[..., None]) * scale_now).astype(
                jnp.bfloat16
            )
            key_term = jnp.einsum(
                "hqk,qhd->khd", grad_scores, query_block, preferred_element_type=jnp.float32
            )
            value_term = jnp.einsum(
                "hqk,qhd->khd",
                shares.astype(jnp.bfloat16),
                grad_block,
                preferred_element_type=jnp.float32,
            )
            return (
                state_now[0] + key_term.reshape(key_term.shape[0], -1),
                state_now[1] + value_term.reshape(value_term.shape[0], -1),
            )

        return lax.fori_loop(0, query_part.shape[0] // size_now, inner_step, state_in)

    return query_step


def gather_forward(shards):
    return (
        lax.all_gather(shards[0], ("fsdp", "ctx"), axis=0, tiled=True),
        lax.all_gather(shards[1], ("fsdp", "ctx"), axis=0, tiled=True),
        lax.all_gather(shards[2], ("fsdp", "ctx"), axis=0, tiled=True),
        lax.all_gather(shards[3], ("fsdp", "ctx"), axis=0, tiled=True),
        lax.all_gather(shards[4], ("fsdp", "ctx"), axis=0, tiled=True),
        lax.all_gather(shards[5], ("fsdp", "ctx"), axis=0, tiled=True),
        lax.all_gather(shards[6], ("fsdp", "ctx"), axis=0, tiled=True),
        lax.all_gather(shards[7], ("fsdp", "ctx"), axis=0, tiled=True),
        lax.all_gather(shards[8], ("fsdp", "ctx"), axis=0, tiled=True),
    )


def scatter_grads(grad_terms):
    return (
        lax.psum_scatter(grad_terms[0], ("fsdp", "ctx"), scatter_dimension=0, tiled=True),
        lax.psum_scatter(grad_terms[1], ("fsdp", "ctx"), scatter_dimension=0, tiled=True),
        lax.psum_scatter(grad_terms[2], ("fsdp", "ctx"), scatter_dimension=0, tiled=True),
        lax.psum_scatter(grad_terms[3], ("fsdp", "ctx"), scatter_dimension=0, tiled=True),
        lax.psum_scatter(grad_terms[4], ("fsdp", "ctx"), scatter_dimension=0, tiled=True),
        lax.psum_scatter(grad_terms[5], ("fsdp", "ctx"), scatter_dimension=0, tiled=True),
        lax.psum_scatter(grad_terms[6], ("fsdp", "ctx"), scatter_dimension=0, tiled=True),
        lax.psum_scatter(grad_terms[7], ("fsdp", "ctx"), scatter_dimension=0, tiled=True),
        lax.psum_scatter(grad_terms[8], ("fsdp", "ctx"), scatter_dimension=0, tiled=True),
    )


def forward_layer(hidden, full_layer, first_values, context):
    prenorm, query_w, keys_w, values_w, outproj, midnorm, gates_w, upproj_w, downproj_w = full_layer
    cosine, sine, own_pos, pos_all = context
    rows_n, model_width = hidden.shape
    normed, inverse_a = row_norm(hidden)
    attn_in = (normed * prenorm.astype(jnp.float32)).astype(jnp.bfloat16)
    query_raw = jnp.dot(attn_in, query_w, preferred_element_type=jnp.float32)
    keys_raw = jnp.dot(attn_in, keys_w, preferred_element_type=jnp.float32)
    values_raw = jnp.dot(attn_in, values_w, preferred_element_type=jnp.float32)
    mixed = values_raw if first_values is None else 0.5 * values_raw + 0.5 * first_values
    queries = rotate(query_raw.reshape(rows_n, HEADS, HD), cosine, sine).astype(jnp.bfloat16)
    keys_flat = (
        rotate(keys_raw.reshape(rows_n, HEADS, HD), cosine, sine)
        .reshape(rows_n, model_width)
        .astype(jnp.bfloat16)
    )
    values_flat = mixed.astype(jnp.bfloat16)
    top_start = jnp.full((HEADS, rows_n), NEG_FILL, jnp.float32)
    total_start = jnp.zeros((HEADS, rows_n), jnp.float32)
    top_now, total_now = make_stats_step(
        queries,
        own_pos,
        pos_all,
        (top_start, total_start),
        lax.all_gather(keys_flat, "ctx", axis=0, tiled=True),
    )
    log_total = top_now + jnp.log(total_now)
    att_out = make_value_step(
        queries,
        log_total,
        own_pos,
        pos_all,
        jnp.zeros((rows_n, HEADS, HD), jnp.float32),
        (
            lax.all_gather(keys_flat, "ctx", axis=0, tiled=True),
            lax.all_gather(values_flat, "ctx", axis=0, tiled=True),
        ),
    )
    att_low = att_out.reshape(rows_n, model_width).astype(jnp.bfloat16)
    middle = hidden + jnp.dot(att_low, outproj, preferred_element_type=jnp.float32)
    normed_mid, inverse_b = row_norm(middle)
    mlp_in = (normed_mid * midnorm.astype(jnp.float32)).astype(jnp.bfloat16)
    gate_raw = jnp.dot(mlp_in, gates_w, preferred_element_type=jnp.float32)
    up_proj = jnp.dot(mlp_in, upproj_w, preferred_element_type=jnp.float32)
    inner_act = (jax.nn.silu(gate_raw) * up_proj).astype(jnp.bfloat16)
    result = middle + jnp.dot(inner_act, downproj_w, preferred_element_type=jnp.float32)
    saved = (
        hidden,
        normed,
        inverse_a,
        attn_in,
        queries,
        keys_flat,
        values_flat,
        log_total,
        att_out,
        att_low,
        normed_mid,
        inverse_b,
        mlp_in,
        gate_raw,
        up_proj,
        inner_act,
    )
    return (result, values_raw, saved)


def backward_layer(grad_out, full_layer, saved, value_extra, is_second, context):
    prenorm, query_w, keys_w, values_w, outproj, midnorm, gates_w, upproj_w, downproj_w = full_layer
    (
        hidden,
        normed,
        inverse_a,
        attn_in,
        queries,
        keys_flat,
        values_flat,
        log_total,
        att_out,
        att_low,
        normed_mid,
        inverse_b,
        mlp_in,
        gate_raw,
        up_proj,
        inner_act,
    ) = saved
    cosine, sine, own_pos, pos_all = context
    rows_n, model_width = hidden.shape
    grad_low = grad_out.astype(jnp.bfloat16)
    grad_down = left_product(inner_act, grad_low)
    grad_inner = right_product(grad_low, downproj_w)
    sigma_gate = jax.nn.sigmoid(gate_raw)
    grad_gate = (grad_inner * up_proj * sigma_gate * (1.0 + gate_raw * (1.0 - sigma_gate))).astype(
        jnp.bfloat16
    )
    grad_up = (grad_inner * gate_raw * sigma_gate).astype(jnp.bfloat16)
    grad_gates = left_product(mlp_in, grad_gate)
    grad_upproj = left_product(mlp_in, grad_up)
    grad_mlp = right_product(grad_gate, gates_w) + right_product(grad_up, upproj_w)
    grad_midnorm = jnp.sum(grad_mlp * normed_mid, axis=0)
    grad_middle = grad_out + norm_back(
        grad_mlp * midnorm.astype(jnp.float32), normed_mid, inverse_b
    )
    branch_low = grad_middle.astype(jnp.bfloat16)
    grad_outproj = left_product(att_low, branch_low)
    grad_att = right_product(branch_low, outproj).astype(jnp.bfloat16).reshape(rows_n, HEADS, HD)
    row_delta = jnp.sum(grad_att.astype(jnp.float32) * att_out, axis=-1).T
    query_start = jnp.zeros((rows_n, HEADS, HD), jnp.float32)
    state_start = (query_start,)
    back_fn = make_back_step(queries, grad_att, log_total, row_delta, own_pos, pos_all)
    state_out = back_fn(
        state_start,
        (
            lax.all_gather(keys_flat, "ctx", axis=0, tiled=True),
            lax.all_gather(values_flat, "ctx", axis=0, tiled=True),
        ),
        jnp.int32(0),
    )
    grad_qr = state_out[0]
    stats_all = (
        lax.all_gather(log_total.T, "ctx", axis=0, tiled=True),
        lax.all_gather(row_delta.T, "ctx", axis=0, tiled=True),
    )
    query_fn = make_query_step(keys_flat, values_flat, own_pos, stats_all, pos_all, HEADS, HD)
    flat_start = jnp.zeros((rows_n, model_width), jnp.float32)
    grad_kr, grad_mix = query_fn(
        (flat_start, flat_start),
        (
            lax.all_gather(queries.reshape(rows_n, model_width), "ctx", axis=0, tiled=True),
            lax.all_gather(grad_att.reshape(rows_n, model_width), "ctx", axis=0, tiled=True),
        ),
        jnp.int32(0),
    )
    grad_query = unrotate(grad_qr, cosine, sine).reshape(rows_n, model_width).astype(jnp.bfloat16)
    grad_keys = (
        unrotate(grad_kr.reshape(rows_n, HEADS, HD), cosine, sine)
        .reshape(rows_n, model_width)
        .astype(jnp.bfloat16)
    )
    if is_second:
        grad_values = (0.5 * grad_mix).astype(jnp.bfloat16)
        passed_on = 0.5 * grad_mix
    else:
        grad_values = (grad_mix + value_extra).astype(jnp.bfloat16)
        passed_on = None
    grad_query_w = left_product(attn_in, grad_query)
    grad_keys_w = left_product(attn_in, grad_keys)
    grad_values_w = left_product(attn_in, grad_values)
    grad_attn = (
        right_product(grad_query, query_w)
        + right_product(grad_keys, keys_w)
        + right_product(grad_values, values_w)
    )
    grad_prenorm = jnp.sum(grad_attn * normed, axis=0)
    grad_hidden = grad_middle + norm_back(
        grad_attn * prenorm.astype(jnp.float32), normed, inverse_a
    )
    grad_terms = (
        grad_prenorm,
        grad_query_w,
        grad_keys_w,
        grad_values_w,
        grad_outproj,
        grad_midnorm,
        grad_gates,
        grad_upproj,
        grad_down,
    )
    return (grad_hidden, grad_terms, passed_on)


def local(
    tokens,
    cotangent,
    pair_of,
    prenorm_one,
    query_one,
    keys_one,
    values_one,
    outproj_one,
    midnorm_one,
    gates_one,
    upproj_one,
    downproj_one,
    prenorm_two,
    query_two,
    keys_two,
    values_two,
    outproj_two,
    midnorm_two,
    gates_two,
    upproj_two,
    downproj_two,
):
    seq_dev = tokens.shape[1]
    model_width = tokens.shape[2]
    pos_all = storage_positions(pair_of, seq_dev)
    own_pos = lax.dynamic_slice_in_dim(pos_all, lax.axis_index("ctx") * seq_dev, seq_dev, 0)
    cosine, sine = rope_tables(own_pos, HD)
    context = (cosine, sine, own_pos, pos_all)
    layer_shards = [
        (
            prenorm_one,
            query_one,
            keys_one,
            values_one,
            outproj_one,
            midnorm_one,
            gates_one,
            upproj_one,
            downproj_one,
        ),
        (
            prenorm_two,
            query_two,
            keys_two,
            values_two,
            outproj_two,
            midnorm_two,
            gates_two,
            upproj_two,
            downproj_two,
        ),
    ]
    hidden = tokens.reshape(seq_dev, model_width).astype(jnp.float32)
    first_values = None
    kept_full = []
    kept_saved = []
    for layer_no in range(2):
        full_layer = gather_forward(layer_shards[layer_no])
        hidden, values_raw, saved = forward_layer(hidden, full_layer, first_values, context)
        if layer_no == 0:
            first_values = values_raw
        kept_full.append(full_layer)
        kept_saved.append(saved)
    output = hidden.astype(jnp.bfloat16).reshape(1, seq_dev, model_width)
    grad_now = cotangent.reshape(seq_dev, model_width).astype(jnp.float32)
    value_extra = None
    layer_grads = [None, None]
    for layer_no in (1, 0):
        full_layer = kept_full[layer_no]
        grad_now, grad_terms, passed_on = backward_layer(
            grad_now, full_layer, kept_saved[layer_no], value_extra, layer_no == 1, context
        )
        if layer_no == 1:
            value_extra = passed_on
        layer_grads[layer_no] = scatter_grads(grad_terms)
    tokens_grad = grad_now.astype(jnp.bfloat16).reshape(1, seq_dev, model_width)
    first_grads = layer_grads[0]
    second_grads = layer_grads[1]
    return (
        output,
        tokens_grad,
        first_grads[0],
        first_grads[1],
        first_grads[2],
        first_grads[3],
        first_grads[4],
        first_grads[5],
        first_grads[6],
        first_grads[7],
        first_grads[8],
        second_grads[0],
        second_grads[1],
        second_grads[2],
        second_grads[3],
        second_grads[4],
        second_grads[5],
        second_grads[6],
        second_grads[7],
        second_grads[8],
    )


ROWS = 128
BF = jnp.bfloat16
F32 = jnp.float32
MESH = pl.DeviceIdType.MESH
VMEM_SPACE = pltpu.VMEM


def flip(value, weight):
    return value + weight * (1 - 2 * ((value // weight) % 2))


def to_device(f, c):
    return {"fsdp": f, "ctx": c}


def remote(src, dst, send_sem, recv_sem, target):
    return pltpu.make_async_remote_copy(
        src_ref=src,
        dst_ref=dst,
        send_sem=send_sem,
        recv_sem=recv_sem,
        device_id=to_device(*target),
        device_id_type=MESH,
    )


def plane_place():
    f = lax.axis_index("fsdp")
    c = lax.axis_index("ctx")
    return f, c, (c // 2) % 2, c // 4


def greet_plane(f, c, z):
    barrier = pltpu.get_barrier_semaphore()

    def hello(target):
        pl.semaphore_signal(barrier, inc=1, device_id=to_device(*target), device_id_type=MESH)

    hello((f, flip(c, 2)))

    @pl.when(z > 0)
    def _():
        hello((f, c - 4))

    @pl.when(z < 3)
    def _():
        hello((f, c + 4))

    pl.semaphore_wait(barrier, 2 + jnp.where((z > 0) & (z < 3), 1, 0))


def send_order(z, step):
    table = ((3, 2, 1, 0), (3, 0, 2, 1), (0, 3, 1, 2), (0, 1, 2, 3))
    column = [row[step] for row in table]
    return jnp.where(
        z == 0, column[0], jnp.where(z == 1, column[1], jnp.where(z == 2, column[2], column[3]))
    )


def reduce_plane(place, product, bufs, sems):
    f, c, y, z = place
    sy, ry, acc, su, ru, sd, rd = bufs
    ys, yr, us, ur, ds, dr = sems
    across = (f, flip(c, 2))
    above = (f, c + 4)
    below = (f, c - 4)

    def y_copy(block):
        return remote(sy.at[block], ry.at[block], ys.at[block], yr.at[block], across)

    def up_copy(block):
        return remote(su.at[block], ru.at[block], us.at[block], ur.at[block], above)

    def down_copy(block):
        return remote(sd.at[block], rd.at[block], ds.at[block], dr.at[block], below)

    for step in range(4):
        block = send_order(z, step)
        sy[block] = product(block * 2 + (1 - y)).astype(BF)
        y_copy(block).start()
    for block in range(4):
        acc[block] = product(block * 2 + y)
    for k in range(3):
        top = 3 - k

        @pl.when(top > z)
        def _():
            y_copy(top).wait_recv()
            acc[top] += ry[top].astype(F32)

            @pl.when(z > 0)
            def _():
                up_copy(top).wait_recv()
                acc[top] += ru[top].astype(F32)

            su[top] = acc[top].astype(BF)
            up_copy(top).start()

        @pl.when(k < z)
        def _():
            y_copy(k).wait_recv()
            acc[k] += ry[k].astype(F32)

            @pl.when(z < 3)
            def _():
                down_copy(k).wait_recv()
                acc[k] += rd[k].astype(F32)

            sd[k] = acc[k].astype(BF)
            down_copy(k).start()

    y_copy(z).wait_recv()
    acc[z] += ry[z].astype(F32)

    @pl.when(z > 0)
    def _():
        up_copy(z).wait_recv()
        acc[z] += ru[z].astype(F32)

    @pl.when(z < 3)
    def _():
        down_copy(z).wait_recv()
        acc[z] += rd[z].astype(F32)

    def finish():
        for block in range(4):
            y_copy(block).wait_send()
        for k in range(3):

            @pl.when(3 - k > z)
            def _():
                up_copy(3 - k).wait_send()

            @pl.when(k < z)
            def _():
                down_copy(k).wait_send()

    return finish


def gather_plane(place, full, sems):
    f, c, y, z = place
    ys, yr, us, ur, ds, dr = sems
    across = (f, flip(c, 2))
    above = (f, c + 4)
    below = (f, c - 4)

    def rows(block, side):
        return full.at[pl.ds(pl.multiple_of((block * 2 + side) * ROWS, ROWS), ROWS)]

    def y_copy(block):
        return remote(rows(block, y), rows(block, y), ys.at[block], yr.at[block], across)

    def up_copy(block):
        return remote(rows(block, y), rows(block, y), us.at[block], ur.at[block], above)

    def down_copy(block):
        return remote(rows(block, y), rows(block, y), ds.at[block], dr.at[block], below)

    @pl.when(z < 3)
    def _():
        up_copy(z).start()

    @pl.when(z > 0)
    def _():
        down_copy(z).start()

    y_copy(z).start()
    for k in range(1, 4):

        @pl.when(z >= k)
        def _():
            up_copy(z - k).wait_recv()

            @pl.when(z < 3)
            def _():
                up_copy(z - k).start()

            y_copy(z - k).start()

        @pl.when(z + k <= 3)
        def _():
            down_copy(z + k).wait_recv()

            @pl.when(z > 0)
            def _():
                down_copy(z + k).start()

            y_copy(z + k).start()

    for block in range(4):
        y_copy(block).wait()
    for k in range(4):

        @pl.when((z < 3) & (z >= k))
        def _():
            up_copy(z - k).wait_send()

        @pl.when((z > 0) & (z + k <= 3))
        def _():
            down_copy(z + k).wait_send()


def norm_rows(hidden):
    return lax.rsqrt(jnp.mean(hidden * hidden, axis=-1, keepdims=True) + NORM_EPS)


def own_rows(place):
    _, _, y, z = place
    return pl.ds(pl.multiple_of((z * 2 + y) * ROWS, ROWS), ROWS)


def make_product(left_ref, right_ref, transposed):
    dims = (((1,), (1,)), ((), ())) if transposed else (((1,), (0,)), ((), ()))

    def product(block):
        rows = left_ref[pl.ds(pl.multiple_of(block * ROWS, ROWS), ROWS), :]
        return lax.dot_general(rows, right_ref[...], dims, preferred_element_type=F32)

    return product


def start_kernel(hid_ref, gain_ref, full_ref, *sems):
    place = plane_place()
    greet_plane(place[0], place[1], place[3])
    hidden = hid_ref[...].astype(F32)
    full_ref[own_rows(place), :] = (hidden * norm_rows(hidden) * gain_ref[...]).astype(BF)
    gather_plane(place, full_ref, sems)


def forward_kernel(left_ref, right_ref, res_ref, gain_ref, new_ref, full_ref, *scratch):
    place = plane_place()
    greet_plane(place[0], place[1], place[3])
    bufs, sems, more = scratch[:7], scratch[7:13], scratch[13:]
    finish = reduce_plane(place, make_product(left_ref, right_ref, False), bufs, sems)
    hidden = res_ref[...].astype(F32) + bufs[2][place[3]]
    new_ref[...] = hidden
    full_ref[own_rows(place), :] = (hidden * norm_rows(hidden) * gain_ref[...]).astype(BF)
    gather_plane(place, full_ref, more)
    finish()


def turn_kernel(left_ref, right_ref, res_ref, cot_ref, out_ref, full_ref, *scratch):
    place = plane_place()
    greet_plane(place[0], place[1], place[3])
    bufs, sems, more = scratch[:7], scratch[7:13], scratch[13:]
    finish = reduce_plane(place, make_product(left_ref, right_ref, False), bufs, sems)
    out_ref[...] = (res_ref[...] + bufs[2][place[3]]).astype(BF)
    full_ref[own_rows(place), :] = cot_ref[...]
    gather_plane(place, full_ref, more)
    finish()


def back_rows(total, grad, hidden, gain):
    inverse = norm_rows(hidden)
    normed = hidden * inverse
    scaled = total * gain
    mean = jnp.mean(scaled * normed, axis=-1, keepdims=True)
    return grad + inverse * (scaled - normed * mean)


def back_kernel(left_ref, right_ref, grad_ref, hid_ref, gain_ref, new_ref, full_ref, *scratch):
    place = plane_place()
    greet_plane(place[0], place[1], place[3])
    bufs, sems, more = scratch[:7], scratch[7:13], scratch[13:]
    finish = reduce_plane(place, make_product(left_ref, right_ref, True), bufs, sems)
    new = back_rows(
        bufs[2][place[3]], grad_ref[...].astype(F32), hid_ref[...].astype(F32), gain_ref[...]
    )
    new_ref[...] = new
    full_ref[own_rows(place), :] = new.astype(BF)
    gather_plane(place, full_ref, more)
    finish()


def last_kernel(left_ref, right_ref, grad_ref, hid_ref, gain_ref, out_ref, *scratch):
    place = plane_place()
    greet_plane(place[0], place[1], place[3])
    bufs, sems = scratch[:7], scratch[7:13]
    finish = reduce_plane(place, make_product(left_ref, right_ref, True), bufs, sems)
    new = back_rows(
        bufs[2][place[3]], grad_ref[...].astype(F32), hid_ref[...].astype(F32), gain_ref[...]
    )
    out_ref[...] = new.astype(BF)
    finish()


def comm_call(kernel, outs, ident, args, reduces, gathers):
    width = 1024
    scratch = []
    if reduces:
        for kind in (BF, BF, F32, BF, BF, BF, BF):
            scratch.append(pltpu.VMEM((4, ROWS, width), kind))
        scratch += [pltpu.SemaphoreType.DMA((4,))] * 6
    if gathers:
        scratch += [pltpu.SemaphoreType.DMA((4,))] * 6
    spec = pl.BlockSpec(memory_space=VMEM_SPACE)
    return pl.pallas_call(
        kernel,
        out_shape=[jax.ShapeDtypeStruct(*o) for o in outs],
        in_specs=[spec] * len(args),
        out_specs=[spec] * len(outs),
        scratch_shapes=scratch,
        compiler_params=pltpu.CompilerParams(
            collective_id=ident, has_side_effects=True, vmem_limit_bytes=40 * 1024 * 1024
        ),
        name=kernel.__name__,
    )(*args)


def chip_peers(f, c):
    chip, core = c // 2, c % 2
    return [(f, 2 * ((chip + i) % 8) + core) for i in range(1, 8)], (f, flip(c, 1)), (1 - f, c)


def greet(targets):
    barrier = pltpu.get_barrier_semaphore()
    for target in targets:
        pl.semaphore_signal(barrier, inc=1, device_id=to_device(*target), device_id_type=MESH)
    pl.semaphore_wait(barrier, len(targets))


def spread_kernel(a1, a2, dn, op, r1, r2, d1, d2, o1, o2, *sems):
    f, c, y, z = plane_place()
    chip, core = c // 2, c % 2
    peers, sibling, twin = chip_peers(f, c)
    near = (f, flip(c, 2))
    greet(peers + [sibling, twin])
    ds, dr, xs, xr, ss, sr, ws, wr = sems
    mine = f * 16 + c
    tables = ((a1, r1), (a2, r2))
    downs = (d1, d2)
    outs = (o1, o2)
    home = y == f
    pending = []

    def send(src, dst, send_sem, recv_sem, target):
        copy = remote(src, dst, send_sem, recv_sem, target)
        copy.start()
        pending.append(copy)
        return copy

    direct = {}
    crossed = {}
    inner = []
    for l, (a, r) in enumerate(tables):
        for i in range(1, 8):
            t = (chip + i) % 8
            direct[l, i] = send(a.at[t], r.at[mine], ds.at[l, i], dr.at[l, i], peers[i - 1])
        r[mine] = a[chip]
        crossed[l, 0] = send(a.at[chip], r.at[mine], xs.at[l, 0], xr.at[l, 0], twin)
        inner.append(send(a.at[chip], r.at[mine], ss.at[l, 0], sr.at[l, 0], sibling))
        part = 2 * f + core
        downs[l][part] = dn[l]
        crossed[l, 8] = send(dn.at[l], downs[l].at[part], xs.at[l, 8], xr.at[l, 8], twin)
        inner.append(send(dn.at[l], downs[l].at[part], ss.at[l, 16], sr.at[l, 16], sibling))

        def out_copy():
            return remote(op.at[l], outs[l].at[2 * y + core], ws.at[l, 0], wr.at[l, 0], near)

        @pl.when(home)
        def _():
            outs[l][2 * y + core] = op[l]

        @pl.when(jnp.logical_not(home))
        def _():
            out_copy().start()

    for l, (a, r) in enumerate(tables):
        for i in range(1, 8):
            direct[l, i].wait_recv()
            source = f * 16 + 2 * ((chip + 8 - i) % 8) + core
            crossed[l, i] = send(r.at[source], r.at[source], xs.at[l, i], xr.at[l, i], twin)
            inner.append(send(r.at[source], r.at[source], ss.at[l, i], sr.at[l, i], sibling))

    def pair(l):
        return [outs[l].at[core], outs[l].at[2 + core]]

    def pair_copies(l, s, r, first, target):
        return [remote(p, p, s.at[l, first + n], r.at[l, first + n], target) for n, p in enumerate(pair(l))]

    for l in range(2):

        @pl.when(home)
        def _():
            remote(op.at[l], outs[l].at[2 * y + core], ws.at[l, 0], wr.at[l, 0], near).wait_recv()
            for copy in pair_copies(l, xs, xr, 9, twin):
                copy.start()

        @pl.when(jnp.logical_not(home))
        def _():
            for copy in pair_copies(l, xs, xr, 9, twin):
                copy.wait_recv()

        for copy in pair_copies(l, ss, sr, 18, sibling):
            copy.start()

    for l, (a, r) in enumerate(tables):
        for i in range(8):
            crossed[l, i].wait_recv()
            source = (1 - f) * 16 + 2 * ((chip + 8 - i) % 8) + core
            inner.append(send(r.at[source], r.at[source], ss.at[l, 8 + i], sr.at[l, 8 + i], sibling))
        crossed[l, 8].wait_recv()
        part = 2 * (1 - f) + core
        inner.append(
            send(downs[l].at[part], downs[l].at[part], ss.at[l, 17], sr.at[l, 17], sibling)
        )
    for copy in inner:
        copy.wait_recv()
    for copy in pending:
        copy.wait_send()
    for l in range(2):
        for copy in pair_copies(l, ss, sr, 18, sibling):
            copy.wait()

        @pl.when(home)
        def _():
            for copy in pair_copies(l, xs, xr, 9, twin):
                copy.wait_send()

        @pl.when(jnp.logical_not(home))
        def _():
            remote(op.at[l], outs[l].at[2 * y + core], ws.at[l, 0], wr.at[l, 0], near).wait_send()


def spread_call(a1, a2, down, out):
    rows, wide = a1.shape[1:]
    block, width = down.shape[1:]
    spec = pl.BlockSpec(memory_space=VMEM_SPACE)
    shapes = [(32, rows, wide)] * 2 + [(4, block, width)] * 2 + [(4, rows, width)] * 2
    counts = (8, 8, 11, 11, 20, 20, 1, 1)
    return pl.pallas_call(
        spread_kernel,
        out_shape=[jax.ShapeDtypeStruct(s, BF) for s in shapes],
        in_specs=[spec] * 4,
        out_specs=[spec] * 6,
        scratch_shapes=[pltpu.SemaphoreType.DMA((2, n)) for n in counts],
        compiler_params=pltpu.CompilerParams(
            collective_id=9, has_side_effects=True, vmem_limit_bytes=40 * 1024 * 1024
        ),
        name="spread",
    )(a1, a2, down, out)


def collect_kernel(g1, g2, gd1, gd2, go1, go2, c1, c2, od1, od2, oo1, oo2, *scratch):
    f, c, y, z = plane_place()
    chip, core = c // 2, c % 2
    peers, sibling, twin = chip_peers(f, c)
    near = (f, flip(c, 2))
    greet(peers + [sibling, twin])
    sb, xb, xt, ut, sd, xd, td, so, xo, to, yo, yt = scratch[:12]
    ss, sr, xs, xr, ps, pr, ys, yr = scratch[12:]
    home = y == f
    pending = []

    def send(src, dst, send_sem, recv_sem, target):
        copy = remote(src, dst, send_sem, recv_sem, target)
        copy.start()
        pending.append(copy)
        return copy

    tables = ((g1, c1, gd1, od1, go1, oo1), (g2, c2, gd2, od2, go2, oo2))
    inner = {}
    for l, (g, _, gd, _, go, _) in enumerate(tables):
        for half in range(2):
            part = 8 * ((1 - f) if half == 0 else f)
            inner[l, half] = send(
                g.at[pl.ds(part, 8), 1 - core], sb.at[l, pl.ds(part, 8)],
                ss.at[l, half], sr.at[l, half], sibling,
            )
        inner[l, 2] = send(gd.at[:, 1 - core], sd.at[l], ss.at[l, 2], sr.at[l, 2], sibling)
        inner[l, 3] = send(go.at[:, 1 - core], so.at[l], ss.at[l, 3], sr.at[l, 3], sibling)
    crossed = {}
    for l, (g, _, gd, _, go, _) in enumerate(tables):
        inner[l, 0].wait_recv()
        for i in range(8):
            t = (chip + i + 1) % 8
            at = (1 - f) * 8 + t
            xt[l, t] = (g[at, core].astype(F32) + sb[l, at].astype(F32)).astype(BF)
            crossed[l, i] = send(xt.at[l, t], xb.at[l, t], xs.at[l, i], xr.at[l, i], twin)
        inner[l, 2].wait_recv()
        td[l] = (gd[1 - f, core].astype(F32) + sd[l, 1 - f].astype(F32)).astype(BF)
        crossed[l, 8] = send(td.at[l], xd.at[l], xs.at[l, 8], xr.at[l, 8], twin)
        inner[l, 3].wait_recv()

        def twin_copy():
            return remote(to.at[l], xo.at[l], xs.at[l, 9], xr.at[l, 9], twin)

        for side in range(2):
            to[l, side] = (go[side, core].astype(F32) + so[l, side].astype(F32)).astype(BF)

        @pl.when(jnp.logical_not(home))
        def _():
            twin_copy().start()

    direct = {}
    for l, (g, out, gd, od, go, oo) in enumerate(tables):
        inner[l, 1].wait_recv()
        for i in range(8):
            t = (chip + i + 1) % 8
            at = f * 8 + t
            crossed[l, i].wait_recv()
            total = g[at, core].astype(F32) + sb[l, at].astype(F32) + xb[l, t].astype(F32)
            if i < 7:
                ut[l, t] = total.astype(BF)
                direct[l, i] = send(ut.at[l, t], out.at[chip], ps.at[l, i], pr.at[l, i], peers[i])
            else:
                out[chip] = total.astype(BF)
        crossed[l, 8].wait_recv()
        od[...] = gd[f, core].astype(F32) + sd[l, f].astype(F32) + xd[l].astype(F32)

        @pl.when(home)
        def _():
            remote(to.at[l], xo.at[l], xs.at[l, 9], xr.at[l, 9], twin).wait_recv()
            oo[...] = to[l, y].astype(F32) + xo[l, y].astype(F32)
            yt[l] = (to[l, 1 - y].astype(F32) + xo[l, 1 - y].astype(F32)).astype(BF)
            remote(yt.at[l], yo.at[l], ys.at[l], yr.at[l], near).start()

    for l, (g, out, gd, od, go, oo) in enumerate(tables):

        @pl.when(home)
        def _():
            remote(yt.at[l], yo.at[l], ys.at[l], yr.at[l], near).wait_send()

        @pl.when(jnp.logical_not(home))
        def _():
            remote(yt.at[l], yo.at[l], ys.at[l], yr.at[l], near).wait_recv()
            oo[...] = yo[l].astype(F32)
            remote(to.at[l], xo.at[l], xs.at[l, 9], xr.at[l, 9], twin).wait_send()

    for copy in direct.values():
        copy.wait_recv()
    for copy in pending:
        copy.wait_send()


def collect_call(packs, downs, outs):
    rows, wide = packs[0].shape[2:]
    block, width = downs[0].shape[2:]
    spec = pl.BlockSpec(memory_space=VMEM_SPACE)
    shapes = [((8, rows, wide), BF)] * 2 + [((block, width), F32)] * 2 + [((rows, width), F32)] * 2
    buffers = [
        (2, 16, rows, wide), (2, 8, rows, wide), (2, 8, rows, wide), (2, 8, rows, wide),
        (2, 2, block, width), (2, block, width), (2, block, width),
        (2, 2, rows, width), (2, 2, rows, width), (2, 2, rows, width), (2, rows, width), (2, rows, width),
    ]
    counts = ((2, 4), (2, 4), (2, 10), (2, 10), (2, 7), (2, 7), (2,), (2,))
    return pl.pallas_call(
        collect_kernel,
        out_shape=[jax.ShapeDtypeStruct(*s) for s in shapes],
        in_specs=[spec] * 6,
        out_specs=[spec] * 6,
        scratch_shapes=[pltpu.VMEM(b, BF) for b in buffers] + [pltpu.SemaphoreType.DMA(n) for n in counts],
        compiler_params=pltpu.CompilerParams(
            collective_id=10, has_side_effects=True, vmem_limit_bytes=56 * 1024 * 1024
        ),
        name="collect",
    )(*packs, *downs, *outs)


def head_lanes(head):
    lane = lax.broadcasted_iota(jnp.int32, (1, 128), 1)
    return (lane // 32) % 2 == head


def value_lanes(head):
    lane = lax.broadcasted_iota(jnp.int32, (1, 128), 1)
    return lane // 64 == head


NT = (((1,), (1,)), ((), ()))
TN = (((0,), (0,)), ((), ()))


def attend_kernel(q_ref, k_ref, v_ref, pq_ref, pk_ref, att_ref, lse_ref):
    allowed = pk_ref[...] <= pq_ref[...]
    queries = q_ref[...]
    parts = []
    for head in range(2):
        masked = jnp.where(head_lanes(head), queries, jnp.zeros_like(queries))
        scores = lax.dot_general(masked, k_ref[...], NT, preferred_element_type=F32) * HD ** (-0.5)
        scores = jnp.where(allowed, scores, NEG_FILL)
        top = jnp.max(scores, axis=-1, keepdims=True)
        shares = jnp.exp(scores - top)
        total = jnp.sum(shares, axis=-1, keepdims=True)
        lse_ref[:, head : head + 1] = top + jnp.log(total)
        mixed = jnp.dot(shares.astype(BF), v_ref[...], preferred_element_type=F32)
        parts.append(mixed / total)
    att_ref[...] = jnp.where(value_lanes(0), parts[0], parts[1]).astype(BF)


def attend_forward(q, k, v, pos_q, pos_k):
    rows = q.shape[0]
    keys = k.shape[0]
    step = 128
    return pl.pallas_call(
        attend_kernel,
        grid=(rows // step,),
        out_shape=[
            jax.ShapeDtypeStruct((rows, 128), BF),
            jax.ShapeDtypeStruct((rows, 2), F32),
        ],
        in_specs=[
            pl.BlockSpec((step, 128), lambda i: (i, 0)),
            pl.BlockSpec((keys, 128), lambda i: (0, 0)),
            pl.BlockSpec((keys, 128), lambda i: (0, 0)),
            pl.BlockSpec((step, 1), lambda i: (i, 0)),
            pl.BlockSpec((1, keys), lambda i: (0, 0)),
        ],
        out_specs=[
            pl.BlockSpec((step, 128), lambda i: (i, 0)),
            pl.BlockSpec((step, 2), lambda i: (i, 0)),
        ],
        compiler_params=pltpu.CompilerParams(vmem_limit_bytes=40 * 1024 * 1024),
        name="attend_forward",
    )(q, k, v, pos_q, pos_k)


def attend_back_kernel(q_ref, k_ref, v_ref, da_ref, lse_ref, pq_ref, pk_ref, dq_ref, dk_ref, dv_ref):
    @pl.when(pl.program_id(0) == 0)
    def _():
        dk_ref[...] = jnp.zeros_like(dk_ref)
        dv_ref[...] = jnp.zeros_like(dv_ref)

    allowed = pk_ref[...] <= pq_ref[...]
    queries = q_ref[...]
    grads = da_ref[...]
    parts = []
    for head in range(2):
        masked = jnp.where(head_lanes(head), queries, jnp.zeros_like(queries))
        grad_h = jnp.where(value_lanes(head), grads, jnp.zeros_like(grads))
        scores = lax.dot_general(k_ref[...], masked, NT, preferred_element_type=F32) * HD ** (-0.5)
        shares = jnp.where(allowed, jnp.exp(scores - lse_ref[head : head + 1, :]), 0.0)
        grad_shares = lax.dot_general(v_ref[...], grad_h, NT, preferred_element_type=F32)
        delta = jnp.sum(shares * grad_shares, axis=0, keepdims=True)
        grad_scores = (shares * (grad_shares - delta) * HD ** (-0.5)).astype(BF)
        dv_ref[...] += jnp.dot(shares.astype(BF), grad_h, preferred_element_type=F32)
        dk_ref[...] += jnp.dot(grad_scores, masked, preferred_element_type=F32)
        parts.append(lax.dot_general(grad_scores, k_ref[...], TN, preferred_element_type=F32))
    dq_ref[...] = jnp.where(head_lanes(0), parts[0], parts[1])


def attend_backward(q, k, v, da, lse_rows, pos_q, pos_k):
    rows = q.shape[0]
    keys = k.shape[0]
    step = 128
    return pl.pallas_call(
        attend_back_kernel,
        grid=(rows // step,),
        out_shape=[
            jax.ShapeDtypeStruct((rows, 128), F32),
            jax.ShapeDtypeStruct((keys, 128), F32),
            jax.ShapeDtypeStruct((keys, 128), F32),
        ],
        in_specs=[
            pl.BlockSpec((step, 128), lambda i: (i, 0)),
            pl.BlockSpec((keys, 128), lambda i: (0, 0)),
            pl.BlockSpec((keys, 128), lambda i: (0, 0)),
            pl.BlockSpec((step, 128), lambda i: (i, 0)),
            pl.BlockSpec((2, step), lambda i: (0, i)),
            pl.BlockSpec((1, step), lambda i: (0, i)),
            pl.BlockSpec((keys, 1), lambda i: (0, 0)),
        ],
        out_specs=[
            pl.BlockSpec((step, 128), lambda i: (i, 0)),
            pl.BlockSpec((keys, 128), lambda i: (0, 0)),
            pl.BlockSpec((keys, 128), lambda i: (0, 0)),
        ],
        compiler_params=pltpu.CompilerParams(vmem_limit_bytes=48 * 1024 * 1024),
        name="attend_backward",
    )(q, k, v, da, lse_rows, pos_q, pos_k)


def chip_first(split):
    order = (2, 1, 0) + tuple(range(3, split.ndim))
    return split.transpose(order).reshape(8, split.shape[0], *split.shape[3:])


def chip_last(packed):
    split = packed.reshape(4, 2, *packed.shape[1:])
    return split.transpose((2, 1, 0) + tuple(range(3, split.ndim)))


def pack_heads(weight):
    rows = weight.shape[0]
    split = chip_first(weight.reshape(rows, 2, 4, 2, 2, 32))
    return split.transpose(0, 1, 3, 2, 4).reshape(8, rows, 128)


def unpack_heads(packed):
    rows = packed.shape[1]
    split = packed.reshape(8, rows, 2, 2, 32).transpose(0, 1, 3, 2, 4)
    return chip_last(split).reshape(rows, 1024)


def pack_values(weight):
    rows = weight.shape[0]
    return chip_first(weight.reshape(rows, 2, 4, 128))


def unpack_values(packed):
    return chip_last(packed).reshape(packed.shape[1], 1024)


def pack_units(weight, block, *extra):
    rows, units = weight.shape
    each = units // 32
    split = weight.reshape(rows, 2, 8, 2, each).transpose(2, 0, 1, 3, 4).reshape(8, rows, 4, each)
    padding = jnp.zeros((8, rows, 4, block - each), weight.dtype)
    if extra:
        columns = jnp.stack(extra, axis=-1)
        columns = jnp.pad(columns, ((0, 0), (0, block - each - len(extra))))
        first = jnp.broadcast_to(columns[None, :, None, :], (8, rows, 1, block - each))
        padding = jnp.concatenate([first, padding[:, :, 1:]], axis=2)
    return jnp.concatenate([split, padding], axis=-1).reshape(8, rows, 4 * block)


def unpack_units(packed, units):
    rows = packed.shape[1]
    each = units // 32
    split = packed.reshape(8, rows, 2, 2, -1)[..., :each]
    return split.transpose(1, 2, 0, 3, 4).reshape(rows, units)


def pair_rope(values, cosine, sine):
    first, second = values[:, :64], values[:, 64:]
    return jnp.concatenate(
        [first * cosine - second * sine, second * cosine + first * sine], axis=-1
    )


def pair_unrope(values, cosine, sine):
    first, second = values[:, :64], values[:, 64:]
    return jnp.concatenate(
        [first * cosine + second * sine, second * cosine - first * sine], axis=-1
    )


def swap_cores(value):
    return lax.ppermute(value, "ctx", [(i, i + 1 - 2 * (i % 2)) for i in range(16)])


def fast_local(tokens, cotangent, pair_of, *shards):
    width = tokens.shape[2]
    units = shards[6].shape[1]
    each = units // 32
    block = (each + 2 + 31) // 32 * 32
    hidden_pad = 4 * block
    c = lax.axis_index("ctx")
    core = c % 2
    chip = c // 2
    pos_all = storage_positions(pair_of, ROWS).reshape(8, 2, ROWS)
    own_pos = lax.dynamic_index_in_dim(pos_all, core, 1, False).reshape(-1)
    sib_pos = lax.dynamic_index_in_dim(pos_all, 1 - core, 1, False).reshape(-1)
    key_pos = jnp.concatenate([own_pos, sib_pos])
    cosine, sine = rope_tables(own_pos, HD)
    cosine = jnp.concatenate([cosine, cosine], axis=-1)
    sine = jnp.concatenate([sine, sine], axis=-1)

    layers = [shards[:9], shards[9:]]
    packs = []
    for layer in layers:
        packs.append(
            jnp.concatenate(
                [
                    pack_heads(layer[1]),
                    pack_heads(layer[2]),
                    pack_values(layer[3]),
                    pack_units(layer[6], block, layer[0], layer[5]),
                    pack_units(layer[7], block),
                ],
                axis=-1,
            )
        )
    rows_each, wide = packs[0].shape[1:]
    down = jnp.pad(jnp.stack([layers[0][8], layers[1][8]]), ((0, 0), (0, block - each), (0, 0)))
    spread = spread_call(*packs, down, jnp.stack([layers[0][4], layers[1][4]]))
    all_w = [w.reshape(32 * rows_each, wide) for w in spread[:2]]
    qkv_w = [w[:, :384] for w in all_w]
    up_w = [w[:, 384:] for w in all_w]
    down_w = [w.reshape(hidden_pad, width) for w in spread[2:4]]
    out_w = [w.reshape(4 * rows_each, width) for w in spread[4:]]
    gains = []
    for w in all_w:
        columns = w[:, 384 + each : 384 + each + 2].astype(F32).T
        gains += [columns[:1], columns[1:]]

    tok = tokens.reshape(ROWS, width)
    cot = cotangent.reshape(ROWS, width)
    plane = 8 * ROWS
    full_type = ((plane, width), BF)
    rows_type = ((ROWS, width), F32)
    saved = []
    (full,) = comm_call(start_kernel, [full_type], 0, (tok, gains[0]), False, True)
    hidden = tok
    first_values = None
    pos_q = own_pos[:, None]
    pos_k = key_pos[None, :]
    for layer in range(2):
        x_full = full
        raw = jnp.dot(x_full, qkv_w[layer], preferred_element_type=F32)
        values = raw[:, 256:]
        mixed = values if layer == 0 else 0.5 * values + 0.5 * first_values
        first_values = values
        q = pair_rope(raw[:, :128], cosine, sine).astype(BF)
        kv = jnp.concatenate(
            [pair_rope(raw[:, 128:256], cosine, sine).astype(BF), mixed.astype(BF)], axis=-1
        )
        kv = jnp.concatenate([kv, swap_cores(kv)], axis=0)
        k, v = kv[:, :128], kv[:, 128:]
        att, lse = attend_forward(q, k, v, pos_q, pos_k)
        middle, mlp_full = comm_call(
            forward_kernel, [rows_type, full_type], 1 + layer,
            (att, out_w[layer], hidden, gains[2 * layer + 1]), True, True,
        )
        both = jnp.dot(mlp_full, up_w[layer], preferred_element_type=F32)
        gate, up = both[:, :hidden_pad], both[:, hidden_pad:]
        inner = (jax.nn.silu(gate) * up).astype(BF)
        saved.append((x_full, q, k, v, lse, att, mlp_full, gate, up, inner, hidden, middle))
        if layer == 0:
            hidden, full = comm_call(
                forward_kernel, [rows_type, full_type], 3,
                (inner, down_w[layer], middle, gains[2]), True, True,
            )
        else:
            output, full = comm_call(
                turn_kernel, [((ROWS, width), BF), full_type], 4,
                (inner, down_w[layer], middle, cot), True, True,
            )
    grad = cot
    passed = None
    grad_packs = [None, None]
    grad_down = [None, None]
    grad_out = [None, None]
    for layer in (1, 0):
        x_full, q, k, v, lse, att, mlp_full, gate, up, inner, hidden, middle = saved[layer]
        grad_down[layer] = left_product(inner, full)
        grad_inner = right_product(full, down_w[layer])
        sigma = jax.nn.sigmoid(gate)
        grad_gate = (grad_inner * up * sigma * (1.0 + gate * (1.0 - sigma))).astype(BF)
        grad_up = (grad_inner * gate * sigma).astype(BF)
        both = jnp.concatenate([grad_gate, grad_up], axis=-1)
        grad_upw = left_product(mlp_full, both)
        grad_mid, full = comm_call(
            back_kernel, [rows_type, full_type], 5 + layer,
            (both, up_w[layer], grad, middle, gains[2 * layer + 1]), True, True,
        )
        grad_out[layer] = left_product(att, full)
        grad_att = right_product(full, out_w[layer]).astype(BF)
        dq, dk, dv = attend_backward(q, k, v, grad_att, lse.T, own_pos[None, :], key_pos[:, None])
        dkv = jnp.concatenate([dk, dv], axis=-1)
        dkv = dkv[: 8 * ROWS] + swap_cores(dkv[8 * ROWS :].astype(BF)).astype(F32)
        dk, dv = dkv[:, :128], dkv[:, 128:]
        if layer == 1:
            passed = 0.5 * dv
            dv = passed
        else:
            dv = dv + passed
        three = jnp.concatenate(
            [pair_unrope(dq, cosine, sine), pair_unrope(dk, cosine, sine), dv], axis=-1
        ).astype(BF)
        grad_qkv = left_product(x_full, three)
        grad_packs[layer] = jnp.concatenate([grad_qkv, grad_upw], axis=-1)
        if layer == 1:
            grad, full = comm_call(
                back_kernel, [rows_type, full_type], 7,
                (three, qkv_w[layer], grad_mid, hidden, gains[2]), True, True,
            )
        else:
            (tokens_grad,) = comm_call(
                last_kernel, [((ROWS, width), BF)], 8,
                (three, qkv_w[layer], grad_mid, hidden, gains[0]), True, False,
            )
    collected = collect_call(
        [g.astype(BF).reshape(16, 2, rows_each, wide) for g in grad_packs],
        [g.astype(BF).reshape(2, 2, block, width) for g in grad_down],
        [g.astype(BF).reshape(2, 2, rows_each, width) for g in grad_out],
    )
    result = [output.reshape(1, ROWS, width), tokens_grad.reshape(1, ROWS, width)]
    for layer in range(2):
        pack = collected[layer].astype(F32)
        both = pack * packs[layer].astype(F32)
        pre_grad = jnp.sum(both[:, :, :384], axis=(0, 2)) / layers[layer][0].astype(F32)
        mid_grad = jnp.sum(both[:, :, 384:], axis=(0, 2)) / layers[layer][5].astype(F32)
        result += [
            pre_grad,
            unpack_heads(pack[:, :, :128]),
            unpack_heads(pack[:, :, 128:256]),
            unpack_values(pack[:, :, 256:384]),
            collected[4 + layer],
            mid_grad,
            unpack_units(pack[:, :, 384 : 384 + hidden_pad], units),
            unpack_units(pack[:, :, 384 + hidden_pad :], units),
            collected[2 + layer][:each],
        ]
    return tuple(result)


def solution(mesh):
    placed = (
        P("fsdp", "ctx", None),
        P("fsdp", "ctx", None),
        P(),
        P(("fsdp", "ctx")),
        P(("fsdp", "ctx"), None),
        P(("fsdp", "ctx"), None),
        P(("fsdp", "ctx"), None),
        P(("fsdp", "ctx"), None),
        P(("fsdp", "ctx")),
        P(("fsdp", "ctx"), None),
        P(("fsdp", "ctx"), None),
        P(("fsdp", "ctx"), None),
        P(("fsdp", "ctx")),
        P(("fsdp", "ctx"), None),
        P(("fsdp", "ctx"), None),
        P(("fsdp", "ctx"), None),
        P(("fsdp", "ctx"), None),
        P(("fsdp", "ctx")),
        P(("fsdp", "ctx"), None),
        P(("fsdp", "ctx"), None),
        P(("fsdp", "ctx"), None),
    )
    fits = mesh.shape["ctx"] == HEADS and mesh.shape["fsdp"] == 2
    return jax.shard_map(
        fast_local if fits else local,
        mesh=mesh,
        in_specs=placed,
        out_specs=(
            P("fsdp", "ctx", None),
            P("fsdp", "ctx", None),
            P(("fsdp", "ctx")),
            P(("fsdp", "ctx"), None),
            P(("fsdp", "ctx"), None),
            P(("fsdp", "ctx"), None),
            P(("fsdp", "ctx"), None),
            P(("fsdp", "ctx")),
            P(("fsdp", "ctx"), None),
            P(("fsdp", "ctx"), None),
            P(("fsdp", "ctx"), None),
            P(("fsdp", "ctx")),
            P(("fsdp", "ctx"), None),
            P(("fsdp", "ctx"), None),
            P(("fsdp", "ctx"), None),
            P(("fsdp", "ctx"), None),
            P(("fsdp", "ctx")),
            P(("fsdp", "ctx"), None),
            P(("fsdp", "ctx"), None),
            P(("fsdp", "ctx"), None),
        ),
        check_vma=False,
    )
```

```python
import math

import jax
import jax.numpy as jnp
from jax import lax
from jax.experimental import pallas as pl
from jax.experimental.pallas import tpu as pltpu
from jax.sharding import PartitionSpec as P

HEADS = 16
HD = 64


NORM_EPS = 1e-05
NEG_FILL = -1e30


def block_size(total_rows):
    size_now = 512
    while total_rows % size_now:
        size_now //= 2
    return size_now


def row_norm(hidden):
    inverse = lax.rsqrt(jnp.mean(hidden * hidden, axis=-1, keepdims=True) + NORM_EPS)
    return (hidden * inverse, inverse)


def norm_back(grad_normed, normed, inverse):
    return inverse * (grad_normed - normed * jnp.mean(grad_normed * normed, axis=-1, keepdims=True))


def rope_tables(positions, head_size):
    half_size = head_size // 2
    freqs = jnp.exp(
        jnp.arange(half_size, dtype=jnp.float32) * (-2.0 * math.log(10000.0) / head_size)
    )
    angles = positions.astype(jnp.float32)[:, None] * freqs[None, :]
    return (jnp.cos(angles), jnp.sin(angles))


def rotate(values_in, cosine, sine):
    half_size = values_in.shape[-1] // 2
    first_half = values_in[..., :half_size]
    second_half = values_in[..., half_size:]
    cos_rows = cosine[:, None, :]
    sin_rows = sine[:, None, :]
    return jnp.concatenate(
        [
            first_half * cos_rows - second_half * sin_rows,
            second_half * cos_rows + first_half * sin_rows,
        ],
        axis=-1,
    )


def unrotate(grads_in, cosine, sine):
    half_size = grads_in.shape[-1] // 2
    first_half = grads_in[..., :half_size]
    second_half = grads_in[..., half_size:]
    cos_rows = cosine[:, None, :]
    sin_rows = sine[:, None, :]
    return jnp.concatenate(
        [
            first_half * cos_rows + second_half * sin_rows,
            second_half * cos_rows - first_half * sin_rows,
        ],
        axis=-1,
    )


def left_product(left, right):
    return lax.dot_general(
        left, right, (((0,), (0,)), ((), ())), preferred_element_type=jnp.float32
    )


def right_product(left, right):
    return lax.dot_general(
        left, right, (((1,), (1,)), ((), ())), preferred_element_type=jnp.float32
    )


def storage_positions(pair_of, seq_dev):
    devices = pair_of.shape[0]
    rows_all = jnp.arange(devices * seq_dev, dtype=jnp.int32)
    owner = rows_all // seq_dev
    local_row = rows_all % seq_dev
    half_rows = seq_dev // 2
    picked = jnp.sum(
        jnp.where(
            owner[:, None] == jnp.arange(devices, dtype=jnp.int32)[None, :], pair_of[None, :], 0
        ),
        axis=1,
    )
    block_id = jnp.where(local_row < half_rows, picked, 2 * devices - 1 - picked)
    return block_id * half_rows + local_row % half_rows


def head_scores(queries, keys_flat, query_pos, key_pos):
    key_heads = keys_flat.reshape(keys_flat.shape[0], queries.shape[1], queries.shape[2])
    scores = jnp.einsum(
        "qhd,khd->hqk", queries, key_heads, preferred_element_type=jnp.float32
    ) * queries.shape[2] ** (-0.5)
    allowed = (key_pos[None, :] <= query_pos[:, None])[None]
    return (jnp.where(allowed, scores, NEG_FILL), allowed)


def make_stats_step(queries, query_pos, pos_all, state_in, key_part):
    size_now = block_size(key_part.shape[0])

    def inner_step(block_no, state_now):
        top_now, total_now = state_now
        offset = block_no * size_now
        key_block = lax.dynamic_slice_in_dim(key_part, offset, size_now, 0)
        key_pos = lax.dynamic_slice_in_dim(pos_all, offset, size_now, 0)
        scores, allowed = head_scores(queries, key_block, query_pos, key_pos)
        new_top = jnp.maximum(top_now, jnp.max(scores, axis=-1))
        total_now = total_now * jnp.exp(top_now - new_top) + jnp.sum(
            jnp.where(allowed, jnp.exp(scores - new_top[..., None]), 0.0), axis=-1
        )
        return (new_top, total_now)

    return lax.fori_loop(0, key_part.shape[0] // size_now, inner_step, state_in)


def make_value_step(queries, log_total, query_pos, pos_all, acc_in, pieces):
    key_part, value_part = pieces
    size_now = block_size(key_part.shape[0])

    def inner_step(block_no, acc_now):
        offset = block_no * size_now
        key_block = lax.dynamic_slice_in_dim(key_part, offset, size_now, 0)
        value_block = lax.dynamic_slice_in_dim(value_part, offset, size_now, 0)
        key_pos = lax.dynamic_slice_in_dim(pos_all, offset, size_now, 0)
        scores, allowed = head_scores(queries, key_block, query_pos, key_pos)
        shares = jnp.exp(scores - log_total[..., None]).astype(jnp.bfloat16)
        value_heads = value_block.reshape(size_now, queries.shape[1], queries.shape[2])
        return acc_now + jnp.einsum(
            "hqk,khd->qhd", shares, value_heads, preferred_element_type=jnp.float32
        )

    return lax.fori_loop(0, key_part.shape[0] // size_now, inner_step, acc_in)


def make_back_step(queries, grad_att, log_total, row_delta, query_pos, pos_all):
    scale_now = queries.shape[2] ** (-0.5)

    def back_step(state_in, pieces, start_row):
        key_part, value_part = pieces
        size_now = block_size(key_part.shape[0])

        def inner_step(block_no, state_now):
            offset = block_no * size_now
            key_block = lax.dynamic_slice_in_dim(key_part, offset, size_now, 0)
            value_block = lax.dynamic_slice_in_dim(value_part, offset, size_now, 0)
            key_pos = lax.dynamic_slice_in_dim(pos_all, offset, size_now, 0)
            scores, allowed = head_scores(queries, key_block, query_pos, key_pos)
            shares = jnp.exp(scores - log_total[..., None])
            value_heads = value_block.reshape(size_now, queries.shape[1], queries.shape[2])
            key_heads = key_block.reshape(size_now, queries.shape[1], queries.shape[2])
            grad_shares = jnp.einsum(
                "qhd,khd->hqk", grad_att, value_heads, preferred_element_type=jnp.float32
            )
            grad_scores = (shares * (grad_shares - row_delta[..., None]) * scale_now).astype(
                jnp.bfloat16
            )
            grad_query = state_now[0] + jnp.einsum(
                "hqk,khd->qhd", grad_scores, key_heads, preferred_element_type=jnp.float32
            )
            return (grad_query,)

        return lax.fori_loop(0, key_part.shape[0] // size_now, inner_step, state_in)

    return back_step


def make_query_step(own_keys, own_values, own_pos, stats_all, pos_all, head_count, head_size):
    scale_now = head_size ** (-0.5)
    value_heads = own_values.reshape(own_values.shape[0], head_count, head_size)

    def query_step(state_in, pieces, start_row):
        query_part, grad_part = pieces
        size_now = block_size(query_part.shape[0])

        def inner_step(block_no, state_now):
            offset = block_no * size_now
            query_block = lax.dynamic_slice_in_dim(query_part, offset, size_now, 0).reshape(
                size_now, head_count, head_size
            )
            grad_block = lax.dynamic_slice_in_dim(grad_part, offset, size_now, 0).reshape(
                size_now, head_count, head_size
            )
            query_pos = lax.dynamic_slice_in_dim(pos_all, offset, size_now, 0)
            log_block = lax.dynamic_slice_in_dim(stats_all[0], offset, size_now, 0).T
            delta_block = lax.dynamic_slice_in_dim(stats_all[1], offset, size_now, 0).T
            scores, allowed = head_scores(query_block, own_keys, query_pos, own_pos)
            shares = jnp.exp(scores - log_block[..., None])
            grad_shares = jnp.einsum(
                "qhd,khd->hqk", grad_block, value_heads, preferred_element_type=jnp.float32
            )
            grad_scores = (shares * (grad_shares - delta_block[..., None]) * scale_now).astype(
                jnp.bfloat16
            )
            key_term = jnp.einsum(
                "hqk,qhd->khd", grad_scores, query_block, preferred_element_type=jnp.float32
            )
            value_term = jnp.einsum(
                "hqk,qhd->khd",
                shares.astype(jnp.bfloat16),
                grad_block,
                preferred_element_type=jnp.float32,
            )
            return (
                state_now[0] + key_term.reshape(key_term.shape[0], -1),
                state_now[1] + value_term.reshape(value_term.shape[0], -1),
            )

        return lax.fori_loop(0, query_part.shape[0] // size_now, inner_step, state_in)

    return query_step


def gather_forward(shards):
    return (
        lax.all_gather(shards[0], ("fsdp", "ctx"), axis=0, tiled=True),
        lax.all_gather(shards[1], ("fsdp", "ctx"), axis=0, tiled=True),
        lax.all_gather(shards[2], ("fsdp", "ctx"), axis=0, tiled=True),
        lax.all_gather(shards[3], ("fsdp", "ctx"), axis=0, tiled=True),
        lax.all_gather(shards[4], ("fsdp", "ctx"), axis=0, tiled=True),
        lax.all_gather(shards[5], ("fsdp", "ctx"), axis=0, tiled=True),
        lax.all_gather(shards[6], ("fsdp", "ctx"), axis=0, tiled=True),
        lax.all_gather(shards[7], ("fsdp", "ctx"), axis=0, tiled=True),
        lax.all_gather(shards[8], ("fsdp", "ctx"), axis=0, tiled=True),
    )


def scatter_grads(grad_terms):
    return (
        lax.psum_scatter(grad_terms[0], ("fsdp", "ctx"), scatter_dimension=0, tiled=True),
        lax.psum_scatter(grad_terms[1], ("fsdp", "ctx"), scatter_dimension=0, tiled=True),
        lax.psum_scatter(grad_terms[2], ("fsdp", "ctx"), scatter_dimension=0, tiled=True),
        lax.psum_scatter(grad_terms[3], ("fsdp", "ctx"), scatter_dimension=0, tiled=True),
        lax.psum_scatter(grad_terms[4], ("fsdp", "ctx"), scatter_dimension=0, tiled=True),
        lax.psum_scatter(grad_terms[5], ("fsdp", "ctx"), scatter_dimension=0, tiled=True),
        lax.psum_scatter(grad_terms[6], ("fsdp", "ctx"), scatter_dimension=0, tiled=True),
        lax.psum_scatter(grad_terms[7], ("fsdp", "ctx"), scatter_dimension=0, tiled=True),
        lax.psum_scatter(grad_terms[8], ("fsdp", "ctx"), scatter_dimension=0, tiled=True),
    )


def forward_layer(hidden, full_layer, first_values, context):
    prenorm, query_w, keys_w, values_w, outproj, midnorm, gates_w, upproj_w, downproj_w = full_layer
    cosine, sine, own_pos, pos_all = context
    rows_n, model_width = hidden.shape
    normed, inverse_a = row_norm(hidden)
    attn_in = (normed * prenorm.astype(jnp.float32)).astype(jnp.bfloat16)
    query_raw = jnp.dot(attn_in, query_w, preferred_element_type=jnp.float32)
    keys_raw = jnp.dot(attn_in, keys_w, preferred_element_type=jnp.float32)
    values_raw = jnp.dot(attn_in, values_w, preferred_element_type=jnp.float32)
    mixed = values_raw if first_values is None else 0.5 * values_raw + 0.5 * first_values
    queries = rotate(query_raw.reshape(rows_n, HEADS, HD), cosine, sine).astype(jnp.bfloat16)
    keys_flat = (
        rotate(keys_raw.reshape(rows_n, HEADS, HD), cosine, sine)
        .reshape(rows_n, model_width)
        .astype(jnp.bfloat16)
    )
    values_flat = mixed.astype(jnp.bfloat16)
    top_start = jnp.full((HEADS, rows_n), NEG_FILL, jnp.float32)
    total_start = jnp.zeros((HEADS, rows_n), jnp.float32)
    top_now, total_now = make_stats_step(
        queries,
        own_pos,
        pos_all,
        (top_start, total_start),
        lax.all_gather(keys_flat, "ctx", axis=0, tiled=True),
    )
    log_total = top_now + jnp.log(total_now)
    att_out = make_value_step(
        queries,
        log_total,
        own_pos,
        pos_all,
        jnp.zeros((rows_n, HEADS, HD), jnp.float32),
        (
            lax.all_gather(keys_flat, "ctx", axis=0, tiled=True),
            lax.all_gather(values_flat, "ctx", axis=0, tiled=True),
        ),
    )
    att_low = att_out.reshape(rows_n, model_width).astype(jnp.bfloat16)
    middle = hidden + jnp.dot(att_low, outproj, preferred_element_type=jnp.float32)
    normed_mid, inverse_b = row_norm(middle)
    mlp_in = (normed_mid * midnorm.astype(jnp.float32)).astype(jnp.bfloat16)
    gate_raw = jnp.dot(mlp_in, gates_w, preferred_element_type=jnp.float32)
    up_proj = jnp.dot(mlp_in, upproj_w, preferred_element_type=jnp.float32)
    inner_act = (jax.nn.silu(gate_raw) * up_proj).astype(jnp.bfloat16)
    result = middle + jnp.dot(inner_act, downproj_w, preferred_element_type=jnp.float32)
    saved = (
        hidden,
        normed,
        inverse_a,
        attn_in,
        queries,
        keys_flat,
        values_flat,
        log_total,
        att_out,
        att_low,
        normed_mid,
        inverse_b,
        mlp_in,
        gate_raw,
        up_proj,
        inner_act,
    )
    return (result, values_raw, saved)


def backward_layer(grad_out, full_layer, saved, value_extra, is_second, context):
    prenorm, query_w, keys_w, values_w, outproj, midnorm, gates_w, upproj_w, downproj_w = full_layer
    (
        hidden,
        normed,
        inverse_a,
        attn_in,
        queries,
        keys_flat,
        values_flat,
        log_total,
        att_out,
        att_low,
        normed_mid,
        inverse_b,
        mlp_in,
        gate_raw,
        up_proj,
        inner_act,
    ) = saved
    cosine, sine, own_pos, pos_all = context
    rows_n, model_width = hidden.shape
    grad_low = grad_out.astype(jnp.bfloat16)
    grad_down = left_product(inner_act, grad_low)
    grad_inner = right_product(grad_low, downproj_w)
    sigma_gate = jax.nn.sigmoid(gate_raw)
    grad_gate = (grad_inner * up_proj * sigma_gate * (1.0 + gate_raw * (1.0 - sigma_gate))).astype(
        jnp.bfloat16
    )
    grad_up = (grad_inner * gate_raw * sigma_gate).astype(jnp.bfloat16)
    grad_gates = left_product(mlp_in, grad_gate)
    grad_upproj = left_product(mlp_in, grad_up)
    grad_mlp = right_product(grad_gate, gates_w) + right_product(grad_up, upproj_w)
    grad_midnorm = jnp.sum(grad_mlp * normed_mid, axis=0)
    grad_middle = grad_out + norm_back(
        grad_mlp * midnorm.astype(jnp.float32), normed_mid, inverse_b
    )
    branch_low = grad_middle.astype(jnp.bfloat16)
    grad_outproj = left_product(att_low, branch_low)
    grad_att = right_product(branch_low, outproj).astype(jnp.bfloat16).reshape(rows_n, HEADS, HD)
    row_delta = jnp.sum(grad_att.astype(jnp.float32) * att_out, axis=-1).T
    query_start = jnp.zeros((rows_n, HEADS, HD), jnp.float32)
    state_start = (query_start,)
    back_fn = make_back_step(queries, grad_att, log_total, row_delta, own_pos, pos_all)
    state_out = back_fn(
        state_start,
        (
            lax.all_gather(keys_flat, "ctx", axis=0, tiled=True),
            lax.all_gather(values_flat, "ctx", axis=0, tiled=True),
        ),
        jnp.int32(0),
    )
    grad_qr = state_out[0]
    stats_all = (
        lax.all_gather(log_total.T, "ctx", axis=0, tiled=True),
        lax.all_gather(row_delta.T, "ctx", axis=0, tiled=True),
    )
    query_fn = make_query_step(keys_flat, values_flat, own_pos, stats_all, pos_all, HEADS, HD)
    flat_start = jnp.zeros((rows_n, model_width), jnp.float32)
    grad_kr, grad_mix = query_fn(
        (flat_start, flat_start),
        (
            lax.all_gather(queries.reshape(rows_n, model_width), "ctx", axis=0, tiled=True),
            lax.all_gather(grad_att.reshape(rows_n, model_width), "ctx", axis=0, tiled=True),
        ),
        jnp.int32(0),
    )
    grad_query = unrotate(grad_qr, cosine, sine).reshape(rows_n, model_width).astype(jnp.bfloat16)
    grad_keys = (
        unrotate(grad_kr.reshape(rows_n, HEADS, HD), cosine, sine)
        .reshape(rows_n, model_width)
        .astype(jnp.bfloat16)
    )
    if is_second:
        grad_values = (0.5 * grad_mix).astype(jnp.bfloat16)
        passed_on = 0.5 * grad_mix
    else:
        grad_values = (grad_mix + value_extra).astype(jnp.bfloat16)
        passed_on = None
    grad_query_w = left_product(attn_in, grad_query)
    grad_keys_w = left_product(attn_in, grad_keys)
    grad_values_w = left_product(attn_in, grad_values)
    grad_attn = (
        right_product(grad_query, query_w)
        + right_product(grad_keys, keys_w)
        + right_product(grad_values, values_w)
    )
    grad_prenorm = jnp.sum(grad_attn * normed, axis=0)
    grad_hidden = grad_middle + norm_back(
        grad_attn * prenorm.astype(jnp.float32), normed, inverse_a
    )
    grad_terms = (
        grad_prenorm,
        grad_query_w,
        grad_keys_w,
        grad_values_w,
        grad_outproj,
        grad_midnorm,
        grad_gates,
        grad_upproj,
        grad_down,
    )
    return (grad_hidden, grad_terms, passed_on)


def local(
    tokens,
    cotangent,
    pair_of,
    prenorm_one,
    query_one,
    keys_one,
    values_one,
    outproj_one,
    midnorm_one,
    gates_one,
    upproj_one,
    downproj_one,
    prenorm_two,
    query_two,
    keys_two,
    values_two,
    outproj_two,
    midnorm_two,
    gates_two,
    upproj_two,
    downproj_two,
):
    seq_dev = tokens.shape[1]
    model_width = tokens.shape[2]
    pos_all = storage_positions(pair_of, seq_dev)
    own_pos = lax.dynamic_slice_in_dim(pos_all, lax.axis_index("ctx") * seq_dev, seq_dev, 0)
    cosine, sine = rope_tables(own_pos, HD)
    context = (cosine, sine, own_pos, pos_all)
    layer_shards = [
        (
            prenorm_one,
            query_one,
            keys_one,
            values_one,
            outproj_one,
            midnorm_one,
            gates_one,
            upproj_one,
            downproj_one,
        ),
        (
            prenorm_two,
            query_two,
            keys_two,
            values_two,
            outproj_two,
            midnorm_two,
            gates_two,
            upproj_two,
            downproj_two,
        ),
    ]
    hidden = tokens.reshape(seq_dev, model_width).astype(jnp.float32)
    first_values = None
    kept_full = []
    kept_saved = []
    for layer_no in range(2):
        full_layer = gather_forward(layer_shards[layer_no])
        hidden, values_raw, saved = forward_layer(hidden, full_layer, first_values, context)
        if layer_no == 0:
            first_values = values_raw
        kept_full.append(full_layer)
        kept_saved.append(saved)
    output = hidden.astype(jnp.bfloat16).reshape(1, seq_dev, model_width)
    grad_now = cotangent.reshape(seq_dev, model_width).astype(jnp.float32)
    value_extra = None
    layer_grads = [None, None]
    for layer_no in (1, 0):
        full_layer = kept_full[layer_no]
        grad_now, grad_terms, passed_on = backward_layer(
            grad_now, full_layer, kept_saved[layer_no], value_extra, layer_no == 1, context
        )
        if layer_no == 1:
            value_extra = passed_on
        layer_grads[layer_no] = scatter_grads(grad_terms)
    tokens_grad = grad_now.astype(jnp.bfloat16).reshape(1, seq_dev, model_width)
    first_grads = layer_grads[0]
    second_grads = layer_grads[1]
    return (
        output,
        tokens_grad,
        first_grads[0],
        first_grads[1],
        first_grads[2],
        first_grads[3],
        first_grads[4],
        first_grads[5],
        first_grads[6],
        first_grads[7],
        first_grads[8],
        second_grads[0],
        second_grads[1],
        second_grads[2],
        second_grads[3],
        second_grads[4],
        second_grads[5],
        second_grads[6],
        second_grads[7],
        second_grads[8],
    )


ROWS = 128
BF = jnp.bfloat16
F32 = jnp.float32
MESH = pl.DeviceIdType.MESH
VMEM_SPACE = pltpu.VMEM


def flip(value, weight):
    return value + weight * (1 - 2 * ((value // weight) % 2))


def to_device(f, c):
    return {"fsdp": f, "ctx": c}


def remote(src, dst, send_sem, recv_sem, target):
    return pltpu.make_async_remote_copy(
        src_ref=src,
        dst_ref=dst,
        send_sem=send_sem,
        recv_sem=recv_sem,
        device_id=to_device(*target),
        device_id_type=MESH,
    )


def arrived(ref, sem, target):
    remote(ref, ref, sem, sem, target).wait_recv()


def plane_place():
    f = lax.axis_index("fsdp")
    c = lax.axis_index("ctx")
    return f, c, (c // 2) % 2, c // 4


def greet_plane(f, c, z):
    barrier = pltpu.get_barrier_semaphore()

    def hello(target):
        pl.semaphore_signal(barrier, inc=1, device_id=to_device(*target), device_id_type=MESH)

    hello((f, flip(c, 2)))

    @pl.when(z > 0)
    def _():
        hello((f, c - 4))

    @pl.when(z < 3)
    def _():
        hello((f, c + 4))

    pl.semaphore_wait(barrier, 2 + jnp.where((z > 0) & (z < 3), 1, 0))


HALF = ROWS // 2
ODD = 8


class Plane:
    def __init__(self, place, inner):
        f, c, y, z = place
        self.y, self.inner = y, inner
        self.mirrored = z // 2
        sign = 1 - 2 * self.mirrored
        self.across = (f, flip(c, 2))
        self.up = (f, c + 4 * sign)
        self.down = (f, c - 4 * sign)
        self.own = 1 if inner else 0
        self.sent = []

    def at(self, near):
        return near + self.mirrored * (3 - 2 * near)

    def slot(self, half, near):
        return 4 * half + self.at(near)

    def start(self, copy):
        copy.start()
        self.sent.append(copy)

    def finish(self):
        for copy in self.sent:
            copy.wait_send()


class Reduce(Plane):
    def __init__(self, place, inner, product, bufs, sems):
        super().__init__(place, inner)
        self.product = product
        self.sy, self.ry, self.acc, self.pb, self.su, self.sd, self.rb, self.ra = bufs
        self.ys, self.yr, self.us, self.ds, self.br, self.ar = sems

    def y_copy(self, slot):
        return remote(self.sy.at[slot], self.ry.at[slot], self.ys.at[slot], self.yr.at[slot], self.across)

    def z_copy(self, slot, upward):
        if not upward:
            return remote(self.sd.at[slot], self.ra.at[slot], self.ds.at[slot], self.ar.at[slot], self.down)
        if self.inner:
            return remote(self.su.at[slot], self.ra.at[slot], self.us.at[slot], self.ar.at[slot], self.up)
        return remote(self.su.at[slot], self.rb.at[slot], self.us.at[slot], self.br.at[slot], self.up)

    def got_y(self, slot):
        self.y_copy(slot).wait_recv()
        return self.ry[slot].astype(F32)

    def got_z(self, slot, below):
        buf, sem = (self.rb, self.br) if below else (self.ra, self.ar)
        arrived(buf.at[slot], sem.at[slot], self.across)
        return buf[slot].astype(F32)

    def pass_z(self, slot, value, upward):
        buf = self.su if upward else self.sd
        buf[slot] = value.astype(BF)
        self.start(self.z_copy(slot, upward))

    def cross(self, slot, value):
        self.sy[slot] = value.astype(BF)
        self.start(self.y_copy(slot))

    def products(self):
        def other_row(step, carry):
            if self.inner:
                near = jnp.where(step == 0, 3, jnp.where(step == 1, 0, 4 - step))
            else:
                near = 3 - step
            block = near + self.mirrored * (3 - 2 * near)
            value = self.product(2 * block + 1 - self.y)
            self.sy[block] = value[:HALF].astype(BF)
            self.y_copy(block).start()
            self.pb[block] = value[HALF:]
            return carry

        lax.fori_loop(0, 4, other_row, 0)
        for near in range(4):
            self.sent.append(self.y_copy(self.at(near)))
        if not self.inner:
            self.pass_z(ODD, self.pb[self.at(3)], True)
        for near in (2, 1):
            self.cross(self.slot(1, near), self.pb[self.at(near)])

        def own_row(step, carry):
            near = 3 - step
            block = near + self.mirrored * (3 - 2 * near)
            value = self.product(2 * block + self.y)
            self.acc[block] = value[:HALF]
            self.acc[4 + block] = value[HALF:]
            return carry

        lax.fori_loop(0, 4, own_row, 0)

    def far_halves(self):
        if not self.inner:
            self.pass_z(self.slot(1, 3), self.acc[self.slot(1, 3)], True)
            return
        self.pass_z(ODD, self.pb[self.at(3)] + self.got_z(ODD, True), True)
        far = self.slot(1, 3)
        self.pass_z(far, self.acc[far] + self.got_z(far, True), True)
        self.pass_z(ODD, self.pb[self.at(0)] + self.got_z(ODD, False), False)
        end = self.slot(1, 0)
        self.pass_z(end, self.acc[end] + self.got_z(end, False), False)

    def chain(self, half):
        if self.inner:
            steps = ((3, True), (0, False), (2, True)) if half == 0 else ((2, True),)
        else:
            steps = ((3, True), (2, True), (1, True)) if half == 0 else ((2, True), (1, True))
        for near, upward in steps:
            slot = self.slot(half, near)
            value = self.acc[slot] + self.got_y(slot)
            if self.inner:
                value += self.got_z(slot, upward)
            self.pass_z(slot, value, upward)
        if half == 1 and not self.inner:
            self.cross(self.slot(1, 0), self.pb[self.at(0)] + self.got_z(ODD, False))
        slot = self.slot(half, self.own)
        total = self.acc[slot] + self.got_z(slot, False)
        if self.inner:
            total += self.got_z(slot, True)
        return total + self.got_y(slot)


class Gather(Plane):
    def __init__(self, place, inner, full, sems):
        super().__init__(place, inner)
        self.full = full
        self.ys, self.yr, self.us, self.ds, self.br, self.ar = sems

    def rows(self, half, near, side):
        start = (self.at(near) * 2 + side) * ROWS + half * HALF
        return self.full.at[pl.ds(pl.multiple_of(start, HALF), HALF)]

    def y_copy(self, half, near):
        part = self.rows(half, near, self.y)
        slot = self.slot(half, near)
        return remote(part, part, self.ys.at[slot], self.yr.at[slot], self.across)

    def send_z(self, part, slot, upward):
        sem = self.us if upward else self.ds
        arrive = self.br if upward and not self.inner else self.ar
        self.start(remote(part, part, sem.at[slot], arrive.at[slot], self.up if upward else self.down))

    def got_z(self, part, slot, below):
        sem = self.br if below else self.ar
        arrived(part, sem.at[slot], self.across)

    def send_own(self, half):
        part = self.rows(half, self.own, self.y)
        slot = self.slot(half, self.own)
        self.send_z(part, slot, True)
        if self.inner:
            self.send_z(part, slot, False)
        self.start(self.y_copy(half, self.own))

    def take(self, half, near, below):
        part = self.rows(half, near, self.y)
        slot = self.slot(half, near)
        self.got_z(part, slot, below)
        if self.inner:
            self.send_z(part, slot, below)
        if half == 0 or near in (1, 2):
            self.start(self.y_copy(half, near))

    def take_odd(self, near, below):
        part = self.rows(1, near, 1 - self.y)
        self.got_z(part, ODD, below)
        if self.inner:
            self.send_z(part, ODD, below)

    def got_y(self, half, near):
        part = self.rows(half, near, 1 - self.y)
        arrived(part, self.yr.at[self.slot(half, near)], self.across)

    def forward(self, half):
        if half == 0:
            for near, below in ((0, True), (2, False), (3, False)) if self.inner else ((1, False), (2, False), (3, False)):
                self.take(0, near, below)
            return
        if self.inner:
            self.take(1, 0, True)
            self.take(1, 2, False)
            self.take(1, 3, False)
            self.take_odd(0, True)
            self.take_odd(3, False)
        else:
            self.take(1, 1, False)
            self.got_y(1, 0)
            self.send_z(self.rows(1, 0, 1 - self.y), ODD, True)
            self.take(1, 2, False)
            self.take(1, 3, False)
            self.take_odd(3, False)
        for near in range(4):
            self.got_y(0, near)
        for near in (1, 2):
            self.got_y(1, near)


def both_kinds(place, run):
    z = place[3]

    @pl.when((z > 0) & (z < 3))
    def _():
        run(True)

    @pl.when((z == 0) | (z == 3))
    def _():
        run(False)


def exchange(place, product, settle, full, scratch, extra=None):
    if extra is None:
        greet_plane(place[0], place[1], place[3])
    else:
        peers, sibling, twin = chip_peers(place[0], place[1])
        greet(peers + [sibling, twin])

    def run(inner):
        parts = []
        more = None if extra is None else extra(place)
        if more is not None:
            more.first()
            parts.append(more)
        reduce = Reduce(place, inner, product, scratch[:8], scratch[8:14])
        reduce.products()
        reduce.far_halves()
        parts.append(reduce)
        if full is not None:
            gather = Gather(place, inner, full, scratch[14:20])
            parts.append(gather)
        if more is not None:
            more.second()
        for half in range(2):
            rows = settle(half, reduce.chain(half))
            if full is not None:
                start = (place[3] * 2 + place[2]) * ROWS + half * HALF
                full[pl.ds(pl.multiple_of(start, HALF), HALF), :] = rows
                gather.send_own(half)
            if more is not None and half == 0:
                more.third()
        if full is not None:
            gather.forward(0)
            gather.forward(1)
        for part in parts:
            part.finish()

    both_kinds(place, run)


def half_rows(half):
    return pl.ds(half * HALF, HALF)


def norm_rows(hidden):
    return lax.rsqrt(jnp.mean(hidden * hidden, axis=-1, keepdims=True) + NORM_EPS)


def make_product(left_ref, right_ref, transposed):
    dims = (((1,), (1,)), ((), ())) if transposed else (((1,), (0,)), ((), ()))

    def product(block):
        rows = left_ref[pl.ds(pl.multiple_of(block * ROWS, ROWS), ROWS), :]
        return lax.dot_general(rows, right_ref[...], dims, preferred_element_type=F32)

    return product


def forward_kernel(left_ref, right_ref, res_ref, gain_ref, new_ref, full_ref, *scratch):
    def settle(half, total):
        hidden = res_ref[half_rows(half), :].astype(F32) + total
        new_ref[half_rows(half), :] = hidden
        return (hidden * norm_rows(hidden) * gain_ref[...]).astype(BF)

    exchange(plane_place(), make_product(left_ref, right_ref, False), settle, full_ref, scratch)


def turn_kernel(left_ref, right_ref, res_ref, cot_ref, out_ref, full_ref, *scratch):
    def settle(half, total):
        out_ref[half_rows(half), :] = (res_ref[half_rows(half), :] + total).astype(BF)
        return cot_ref[half_rows(half), :]

    exchange(plane_place(), make_product(left_ref, right_ref, False), settle, full_ref, scratch)


def back_rows(total, grad, hidden, gain):
    inverse = norm_rows(hidden)
    normed = hidden * inverse
    scaled = total * gain
    mean = jnp.mean(scaled * normed, axis=-1, keepdims=True)
    return grad + inverse * (scaled - normed * mean)


def back_kernel(left_ref, right_ref, grad_ref, hid_ref, gain_ref, new_ref, full_ref, *scratch):
    def settle(half, total):
        at = half_rows(half)
        new = back_rows(total, grad_ref[at, :].astype(F32), hid_ref[at, :].astype(F32), gain_ref[...])
        new_ref[at, :] = new
        return new.astype(BF)

    exchange(plane_place(), make_product(left_ref, right_ref, True), settle, full_ref, scratch)


def comm_call(kernel, outs, ident, args, gathers, more=()):
    width = 1024
    scratch = []
    for count, kind in ((8, BF), (8, BF), (8, F32), (4, F32), (9, BF), (9, BF), (9, BF), (9, BF)):
        scratch.append(pltpu.VMEM((count, HALF, width), kind))
    scratch += [pltpu.SemaphoreType.DMA((9,))] * 6
    if gathers:
        scratch += [pltpu.SemaphoreType.DMA((9,))] * 6
    scratch += list(more)
    spec = pl.BlockSpec(memory_space=VMEM_SPACE)
    return pl.pallas_call(
        kernel,
        out_shape=[jax.ShapeDtypeStruct(*o) for o in outs],
        in_specs=[spec] * len(args),
        out_specs=[spec] * len(outs),
        scratch_shapes=scratch,
        compiler_params=pltpu.CompilerParams(
            collective_id=ident, has_side_effects=True, vmem_limit_bytes=40 * 1024 * 1024
        ),
        name=kernel.__name__,
    )(*args)


def chip_peers(f, c):
    chip, core = c // 2, c % 2
    return [(f, 2 * ((chip + i) % 8) + core) for i in range(1, 8)], (f, flip(c, 1)), (1 - f, c)


def greet(targets):
    barrier = pltpu.get_barrier_semaphore()
    for target in targets:
        pl.semaphore_signal(barrier, inc=1, device_id=to_device(*target), device_id_type=MESH)
    pl.semaphore_wait(barrier, len(targets))


class Spread:
    def __init__(self, place, tables, downs, outs, sems):
        self.f, self.c, self.y, _ = place
        self.chip, self.core = self.c // 2, self.c % 2
        self.peers, self.sibling, self.twin = chip_peers(self.f, self.c)
        self.near = (self.f, flip(self.c, 2))
        self.tables, self.downs, self.outs = tables, downs, outs
        self.ds, self.dr, self.xs, self.xr, self.ss, self.sr, self.ws, self.wr = sems
        self.home = self.y == self.f
        self.direct, self.crossed, self.inner, self.sent = {}, {}, [], []

    def send(self, src, dst, send_sem, recv_sem, target):
        copy = remote(src, dst, send_sem, recv_sem, target)
        copy.start()
        self.sent.append(copy)
        return copy

    def to_twin(self, src, dst, l, n):
        self.crossed[l, n] = self.send(src, dst, self.xs.at[l, n], self.xr.at[l, n], self.twin)

    def to_sibling(self, src, dst, l, n):
        self.inner.append(self.send(src, dst, self.ss.at[l, n], self.sr.at[l, n], self.sibling))

    def out_copy(self, l):
        op, out = self.outs[l]
        part = 2 * self.y + self.core
        return remote(op, out.at[part], self.ws.at[l], self.wr.at[l], self.near)

    def pair_copies(self, l, s, r, first, target):
        parts = [self.outs[l][1].at[self.core], self.outs[l][1].at[2 + self.core]]
        return [remote(p, p, s.at[l, first + n], r.at[l, first + n], target) for n, p in enumerate(parts)]

    def first(self, l):
        a, r = self.tables[l]
        down, down_all = self.downs[l]
        op, out = self.outs[l]
        mine = self.f * 16 + self.c
        part = 2 * self.f + self.core
        self.to_twin(a.at[self.chip], r.at[mine], l, 0)
        for i in range(1, 8):
            t = (self.chip + i) % 8
            self.direct[l, i] = self.send(
                a.at[t], r.at[mine], self.ds.at[l, i], self.dr.at[l, i], self.peers[i - 1]
            )
        r[mine] = a[self.chip]
        self.to_sibling(a.at[self.chip], r.at[mine], l, 0)
        down_all[part] = down[...]
        self.to_twin(down, down_all.at[part], l, 8)
        self.to_sibling(down, down_all.at[part], l, 16)

        @pl.when(self.home)
        def _():
            out[2 * self.y + self.core] = op[...]

        @pl.when(jnp.logical_not(self.home))
        def _():
            self.out_copy(l).start()

    def second(self, l):
        r = self.tables[l][1]
        for i in range(1, 8):
            self.direct[l, i].wait_recv()
            source = self.f * 16 + 2 * ((self.chip + 8 - i) % 8) + self.core
            self.to_twin(r.at[source], r.at[source], l, i)
            self.to_sibling(r.at[source], r.at[source], l, i)

        @pl.when(self.home)
        def _():
            self.out_copy(l).wait_recv()
            for copy in self.pair_copies(l, self.xs, self.xr, 9, self.twin):
                copy.start()

    def third(self, l):
        r = self.tables[l][1]

        @pl.when(jnp.logical_not(self.home))
        def _():
            for copy in self.pair_copies(l, self.xs, self.xr, 9, self.twin):
                copy.wait_recv()

        for copy in self.pair_copies(l, self.ss, self.sr, 18, self.sibling):
            copy.start()
        for i in range(8):
            self.crossed[l, i].wait_recv()
            source = (1 - self.f) * 16 + 2 * ((self.chip + 8 - i) % 8) + self.core
            self.to_sibling(r.at[source], r.at[source], l, 8 + i)
        self.crossed[l, 8].wait_recv()
        part = 2 * (1 - self.f) + self.core
        down_all = self.downs[l][1]
        self.to_sibling(down_all.at[part], down_all.at[part], l, 17)

    def finish(self):
        for copy in self.inner:
            copy.wait_recv()
        for copy in self.sent:
            copy.wait_send()
        for l in range(len(self.tables)):
            for copy in self.pair_copies(l, self.ss, self.sr, 18, self.sibling):
                copy.wait()

            @pl.when(self.home)
            def _():
                for copy in self.pair_copies(l, self.xs, self.xr, 9, self.twin):
                    copy.wait_send()

            @pl.when(jnp.logical_not(self.home))
            def _():
                self.out_copy(l).wait_send()


def begin_kernel(tok, a1, a2, dn, op, full, r1, r2, d1, d2, o1, o2, *sems):
    place = plane_place()
    f, c, y, z = place
    peers, sibling, twin = chip_peers(f, c)
    greet(peers + [sibling, twin])
    start = (z * 2 + y) * ROWS
    full[pl.ds(pl.multiple_of(start, ROWS), ROWS), :] = tok[...]

    def run(inner):
        gather = Gather(place, inner, full, sems[:6])
        spread = Spread(
            place, ((a1, r1), (a2, r2)), ((dn.at[0], d1), (dn.at[1], d2)), ((op.at[0], o1), (op.at[1], o2)), sems[6:]
        )
        gather.send_own(0)
        gather.send_own(1)
        spread.first(0)
        spread.first(1)
        gather.forward(0)
        spread.second(0)
        gather.forward(1)
        spread.second(1)
        spread.third(0)
        spread.third(1)
        gather.finish()
        spread.finish()

    both_kinds(place, run)


def begin_call(tok, a1, a2, down, out):
    rows, wide = a1.shape[1:]
    block, width = down.shape[1:]
    spec = pl.BlockSpec(memory_space=VMEM_SPACE)
    shapes = [(8 * ROWS, width)] + [(32, rows, wide)] * 2 + [(4, block, width)] * 2 + [(4, rows, width)] * 2
    counts = [(9,)] * 6 + [(2, 8), (2, 8), (2, 11), (2, 11), (2, 20), (2, 20), (2,), (2,)]
    return pl.pallas_call(
        begin_kernel,
        out_shape=[jax.ShapeDtypeStruct(s, BF) for s in shapes],
        in_specs=[spec] * 5,
        out_specs=[spec] * 7,
        scratch_shapes=[pltpu.SemaphoreType.DMA(n) for n in counts],
        compiler_params=pltpu.CompilerParams(
            collective_id=9, has_side_effects=True, vmem_limit_bytes=40 * 1024 * 1024
        ),
        name="begin",
    )(tok, a1, a2, down, out)


class Collect:
    def __init__(self, place, ins, results, scratch):
        self.f, self.c, self.y, _ = place
        self.chip, self.core = self.c // 2, self.c % 2
        self.peers, self.sibling, self.twin = chip_peers(self.f, self.c)
        self.near = (self.f, flip(self.c, 2))
        self.g, self.gd, self.go = ins
        self.out, self.od, self.oo = results
        self.sb, self.xb, self.xt, self.ut, self.sd, self.xd, self.td, self.so, self.xo, self.to, self.yo, self.yt = (
            scratch[:12]
        )
        self.ss, self.sr, self.xs, self.xr, self.ps, self.pr, self.ys, self.yr = scratch[12:]
        self.home = self.y == self.f
        self.sent = []

    def send(self, src, dst, send_sem, recv_sem, target):
        copy = remote(src, dst, send_sem, recv_sem, target)
        copy.start()
        self.sent.append(copy)
        return copy

    def inner_send(self, src, dst, n):
        return self.send(src, dst, self.ss.at[n], self.sr.at[n], self.sibling)

    def twin_copy(self):
        return remote(self.to, self.xo, self.xs.at[9], self.xr.at[9], self.twin)

    def near_copy(self):
        return remote(self.yt, self.yo, self.ys, self.yr, self.near)

    def first(self):
        other = 1 - self.core
        self.inner = []
        for half in range(2):
            part = 8 * ((1 - self.f) if half == 0 else self.f)
            self.inner.append(
                self.inner_send(self.g.at[pl.ds(part, 8), other], self.sb.at[pl.ds(part, 8)], half)
            )
        self.inner.append(self.inner_send(self.gd.at[:, other], self.sd, 2))
        self.inner.append(self.inner_send(self.go.at[:, other], self.so, 3))

    def second(self):
        f, core = self.f, self.core
        self.crossed = []
        self.inner[0].wait_recv()
        for i in range(8):
            t = (self.chip + i + 1) % 8
            at = (1 - f) * 8 + t
            self.xt[t] = (self.g[at, core].astype(F32) + self.sb[at].astype(F32)).astype(BF)
            self.crossed.append(
                self.send(self.xt.at[t], self.xb.at[t], self.xs.at[i], self.xr.at[i], self.twin)
            )
        self.inner[2].wait_recv()
        self.td[...] = (self.gd[1 - f, core].astype(F32) + self.sd[1 - f].astype(F32)).astype(BF)
        self.crossed.append(self.send(self.td, self.xd, self.xs.at[8], self.xr.at[8], self.twin))
        self.inner[3].wait_recv()
        for side in range(2):
            self.to[side] = (self.go[side, core].astype(F32) + self.so[side].astype(F32)).astype(BF)

        @pl.when(jnp.logical_not(self.home))
        def _():
            self.twin_copy().start()

    def third(self):
        f, core = self.f, self.core
        self.direct = []
        self.inner[1].wait_recv()
        for i in range(8):
            t = (self.chip + i + 1) % 8
            at = f * 8 + t
            self.crossed[i].wait_recv()
            total = self.g[at, core].astype(F32) + self.sb[at].astype(F32) + self.xb[t].astype(F32)
            if i < 7:
                self.ut[t] = total.astype(BF)
                self.direct.append(
                    self.send(self.ut.at[t], self.out.at[self.chip], self.ps.at[i], self.pr.at[i], self.peers[i])
                )
            else:
                self.out[self.chip] = total.astype(BF)
        self.crossed[8].wait_recv()
        self.od[...] = self.gd[f, core].astype(F32) + self.sd[f].astype(F32) + self.xd[...].astype(F32)

        @pl.when(self.home)
        def _():
            self.twin_copy().wait_recv()
            y = self.y
            self.oo[...] = self.to[y].astype(F32) + self.xo[y].astype(F32)
            self.yt[...] = (self.to[1 - y].astype(F32) + self.xo[1 - y].astype(F32)).astype(BF)
            self.near_copy().start()

    def finish(self):
        @pl.when(self.home)
        def _():
            self.near_copy().wait_send()

        @pl.when(jnp.logical_not(self.home))
        def _():
            self.near_copy().wait_recv()
            self.oo[...] = self.yo[...].astype(F32)
            self.twin_copy().wait_send()

        for copy in self.direct:
            copy.wait_recv()
        for copy in self.sent:
            copy.wait_send()


def collect_shapes(rows, wide, block, width):
    results = [((8, rows, wide), BF), ((block, width), F32), ((rows, width), F32)]
    buffers = [
        (16, rows, wide), (8, rows, wide), (8, rows, wide), (8, rows, wide),
        (2, block, width), (block, width), (block, width),
        (2, rows, width), (2, rows, width), (2, rows, width), (rows, width), (rows, width),
    ]
    counts = ((4,), (4,), (10,), (10,), (7,), (7,), (), ())
    scratch = [pltpu.VMEM(b, BF) for b in buffers] + [pltpu.SemaphoreType.DMA(n) for n in counts]
    return results, scratch


def back_collect_kernel(
    left_ref, right_ref, grad_ref, hid_ref, gain_ref, g, gd, go, new_ref, full_ref, c, od, oo, *scratch
):
    def settle(half, total):
        at = half_rows(half)
        new = back_rows(total, grad_ref[at, :].astype(F32), hid_ref[at, :].astype(F32), gain_ref[...])
        new_ref[at, :] = new
        return new.astype(BF)

    def extra(place):
        return Collect(place, (g, gd, go), (c, od, oo), scratch[20:])

    product = make_product(left_ref, right_ref, True)
    exchange(plane_place(), product, settle, full_ref, scratch, extra)


def last_collect_kernel(left_ref, right_ref, grad_ref, hid_ref, gain_ref, g, gd, go, out_ref, c, od, oo, *scratch):
    def settle(half, total):
        at = half_rows(half)
        new = back_rows(total, grad_ref[at, :].astype(F32), hid_ref[at, :].astype(F32), gain_ref[...])
        out_ref[at, :] = new.astype(BF)

    def extra(place):
        return Collect(place, (g, gd, go), (c, od, oo), scratch[14:])

    product = make_product(left_ref, right_ref, True)
    exchange(plane_place(), product, settle, None, scratch, extra)


def head_lanes(head):
    lane = lax.broadcasted_iota(jnp.int32, (1, 128), 1)
    return (lane // 32) % 2 == head


def value_lanes(head):
    lane = lax.broadcasted_iota(jnp.int32, (1, 128), 1)
    return lane // 64 == head


NT = (((1,), (1,)), ((), ()))
TN = (((0,), (0,)), ((), ()))


def attend_kernel(q_ref, k_ref, v_ref, pq_ref, pk_ref, att_ref, lse_ref):
    allowed = pk_ref[...] <= pq_ref[...]
    queries = q_ref[...]
    parts = []
    for head in range(2):
        masked = jnp.where(head_lanes(head), queries, jnp.zeros_like(queries))
        scores = lax.dot_general(masked, k_ref[...], NT, preferred_element_type=F32) * HD ** (-0.5)
        scores = jnp.where(allowed, scores, NEG_FILL)
        top = jnp.max(scores, axis=-1, keepdims=True)
        shares = jnp.exp(scores - top)
        total = jnp.sum(shares, axis=-1, keepdims=True)
        lse_ref[:, head : head + 1] = top + jnp.log(total)
        mixed = jnp.dot(shares.astype(BF), v_ref[...], preferred_element_type=F32)
        parts.append(mixed / total)
    att_ref[...] = jnp.where(value_lanes(0), parts[0], parts[1]).astype(BF)


def attend_forward(q, k, v, pos_q, pos_k):
    rows = q.shape[0]
    keys = k.shape[0]
    step = 128
    return pl.pallas_call(
        attend_kernel,
        grid=(rows // step,),
        out_shape=[
            jax.ShapeDtypeStruct((rows, 128), BF),
            jax.ShapeDtypeStruct((rows, 2), F32),
        ],
        in_specs=[
            pl.BlockSpec((step, 128), lambda i: (i, 0)),
            pl.BlockSpec((keys, 128), lambda i: (0, 0)),
            pl.BlockSpec((keys, 128), lambda i: (0, 0)),
            pl.BlockSpec((step, 1), lambda i: (i, 0)),
            pl.BlockSpec((1, keys), lambda i: (0, 0)),
        ],
        out_specs=[
            pl.BlockSpec((step, 128), lambda i: (i, 0)),
            pl.BlockSpec((step, 2), lambda i: (i, 0)),
        ],
        compiler_params=pltpu.CompilerParams(vmem_limit_bytes=40 * 1024 * 1024),
        name="attend_forward",
    )(q, k, v, pos_q, pos_k)


def attend_back_kernel(q_ref, k_ref, v_ref, da_ref, lse_ref, pq_ref, pk_ref, dq_ref, dk_ref, dv_ref):
    @pl.when(pl.program_id(0) == 0)
    def _():
        dk_ref[...] = jnp.zeros_like(dk_ref)
        dv_ref[...] = jnp.zeros_like(dv_ref)

    allowed = pk_ref[...] <= pq_ref[...]
    queries = q_ref[...]
    grads = da_ref[...]
    parts = []
    for head in range(2):
        masked = jnp.where(head_lanes(head), queries, jnp.zeros_like(queries))
        grad_h = jnp.where(value_lanes(head), grads, jnp.zeros_like(grads))
        scores = lax.dot_general(k_ref[...], masked, NT, preferred_element_type=F32) * HD ** (-0.5)
        shares = jnp.where(allowed, jnp.exp(scores - lse_ref[head : head + 1, :]), 0.0)
        grad_shares = lax.dot_general(v_ref[...], grad_h, NT, preferred_element_type=F32)
        delta = jnp.sum(shares * grad_shares, axis=0, keepdims=True)
        grad_scores = (shares * (grad_shares - delta) * HD ** (-0.5)).astype(BF)
        dv_ref[...] += jnp.dot(shares.astype(BF), grad_h, preferred_element_type=F32)
        dk_ref[...] += jnp.dot(grad_scores, masked, preferred_element_type=F32)
        parts.append(lax.dot_general(grad_scores, k_ref[...], TN, preferred_element_type=F32))
    dq_ref[...] = jnp.where(head_lanes(0), parts[0], parts[1])


def attend_backward(q, k, v, da, lse_rows, pos_q, pos_k):
    rows = q.shape[0]
    keys = k.shape[0]
    step = 128
    return pl.pallas_call(
        attend_back_kernel,
        grid=(rows // step,),
        out_shape=[
            jax.ShapeDtypeStruct((rows, 128), F32),
            jax.ShapeDtypeStruct((keys, 128), F32),
            jax.ShapeDtypeStruct((keys, 128), F32),
        ],
        in_specs=[
            pl.BlockSpec((step, 128), lambda i: (i, 0)),
            pl.BlockSpec((keys, 128), lambda i: (0, 0)),
            pl.BlockSpec((keys, 128), lambda i: (0, 0)),
            pl.BlockSpec((step, 128), lambda i: (i, 0)),
            pl.BlockSpec((2, step), lambda i: (0, i)),
            pl.BlockSpec((1, step), lambda i: (0, i)),
            pl.BlockSpec((keys, 1), lambda i: (0, 0)),
        ],
        out_specs=[
            pl.BlockSpec((step, 128), lambda i: (i, 0)),
            pl.BlockSpec((keys, 128), lambda i: (0, 0)),
            pl.BlockSpec((keys, 128), lambda i: (0, 0)),
        ],
        compiler_params=pltpu.CompilerParams(vmem_limit_bytes=48 * 1024 * 1024),
        name="attend_backward",
    )(q, k, v, da, lse_rows, pos_q, pos_k)


def chip_first(split):
    order = (2, 1, 0) + tuple(range(3, split.ndim))
    return split.transpose(order).reshape(8, split.shape[0], *split.shape[3:])


def chip_last(packed):
    split = packed.reshape(4, 2, *packed.shape[1:])
    return split.transpose((2, 1, 0) + tuple(range(3, split.ndim)))


def pack_heads(weight):
    rows = weight.shape[0]
    split = chip_first(weight.reshape(rows, 2, 4, 2, 2, 32))
    return split.transpose(0, 1, 3, 2, 4).reshape(8, rows, 128)


def unpack_heads(packed):
    rows = packed.shape[1]
    split = packed.reshape(8, rows, 2, 2, 32).transpose(0, 1, 3, 2, 4)
    return chip_last(split).reshape(rows, 1024)


def pack_values(weight):
    rows = weight.shape[0]
    return chip_first(weight.reshape(rows, 2, 4, 128))


def unpack_values(packed):
    return chip_last(packed).reshape(packed.shape[1], 1024)


def pack_units(weight, block, *extra):
    rows, units = weight.shape
    each = units // 32
    split = weight.reshape(rows, 2, 8, 2, each).transpose(2, 0, 1, 3, 4).reshape(8, rows, 4, each)
    padding = jnp.zeros((8, rows, 4, block - each), weight.dtype)
    if extra:
        columns = jnp.stack(extra, axis=-1)
        columns = jnp.pad(columns, ((0, 0), (0, block - each - len(extra))))
        first = jnp.broadcast_to(columns[None, :, None, :], (8, rows, 1, block - each))
        padding = jnp.concatenate([first, padding[:, :, 1:]], axis=2)
    return jnp.concatenate([split, padding], axis=-1).reshape(8, rows, 4 * block)


def unpack_units(packed, units):
    rows = packed.shape[1]
    each = units // 32
    split = packed.reshape(8, rows, 2, 2, -1)[..., :each]
    return split.transpose(1, 2, 0, 3, 4).reshape(rows, units)


def pair_rope(values, cosine, sine):
    first, second = values[:, :64], values[:, 64:]
    return jnp.concatenate(
        [first * cosine - second * sine, second * cosine + first * sine], axis=-1
    )


def pair_unrope(values, cosine, sine):
    first, second = values[:, :64], values[:, 64:]
    return jnp.concatenate(
        [first * cosine + second * sine, second * cosine - first * sine], axis=-1
    )


def swap_cores(value):
    return lax.ppermute(value, "ctx", [(i, i + 1 - 2 * (i % 2)) for i in range(16)])


def fast_local(tokens, cotangent, pair_of, *shards):
    width = tokens.shape[2]
    units = shards[6].shape[1]
    each = units // 32
    block = (each + 2 + 31) // 32 * 32
    hidden_pad = 4 * block
    c = lax.axis_index("ctx")
    core = c % 2
    chip = c // 2
    pos_all = storage_positions(pair_of, ROWS).reshape(8, 2, ROWS)
    own_pos = lax.dynamic_index_in_dim(pos_all, core, 1, False).reshape(-1)
    sib_pos = lax.dynamic_index_in_dim(pos_all, 1 - core, 1, False).reshape(-1)
    key_pos = jnp.concatenate([own_pos, sib_pos])
    cosine, sine = rope_tables(own_pos, HD)
    cosine = jnp.concatenate([cosine, cosine], axis=-1)
    sine = jnp.concatenate([sine, sine], axis=-1)

    layers = [shards[:9], shards[9:]]
    packs = []
    for layer in layers:
        packs.append(
            jnp.concatenate(
                [
                    pack_heads(layer[1]),
                    pack_heads(layer[2]),
                    pack_values(layer[3]),
                    pack_units(layer[6], block, layer[0], layer[5]),
                    pack_units(layer[7], block),
                ],
                axis=-1,
            )
        )
    rows_each, wide = packs[0].shape[1:]
    down = jnp.pad(jnp.stack([layers[0][8], layers[1][8]]), ((0, 0), (0, block - each), (0, 0)))
    tok = tokens.reshape(ROWS, width)
    cot = cotangent.reshape(ROWS, width)
    tok_full, *spread = begin_call(tok, *packs, down, jnp.stack([layers[0][4], layers[1][4]]))
    all_w = [w.reshape(32 * rows_each, wide) for w in spread[:2]]
    qkv_w = [w[:, :384] for w in all_w]
    up_w = [w[:, 384:] for w in all_w]
    down_w = [w.reshape(hidden_pad, width) for w in spread[2:4]]
    out_w = [w.reshape(4 * rows_each, width) for w in spread[4:]]
    gains = []
    for w in all_w:
        columns = w[:, 384 + each : 384 + each + 2].astype(F32).T
        gains += [columns[:1], columns[1:]]

    plane = 8 * ROWS
    full_type = ((plane, width), BF)
    rows_type = ((ROWS, width), F32)
    saved = []
    tok_wide = tok_full.astype(F32)
    full = (tok_wide * norm_rows(tok_wide) * gains[0]).astype(BF)
    hidden = tok
    first_values = None
    pos_q = own_pos[:, None]
    pos_k = key_pos[None, :]
    for layer in range(2):
        x_full = full
        raw = jnp.dot(x_full, qkv_w[layer], preferred_element_type=F32)
        values = raw[:, 256:]
        mixed = values if layer == 0 else 0.5 * values + 0.5 * first_values
        first_values = values
        q = pair_rope(raw[:, :128], cosine, sine).astype(BF)
        kv = jnp.concatenate(
            [pair_rope(raw[:, 128:256], cosine, sine).astype(BF), mixed.astype(BF)], axis=-1
        )
        kv = jnp.concatenate([kv, swap_cores(kv)], axis=0)
        k, v = kv[:, :128], kv[:, 128:]
        att, lse = attend_forward(q, k, v, pos_q, pos_k)
        middle, mlp_full = comm_call(
            forward_kernel, [rows_type, full_type], 1 + layer,
            (att, out_w[layer], hidden, gains[2 * layer + 1]), True,
        )
        both = jnp.dot(mlp_full, up_w[layer], preferred_element_type=F32)
        gate, up = both[:, :hidden_pad], both[:, hidden_pad:]
        inner = (jax.nn.silu(gate) * up).astype(BF)
        saved.append((x_full, q, k, v, lse, att, mlp_full, gate, up, inner, hidden, middle))
        if layer == 0:
            hidden, full = comm_call(
                forward_kernel, [rows_type, full_type], 3,
                (inner, down_w[layer], middle, gains[2]), True,
            )
        else:
            output, full = comm_call(
                turn_kernel, [((ROWS, width), BF), full_type], 4,
                (inner, down_w[layer], middle, cot), True,
            )
    grad = cot
    passed = None
    packed_grads = None
    collected = [None, None]
    for layer in (1, 0):
        x_full, q, k, v, lse, att, mlp_full, gate, up, inner, hidden, middle = saved[layer]
        grad_down = left_product(inner, full)
        grad_inner = right_product(full, down_w[layer])
        sigma = jax.nn.sigmoid(gate)
        grad_gate = (grad_inner * up * sigma * (1.0 + gate * (1.0 - sigma))).astype(BF)
        grad_up = (grad_inner * gate * sigma).astype(BF)
        both = jnp.concatenate([grad_gate, grad_up], axis=-1)
        grad_upw = left_product(mlp_full, both)
        args = (both, up_w[layer], grad, middle, gains[2 * layer + 1])
        results, more = collect_shapes(rows_each, wide, block, width)
        if layer == 1:
            grad_mid, full = comm_call(back_kernel, [rows_type, full_type], 5, args, True)
        else:
            grad_mid, full, *collected[1] = comm_call(
                back_collect_kernel, [rows_type, full_type] + results, 6, args + packed_grads, True, more
            )
        grad_out = left_product(att, full)
        grad_att = right_product(full, out_w[layer]).astype(BF)
        dq, dk, dv = attend_backward(q, k, v, grad_att, lse.T, own_pos[None, :], key_pos[:, None])
        dkv = jnp.concatenate([dk, dv], axis=-1)
        dkv = dkv[: 8 * ROWS] + swap_cores(dkv[8 * ROWS :].astype(BF)).astype(F32)
        dk, dv = dkv[:, :128], dkv[:, 128:]
        if layer == 1:
            passed = 0.5 * dv
            dv = passed
        else:
            dv = dv + passed
        three = jnp.concatenate(
            [pair_unrope(dq, cosine, sine), pair_unrope(dk, cosine, sine), dv], axis=-1
        ).astype(BF)
        grad_qkv = left_product(x_full, three)
        grad_pack = jnp.concatenate([grad_qkv, grad_upw], axis=-1)
        packed_grads = (
            grad_pack.astype(BF).reshape(16, 2, rows_each, wide),
            grad_down.astype(BF).reshape(2, 2, block, width),
            grad_out.astype(BF).reshape(2, 2, rows_each, width),
        )
        args = (three, qkv_w[layer], grad_mid, hidden, gains[2 * layer])
        if layer == 1:
            grad, full = comm_call(back_kernel, [rows_type, full_type], 7, args, True)
        else:
            tokens_grad, *collected[0] = comm_call(
                last_collect_kernel, [((ROWS, width), BF)] + results, 8, args + packed_grads, False, more
            )
    result = [output.reshape(1, ROWS, width), tokens_grad.reshape(1, ROWS, width)]
    for layer in range(2):
        pack = collected[layer][0].astype(F32)
        both = pack * packs[layer].astype(F32)
        pre_grad = jnp.sum(both[:, :, :384], axis=(0, 2)) / layers[layer][0].astype(F32)
        mid_grad = jnp.sum(both[:, :, 384:], axis=(0, 2)) / layers[layer][5].astype(F32)
        result += [
            pre_grad,
            unpack_heads(pack[:, :, :128]),
            unpack_heads(pack[:, :, 128:256]),
            unpack_values(pack[:, :, 256:384]),
            collected[layer][2],
            mid_grad,
            unpack_units(pack[:, :, 384 : 384 + hidden_pad], units),
            unpack_units(pack[:, :, 384 + hidden_pad :], units),
            collected[layer][1][:each],
        ]
    return tuple(result)


def solution(mesh):
    placed = (
        P("fsdp", "ctx", None),
        P("fsdp", "ctx", None),
        P(),
        P(("fsdp", "ctx")),
        P(("fsdp", "ctx"), None),
        P(("fsdp", "ctx"), None),
        P(("fsdp", "ctx"), None),
        P(("fsdp", "ctx"), None),
        P(("fsdp", "ctx")),
        P(("fsdp", "ctx"), None),
        P(("fsdp", "ctx"), None),
        P(("fsdp", "ctx"), None),
        P(("fsdp", "ctx")),
        P(("fsdp", "ctx"), None),
        P(("fsdp", "ctx"), None),
        P(("fsdp", "ctx"), None),
        P(("fsdp", "ctx"), None),
        P(("fsdp", "ctx")),
        P(("fsdp", "ctx"), None),
        P(("fsdp", "ctx"), None),
        P(("fsdp", "ctx"), None),
    )
    fits = mesh.shape["ctx"] == HEADS and mesh.shape["fsdp"] == 2
    return jax.shard_map(
        fast_local if fits else local,
        mesh=mesh,
        in_specs=placed,
        out_specs=(
            P("fsdp", "ctx", None),
            P("fsdp", "ctx", None),
            P(("fsdp", "ctx")),
            P(("fsdp", "ctx"), None),
            P(("fsdp", "ctx"), None),
            P(("fsdp", "ctx"), None),
            P(("fsdp", "ctx"), None),
            P(("fsdp", "ctx")),
            P(("fsdp", "ctx"), None),
            P(("fsdp", "ctx"), None),
            P(("fsdp", "ctx"), None),
            P(("fsdp", "ctx")),
            P(("fsdp", "ctx"), None),
            P(("fsdp", "ctx"), None),
            P(("fsdp", "ctx"), None),
            P(("fsdp", "ctx"), None),
            P(("fsdp", "ctx")),
            P(("fsdp", "ctx"), None),
            P(("fsdp", "ctx"), None),
            P(("fsdp", "ctx"), None),
        ),
        check_vma=False,
    )
```

```python
import functools
import math

import jax
import jax.numpy as jnp
from jax import lax
from jax.experimental import pallas as pl
from jax.experimental.pallas import tpu as pltpu
from jax.sharding import PartitionSpec as P

HEADS = 16
HD = 64


NORM_EPS = 1e-05
NEG_FILL = -1e30


def block_size(total_rows):
    size_now = 512
    while total_rows % size_now:
        size_now //= 2
    return size_now


def row_norm(hidden):
    inverse = lax.rsqrt(jnp.mean(hidden * hidden, axis=-1, keepdims=True) + NORM_EPS)
    return (hidden * inverse, inverse)


def norm_back(grad_normed, normed, inverse):
    return inverse * (grad_normed - normed * jnp.mean(grad_normed * normed, axis=-1, keepdims=True))


def rope_tables(positions, head_size):
    half_size = head_size // 2
    freqs = jnp.exp(
        jnp.arange(half_size, dtype=jnp.float32) * (-2.0 * math.log(10000.0) / head_size)
    )
    angles = positions.astype(jnp.float32)[:, None] * freqs[None, :]
    return (jnp.cos(angles), jnp.sin(angles))


def rotate(values_in, cosine, sine):
    half_size = values_in.shape[-1] // 2
    first_half = values_in[..., :half_size]
    second_half = values_in[..., half_size:]
    cos_rows = cosine[:, None, :]
    sin_rows = sine[:, None, :]
    return jnp.concatenate(
        [
            first_half * cos_rows - second_half * sin_rows,
            second_half * cos_rows + first_half * sin_rows,
        ],
        axis=-1,
    )


def unrotate(grads_in, cosine, sine):
    half_size = grads_in.shape[-1] // 2
    first_half = grads_in[..., :half_size]
    second_half = grads_in[..., half_size:]
    cos_rows = cosine[:, None, :]
    sin_rows = sine[:, None, :]
    return jnp.concatenate(
        [
            first_half * cos_rows + second_half * sin_rows,
            second_half * cos_rows - first_half * sin_rows,
        ],
        axis=-1,
    )


def left_product(left, right):
    return lax.dot_general(
        left, right, (((0,), (0,)), ((), ())), preferred_element_type=jnp.float32
    )


def right_product(left, right):
    return lax.dot_general(
        left, right, (((1,), (1,)), ((), ())), preferred_element_type=jnp.float32
    )


def storage_positions(pair_of, seq_dev):
    devices = pair_of.shape[0]
    rows_all = jnp.arange(devices * seq_dev, dtype=jnp.int32)
    owner = rows_all // seq_dev
    local_row = rows_all % seq_dev
    half_rows = seq_dev // 2
    picked = jnp.sum(
        jnp.where(
            owner[:, None] == jnp.arange(devices, dtype=jnp.int32)[None, :], pair_of[None, :], 0
        ),
        axis=1,
    )
    block_id = jnp.where(local_row < half_rows, picked, 2 * devices - 1 - picked)
    return block_id * half_rows + local_row % half_rows


def head_scores(queries, keys_flat, query_pos, key_pos):
    key_heads = keys_flat.reshape(keys_flat.shape[0], queries.shape[1], queries.shape[2])
    scores = jnp.einsum(
        "qhd,khd->hqk", queries, key_heads, preferred_element_type=jnp.float32
    ) * queries.shape[2] ** (-0.5)
    allowed = (key_pos[None, :] <= query_pos[:, None])[None]
    return (jnp.where(allowed, scores, NEG_FILL), allowed)


def make_stats_step(queries, query_pos, pos_all, state_in, key_part):
    size_now = block_size(key_part.shape[0])

    def inner_step(block_no, state_now):
        top_now, total_now = state_now
        offset = block_no * size_now
        key_block = lax.dynamic_slice_in_dim(key_part, offset, size_now, 0)
        key_pos = lax.dynamic_slice_in_dim(pos_all, offset, size_now, 0)
        scores, allowed = head_scores(queries, key_block, query_pos, key_pos)
        new_top = jnp.maximum(top_now, jnp.max(scores, axis=-1))
        total_now = total_now * jnp.exp(top_now - new_top) + jnp.sum(
            jnp.where(allowed, jnp.exp(scores - new_top[..., None]), 0.0), axis=-1
        )
        return (new_top, total_now)

    return lax.fori_loop(0, key_part.shape[0] // size_now, inner_step, state_in)


def make_value_step(queries, log_total, query_pos, pos_all, acc_in, pieces):
    key_part, value_part = pieces
    size_now = block_size(key_part.shape[0])

    def inner_step(block_no, acc_now):
        offset = block_no * size_now
        key_block = lax.dynamic_slice_in_dim(key_part, offset, size_now, 0)
        value_block = lax.dynamic_slice_in_dim(value_part, offset, size_now, 0)
        key_pos = lax.dynamic_slice_in_dim(pos_all, offset, size_now, 0)
        scores, allowed = head_scores(queries, key_block, query_pos, key_pos)
        shares = jnp.exp(scores - log_total[..., None]).astype(jnp.bfloat16)
        value_heads = value_block.reshape(size_now, queries.shape[1], queries.shape[2])
        return acc_now + jnp.einsum(
            "hqk,khd->qhd", shares, value_heads, preferred_element_type=jnp.float32
        )

    return lax.fori_loop(0, key_part.shape[0] // size_now, inner_step, acc_in)


def make_back_step(queries, grad_att, log_total, row_delta, query_pos, pos_all):
    scale_now = queries.shape[2] ** (-0.5)

    def back_step(state_in, pieces, start_row):
        key_part, value_part = pieces
        size_now = block_size(key_part.shape[0])

        def inner_step(block_no, state_now):
            offset = block_no * size_now
            key_block = lax.dynamic_slice_in_dim(key_part, offset, size_now, 0)
            value_block = lax.dynamic_slice_in_dim(value_part, offset, size_now, 0)
            key_pos = lax.dynamic_slice_in_dim(pos_all, offset, size_now, 0)
            scores, allowed = head_scores(queries, key_block, query_pos, key_pos)
            shares = jnp.exp(scores - log_total[..., None])
            value_heads = value_block.reshape(size_now, queries.shape[1], queries.shape[2])
            key_heads = key_block.reshape(size_now, queries.shape[1], queries.shape[2])
            grad_shares = jnp.einsum(
                "qhd,khd->hqk", grad_att, value_heads, preferred_element_type=jnp.float32
            )
            grad_scores = (shares * (grad_shares - row_delta[..., None]) * scale_now).astype(
                jnp.bfloat16
            )
            grad_query = state_now[0] + jnp.einsum(
                "hqk,khd->qhd", grad_scores, key_heads, preferred_element_type=jnp.float32
            )
            return (grad_query,)

        return lax.fori_loop(0, key_part.shape[0] // size_now, inner_step, state_in)

    return back_step


def make_query_step(own_keys, own_values, own_pos, stats_all, pos_all, head_count, head_size):
    scale_now = head_size ** (-0.5)
    value_heads = own_values.reshape(own_values.shape[0], head_count, head_size)

    def query_step(state_in, pieces, start_row):
        query_part, grad_part = pieces
        size_now = block_size(query_part.shape[0])

        def inner_step(block_no, state_now):
            offset = block_no * size_now
            query_block = lax.dynamic_slice_in_dim(query_part, offset, size_now, 0).reshape(
                size_now, head_count, head_size
            )
            grad_block = lax.dynamic_slice_in_dim(grad_part, offset, size_now, 0).reshape(
                size_now, head_count, head_size
            )
            query_pos = lax.dynamic_slice_in_dim(pos_all, offset, size_now, 0)
            log_block = lax.dynamic_slice_in_dim(stats_all[0], offset, size_now, 0).T
            delta_block = lax.dynamic_slice_in_dim(stats_all[1], offset, size_now, 0).T
            scores, allowed = head_scores(query_block, own_keys, query_pos, own_pos)
            shares = jnp.exp(scores - log_block[..., None])
            grad_shares = jnp.einsum(
                "qhd,khd->hqk", grad_block, value_heads, preferred_element_type=jnp.float32
            )
            grad_scores = (shares * (grad_shares - delta_block[..., None]) * scale_now).astype(
                jnp.bfloat16
            )
            key_term = jnp.einsum(
                "hqk,qhd->khd", grad_scores, query_block, preferred_element_type=jnp.float32
            )
            value_term = jnp.einsum(
                "hqk,qhd->khd",
                shares.astype(jnp.bfloat16),
                grad_block,
                preferred_element_type=jnp.float32,
            )
            return (
                state_now[0] + key_term.reshape(key_term.shape[0], -1),
                state_now[1] + value_term.reshape(value_term.shape[0], -1),
            )

        return lax.fori_loop(0, query_part.shape[0] // size_now, inner_step, state_in)

    return query_step


def gather_forward(shards):
    return (
        lax.all_gather(shards[0], ("fsdp", "ctx"), axis=0, tiled=True),
        lax.all_gather(shards[1], ("fsdp", "ctx"), axis=0, tiled=True),
        lax.all_gather(shards[2], ("fsdp", "ctx"), axis=0, tiled=True),
        lax.all_gather(shards[3], ("fsdp", "ctx"), axis=0, tiled=True),
        lax.all_gather(shards[4], ("fsdp", "ctx"), axis=0, tiled=True),
        lax.all_gather(shards[5], ("fsdp", "ctx"), axis=0, tiled=True),
        lax.all_gather(shards[6], ("fsdp", "ctx"), axis=0, tiled=True),
        lax.all_gather(shards[7], ("fsdp", "ctx"), axis=0, tiled=True),
        lax.all_gather(shards[8], ("fsdp", "ctx"), axis=0, tiled=True),
    )


def scatter_grads(grad_terms):
    return (
        lax.psum_scatter(grad_terms[0], ("fsdp", "ctx"), scatter_dimension=0, tiled=True),
        lax.psum_scatter(grad_terms[1], ("fsdp", "ctx"), scatter_dimension=0, tiled=True),
        lax.psum_scatter(grad_terms[2], ("fsdp", "ctx"), scatter_dimension=0, tiled=True),
        lax.psum_scatter(grad_terms[3], ("fsdp", "ctx"), scatter_dimension=0, tiled=True),
        lax.psum_scatter(grad_terms[4], ("fsdp", "ctx"), scatter_dimension=0, tiled=True),
        lax.psum_scatter(grad_terms[5], ("fsdp", "ctx"), scatter_dimension=0, tiled=True),
        lax.psum_scatter(grad_terms[6], ("fsdp", "ctx"), scatter_dimension=0, tiled=True),
        lax.psum_scatter(grad_terms[7], ("fsdp", "ctx"), scatter_dimension=0, tiled=True),
        lax.psum_scatter(grad_terms[8], ("fsdp", "ctx"), scatter_dimension=0, tiled=True),
    )


def forward_layer(hidden, full_layer, first_values, context):
    prenorm, query_w, keys_w, values_w, outproj, midnorm, gates_w, upproj_w, downproj_w = full_layer
    cosine, sine, own_pos, pos_all = context
    rows_n, model_width = hidden.shape
    normed, inverse_a = row_norm(hidden)
    attn_in = (normed * prenorm.astype(jnp.float32)).astype(jnp.bfloat16)
    query_raw = jnp.dot(attn_in, query_w, preferred_element_type=jnp.float32)
    keys_raw = jnp.dot(attn_in, keys_w, preferred_element_type=jnp.float32)
    values_raw = jnp.dot(attn_in, values_w, preferred_element_type=jnp.float32)
    mixed = values_raw if first_values is None else 0.5 * values_raw + 0.5 * first_values
    queries = rotate(query_raw.reshape(rows_n, HEADS, HD), cosine, sine).astype(jnp.bfloat16)
    keys_flat = (
        rotate(keys_raw.reshape(rows_n, HEADS, HD), cosine, sine)
        .reshape(rows_n, model_width)
        .astype(jnp.bfloat16)
    )
    values_flat = mixed.astype(jnp.bfloat16)
    top_start = jnp.full((HEADS, rows_n), NEG_FILL, jnp.float32)
    total_start = jnp.zeros((HEADS, rows_n), jnp.float32)
    top_now, total_now = make_stats_step(
        queries,
        own_pos,
        pos_all,
        (top_start, total_start),
        lax.all_gather(keys_flat, "ctx", axis=0, tiled=True),
    )
    log_total = top_now + jnp.log(total_now)
    att_out = make_value_step(
        queries,
        log_total,
        own_pos,
        pos_all,
        jnp.zeros((rows_n, HEADS, HD), jnp.float32),
        (
            lax.all_gather(keys_flat, "ctx", axis=0, tiled=True),
            lax.all_gather(values_flat, "ctx", axis=0, tiled=True),
        ),
    )
    att_low = att_out.reshape(rows_n, model_width).astype(jnp.bfloat16)
    middle = hidden + jnp.dot(att_low, outproj, preferred_element_type=jnp.float32)
    normed_mid, inverse_b = row_norm(middle)
    mlp_in = (normed_mid * midnorm.astype(jnp.float32)).astype(jnp.bfloat16)
    gate_raw = jnp.dot(mlp_in, gates_w, preferred_element_type=jnp.float32)
    up_proj = jnp.dot(mlp_in, upproj_w, preferred_element_type=jnp.float32)
    inner_act = (jax.nn.silu(gate_raw) * up_proj).astype(jnp.bfloat16)
    result = middle + jnp.dot(inner_act, downproj_w, preferred_element_type=jnp.float32)
    saved = (
        hidden,
        normed,
        inverse_a,
        attn_in,
        queries,
        keys_flat,
        values_flat,
        log_total,
        att_out,
        att_low,
        normed_mid,
        inverse_b,
        mlp_in,
        gate_raw,
        up_proj,
        inner_act,
    )
    return (result, values_raw, saved)


def backward_layer(grad_out, full_layer, saved, value_extra, is_second, context):
    prenorm, query_w, keys_w, values_w, outproj, midnorm, gates_w, upproj_w, downproj_w = full_layer
    (
        hidden,
        normed,
        inverse_a,
        attn_in,
        queries,
        keys_flat,
        values_flat,
        log_total,
        att_out,
        att_low,
        normed_mid,
        inverse_b,
        mlp_in,
        gate_raw,
        up_proj,
        inner_act,
    ) = saved
    cosine, sine, own_pos, pos_all = context
    rows_n, model_width = hidden.shape
    grad_low = grad_out.astype(jnp.bfloat16)
    grad_down = left_product(inner_act, grad_low)
    grad_inner = right_product(grad_low, downproj_w)
    sigma_gate = jax.nn.sigmoid(gate_raw)
    grad_gate = (grad_inner * up_proj * sigma_gate * (1.0 + gate_raw * (1.0 - sigma_gate))).astype(
        jnp.bfloat16
    )
    grad_up = (grad_inner * gate_raw * sigma_gate).astype(jnp.bfloat16)
    grad_gates = left_product(mlp_in, grad_gate)
    grad_upproj = left_product(mlp_in, grad_up)
    grad_mlp = right_product(grad_gate, gates_w) + right_product(grad_up, upproj_w)
    grad_midnorm = jnp.sum(grad_mlp * normed_mid, axis=0)
    grad_middle = grad_out + norm_back(
        grad_mlp * midnorm.astype(jnp.float32), normed_mid, inverse_b
    )
    branch_low = grad_middle.astype(jnp.bfloat16)
    grad_outproj = left_product(att_low, branch_low)
    grad_att = right_product(branch_low, outproj).astype(jnp.bfloat16).reshape(rows_n, HEADS, HD)
    row_delta = jnp.sum(grad_att.astype(jnp.float32) * att_out, axis=-1).T
    query_start = jnp.zeros((rows_n, HEADS, HD), jnp.float32)
    state_start = (query_start,)
    back_fn = make_back_step(queries, grad_att, log_total, row_delta, own_pos, pos_all)
    state_out = back_fn(
        state_start,
        (
            lax.all_gather(keys_flat, "ctx", axis=0, tiled=True),
            lax.all_gather(values_flat, "ctx", axis=0, tiled=True),
        ),
        jnp.int32(0),
    )
    grad_qr = state_out[0]
    stats_all = (
        lax.all_gather(log_total.T, "ctx", axis=0, tiled=True),
        lax.all_gather(row_delta.T, "ctx", axis=0, tiled=True),
    )
    query_fn = make_query_step(keys_flat, values_flat, own_pos, stats_all, pos_all, HEADS, HD)
    flat_start = jnp.zeros((rows_n, model_width), jnp.float32)
    grad_kr, grad_mix = query_fn(
        (flat_start, flat_start),
        (
            lax.all_gather(queries.reshape(rows_n, model_width), "ctx", axis=0, tiled=True),
            lax.all_gather(grad_att.reshape(rows_n, model_width), "ctx", axis=0, tiled=True),
        ),
        jnp.int32(0),
    )
    grad_query = unrotate(grad_qr, cosine, sine).reshape(rows_n, model_width).astype(jnp.bfloat16)
    grad_keys = (
        unrotate(grad_kr.reshape(rows_n, HEADS, HD), cosine, sine)
        .reshape(rows_n, model_width)
        .astype(jnp.bfloat16)
    )
    if is_second:
        grad_values = (0.5 * grad_mix).astype(jnp.bfloat16)
        passed_on = 0.5 * grad_mix
    else:
        grad_values = (grad_mix + value_extra).astype(jnp.bfloat16)
        passed_on = None
    grad_query_w = left_product(attn_in, grad_query)
    grad_keys_w = left_product(attn_in, grad_keys)
    grad_values_w = left_product(attn_in, grad_values)
    grad_attn = (
        right_product(grad_query, query_w)
        + right_product(grad_keys, keys_w)
        + right_product(grad_values, values_w)
    )
    grad_prenorm = jnp.sum(grad_attn * normed, axis=0)
    grad_hidden = grad_middle + norm_back(
        grad_attn * prenorm.astype(jnp.float32), normed, inverse_a
    )
    grad_terms = (
        grad_prenorm,
        grad_query_w,
        grad_keys_w,
        grad_values_w,
        grad_outproj,
        grad_midnorm,
        grad_gates,
        grad_upproj,
        grad_down,
    )
    return (grad_hidden, grad_terms, passed_on)


def local(
    tokens,
    cotangent,
    pair_of,
    prenorm_one,
    query_one,
    keys_one,
    values_one,
    outproj_one,
    midnorm_one,
    gates_one,
    upproj_one,
    downproj_one,
    prenorm_two,
    query_two,
    keys_two,
    values_two,
    outproj_two,
    midnorm_two,
    gates_two,
    upproj_two,
    downproj_two,
):
    seq_dev = tokens.shape[1]
    model_width = tokens.shape[2]
    pos_all = storage_positions(pair_of, seq_dev)
    own_pos = lax.dynamic_slice_in_dim(pos_all, lax.axis_index("ctx") * seq_dev, seq_dev, 0)
    cosine, sine = rope_tables(own_pos, HD)
    context = (cosine, sine, own_pos, pos_all)
    layer_shards = [
        (
            prenorm_one,
            query_one,
            keys_one,
            values_one,
            outproj_one,
            midnorm_one,
            gates_one,
            upproj_one,
            downproj_one,
        ),
        (
            prenorm_two,
            query_two,
            keys_two,
            values_two,
            outproj_two,
            midnorm_two,
            gates_two,
            upproj_two,
            downproj_two,
        ),
    ]
    hidden = tokens.reshape(seq_dev, model_width).astype(jnp.float32)
    first_values = None
    kept_full = []
    kept_saved = []
    for layer_no in range(2):
        full_layer = gather_forward(layer_shards[layer_no])
        hidden, values_raw, saved = forward_layer(hidden, full_layer, first_values, context)
        if layer_no == 0:
            first_values = values_raw
        kept_full.append(full_layer)
        kept_saved.append(saved)
    output = hidden.astype(jnp.bfloat16).reshape(1, seq_dev, model_width)
    grad_now = cotangent.reshape(seq_dev, model_width).astype(jnp.float32)
    value_extra = None
    layer_grads = [None, None]
    for layer_no in (1, 0):
        full_layer = kept_full[layer_no]
        grad_now, grad_terms, passed_on = backward_layer(
            grad_now, full_layer, kept_saved[layer_no], value_extra, layer_no == 1, context
        )
        if layer_no == 1:
            value_extra = passed_on
        layer_grads[layer_no] = scatter_grads(grad_terms)
    tokens_grad = grad_now.astype(jnp.bfloat16).reshape(1, seq_dev, model_width)
    first_grads = layer_grads[0]
    second_grads = layer_grads[1]
    return (
        output,
        tokens_grad,
        first_grads[0],
        first_grads[1],
        first_grads[2],
        first_grads[3],
        first_grads[4],
        first_grads[5],
        first_grads[6],
        first_grads[7],
        first_grads[8],
        second_grads[0],
        second_grads[1],
        second_grads[2],
        second_grads[3],
        second_grads[4],
        second_grads[5],
        second_grads[6],
        second_grads[7],
        second_grads[8],
    )


ROWS = 128
BF = jnp.bfloat16
F32 = jnp.float32
MESH = pl.DeviceIdType.MESH
VMEM_SPACE = pltpu.VMEM


def flip(value, weight):
    return value + weight * (1 - 2 * ((value // weight) % 2))


def to_device(f, c):
    return {"fsdp": f, "ctx": c}


def remote(src, dst, send_sem, recv_sem, target):
    return pltpu.make_async_remote_copy(
        src_ref=src,
        dst_ref=dst,
        send_sem=send_sem,
        recv_sem=recv_sem,
        device_id=to_device(*target),
        device_id_type=MESH,
    )


def arrived(ref, sem, target):
    remote(ref, ref, sem, sem, target).wait_recv()


def plane_place():
    f = lax.axis_index("fsdp")
    c = lax.axis_index("ctx")
    return f, c, (c // 2) % 2, c // 4


def row_peers(f, c, z):
    return [(f, c + 4 * ((z + i) % 4 - z)) for i in range(1, 4)]


HALF = ROWS // 2
ODD = 8


class Plane:
    def __init__(self, place, inner):
        f, c, y, z = place
        self.y, self.inner = y, inner
        self.mirrored = z // 2
        sign = 1 - 2 * self.mirrored
        self.own = 1 if inner else 0
        self.across = (f, flip(c, 2))
        self.chip_at = [(f, c + 4 * sign * (near - self.own)) for near in range(4)]
        self.sent = []

    def at(self, near):
        return near + self.mirrored * (3 - 2 * near)

    def slot(self, half, near):
        return 4 * half + self.at(near)

    def start(self, copy):
        copy.start()
        self.sent.append(copy)

    def finish(self):
        for copy in self.sent:
            copy.wait_send()


class Reduce(Plane):
    def __init__(self, place, inner, product, bufs, sems):
        super().__init__(place, inner)
        self.product = product
        self.sy, self.ry, self.acc, self.pb, self.su, self.sd, self.rb, self.ra = bufs
        self.ys, self.yr, self.us, self.ds, self.br, self.ar = sems

    def y_copy(self, slot):
        return remote(self.sy.at[slot], self.ry.at[slot], self.ys.at[slot], self.yr.at[slot], self.across)

    def got_y(self, slot):
        self.y_copy(slot).wait_recv()
        return self.ry[slot].astype(F32)

    def got(self, first, slot):
        buf, sem = (self.rb, self.br) if first else (self.ra, self.ar)
        arrived(buf.at[slot], sem.at[slot], self.across)
        return buf[slot].astype(F32)

    def pass_on(self, value, upward, slot, target, first, there=None):
        there = slot if there is None else there
        src, send = (self.su, self.us) if upward else (self.sd, self.ds)
        dst, sem = (self.rb, self.br) if first else (self.ra, self.ar)
        src[slot] = value.astype(BF)
        self.start(remote(src.at[slot], dst.at[there], send.at[slot], sem.at[there], self.chip_at[target]))

    def cross(self, slot, value):
        self.sy[slot] = value.astype(BF)
        self.start(self.y_copy(slot))

    def order(self, step):
        near = 3 - step
        if self.inner:
            near = jnp.where(step == 0, 3, jnp.where(step == 1, 0, 4 - step))
        return near, near + self.mirrored * (3 - 2 * near)

    def products(self):
        def other_row(step, carry):
            near, block = self.order(step)
            value = self.product(2 * block + 1 - self.y)
            self.sy[block] = value[:HALF].astype(BF)
            self.y_copy(block).start()
            self.pb[block] = value[HALF:]

            @pl.when((near == 1) | (near == 2))
            def _():
                self.sy[4 + block] = value[HALF:].astype(BF)
                self.y_copy(4 + block).start()

            return carry

        lax.fori_loop(0, 4, other_row, 0)
        for near in range(4):
            self.sent.append(self.y_copy(self.slot(0, near)))
        for near in (1, 2):
            self.sent.append(self.y_copy(self.slot(1, near)))
        if self.inner:
            self.pass_on(self.pb[self.at(3)], True, ODD, 3, True)
            self.pass_on(self.pb[self.at(0)], False, ODD, 0, False)
        else:
            self.pass_on(self.pb[self.at(3)], True, ODD, 3, False, ODD + 1)

        def own_row(step, carry):
            near, block = self.order(step)
            value = self.product(2 * block + self.y)
            self.acc[block] = value[:HALF]
            self.acc[4 + block] = value[HALF:]
            return carry

        lax.fori_loop(0, 4, own_row, 0)
        far = self.slot(1, 3)
        if self.inner:
            end = self.slot(1, 0)
            self.pass_on(self.acc[end], False, end, 0, False)
            self.pass_on(self.acc[far] + self.got(True, far), True, far, 3, True)
        else:
            self.pass_on(self.acc[far], True, far, 1, True)

    def relay(self, half, near):
        slot = self.slot(half, near)
        value = self.acc[slot] + self.got_y(slot)
        if not self.inner:
            self.pass_on(value, True, slot, 1, True)
        elif near == 0:
            self.pass_on(value, False, slot, 0, False)
        else:
            self.pass_on(value + self.got(True, slot), True, slot, near, near == 3)

    def relays(self):
        if self.inner:
            self.relay(0, 3)
            self.relay(0, 0)
            self.relay(0, 2)
            self.relay(1, 2)
            return
        self.relay(0, 3)
        self.relay(0, 2)
        self.relay(1, 2)
        odd = self.pb[self.at(0)] + self.got(False, ODD) + self.got(True, ODD) + self.got(False, ODD + 1)
        self.cross(self.slot(1, 0), odd)
        self.relay(0, 1)
        self.relay(1, 1)

    def own_sum(self, half):
        slot = self.slot(half, self.own)
        return self.acc[slot] + self.got_y(slot) + self.got(True, slot) + self.got(False, slot)


class Gather(Plane):
    def __init__(self, place, inner, full, sems):
        super().__init__(place, inner)
        self.full = full
        self.ys, self.yr, self.us, self.ds, self.zr = sems

    def rows(self, half, near, side):
        start = (self.at(near) * 2 + side) * ROWS + half * HALF
        return self.full.at[pl.ds(pl.multiple_of(start, HALF), HALF)]

    def to_row(self, part, sem, slot, target):
        self.start(remote(part, part, sem, self.zr.at[slot], self.chip_at[target]))

    def to_other_row(self, half, near):
        part = self.rows(half, near, self.y)
        slot = self.slot(half, near)
        self.start(remote(part, part, self.ys.at[slot], self.yr.at[slot], self.across))

    def send_own(self, half):
        part = self.rows(half, self.own, self.y)
        slot = self.slot(half, self.own)
        self.to_row(part, self.us.at[slot], slot, 2)
        self.to_row(part, self.ds.at[slot], slot, 0 if self.inner else 1)
        self.to_other_row(half, self.own)

    def take(self, half, near):
        part = self.rows(half, near, self.y)
        slot = self.slot(half, near)
        arrived(part, self.zr.at[slot], self.across)
        if self.inner and near in (2, 3):
            self.to_row(part, self.ds.at[slot], slot, 0)
        if half == 0 or near in (1, 2):
            self.to_other_row(half, near)

    def odd_slot(self, near):
        return ODD + self.at(near) // 3

    def take_odd(self, near):
        arrived(self.rows(1, near, 1 - self.y), self.zr.at[self.odd_slot(near)], self.across)

    def got_y(self, half, near):
        arrived(self.rows(half, near, 1 - self.y), self.yr.at[self.slot(half, near)], self.across)

    def forward(self, half):
        others = (0, 2, 3) if self.inner else (1, 2, 3)
        if half == 0:
            for near in others:
                self.take(0, near)
            return
        if not self.inner:
            self.got_y(1, 0)
            part = self.rows(1, 0, 1 - self.y)
            slot = self.odd_slot(0)
            self.to_row(part, self.us.at[8], slot, 3)
            self.to_row(part, self.us.at[9], slot, 2)
            self.to_row(part, self.ds.at[8], slot, 1)
        for near in others:
            self.take(1, near)
        if self.inner:
            self.take_odd(0)
        self.take_odd(3)
        for near in range(4):
            self.got_y(0, near)
        for near in (1, 2):
            self.got_y(1, near)


def both_kinds(place, run):
    z = place[3]

    @pl.when((z > 0) & (z < 3))
    def _():
        run(True)

    @pl.when((z == 0) | (z == 3))
    def _():
        run(False)


def exchange(place, product, settle, full, scratch, extra=None):
    if extra is None:
        f, c, y, z = place
        greet(row_peers(f, c, z) + [(f, flip(c, 2))])
    else:
        peers, sibling, twin = chip_peers(place[0], place[1])
        greet(peers + [sibling, twin])

    def run(inner):
        parts = []
        more = None if extra is None else extra(place)
        if more is not None:
            more.first()
            parts.append(more)
        reduce = Reduce(place, inner, product, scratch[:8], scratch[8:14])
        reduce.products()
        parts.append(reduce)
        if full is not None:
            gather = Gather(place, inner, full, scratch[14:19])
            parts.append(gather)
        if more is not None:
            more.second()
        reduce.relays()
        for half in range(2):
            rows = settle(half, reduce.own_sum(half))
            if full is not None:
                start = (place[3] * 2 + place[2]) * ROWS + half * HALF
                full[pl.ds(pl.multiple_of(start, HALF), HALF), :] = rows
                gather.send_own(half)
            if more is not None and half == 0:
                more.third()
        if full is not None:
            gather.forward(0)
            gather.forward(1)
        for part in parts:
            part.finish()

    both_kinds(place, run)


def half_rows(half):
    return pl.ds(half * HALF, HALF)


def norm_rows(hidden):
    return lax.rsqrt(jnp.mean(hidden * hidden, axis=-1, keepdims=True) + NORM_EPS)


def make_product(left_ref, right_ref, transposed, lanes=None):
    dims = (((1,), (1,)), ((), ())) if transposed else (((1,), (0,)), ((), ()))

    def product(block):
        rows = left_ref[pl.ds(pl.multiple_of(block * ROWS, ROWS), ROWS), :]
        right = right_ref[...] if lanes is None else right_ref[:, lanes[0] : lanes[1]]
        return lax.dot_general(rows, right, dims, preferred_element_type=F32)

    return product


def forward_kernel(left_ref, right_ref, res_ref, gain_ref, new_ref, full_ref, *scratch):
    def settle(half, total):
        hidden = res_ref[half_rows(half), :].astype(F32) + total
        new_ref[half_rows(half), :] = hidden
        return (hidden * norm_rows(hidden) * gain_ref[...]).astype(BF)

    exchange(plane_place(), make_product(left_ref, right_ref, False), settle, full_ref, scratch)


def turn_kernel(left_ref, right_ref, res_ref, cot_ref, out_ref, full_ref, *scratch):
    def settle(half, total):
        out_ref[half_rows(half), :] = (res_ref[half_rows(half), :] + total).astype(BF)
        return cot_ref[half_rows(half), :]

    exchange(plane_place(), make_product(left_ref, right_ref, False), settle, full_ref, scratch)


def back_rows(total, grad, hidden, gain):
    inverse = norm_rows(hidden)
    normed = hidden * inverse
    scaled = total * gain
    mean = jnp.mean(scaled * normed, axis=-1, keepdims=True)
    return grad + inverse * (scaled - normed * mean)


def comm_call(kernel, outs, ident, args, gathers, name, more=()):
    width = 1024
    scratch = []
    for count, kind in ((8, BF), (8, BF), (8, F32), (4, F32), (9, BF), (9, BF), (9, BF), (10, BF)):
        scratch.append(pltpu.VMEM((count, HALF, width), kind))
    scratch += [pltpu.SemaphoreType.DMA((10,))] * 6
    if gathers:
        scratch += [pltpu.SemaphoreType.DMA((10,))] * 5
    scratch += list(more)
    spec = pl.BlockSpec(memory_space=VMEM_SPACE)
    return pl.pallas_call(
        kernel,
        out_shape=[jax.ShapeDtypeStruct(*o) for o in outs],
        in_specs=[spec] * len(args),
        out_specs=[spec] * len(outs),
        scratch_shapes=scratch,
        compiler_params=pltpu.CompilerParams(
            collective_id=ident, has_side_effects=True, vmem_limit_bytes=(24 if more else 14) * 1024 * 1024
        ),
        name=name,
    )(*args)


def chip_peers(f, c):
    chip, core = c // 2, c % 2
    return [(f, 2 * ((chip + i) % 8) + core) for i in range(1, 8)], (f, flip(c, 1)), (1 - f, c)


def greet(targets):
    barrier = pltpu.get_barrier_semaphore()
    for target in targets:
        pl.semaphore_signal(barrier, inc=1, device_id=to_device(*target), device_id_type=MESH)
    pl.semaphore_wait(barrier, len(targets))


class Spread:
    def __init__(self, place, tables, downs, outs, sems):
        self.f, self.c, self.y, _ = place
        self.chip, self.core = self.c // 2, self.c % 2
        self.peers, self.sibling, self.twin = chip_peers(self.f, self.c)
        self.near = (self.f, flip(self.c, 2))
        self.tables, self.downs, self.outs = tables, downs, outs
        self.ds, self.dr, self.xs, self.xr, self.ss, self.sr, self.ws, self.wr = sems
        self.home = self.y == self.f
        self.direct, self.crossed, self.inner, self.sent = {}, {}, [], []

    def send(self, src, dst, send_sem, recv_sem, target):
        copy = remote(src, dst, send_sem, recv_sem, target)
        copy.start()
        self.sent.append(copy)
        return copy

    def to_twin(self, src, dst, l, n):
        self.crossed[l, n] = self.send(src, dst, self.xs.at[l, n], self.xr.at[l, n], self.twin)

    def to_sibling(self, src, dst, l, n):
        self.inner.append(self.send(src, dst, self.ss.at[l, n], self.sr.at[l, n], self.sibling))

    def out_copy(self, l):
        op, out = self.outs[l]
        part = 2 * self.y + self.core
        return remote(op, out.at[part], self.ws.at[l], self.wr.at[l], self.near)

    def pair_copies(self, l, s, r, first, target):
        parts = [self.outs[l][1].at[self.core], self.outs[l][1].at[2 + self.core]]
        return [remote(p, p, s.at[l, first + n], r.at[l, first + n], target) for n, p in enumerate(parts)]

    def first(self, l):
        a, r = self.tables[l]
        down, down_all = self.downs[l]
        op, out = self.outs[l]
        mine = self.f * 16 + self.c
        part = 2 * self.f + self.core
        self.to_twin(a.at[self.chip], r.at[mine], l, 0)
        for i in range(1, 8):
            t = (self.chip + i) % 8
            self.direct[l, i] = self.send(
                a.at[t], r.at[mine], self.ds.at[l, i], self.dr.at[l, i], self.peers[i - 1]
            )
        r[mine] = a[self.chip]
        self.to_sibling(a.at[self.chip], r.at[mine], l, 0)
        down_all[part] = down[...]
        self.to_twin(down, down_all.at[part], l, 8)
        self.to_sibling(down, down_all.at[part], l, 16)

        @pl.when(self.home)
        def _():
            out[2 * self.y + self.core] = op[...]

        @pl.when(jnp.logical_not(self.home))
        def _():
            self.out_copy(l).start()

    def second(self, l):
        r = self.tables[l][1]
        for i in range(1, 8):
            self.direct[l, i].wait_recv()
            source = self.f * 16 + 2 * ((self.chip + 8 - i) % 8) + self.core
            self.to_twin(r.at[source], r.at[source], l, i)
            self.to_sibling(r.at[source], r.at[source], l, i)

        @pl.when(self.home)
        def _():
            self.out_copy(l).wait_recv()
            for copy in self.pair_copies(l, self.xs, self.xr, 9, self.twin):
                copy.start()

    def third(self, l):
        r = self.tables[l][1]

        @pl.when(jnp.logical_not(self.home))
        def _():
            for copy in self.pair_copies(l, self.xs, self.xr, 9, self.twin):
                copy.wait_recv()

        for copy in self.pair_copies(l, self.ss, self.sr, 18, self.sibling):
            copy.start()
        for i in range(8):
            self.crossed[l, i].wait_recv()
            source = (1 - self.f) * 16 + 2 * ((self.chip + 8 - i) % 8) + self.core
            self.to_sibling(r.at[source], r.at[source], l, 8 + i)
        self.crossed[l, 8].wait_recv()
        part = 2 * (1 - self.f) + self.core
        down_all = self.downs[l][1]
        self.to_sibling(down_all.at[part], down_all.at[part], l, 17)

    def finish(self):
        for copy in self.inner:
            copy.wait_recv()
        for copy in self.sent:
            copy.wait_send()
        for l in range(len(self.tables)):
            for copy in self.pair_copies(l, self.ss, self.sr, 18, self.sibling):
                copy.wait()

            @pl.when(self.home)
            def _():
                for copy in self.pair_copies(l, self.xs, self.xr, 9, self.twin):
                    copy.wait_send()

            @pl.when(jnp.logical_not(self.home))
            def _():
                self.out_copy(l).wait_send()


def pack_shards(shards, block, a):
    pre, query, keys, values, mid, gates, upproj = shards
    rows, units = gates.shape
    each = units // 32
    lane = lax.broadcasted_iota(jnp.int32, (rows, block - each), 1)
    empty = jnp.zeros((rows, block - each), F32)
    riders = jnp.where(lane == 0, pre[...].astype(F32), jnp.where(lane == 1, mid[...].astype(F32), empty))
    for chip in range(8):
        pair = 4 * (chip % 2) + chip // 2
        for n, w in enumerate((query, keys, values)):
            a[chip, :, 128 * n : 128 * n + 128] = w[:, 128 * pair : 128 * pair + 128]
        for n, w in enumerate((gates, upproj)):
            parts = []
            for i in range(4):
                owner = 16 * (i // 2) + 2 * chip + i % 2
                parts.append(w[:, each * owner : each * owner + each].astype(F32))
                parts.append(riders if n == 0 and i == 0 else empty)
            first = 384 + 4 * block * n
            a[chip, :, first : first + 4 * block] = jnp.concatenate(parts, axis=-1).astype(BF)


def begin_kernel(tok, *refs):
    ins, results, scratch = refs[:18], refs[18:25], refs[25:]
    full, r1, r2, d1, d2, o1, o2 = results
    a1, a2, dn, sems = scratch[0], scratch[1], scratch[2], scratch[3:]
    block = dn.shape[1]
    place = plane_place()
    f, c, y, z = place
    peers, sibling, twin = chip_peers(f, c)
    greet(peers + [sibling, twin])
    start = (z * 2 + y) * ROWS
    full[pl.ds(pl.multiple_of(start, ROWS), ROWS), :] = tok[...]
    outs = []
    for l, a in enumerate((a1, a2)):
        pre, query, keys, values, out, mid, gates, upproj, down = ins[9 * l : 9 * l + 9]
        outs.append(out)
        pack_shards((pre, query, keys, values, mid, gates, upproj), block, a)
        each = down.shape[0]
        dn[l, :each] = down[...]
        dn[l, each:] = jnp.zeros((block - each, down.shape[1]), BF)

    def run(inner):
        gather = Gather(place, inner, full, sems[:5])
        spread = Spread(
            place, ((a1, r1), (a2, r2)), ((dn.at[0], d1), (dn.at[1], d2)), ((outs[0], o1), (outs[1], o2)), sems[5:]
        )
        gather.send_own(0)
        gather.send_own(1)
        spread.first(0)
        spread.first(1)
        gather.forward(0)
        spread.second(0)
        gather.forward(1)
        spread.second(1)
        spread.third(0)
        spread.third(1)
        gather.finish()
        spread.finish()

    both_kinds(place, run)


def begin_call(tok, shards, block):
    rows, width = shards[1].shape
    wide = 384 + 8 * block
    spec = pl.BlockSpec(memory_space=VMEM_SPACE)
    shapes = [(8 * ROWS, width)] + [(32, rows, wide)] * 2 + [(4, block, width)] * 2 + [(4, rows, width)] * 2
    counts = [(10,)] * 5 + [(2, 8), (2, 8), (2, 11), (2, 11), (2, 20), (2, 20), (2,), (2,)]
    return pl.pallas_call(
        begin_kernel,
        out_shape=[jax.ShapeDtypeStruct(s, BF) for s in shapes],
        in_specs=[spec] * 19,
        out_specs=[spec] * 7,
        scratch_shapes=[pltpu.VMEM((8, rows, wide), BF)] * 2
        + [pltpu.VMEM((2, block, width), BF)]
        + [pltpu.SemaphoreType.DMA(n) for n in counts],
        compiler_params=pltpu.CompilerParams(
            collective_id=9, has_side_effects=True, vmem_limit_bytes=60 * 1024 * 1024
        ),
        name="begin",
    )(tok, *[s[:, None] if s.ndim == 1 else s for s in shards])


class Collect:
    def __init__(self, place, ins, results, scratch):
        self.f, self.c, self.y, _ = place
        self.chip, self.core = self.c // 2, self.c % 2
        self.peers, self.sibling, self.twin = chip_peers(self.f, self.c)
        self.near = (self.f, flip(self.c, 2))
        self.g, self.h = ins
        self.out, self.oh = results
        self.sb, self.xb, self.xt, self.ut, self.sh, self.xh, self.th, *near = scratch[: -6]
        self.ss, self.sr, self.xs, self.xr, self.ps, self.pr = scratch[-6:]
        self.crosses_near = bool(near)
        if near:
            self.yo, self.yt = near
        self.home = self.y == self.f
        self.sent = []

    def send(self, src, dst, send_sem, recv_sem, target):
        copy = remote(src, dst, send_sem, recv_sem, target)
        copy.start()
        self.sent.append(copy)
        return copy

    def inner_send(self, src, dst, n):
        return self.send(src, dst, self.ss.at[n], self.sr.at[n], self.sibling)

    def twin_copy(self):
        return remote(self.th, self.xh, self.xs.at[8], self.xr.at[8], self.twin)

    def near_copy(self):
        return remote(self.yt, self.yo, self.xs.at[9], self.xr.at[9], self.near)

    def first(self):
        other = 1 - self.core
        self.inner = []
        for half in range(2):
            part = 8 * ((1 - self.f) if half == 0 else self.f)
            self.inner.append(
                self.inner_send(self.g.at[pl.ds(part, 8), other], self.sb.at[pl.ds(part, 8)], half)
            )
        self.inner.append(self.inner_send(self.h.at[:, other], self.sh, 2))

    def second(self):
        f, core = self.f, self.core
        self.crossed = []
        self.inner[0].wait_recv()
        for i in range(8):
            t = (self.chip + i + 1) % 8
            at = (1 - f) * 8 + t
            self.xt[t] = (self.g[at, core].astype(F32) + self.sb[at].astype(F32)).astype(BF)
            self.crossed.append(
                self.send(self.xt.at[t], self.xb.at[t], self.xs.at[i], self.xr.at[i], self.twin)
            )
        self.inner[2].wait_recv()
        if not self.crosses_near:
            self.th[...] = (self.h[1 - f, core].astype(F32) + self.sh[1 - f].astype(F32)).astype(BF)
            self.twin_copy().start()
            return
        for side in range(2):
            self.th[side] = (self.h[side, core].astype(F32) + self.sh[side].astype(F32)).astype(BF)

        @pl.when(jnp.logical_not(self.home))
        def _():
            self.twin_copy().start()

    def third(self):
        f, core = self.f, self.core
        self.direct = []
        self.inner[1].wait_recv()
        for i in range(8):
            t = (self.chip + i + 1) % 8
            at = f * 8 + t
            self.crossed[i].wait_recv()
            total = self.g[at, core].astype(F32) + self.sb[at].astype(F32) + self.xb[t].astype(F32)
            if i < 7:
                self.ut[t] = total.astype(BF)
                self.direct.append(
                    self.send(self.ut.at[t], self.out.at[self.chip], self.ps.at[i], self.pr.at[i], self.peers[i])
                )
            else:
                self.out[self.chip] = total.astype(BF)
        if not self.crosses_near:
            self.twin_copy().wait_recv()
            self.oh[...] = self.h[f, core].astype(F32) + self.sh[f].astype(F32) + self.xh[...].astype(F32)
            return

        @pl.when(self.home)
        def _():
            self.twin_copy().wait_recv()
            y = self.y
            self.oh[...] = self.th[y].astype(F32) + self.xh[y].astype(F32)
            self.yt[...] = (self.th[1 - y].astype(F32) + self.xh[1 - y].astype(F32)).astype(BF)
            self.near_copy().start()

    def finish(self):
        if self.crosses_near:

            @pl.when(self.home)
            def _():
                self.near_copy().wait_send()

            @pl.when(jnp.logical_not(self.home))
            def _():
                self.near_copy().wait_recv()
                self.oh[...] = self.yo[...].astype(F32)
                self.twin_copy().wait_send()
        else:
            self.twin_copy().wait_send()
        for copy in self.direct:
            copy.wait_recv()
        for copy in self.sent:
            copy.wait_send()


def collect_shapes(rows, wide, block, width, crosses_near):
    results = [((8, rows, wide), BF), ((block, width), F32)]
    buffers = [(16, rows, wide), (8, rows, wide), (8, rows, wide), (8, rows, wide), (2, block, width)]
    if crosses_near:
        buffers += [(2, block, width), (2, block, width), (block, width), (block, width)]
    else:
        buffers += [(block, width), (block, width)]
    counts = ((3,), (3,), (10,), (10,), (7,), (7,))
    scratch = [pltpu.VMEM(b, BF) for b in buffers] + [pltpu.SemaphoreType.DMA(n) for n in counts]
    return results, scratch


def back_kernel(gathers, lanes, left_ref, right_ref, grad_ref, hid_ref, gain_ref, g, gd, new_ref, *rest):
    full_ref = rest[0] if gathers else None
    c, od = rest[gathers : gathers + 2]
    scratch = rest[gathers + 2 :]

    def settle(half, total):
        at = half_rows(half)
        new = back_rows(total, grad_ref[at, :].astype(F32), hid_ref[at, :].astype(F32), gain_ref[...])
        new_ref[at, :] = new.astype(new_ref.dtype)
        return new.astype(BF)

    def extra(place):
        return Collect(place, (g, gd), (c, od), scratch[14 + 5 * gathers :])

    product = make_product(left_ref, right_ref, True, lanes)
    exchange(plane_place(), product, settle, full_ref, scratch, extra)


def head_lanes(head):
    lane = lax.broadcasted_iota(jnp.int32, (1, 128), 1)
    return lane // 64 == head


def swap_halves(values):
    lane = lax.broadcasted_iota(jnp.int32, (1, 128), 1)
    return jnp.where(lane % 64 < 32, pltpu.roll(values, 96, 1), pltpu.roll(values, 32, 1))


NT = (((1,), (1,)), ((), ()))
TN = (((0,), (0,)), ((), ()))


def attend_kernel(q_ref, k_ref, v_ref, pq_ref, pk_ref, att_ref, lse_ref):
    allowed = pk_ref[...] <= pq_ref[...]
    queries = q_ref[...]
    parts = []
    for head in range(2):
        masked = jnp.where(head_lanes(head), queries, jnp.zeros_like(queries))
        scores = lax.dot_general(masked, k_ref[...], NT, preferred_element_type=F32) * HD ** (-0.5)
        scores = jnp.where(allowed, scores, NEG_FILL)
        top = jnp.max(scores, axis=-1, keepdims=True)
        shares = jnp.exp(scores - top)
        total = jnp.sum(shares, axis=-1, keepdims=True)
        lse_ref[:, head : head + 1] = top + jnp.log(total)
        mixed = jnp.dot(shares.astype(BF), v_ref[...], preferred_element_type=F32)
        parts.append(mixed / total)
    att_ref[...] = jnp.where(head_lanes(0), parts[0], parts[1]).astype(BF)


def attend_forward(q, k, v, pos_q, pos_k):
    rows = q.shape[0]
    keys = k.shape[0]
    step = 128
    return pl.pallas_call(
        attend_kernel,
        grid=(rows // step,),
        out_shape=[
            jax.ShapeDtypeStruct((rows, 128), BF),
            jax.ShapeDtypeStruct((rows, 2), F32),
        ],
        in_specs=[
            pl.BlockSpec((step, 128), lambda i: (i, 0)),
            pl.BlockSpec((keys, 128), lambda i: (0, 0)),
            pl.BlockSpec((keys, 128), lambda i: (0, 0)),
            pl.BlockSpec((step, 1), lambda i: (i, 0)),
            pl.BlockSpec((1, keys), lambda i: (0, 0)),
        ],
        out_specs=[
            pl.BlockSpec((step, 128), lambda i: (i, 0)),
            pl.BlockSpec((step, 2), lambda i: (i, 0)),
        ],
        compiler_params=pltpu.CompilerParams(vmem_limit_bytes=14 * 1024 * 1024),
        name="attend_forward",
    )(q, k, v, pos_q, pos_k)


def attend_back_kernel(
    q_ref, k_ref, v_ref, full_ref, out_ref, att_ref, lse_ref, pq_ref, pk_ref, dq_ref, dk_ref, dv_ref, dw_ref, acc_ref
):
    step_no = pl.program_id(0)

    @pl.when(step_no == 0)
    def _():
        dk_ref[...] = jnp.zeros_like(dk_ref)
        dv_ref[...] = jnp.zeros_like(dv_ref)
        acc_ref[...] = jnp.zeros_like(acc_ref)

    allowed = pk_ref[...] <= pq_ref[...]
    queries = q_ref[...]
    full = full_ref[...]
    grads = lax.dot_general(full, out_ref[...], NT, preferred_element_type=F32).astype(BF)
    acc_ref[...] += lax.dot_general(att_ref[...], full, TN, preferred_element_type=F32)
    parts = []
    for head in range(2):
        masked = jnp.where(head_lanes(head), queries, jnp.zeros_like(queries))
        grad_h = jnp.where(head_lanes(head), grads, jnp.zeros_like(grads))
        scores = lax.dot_general(k_ref[...], masked, NT, preferred_element_type=F32) * HD ** (-0.5)
        shares = jnp.where(allowed, jnp.exp(scores - lse_ref[head : head + 1, :]), 0.0)
        grad_shares = lax.dot_general(v_ref[...], grad_h, NT, preferred_element_type=F32)
        delta = jnp.sum(shares * grad_shares, axis=0, keepdims=True)
        grad_scores = (shares * (grad_shares - delta) * HD ** (-0.5)).astype(BF)
        dv_ref[...] += jnp.dot(shares.astype(BF), grad_h, preferred_element_type=F32)
        dk_ref[...] += jnp.dot(grad_scores, masked, preferred_element_type=F32)
        parts.append(lax.dot_general(grad_scores, k_ref[...], TN, preferred_element_type=F32))
    dq_ref[...] = jnp.where(head_lanes(0), parts[0], parts[1])

    @pl.when(step_no == pl.num_programs(0) - 1)
    def _():
        dw_ref[...] = acc_ref[...].astype(BF)


def attend_backward(q, k, v, full, out_w, att, lse_rows, pos_q, pos_k):
    rows = q.shape[0]
    keys = k.shape[0]
    width = full.shape[1]
    step = 128
    row_block = pl.BlockSpec((step, 128), lambda i: (i, 0))
    key_block = pl.BlockSpec((keys, 128), lambda i: (0, 0))
    weight_block = pl.BlockSpec((128, width), lambda i: (0, 0))
    return pl.pallas_call(
        attend_back_kernel,
        grid=(rows // step,),
        out_shape=[
            jax.ShapeDtypeStruct((rows, 128), F32),
            jax.ShapeDtypeStruct((keys, 128), F32),
            jax.ShapeDtypeStruct((keys, 128), F32),
            jax.ShapeDtypeStruct((128, width), BF),
        ],
        in_specs=[
            row_block, key_block, key_block,
            pl.BlockSpec((step, width), lambda i: (i, 0)),
            weight_block, row_block,
            pl.BlockSpec((2, step), lambda i: (0, i)),
            pl.BlockSpec((1, step), lambda i: (0, i)),
            pl.BlockSpec((keys, 1), lambda i: (0, 0)),
        ],
        out_specs=[row_block, key_block, key_block, weight_block],
        scratch_shapes=[pltpu.VMEM((128, width), F32)],
        compiler_params=pltpu.CompilerParams(vmem_limit_bytes=60 * 1024 * 1024),
        name="attend_backward",
    )(q, k, v, full, out_w, att, lse_rows, pos_q, pos_k)


def project_kernel(layer, *refs):
    x_ref, w_ref, cos_ref, sin_ref, more_ref = refs[:5]
    q_ref, k_ref, v_ref, keep_ref = refs[5:9]
    ss, sr = refs[-2:]
    f, c, _, _ = plane_place()
    sibling = (f, flip(c, 1))
    greet([sibling])
    rows_n = x_ref.shape[0]

    def copies(i):
        here = pl.ds(pl.multiple_of(i * ROWS, ROWS), ROWS)
        there = pl.ds(pl.multiple_of(rows_n + i * ROWS, ROWS), ROWS)
        return [
            remote(ref.at[here], ref.at[there], ss.at[2 * i + n], sr.at[2 * i + n], sibling)
            for n, ref in enumerate((k_ref, v_ref))
        ]

    def step(i, carry):
        at = pl.ds(pl.multiple_of(i * ROWS, ROWS), ROWS)
        rows = x_ref[at, :]
        if layer == 0:
            wide = rows.astype(F32)
            rows = (wide * norm_rows(wide) * more_ref[...]).astype(BF)
            keep_ref[at, :] = rows
        raw = jnp.dot(rows, w_ref[:, :384], preferred_element_type=F32)
        cosine, sine = cos_ref[at, :], sin_ref[at, :]
        q, k, v = raw[:, :128], raw[:, 128:256], raw[:, 256:]
        q_ref[at, :] = (q * cosine + swap_halves(q) * sine).astype(BF)
        k_ref[at, :] = (k * cosine + swap_halves(k) * sine).astype(BF)
        if layer == 0:
            refs[9][at, :] = v
        else:
            v = 0.5 * v + 0.5 * more_ref[at, :]
        v_ref[at, :] = v.astype(BF)
        for copy in copies(i):
            copy.start()
        return carry

    lax.fori_loop(0, rows_n // ROWS, step, 0)
    if layer == 1:
        keep_ref[...] = jnp.zeros_like(keep_ref)
    for i in range(rows_n // ROWS):
        for copy in copies(i):
            copy.wait()


def project(layer, x, w, cosine, sine, more):
    rows_n = x.shape[0]
    spec = pl.BlockSpec(memory_space=VMEM_SPACE)
    outs = [((rows_n, 128), BF), ((2 * rows_n, 128), BF), ((2 * rows_n, 128), BF)]
    outs += [(x.shape, BF), ((rows_n, 128), F32)] if layer == 0 else [((8, 128), F32)]
    count = 2 * (rows_n // ROWS)
    return pl.pallas_call(
        functools.partial(project_kernel, layer),
        out_shape=[jax.ShapeDtypeStruct(*o) for o in outs],
        in_specs=[spec] * 5,
        out_specs=[spec] * len(outs),
        scratch_shapes=[pltpu.SemaphoreType.DMA((count,))] * 2,
        compiler_params=pltpu.CompilerParams(
            collective_id=10 + layer, has_side_effects=True, vmem_limit_bytes=8 * 1024 * 1024
        ),
        name="project",
    )(x, w, cosine, sine, more)


def turn_back_kernel(layer, dq_ref, dk_ref, dv_ref, cos_ref, sin_ref, more_ref, three_ref, pass_ref, sb, rb, ss, sr):
    f, c, _, _ = plane_place()
    sibling = (f, flip(c, 1))
    greet([sibling])
    rows_n = dq_ref.shape[0]
    copies = []
    for n, ref in enumerate((dk_ref, dv_ref)):
        sb[n] = ref[rows_n:, :].astype(BF)
        copies.append(remote(sb.at[n], rb.at[n], ss.at[n], sr.at[n], sibling))
        copies[n].start()
    cosine, sine = cos_ref[...], sin_ref[...]
    dq = dq_ref[...]
    three_ref[:, :128] = (dq * cosine - swap_halves(dq) * sine).astype(BF)
    copies[0].wait()
    dk = dk_ref[:rows_n, :] + rb[0].astype(F32)
    three_ref[:, 128:256] = (dk * cosine - swap_halves(dk) * sine).astype(BF)
    copies[1].wait()
    dv = dv_ref[:rows_n, :] + rb[1].astype(F32)
    if layer == 1:
        dv = 0.5 * dv
        pass_ref[...] = dv
    else:
        dv = dv + more_ref[...]
        pass_ref[...] = jnp.zeros_like(pass_ref)
    three_ref[:, 256:] = dv.astype(BF)


def turn_back(layer, dq, dk, dv, cosine, sine, more):
    rows_n = dq.shape[0]
    spec = pl.BlockSpec(memory_space=VMEM_SPACE)
    outs = [((rows_n, 384), BF), ((rows_n if layer == 1 else 8, 128), F32)]
    return pl.pallas_call(
        functools.partial(turn_back_kernel, layer),
        out_shape=[jax.ShapeDtypeStruct(*o) for o in outs],
        in_specs=[spec] * 6,
        out_specs=[spec] * 2,
        scratch_shapes=[pltpu.VMEM((2, rows_n, 128), BF)] * 2 + [pltpu.SemaphoreType.DMA((2,))] * 2,
        compiler_params=pltpu.CompilerParams(
            collective_id=12 + layer, has_side_effects=True, vmem_limit_bytes=8 * 1024 * 1024
        ),
        name="turn_back",
    )(dq, dk, dv, cosine, sine, more)


def unpack_kernel(*refs):
    for l in range(2):
        cu, od, cq, oo, pre, query, keys, values, mid, gates, upproj = refs[11 * l : 11 * l + 11]
        g_pre, gq, gk, gv, g_out, g_mid, gg, gu, g_down = refs[22 + 9 * l : 31 + 9 * l]
        rows, units = gates.shape
        each = units // 32
        block = cu.shape[2] // 8
        total = jnp.zeros((rows, 1), F32)
        for chip in range(8):
            pair = 4 * (chip % 2) + chip // 2
            for n, (w, g) in enumerate(((query, gq), (keys, gk), (values, gv))):
                at = slice(128 * pair, 128 * pair + 128)
                part = cq[chip, :, 128 * n : 128 * n + 128].astype(F32)
                g[:, at] = part
                total += jnp.sum(part * w[:, at].astype(F32), axis=-1, keepdims=True)
        g_pre[...] = total / pre[...].astype(F32)
        for n, g in enumerate((gg, gu)):
            for chip in range(8):
                wide = cu[chip, :, 4 * block * n : 4 * block * (n + 1)].astype(F32)
                for i in range(4):
                    owner = 16 * (i // 2) + 2 * chip + i % 2
                    g[:, each * owner : each * owner + each] = wide[:, block * i : block * i + each]
        both = gg[...] * gates[...].astype(F32) + gu[...] * upproj[...].astype(F32)
        g_mid[...] = jnp.sum(both, axis=-1, keepdims=True) / mid[...].astype(F32)
        g_out[...] = oo[...]
        g_down[...] = od[: g_down.shape[0], :]


def unpack(collected, layers):
    args, outs = [], []
    for l, layer in enumerate(layers):
        pre, query, keys, values, out, mid, gates, upproj, down = layer
        args += [*collected[l], pre[:, None], query, keys, values, mid[:, None], gates, upproj]
        for w in layer:
            outs.append(w.shape + (1,) if w.ndim == 1 else w.shape)
    spec = pl.BlockSpec(memory_space=VMEM_SPACE)
    found = pl.pallas_call(
        unpack_kernel,
        out_shape=[jax.ShapeDtypeStruct(o, F32) for o in outs],
        in_specs=[spec] * len(args),
        out_specs=[spec] * len(outs),
        compiler_params=pltpu.CompilerParams(vmem_limit_bytes=60 * 1024 * 1024),
        name="unpack",
    )(*args)
    return [g[:, 0] if g.shape[-1] == 1 else g for g in found]


def fast_local(tokens, cotangent, pair_of, *shards):
    width = tokens.shape[2]
    rows_each, units = shards[6].shape
    each = units // 32
    block = (each + 2 + 31) // 32 * 32
    hidden_pad = 4 * block
    wide = 384 + 2 * hidden_pad
    core = lax.axis_index("ctx") % 2
    pos_all = storage_positions(pair_of, ROWS).reshape(8, 2, ROWS)
    own_pos = lax.dynamic_index_in_dim(pos_all, core, 1, False).reshape(-1)
    sib_pos = lax.dynamic_index_in_dim(pos_all, 1 - core, 1, False).reshape(-1)
    key_pos = jnp.concatenate([own_pos, sib_pos])
    cosine, sine = rope_tables(own_pos, HD)
    cosine = jnp.concatenate([cosine] * 4, axis=-1)
    sine = jnp.concatenate([-sine, sine, -sine, sine], axis=-1)

    layers = [shards[:9], shards[9:]]
    tok = tokens.reshape(ROWS, width)
    cot = cotangent.reshape(ROWS, width)
    full, *spread = begin_call(tok, shards, block)
    all_w = [w.reshape(32 * rows_each, wide) for w in spread[:2]]
    up_w = [w[:, 384:] for w in all_w]
    down_w = [w.reshape(hidden_pad, width) for w in spread[2:4]]
    out_w = [w.reshape(4 * rows_each, width) for w in spread[4:]]
    gains = []
    for w in all_w:
        columns = w[:, 384 + each : 384 + each + 2].astype(F32).T
        gains += [columns[:1], columns[1:]]

    plane = 8 * ROWS
    full_type = ((plane, width), BF)
    rows_type = ((ROWS, width), F32)
    saved = []
    hidden = tok
    first_values = None
    pos_q = own_pos[:, None]
    pos_k = key_pos[None, :]
    for layer in range(2):
        if layer == 0:
            q, k, v, x_full, first_values = project(0, full, all_w[0], cosine, sine, gains[0])
        else:
            x_full = full
            q, k, v, _ = project(1, full, all_w[1], cosine, sine, first_values)
        att, lse = attend_forward(q, k, v, pos_q, pos_k)
        middle, mlp_full = comm_call(
            forward_kernel, [rows_type, full_type], 1 + layer,
            (att, out_w[layer], hidden, gains[2 * layer + 1]), True, "middle",
        )
        both = jnp.dot(mlp_full, up_w[layer], preferred_element_type=F32)
        gate, up = both[:, :hidden_pad], both[:, hidden_pad:]
        inner = (jax.nn.silu(gate) * up).astype(BF)
        saved.append((x_full, q, k, v, lse, att, mlp_full, gate, up, inner, hidden, middle))
        if layer == 0:
            hidden, full = comm_call(
                forward_kernel, [rows_type, full_type], 3,
                (inner, down_w[layer], middle, gains[2]), True, "result",
            )
        else:
            output, full = comm_call(
                turn_kernel, [((ROWS, width), BF), full_type], 4,
                (inner, down_w[layer], middle, cot), True, "turn",
            )
    grad = cot
    passed = cosine
    collected = [None, None]
    for layer in (1, 0):
        x_full, q, k, v, lse, att, mlp_full, gate, up, inner, hidden, middle = saved[layer]
        grad_down = left_product(inner, full)
        grad_inner = right_product(full, down_w[layer])
        sigma = jax.nn.sigmoid(gate)
        grad_gate = (grad_inner * up * sigma * (1.0 + gate * (1.0 - sigma))).astype(BF)
        grad_up = (grad_inner * gate * sigma).astype(BF)
        both = jnp.concatenate([grad_gate, grad_up], axis=-1)
        grad_upw = left_product(mlp_full, both)
        results, more = collect_shapes(rows_each, 2 * hidden_pad, block, width, False)
        grad_mid, full, *got_up = comm_call(
            functools.partial(back_kernel, 1, (384, wide)), [rows_type, full_type] + results, 5 + layer,
            (
                both, all_w[layer], grad, middle, gains[2 * layer + 1],
                grad_upw.astype(BF).reshape(16, 2, rows_each, 2 * hidden_pad),
                grad_down.astype(BF).reshape(2, 2, block, width),
            ),
            True, "middle_back", more,
        )
        dq, dk, dv, grad_out = attend_backward(q, k, v, full, out_w[layer], att, lse.T, own_pos[None, :], key_pos[:, None])
        three, passed = turn_back(layer, dq, dk, dv, cosine, sine, passed)
        grad_qkv = left_product(x_full, three)
        results, more = collect_shapes(rows_each, 384, rows_each, width, True)
        args = (
            three, all_w[layer], grad_mid, hidden, gains[2 * layer],
            grad_qkv.astype(BF).reshape(16, 2, rows_each, 384),
            grad_out.reshape(2, 2, rows_each, width),
        )
        if layer == 1:
            grad, full, *got_qkv = comm_call(
                functools.partial(back_kernel, 1, (0, 384)), [rows_type, full_type] + results, 7, args, True,
                "layer_back", more,
            )
        else:
            tokens_grad, *got_qkv = comm_call(
                functools.partial(back_kernel, 0, (0, 384)), [((ROWS, width), BF)] + results, 8, args, False,
                "last_back", more,
            )
        collected[layer] = got_up + got_qkv
    found = unpack(collected, layers)
    return (output.reshape(1, ROWS, width), tokens_grad.reshape(1, ROWS, width), *found)


def solution(mesh):
    placed = (
        P("fsdp", "ctx", None),
        P("fsdp", "ctx", None),
        P(),
        P(("fsdp", "ctx")),
        P(("fsdp", "ctx"), None),
        P(("fsdp", "ctx"), None),
        P(("fsdp", "ctx"), None),
        P(("fsdp", "ctx"), None),
        P(("fsdp", "ctx")),
        P(("fsdp", "ctx"), None),
        P(("fsdp", "ctx"), None),
        P(("fsdp", "ctx"), None),
        P(("fsdp", "ctx")),
        P(("fsdp", "ctx"), None),
        P(("fsdp", "ctx"), None),
        P(("fsdp", "ctx"), None),
        P(("fsdp", "ctx"), None),
        P(("fsdp", "ctx")),
        P(("fsdp", "ctx"), None),
        P(("fsdp", "ctx"), None),
        P(("fsdp", "ctx"), None),
    )
    fits = mesh.shape["ctx"] == HEADS and mesh.shape["fsdp"] == 2
    return jax.shard_map(
        fast_local if fits else local,
        mesh=mesh,
        in_specs=placed,
        out_specs=(
            P("fsdp", "ctx", None),
            P("fsdp", "ctx", None),
            P(("fsdp", "ctx")),
            P(("fsdp", "ctx"), None),
            P(("fsdp", "ctx"), None),
            P(("fsdp", "ctx"), None),
            P(("fsdp", "ctx"), None),
            P(("fsdp", "ctx")),
            P(("fsdp", "ctx"), None),
            P(("fsdp", "ctx"), None),
            P(("fsdp", "ctx"), None),
            P(("fsdp", "ctx")),
            P(("fsdp", "ctx"), None),
            P(("fsdp", "ctx"), None),
            P(("fsdp", "ctx"), None),
            P(("fsdp", "ctx"), None),
            P(("fsdp", "ctx")),
            P(("fsdp", "ctx"), None),
            P(("fsdp", "ctx"), None),
            P(("fsdp", "ctx"), None),
        ),
        check_vma=False,
    )
```

```python
import functools
import math

import jax
import jax.numpy as jnp
from jax import lax
from jax.experimental import pallas as pl
from jax.experimental.pallas import tpu as pltpu
from jax.sharding import PartitionSpec as P

HEADS = 16
HD = 64


NORM_EPS = 1e-05
NEG_FILL = -1e30


def block_size(total_rows):
    size_now = 512
    while total_rows % size_now:
        size_now //= 2
    return size_now


def row_norm(hidden):
    inverse = lax.rsqrt(jnp.mean(hidden * hidden, axis=-1, keepdims=True) + NORM_EPS)
    return (hidden * inverse, inverse)


def norm_back(grad_normed, normed, inverse):
    return inverse * (grad_normed - normed * jnp.mean(grad_normed * normed, axis=-1, keepdims=True))


def rope_tables(positions, head_size):
    half_size = head_size // 2
    freqs = jnp.exp(
        jnp.arange(half_size, dtype=jnp.float32) * (-2.0 * math.log(10000.0) / head_size)
    )
    angles = positions.astype(jnp.float32)[:, None] * freqs[None, :]
    return (jnp.cos(angles), jnp.sin(angles))


def rotate(values_in, cosine, sine):
    half_size = values_in.shape[-1] // 2
    first_half = values_in[..., :half_size]
    second_half = values_in[..., half_size:]
    cos_rows = cosine[:, None, :]
    sin_rows = sine[:, None, :]
    return jnp.concatenate(
        [
            first_half * cos_rows - second_half * sin_rows,
            second_half * cos_rows + first_half * sin_rows,
        ],
        axis=-1,
    )


def unrotate(grads_in, cosine, sine):
    half_size = grads_in.shape[-1] // 2
    first_half = grads_in[..., :half_size]
    second_half = grads_in[..., half_size:]
    cos_rows = cosine[:, None, :]
    sin_rows = sine[:, None, :]
    return jnp.concatenate(
        [
            first_half * cos_rows + second_half * sin_rows,
            second_half * cos_rows - first_half * sin_rows,
        ],
        axis=-1,
    )


def left_product(left, right):
    return lax.dot_general(
        left, right, (((0,), (0,)), ((), ())), preferred_element_type=jnp.float32
    )


def right_product(left, right):
    return lax.dot_general(
        left, right, (((1,), (1,)), ((), ())), preferred_element_type=jnp.float32
    )


def storage_positions(pair_of, seq_dev):
    devices = pair_of.shape[0]
    rows_all = jnp.arange(devices * seq_dev, dtype=jnp.int32)
    owner = rows_all // seq_dev
    local_row = rows_all % seq_dev
    half_rows = seq_dev // 2
    picked = jnp.sum(
        jnp.where(
            owner[:, None] == jnp.arange(devices, dtype=jnp.int32)[None, :], pair_of[None, :], 0
        ),
        axis=1,
    )
    block_id = jnp.where(local_row < half_rows, picked, 2 * devices - 1 - picked)
    return block_id * half_rows + local_row % half_rows


def head_scores(queries, keys_flat, query_pos, key_pos):
    key_heads = keys_flat.reshape(keys_flat.shape[0], queries.shape[1], queries.shape[2])
    scores = jnp.einsum(
        "qhd,khd->hqk", queries, key_heads, preferred_element_type=jnp.float32
    ) * queries.shape[2] ** (-0.5)
    allowed = (key_pos[None, :] <= query_pos[:, None])[None]
    return (jnp.where(allowed, scores, NEG_FILL), allowed)


def make_stats_step(queries, query_pos, pos_all, state_in, key_part):
    size_now = block_size(key_part.shape[0])

    def inner_step(block_no, state_now):
        top_now, total_now = state_now
        offset = block_no * size_now
        key_block = lax.dynamic_slice_in_dim(key_part, offset, size_now, 0)
        key_pos = lax.dynamic_slice_in_dim(pos_all, offset, size_now, 0)
        scores, allowed = head_scores(queries, key_block, query_pos, key_pos)
        new_top = jnp.maximum(top_now, jnp.max(scores, axis=-1))
        total_now = total_now * jnp.exp(top_now - new_top) + jnp.sum(
            jnp.where(allowed, jnp.exp(scores - new_top[..., None]), 0.0), axis=-1
        )
        return (new_top, total_now)

    return lax.fori_loop(0, key_part.shape[0] // size_now, inner_step, state_in)


def make_value_step(queries, log_total, query_pos, pos_all, acc_in, pieces):
    key_part, value_part = pieces
    size_now = block_size(key_part.shape[0])

    def inner_step(block_no, acc_now):
        offset = block_no * size_now
        key_block = lax.dynamic_slice_in_dim(key_part, offset, size_now, 0)
        value_block = lax.dynamic_slice_in_dim(value_part, offset, size_now, 0)
        key_pos = lax.dynamic_slice_in_dim(pos_all, offset, size_now, 0)
        scores, allowed = head_scores(queries, key_block, query_pos, key_pos)
        shares = jnp.exp(scores - log_total[..., None]).astype(jnp.bfloat16)
        value_heads = value_block.reshape(size_now, queries.shape[1], queries.shape[2])
        return acc_now + jnp.einsum(
            "hqk,khd->qhd", shares, value_heads, preferred_element_type=jnp.float32
        )

    return lax.fori_loop(0, key_part.shape[0] // size_now, inner_step, acc_in)


def make_back_step(queries, grad_att, log_total, row_delta, query_pos, pos_all):
    scale_now = queries.shape[2] ** (-0.5)

    def back_step(state_in, pieces, start_row):
        key_part, value_part = pieces
        size_now = block_size(key_part.shape[0])

        def inner_step(block_no, state_now):
            offset = block_no * size_now
            key_block = lax.dynamic_slice_in_dim(key_part, offset, size_now, 0)
            value_block = lax.dynamic_slice_in_dim(value_part, offset, size_now, 0)
            key_pos = lax.dynamic_slice_in_dim(pos_all, offset, size_now, 0)
            scores, allowed = head_scores(queries, key_block, query_pos, key_pos)
            shares = jnp.exp(scores - log_total[..., None])
            value_heads = value_block.reshape(size_now, queries.shape[1], queries.shape[2])
            key_heads = key_block.reshape(size_now, queries.shape[1], queries.shape[2])
            grad_shares = jnp.einsum(
                "qhd,khd->hqk", grad_att, value_heads, preferred_element_type=jnp.float32
            )
            grad_scores = (shares * (grad_shares - row_delta[..., None]) * scale_now).astype(
                jnp.bfloat16
            )
            grad_query = state_now[0] + jnp.einsum(
                "hqk,khd->qhd", grad_scores, key_heads, preferred_element_type=jnp.float32
            )
            return (grad_query,)

        return lax.fori_loop(0, key_part.shape[0] // size_now, inner_step, state_in)

    return back_step


def make_query_step(own_keys, own_values, own_pos, stats_all, pos_all, head_count, head_size):
    scale_now = head_size ** (-0.5)
    value_heads = own_values.reshape(own_values.shape[0], head_count, head_size)

    def query_step(state_in, pieces, start_row):
        query_part, grad_part = pieces
        size_now = block_size(query_part.shape[0])

        def inner_step(block_no, state_now):
            offset = block_no * size_now
            query_block = lax.dynamic_slice_in_dim(query_part, offset, size_now, 0).reshape(
                size_now, head_count, head_size
            )
            grad_block = lax.dynamic_slice_in_dim(grad_part, offset, size_now, 0).reshape(
                size_now, head_count, head_size
            )
            query_pos = lax.dynamic_slice_in_dim(pos_all, offset, size_now, 0)
            log_block = lax.dynamic_slice_in_dim(stats_all[0], offset, size_now, 0).T
            delta_block = lax.dynamic_slice_in_dim(stats_all[1], offset, size_now, 0).T
            scores, allowed = head_scores(query_block, own_keys, query_pos, own_pos)
            shares = jnp.exp(scores - log_block[..., None])
            grad_shares = jnp.einsum(
                "qhd,khd->hqk", grad_block, value_heads, preferred_element_type=jnp.float32
            )
            grad_scores = (shares * (grad_shares - delta_block[..., None]) * scale_now).astype(
                jnp.bfloat16
            )
            key_term = jnp.einsum(
                "hqk,qhd->khd", grad_scores, query_block, preferred_element_type=jnp.float32
            )
            value_term = jnp.einsum(
                "hqk,qhd->khd",
                shares.astype(jnp.bfloat16),
                grad_block,
                preferred_element_type=jnp.float32,
            )
            return (
                state_now[0] + key_term.reshape(key_term.shape[0], -1),
                state_now[1] + value_term.reshape(value_term.shape[0], -1),
            )

        return lax.fori_loop(0, query_part.shape[0] // size_now, inner_step, state_in)

    return query_step


def gather_forward(shards):
    return (
        lax.all_gather(shards[0], ("fsdp", "ctx"), axis=0, tiled=True),
        lax.all_gather(shards[1], ("fsdp", "ctx"), axis=0, tiled=True),
        lax.all_gather(shards[2], ("fsdp", "ctx"), axis=0, tiled=True),
        lax.all_gather(shards[3], ("fsdp", "ctx"), axis=0, tiled=True),
        lax.all_gather(shards[4], ("fsdp", "ctx"), axis=0, tiled=True),
        lax.all_gather(shards[5], ("fsdp", "ctx"), axis=0, tiled=True),
        lax.all_gather(shards[6], ("fsdp", "ctx"), axis=0, tiled=True),
        lax.all_gather(shards[7], ("fsdp", "ctx"), axis=0, tiled=True),
        lax.all_gather(shards[8], ("fsdp", "ctx"), axis=0, tiled=True),
    )


def scatter_grads(grad_terms):
    return (
        lax.psum_scatter(grad_terms[0], ("fsdp", "ctx"), scatter_dimension=0, tiled=True),
        lax.psum_scatter(grad_terms[1], ("fsdp", "ctx"), scatter_dimension=0, tiled=True),
        lax.psum_scatter(grad_terms[2], ("fsdp", "ctx"), scatter_dimension=0, tiled=True),
        lax.psum_scatter(grad_terms[3], ("fsdp", "ctx"), scatter_dimension=0, tiled=True),
        lax.psum_scatter(grad_terms[4], ("fsdp", "ctx"), scatter_dimension=0, tiled=True),
        lax.psum_scatter(grad_terms[5], ("fsdp", "ctx"), scatter_dimension=0, tiled=True),
        lax.psum_scatter(grad_terms[6], ("fsdp", "ctx"), scatter_dimension=0, tiled=True),
        lax.psum_scatter(grad_terms[7], ("fsdp", "ctx"), scatter_dimension=0, tiled=True),
        lax.psum_scatter(grad_terms[8], ("fsdp", "ctx"), scatter_dimension=0, tiled=True),
    )


def forward_layer(hidden, full_layer, first_values, context):
    prenorm, query_w, keys_w, values_w, outproj, midnorm, gates_w, upproj_w, downproj_w = full_layer
    cosine, sine, own_pos, pos_all = context
    rows_n, model_width = hidden.shape
    normed, inverse_a = row_norm(hidden)
    attn_in = (normed * prenorm.astype(jnp.float32)).astype(jnp.bfloat16)
    query_raw = jnp.dot(attn_in, query_w, preferred_element_type=jnp.float32)
    keys_raw = jnp.dot(attn_in, keys_w, preferred_element_type=jnp.float32)
    values_raw = jnp.dot(attn_in, values_w, preferred_element_type=jnp.float32)
    mixed = values_raw if first_values is None else 0.5 * values_raw + 0.5 * first_values
    queries = rotate(query_raw.reshape(rows_n, HEADS, HD), cosine, sine).astype(jnp.bfloat16)
    keys_flat = (
        rotate(keys_raw.reshape(rows_n, HEADS, HD), cosine, sine)
        .reshape(rows_n, model_width)
        .astype(jnp.bfloat16)
    )
    values_flat = mixed.astype(jnp.bfloat16)
    top_start = jnp.full((HEADS, rows_n), NEG_FILL, jnp.float32)
    total_start = jnp.zeros((HEADS, rows_n), jnp.float32)
    top_now, total_now = make_stats_step(
        queries,
        own_pos,
        pos_all,
        (top_start, total_start),
        lax.all_gather(keys_flat, "ctx", axis=0, tiled=True),
    )
    log_total = top_now + jnp.log(total_now)
    att_out = make_value_step(
        queries,
        log_total,
        own_pos,
        pos_all,
        jnp.zeros((rows_n, HEADS, HD), jnp.float32),
        (
            lax.all_gather(keys_flat, "ctx", axis=0, tiled=True),
            lax.all_gather(values_flat, "ctx", axis=0, tiled=True),
        ),
    )
    att_low = att_out.reshape(rows_n, model_width).astype(jnp.bfloat16)
    middle = hidden + jnp.dot(att_low, outproj, preferred_element_type=jnp.float32)
    normed_mid, inverse_b = row_norm(middle)
    mlp_in = (normed_mid * midnorm.astype(jnp.float32)).astype(jnp.bfloat16)
    gate_raw = jnp.dot(mlp_in, gates_w, preferred_element_type=jnp.float32)
    up_proj = jnp.dot(mlp_in, upproj_w, preferred_element_type=jnp.float32)
    inner_act = (jax.nn.silu(gate_raw) * up_proj).astype(jnp.bfloat16)
    result = middle + jnp.dot(inner_act, downproj_w, preferred_element_type=jnp.float32)
    saved = (
        hidden,
        normed,
        inverse_a,
        attn_in,
        queries,
        keys_flat,
        values_flat,
        log_total,
        att_out,
        att_low,
        normed_mid,
        inverse_b,
        mlp_in,
        gate_raw,
        up_proj,
        inner_act,
    )
    return (result, values_raw, saved)


def backward_layer(grad_out, full_layer, saved, value_extra, is_second, context):
    prenorm, query_w, keys_w, values_w, outproj, midnorm, gates_w, upproj_w, downproj_w = full_layer
    (
        hidden,
        normed,
        inverse_a,
        attn_in,
        queries,
        keys_flat,
        values_flat,
        log_total,
        att_out,
        att_low,
        normed_mid,
        inverse_b,
        mlp_in,
        gate_raw,
        up_proj,
        inner_act,
    ) = saved
    cosine, sine, own_pos, pos_all = context
    rows_n, model_width = hidden.shape
    grad_low = grad_out.astype(jnp.bfloat16)
    grad_down = left_product(inner_act, grad_low)
    grad_inner = right_product(grad_low, downproj_w)
    sigma_gate = jax.nn.sigmoid(gate_raw)
    grad_gate = (grad_inner * up_proj * sigma_gate * (1.0 + gate_raw * (1.0 - sigma_gate))).astype(
        jnp.bfloat16
    )
    grad_up = (grad_inner * gate_raw * sigma_gate).astype(jnp.bfloat16)
    grad_gates = left_product(mlp_in, grad_gate)
    grad_upproj = left_product(mlp_in, grad_up)
    grad_mlp = right_product(grad_gate, gates_w) + right_product(grad_up, upproj_w)
    grad_midnorm = jnp.sum(grad_mlp * normed_mid, axis=0)
    grad_middle = grad_out + norm_back(
        grad_mlp * midnorm.astype(jnp.float32), normed_mid, inverse_b
    )
    branch_low = grad_middle.astype(jnp.bfloat16)
    grad_outproj = left_product(att_low, branch_low)
    grad_att = right_product(branch_low, outproj).astype(jnp.bfloat16).reshape(rows_n, HEADS, HD)
    row_delta = jnp.sum(grad_att.astype(jnp.float32) * att_out, axis=-1).T
    query_start = jnp.zeros((rows_n, HEADS, HD), jnp.float32)
    state_start = (query_start,)
    back_fn = make_back_step(queries, grad_att, log_total, row_delta, own_pos, pos_all)
    state_out = back_fn(
        state_start,
        (
            lax.all_gather(keys_flat, "ctx", axis=0, tiled=True),
            lax.all_gather(values_flat, "ctx", axis=0, tiled=True),
        ),
        jnp.int32(0),
    )
    grad_qr = state_out[0]
    stats_all = (
        lax.all_gather(log_total.T, "ctx", axis=0, tiled=True),
        lax.all_gather(row_delta.T, "ctx", axis=0, tiled=True),
    )
    query_fn = make_query_step(keys_flat, values_flat, own_pos, stats_all, pos_all, HEADS, HD)
    flat_start = jnp.zeros((rows_n, model_width), jnp.float32)
    grad_kr, grad_mix = query_fn(
        (flat_start, flat_start),
        (
            lax.all_gather(queries.reshape(rows_n, model_width), "ctx", axis=0, tiled=True),
            lax.all_gather(grad_att.reshape(rows_n, model_width), "ctx", axis=0, tiled=True),
        ),
        jnp.int32(0),
    )
    grad_query = unrotate(grad_qr, cosine, sine).reshape(rows_n, model_width).astype(jnp.bfloat16)
    grad_keys = (
        unrotate(grad_kr.reshape(rows_n, HEADS, HD), cosine, sine)
        .reshape(rows_n, model_width)
        .astype(jnp.bfloat16)
    )
    if is_second:
        grad_values = (0.5 * grad_mix).astype(jnp.bfloat16)
        passed_on = 0.5 * grad_mix
    else:
        grad_values = (grad_mix + value_extra).astype(jnp.bfloat16)
        passed_on = None
    grad_query_w = left_product(attn_in, grad_query)
    grad_keys_w = left_product(attn_in, grad_keys)
    grad_values_w = left_product(attn_in, grad_values)
    grad_attn = (
        right_product(grad_query, query_w)
        + right_product(grad_keys, keys_w)
        + right_product(grad_values, values_w)
    )
    grad_prenorm = jnp.sum(grad_attn * normed, axis=0)
    grad_hidden = grad_middle + norm_back(
        grad_attn * prenorm.astype(jnp.float32), normed, inverse_a
    )
    grad_terms = (
        grad_prenorm,
        grad_query_w,
        grad_keys_w,
        grad_values_w,
        grad_outproj,
        grad_midnorm,
        grad_gates,
        grad_upproj,
        grad_down,
    )
    return (grad_hidden, grad_terms, passed_on)


def local(
    tokens,
    cotangent,
    pair_of,
    prenorm_one,
    query_one,
    keys_one,
    values_one,
    outproj_one,
    midnorm_one,
    gates_one,
    upproj_one,
    downproj_one,
    prenorm_two,
    query_two,
    keys_two,
    values_two,
    outproj_two,
    midnorm_two,
    gates_two,
    upproj_two,
    downproj_two,
):
    seq_dev = tokens.shape[1]
    model_width = tokens.shape[2]
    pos_all = storage_positions(pair_of, seq_dev)
    own_pos = lax.dynamic_slice_in_dim(pos_all, lax.axis_index("ctx") * seq_dev, seq_dev, 0)
    cosine, sine = rope_tables(own_pos, HD)
    context = (cosine, sine, own_pos, pos_all)
    layer_shards = [
        (
            prenorm_one,
            query_one,
            keys_one,
            values_one,
            outproj_one,
            midnorm_one,
            gates_one,
            upproj_one,
            downproj_one,
        ),
        (
            prenorm_two,
            query_two,
            keys_two,
            values_two,
            outproj_two,
            midnorm_two,
            gates_two,
            upproj_two,
            downproj_two,
        ),
    ]
    hidden = tokens.reshape(seq_dev, model_width).astype(jnp.float32)
    first_values = None
    kept_full = []
    kept_saved = []
    for layer_no in range(2):
        full_layer = gather_forward(layer_shards[layer_no])
        hidden, values_raw, saved = forward_layer(hidden, full_layer, first_values, context)
        if layer_no == 0:
            first_values = values_raw
        kept_full.append(full_layer)
        kept_saved.append(saved)
    output = hidden.astype(jnp.bfloat16).reshape(1, seq_dev, model_width)
    grad_now = cotangent.reshape(seq_dev, model_width).astype(jnp.float32)
    value_extra = None
    layer_grads = [None, None]
    for layer_no in (1, 0):
        full_layer = kept_full[layer_no]
        grad_now, grad_terms, passed_on = backward_layer(
            grad_now, full_layer, kept_saved[layer_no], value_extra, layer_no == 1, context
        )
        if layer_no == 1:
            value_extra = passed_on
        layer_grads[layer_no] = scatter_grads(grad_terms)
    tokens_grad = grad_now.astype(jnp.bfloat16).reshape(1, seq_dev, model_width)
    first_grads = layer_grads[0]
    second_grads = layer_grads[1]
    return (
        output,
        tokens_grad,
        first_grads[0],
        first_grads[1],
        first_grads[2],
        first_grads[3],
        first_grads[4],
        first_grads[5],
        first_grads[6],
        first_grads[7],
        first_grads[8],
        second_grads[0],
        second_grads[1],
        second_grads[2],
        second_grads[3],
        second_grads[4],
        second_grads[5],
        second_grads[6],
        second_grads[7],
        second_grads[8],
    )


ROWS = 128
BF = jnp.bfloat16
F32 = jnp.float32
MESH = pl.DeviceIdType.MESH
VMEM_SPACE = pltpu.VMEM


def flip(value, weight):
    return value + weight * (1 - 2 * ((value // weight) % 2))


def to_device(f, c):
    return {"fsdp": f, "ctx": c}


def remote(src, dst, send_sem, recv_sem, target):
    return pltpu.make_async_remote_copy(
        src_ref=src,
        dst_ref=dst,
        send_sem=send_sem,
        recv_sem=recv_sem,
        device_id=to_device(*target),
        device_id_type=MESH,
    )


def arrived(ref, sem, target):
    remote(ref, ref, sem, sem, target).wait_recv()


def plane_place():
    f = lax.axis_index("fsdp")
    c = lax.axis_index("ctx")
    return f, c, (c // 2) % 2, c // 4


def row_peers(f, c, z):
    return [(f, c + 4 * ((z + i) % 4 - z)) for i in range(1, 4)]


HALF = ROWS // 2
ODD = 8


class Plane:
    def __init__(self, place, inner):
        f, c, y, z = place
        self.y, self.inner = y, inner
        self.mirrored = z // 2
        sign = 1 - 2 * self.mirrored
        self.own = 1 if inner else 0
        self.across = (f, flip(c, 2))
        self.chip_at = [(f, c + 4 * sign * (near - self.own)) for near in range(4)]
        self.sent = []

    def at(self, near):
        return near + self.mirrored * (3 - 2 * near)

    def slot(self, half, near):
        return 4 * half + self.at(near)

    def start(self, copy):
        copy.start()
        self.sent.append(copy)

    def finish(self):
        for copy in self.sent:
            copy.wait_send()


class Reduce(Plane):
    def __init__(self, place, inner, product, bufs, sems):
        super().__init__(place, inner)
        self.product = product
        self.sy, self.ry, self.acc, self.pb, self.su, self.sd, self.rb, self.ra = bufs
        self.ys, self.yr, self.us, self.ds, self.br, self.ar = sems

    def y_copy(self, slot):
        return remote(self.sy.at[slot], self.ry.at[slot], self.ys.at[slot], self.yr.at[slot], self.across)

    def got_y(self, slot):
        self.y_copy(slot).wait_recv()
        return self.ry[slot].astype(F32)

    def got(self, first, slot):
        buf, sem = (self.rb, self.br) if first else (self.ra, self.ar)
        arrived(buf.at[slot], sem.at[slot], self.across)
        return buf[slot].astype(F32)

    def pass_on(self, value, upward, slot, target, first, there=None):
        there = slot if there is None else there
        src, send = (self.su, self.us) if upward else (self.sd, self.ds)
        dst, sem = (self.rb, self.br) if first else (self.ra, self.ar)
        src[slot] = value.astype(BF)
        self.start(remote(src.at[slot], dst.at[there], send.at[slot], sem.at[there], self.chip_at[target]))

    def cross(self, slot, value):
        self.sy[slot] = value.astype(BF)
        self.start(self.y_copy(slot))

    def order(self, step):
        near = 3 - step
        if self.inner:
            near = jnp.where(step == 0, 3, jnp.where(step == 1, 0, 4 - step))
        return near, near + self.mirrored * (3 - 2 * near)

    def products(self):
        def other_row(step, carry):
            near, block = self.order(step)
            value = self.product(2 * block + 1 - self.y)
            self.sy[block] = value[:HALF].astype(BF)
            self.y_copy(block).start()
            self.pb[block] = value[HALF:]

            @pl.when((near == 1) | (near == 2))
            def _():
                self.sy[4 + block] = value[HALF:].astype(BF)
                self.y_copy(4 + block).start()

            return carry

        lax.fori_loop(0, 4, other_row, 0)
        for near in range(4):
            self.sent.append(self.y_copy(self.slot(0, near)))
        for near in (1, 2):
            self.sent.append(self.y_copy(self.slot(1, near)))
        if self.inner:
            self.pass_on(self.pb[self.at(3)], True, ODD, 3, True)
            self.pass_on(self.pb[self.at(0)], False, ODD, 0, False)
        else:
            self.pass_on(self.pb[self.at(3)], True, ODD, 3, False, ODD + 1)

        def own_row(step, carry):
            near, block = self.order(step)
            value = self.product(2 * block + self.y)
            self.acc[block] = value[:HALF]
            self.acc[4 + block] = value[HALF:]
            return carry

        lax.fori_loop(0, 4, own_row, 0)
        far = self.slot(1, 3)
        if self.inner:
            end = self.slot(1, 0)
            self.pass_on(self.acc[end], False, end, 0, False)
            self.pass_on(self.acc[far] + self.got(True, far), True, far, 3, True)
        else:
            self.pass_on(self.acc[far], True, far, 1, True)

    def relay(self, half, near):
        slot = self.slot(half, near)
        value = self.acc[slot] + self.got_y(slot)
        if not self.inner:
            self.pass_on(value, True, slot, 1, True)
        elif near == 0:
            self.pass_on(value, False, slot, 0, False)
        else:
            self.pass_on(value + self.got(True, slot), True, slot, near, near == 3)

    def relays(self):
        if self.inner:
            self.relay(0, 3)
            self.relay(0, 0)
            self.relay(0, 2)
            self.relay(1, 2)
            return
        self.relay(0, 3)
        self.relay(0, 2)
        self.relay(1, 2)
        odd = self.pb[self.at(0)] + self.got(False, ODD) + self.got(True, ODD) + self.got(False, ODD + 1)
        self.cross(self.slot(1, 0), odd)
        self.relay(0, 1)
        self.relay(1, 1)

    def own_sum(self, half):
        slot = self.slot(half, self.own)
        return self.acc[slot] + self.got_y(slot) + self.got(True, slot) + self.got(False, slot)


class Gather(Plane):
    def __init__(self, place, inner, full, sems):
        super().__init__(place, inner)
        self.full = full
        self.ys, self.yr, self.us, self.ds, self.zr = sems

    def rows(self, half, near, side):
        start = (self.at(near) * 2 + side) * ROWS + half * HALF
        return self.full.at[pl.ds(pl.multiple_of(start, HALF), HALF)]

    def to_row(self, part, sem, slot, target):
        self.start(remote(part, part, sem, self.zr.at[slot], self.chip_at[target]))

    def to_other_row(self, half, near):
        part = self.rows(half, near, self.y)
        slot = self.slot(half, near)
        self.start(remote(part, part, self.ys.at[slot], self.yr.at[slot], self.across))

    def send_own(self, half):
        part = self.rows(half, self.own, self.y)
        slot = self.slot(half, self.own)
        self.to_row(part, self.us.at[slot], slot, 2)
        self.to_row(part, self.ds.at[slot], slot, 0 if self.inner else 1)
        self.to_other_row(half, self.own)

    def take(self, half, near):
        part = self.rows(half, near, self.y)
        slot = self.slot(half, near)
        arrived(part, self.zr.at[slot], self.across)
        if self.inner and near in (2, 3):
            self.to_row(part, self.ds.at[slot], slot, 0)
        if half == 0 or near in (1, 2):
            self.to_other_row(half, near)

    def odd_slot(self, near):
        return ODD + self.at(near) // 3

    def take_odd(self, near):
        arrived(self.rows(1, near, 1 - self.y), self.zr.at[self.odd_slot(near)], self.across)

    def got_y(self, half, near):
        arrived(self.rows(half, near, 1 - self.y), self.yr.at[self.slot(half, near)], self.across)

    def forward(self, half):
        others = (0, 2, 3) if self.inner else (1, 2, 3)
        if half == 0:
            for near in others:
                self.take(0, near)
            return
        if not self.inner:
            self.got_y(1, 0)
            part = self.rows(1, 0, 1 - self.y)
            slot = self.odd_slot(0)
            self.to_row(part, self.us.at[8], slot, 3)
            self.to_row(part, self.us.at[9], slot, 2)
            self.to_row(part, self.ds.at[8], slot, 1)
        for near in others:
            self.take(1, near)
        if self.inner:
            self.take_odd(0)
        self.take_odd(3)
        for near in range(4):
            self.got_y(0, near)
        for near in (1, 2):
            self.got_y(1, near)


def both_kinds(place, run):
    z = place[3]

    @pl.when((z > 0) & (z < 3))
    def _():
        run(True)

    @pl.when((z == 0) | (z == 3))
    def _():
        run(False)


def exchange(place, product, settle, full, scratch, extra=None):
    if extra is None:
        f, c, y, z = place
        greet(row_peers(f, c, z) + [(f, flip(c, 2))])
    else:
        peers, sibling, twin = chip_peers(place[0], place[1])
        greet(peers + [sibling, twin])

    def run(inner):
        parts = []
        more = None if extra is None else extra(place)
        reduce = Reduce(place, inner, product, scratch[:8], scratch[8:14])
        reduce.products()
        if more is not None:
            more.first()
            parts.append(more)
        parts.append(reduce)
        if full is not None:
            gather = Gather(place, inner, full, scratch[14:19])
            parts.append(gather)
        reduce.relays()
        if more is not None:
            more.second()
        for half in range(2):
            rows = settle(half, reduce.own_sum(half))
            if full is not None:
                start = (place[3] * 2 + place[2]) * ROWS + half * HALF
                full[pl.ds(pl.multiple_of(start, HALF), HALF), :] = rows
                gather.send_own(half)
            if more is not None and half == 0:
                more.third()
        if full is not None:
            gather.forward(0)
            gather.forward(1)
        for part in parts:
            part.finish()

    both_kinds(place, run)


def half_rows(half):
    return pl.ds(half * HALF, HALF)


def norm_rows(hidden):
    return lax.rsqrt(jnp.mean(hidden * hidden, axis=-1, keepdims=True) + NORM_EPS)


def make_product(left_ref, right_ref, transposed, lanes=None):
    dims = (((1,), (1,)), ((), ())) if transposed else (((1,), (0,)), ((), ()))

    def product(block):
        rows = left_ref[pl.ds(pl.multiple_of(block * ROWS, ROWS), ROWS), :]
        right = right_ref[...] if lanes is None else right_ref[:, lanes[0] : lanes[1]]
        return lax.dot_general(rows, right, dims, preferred_element_type=F32)

    return product


def forward_kernel(row, left_ref, right_ref, res_ref, gain_ref, new_ref, full_ref, *scratch):
    def settle(half, total):
        hidden = res_ref[half_rows(half), :].astype(F32) + total
        new_ref[half_rows(half), :] = hidden
        return (hidden * norm_rows(hidden) * gain_ref[row : row + 1, :]).astype(BF)

    exchange(plane_place(), make_product(left_ref, right_ref, False), settle, full_ref, scratch)


def turn_kernel(left_ref, right_ref, res_ref, cot_ref, out_ref, full_ref, *scratch):
    def settle(half, total):
        out_ref[half_rows(half), :] = (res_ref[half_rows(half), :] + total).astype(BF)
        return cot_ref[half_rows(half), :]

    exchange(plane_place(), make_product(left_ref, right_ref, False), settle, full_ref, scratch)


def back_rows(total, grad, hidden, gain):
    inverse = norm_rows(hidden)
    normed = hidden * inverse
    scaled = total * gain
    mean = jnp.mean(scaled * normed, axis=-1, keepdims=True)
    return grad + inverse * (scaled - normed * mean)


def comm_call(kernel, outs, ident, args, gathers, name, more=()):
    width = 1024
    scratch = []
    for count, kind in ((8, BF), (8, BF), (8, F32), (4, F32), (9, BF), (9, BF), (9, BF), (10, BF)):
        scratch.append(pltpu.VMEM((count, HALF, width), kind))
    scratch += [pltpu.SemaphoreType.DMA((10,))] * 6
    if gathers:
        scratch += [pltpu.SemaphoreType.DMA((10,))] * 5
    scratch += list(more)
    spec = pl.BlockSpec(memory_space=VMEM_SPACE)
    return pl.pallas_call(
        kernel,
        out_shape=[jax.ShapeDtypeStruct(*o) for o in outs],
        in_specs=[spec] * len(args),
        out_specs=[spec] * len(outs),
        scratch_shapes=scratch,
        compiler_params=pltpu.CompilerParams(
            collective_id=ident, has_side_effects=True, vmem_limit_bytes=(24 if more else 14) * 1024 * 1024
        ),
        name=name,
    )(*args)


def chip_peers(f, c):
    chip, core = c // 2, c % 2
    return [(f, 2 * ((chip + i) % 8) + core) for i in range(1, 8)], (f, flip(c, 1)), (1 - f, c)


def greet(targets):
    barrier = pltpu.get_barrier_semaphore()
    for target in targets:
        pl.semaphore_signal(barrier, inc=1, device_id=to_device(*target), device_id_type=MESH)
    pl.semaphore_wait(barrier, len(targets))


class Spread:
    def __init__(self, place, table, down, out, sems):
        self.f, self.c, self.y, _ = place
        self.chip, self.core = self.c // 2, self.c % 2
        self.peers, self.sibling, self.twin = chip_peers(self.f, self.c)
        self.near = (self.f, flip(self.c, 2))
        self.table, self.down, self.out = table, down, out
        self.ds, self.dr, self.xs, self.xr, self.ss, self.sr, self.ws, self.wr = sems
        self.home = self.y == self.f
        self.direct, self.crossed, self.inner, self.sent = {}, {}, [], []

    def send(self, src, dst, send_sem, recv_sem, target):
        copy = remote(src, dst, send_sem, recv_sem, target)
        copy.start()
        self.sent.append(copy)
        return copy

    def to_twin(self, src, dst, n):
        self.crossed[n] = self.send(src, dst, self.xs.at[n], self.xr.at[n], self.twin)

    def to_sibling(self, src, dst, n):
        self.inner.append(self.send(src, dst, self.ss.at[n], self.sr.at[n], self.sibling))

    def out_copy(self):
        op, out = self.out
        part = 2 * self.y + self.core
        return remote(op, out.at[part], self.ws, self.wr, self.near)

    def pair_copies(self, s, r, first, target):
        parts = [self.out[1].at[self.core], self.out[1].at[2 + self.core]]
        return [remote(p, p, s.at[first + n], r.at[first + n], target) for n, p in enumerate(parts)]

    def first(self):
        a, r = self.table
        down, down_all = self.down
        op, out = self.out
        mine = self.f * 16 + self.c
        part = 2 * self.f + self.core
        self.to_twin(a.at[self.chip], r.at[mine], 0)
        for i in range(1, 8):
            t = (self.chip + i) % 8
            self.direct[i] = self.send(
                a.at[t], r.at[mine], self.ds.at[i], self.dr.at[i], self.peers[i - 1]
            )
        r[mine] = a[self.chip]
        self.to_sibling(a.at[self.chip], r.at[mine], 0)
        down_all[part] = down[...]
        self.to_twin(down, down_all.at[part], 8)
        self.to_sibling(down, down_all.at[part], 16)

        @pl.when(self.home)
        def _():
            out[2 * self.y + self.core] = op[...]

        @pl.when(jnp.logical_not(self.home))
        def _():
            self.out_copy().start()

    def second(self):
        r = self.table[1]
        for i in range(1, 8):
            self.direct[i].wait_recv()
            source = self.f * 16 + 2 * ((self.chip + 8 - i) % 8) + self.core
            self.to_twin(r.at[source], r.at[source], i)
            self.to_sibling(r.at[source], r.at[source], i)

        @pl.when(self.home)
        def _():
            self.out_copy().wait_recv()
            for copy in self.pair_copies(self.xs, self.xr, 9, self.twin):
                copy.start()

    def third(self):
        r = self.table[1]

        @pl.when(jnp.logical_not(self.home))
        def _():
            for copy in self.pair_copies(self.xs, self.xr, 9, self.twin):
                copy.wait_recv()

        for copy in self.pair_copies(self.ss, self.sr, 18, self.sibling):
            copy.start()
        for i in range(8):
            self.crossed[i].wait_recv()
            source = (1 - self.f) * 16 + 2 * ((self.chip + 8 - i) % 8) + self.core
            self.to_sibling(r.at[source], r.at[source], 8 + i)
        self.crossed[8].wait_recv()
        part = 2 * (1 - self.f) + self.core
        down_all = self.down[1]
        self.to_sibling(down_all.at[part], down_all.at[part], 17)

    def finish(self):
        for copy in self.inner:
            copy.wait_recv()
        for copy in self.sent:
            copy.wait_send()
        for copy in self.pair_copies(self.ss, self.sr, 18, self.sibling):
            copy.wait()

        @pl.when(self.home)
        def _():
            for copy in self.pair_copies(self.xs, self.xr, 9, self.twin):
                copy.wait_send()

        @pl.when(jnp.logical_not(self.home))
        def _():
            self.out_copy().wait_send()


def turn_row(row):
    size = row.shape[1]
    same = lax.broadcasted_iota(jnp.int32, (size, size), 0) == lax.broadcasted_iota(jnp.int32, (size, size), 1)
    return jnp.sum(jnp.where(same, row, 0.0), axis=1, keepdims=True)


def turn_column(column):
    size = column.shape[0]
    same = lax.broadcasted_iota(jnp.int32, (size, size), 0) == lax.broadcasted_iota(jnp.int32, (size, size), 1)
    return jnp.sum(jnp.where(same, column, 0.0), axis=0, keepdims=True)


def pack_shards(shards, block, a, dn):
    pre, query, keys, values, _, mid, gates, upproj, down = shards
    rows, units = gates.shape
    each = units // 32
    lane = lax.broadcasted_iota(jnp.int32, (rows, block - each), 1)
    empty = jnp.zeros((rows, block - each), F32)
    pre, mid = turn_row(pre[...].astype(F32)), turn_row(mid[...].astype(F32))
    riders = jnp.where(lane == 0, pre, jnp.where(lane == 1, mid, empty))
    for chip in range(8):
        pair = 4 * (chip % 2) + chip // 2
        for n, w in enumerate((query, keys, values)):
            a[chip, :, 128 * n : 128 * n + 128] = w[:, 128 * pair : 128 * pair + 128]
        for n, w in enumerate((gates, upproj)):
            parts = []
            for i in range(4):
                owner = 16 * (i // 2) + 2 * chip + i % 2
                parts.append(w[:, each * owner : each * owner + each].astype(F32))
                parts.append(riders if n == 0 and i == 0 else empty)
            first = 384 + 4 * block * n
            a[chip, :, first : first + 4 * block] = jnp.concatenate(parts, axis=-1).astype(BF)
    dn[:each] = down[...]
    dn[each:] = jnp.zeros((block - each, down.shape[1]), BF)


def read_gains(r, each, gains):
    count = r.shape[0] * r.shape[1]
    columns = r[:, :, 384:512].reshape(count, 128)
    row = lax.broadcasted_iota(jnp.int32, (8, 128), 0)
    lane = lax.broadcasted_iota(jnp.int32, (8, 128), 1)
    pick = jnp.where(lane == row + each, 1.0, 0.0).astype(BF)
    gains[...] = lax.dot_general(pick, columns, NT, preferred_element_type=F32)


def begin_kernel(tok, *refs):
    shards, (full, r, d, o, gains), (a, dn, *sems) = refs[:9], refs[9:14], refs[14:]
    place = plane_place()
    f, c, y, z = place
    peers, sibling, twin = chip_peers(f, c)
    start = (z * 2 + y) * ROWS
    full[pl.ds(pl.multiple_of(start, ROWS), ROWS), :] = tok[...]
    pack_shards(shards, dn.shape[0], a, dn)
    greet(peers + [sibling, twin])

    def run(inner):
        gather = Gather(place, inner, full, sems[:5])
        spread = Spread(place, (a, r), (dn, d), (shards[4], o), sems[5:])
        gather.send_own(0)
        spread.first()
        gather.send_own(1)
        gather.forward(0)
        spread.second()
        gather.forward(1)
        spread.third()
        gather.finish()
        spread.finish()

    both_kinds(place, run)
    read_gains(r, shards[8].shape[0], gains)


def spread_shapes(rows, width, block):
    wide = 384 + 8 * block
    outs = [((32, rows, wide), BF), ((4, block, width), BF), ((4, rows, width), BF), ((8, 32 * rows), F32)]
    scratch = [pltpu.VMEM((8, rows, wide), BF), pltpu.VMEM((block, width), BF)]
    sems = [pltpu.SemaphoreType.DMA(n) for n in ((8,), (8,), (11,), (11,), (20,), (20,), (), ())]
    return outs, scratch, sems


def begin_call(tok, shards, block):
    rows, width = shards[1].shape
    outs, scratch, sems = spread_shapes(rows, width, block)
    outs = [((8 * ROWS, width), BF)] + outs
    spec = pl.BlockSpec(memory_space=VMEM_SPACE)
    return pl.pallas_call(
        begin_kernel,
        out_shape=[jax.ShapeDtypeStruct(*o) for o in outs],
        in_specs=[spec] * 10,
        out_specs=[spec] * len(outs),
        scratch_shapes=scratch + [pltpu.SemaphoreType.DMA((10,))] * 5 + sems,
        compiler_params=pltpu.CompilerParams(
            collective_id=9, has_side_effects=True, vmem_limit_bytes=60 * 1024 * 1024
        ),
        name="begin",
    )(tok, *shards)


def first_middle_kernel(left_ref, right_ref, res_ref, gain_ref, *refs):
    shards, (new_ref, full_ref, r, d, o, gains), scratch = refs[:9], refs[9:15], refs[15:]
    a, dn, *sems = scratch[19:]

    def settle(half, total):
        hidden = res_ref[half_rows(half), :].astype(F32) + total
        new_ref[half_rows(half), :] = hidden
        return (hidden * norm_rows(hidden) * gain_ref[1:2, :]).astype(BF)

    def extra(place):
        return Spread(place, (a, r), (dn, d), (shards[4], o), sems)

    pack_shards(shards, dn.shape[0], a, dn)
    exchange(plane_place(), make_product(left_ref, right_ref, False), settle, full_ref, scratch, extra)
    read_gains(r, shards[8].shape[0], gains)


class Collect:
    def __init__(self, place, ins, results, scratch):
        self.f, self.c, self.y, _ = place
        self.chip, self.core = self.c // 2, self.c % 2
        self.peers, self.sibling, self.twin = chip_peers(self.f, self.c)
        self.near = (self.f, flip(self.c, 2))
        self.g, self.h = ins
        self.out, self.oh = results
        self.sb, self.xb, self.xt, self.ut, self.sh, self.xh, self.th, *near = scratch[: -6]
        self.ss, self.sr, self.xs, self.xr, self.ps, self.pr = scratch[-6:]
        self.crosses_near = bool(near)
        if near:
            self.yo, self.yt = near
        self.home = self.y == self.f
        self.sent = []

    def send(self, src, dst, send_sem, recv_sem, target):
        copy = remote(src, dst, send_sem, recv_sem, target)
        copy.start()
        self.sent.append(copy)
        return copy

    def inner_send(self, src, dst, n):
        return self.send(src, dst, self.ss.at[n], self.sr.at[n], self.sibling)

    def twin_copy(self):
        return remote(self.th, self.xh, self.xs.at[8], self.xr.at[8], self.twin)

    def near_copy(self):
        return remote(self.yt, self.yo, self.xs.at[9], self.xr.at[9], self.near)

    def first(self):
        other = 1 - self.core
        self.inner = []
        for half in range(2):
            part = 8 * ((1 - self.f) if half == 0 else self.f)
            self.inner.append(
                self.inner_send(self.g.at[pl.ds(part, 8), other], self.sb.at[pl.ds(part, 8)], half)
            )
        self.inner.append(self.inner_send(self.h.at[:, other], self.sh, 2))

    def second(self):
        f, core = self.f, self.core
        self.crossed = []
        self.inner[0].wait_recv()
        for i in range(8):
            t = (self.chip + i + 1) % 8
            at = (1 - f) * 8 + t
            self.xt[t] = (self.g[at, core].astype(F32) + self.sb[at].astype(F32)).astype(BF)
            self.crossed.append(
                self.send(self.xt.at[t], self.xb.at[t], self.xs.at[i], self.xr.at[i], self.twin)
            )
        self.inner[2].wait_recv()
        if not self.crosses_near:
            self.th[...] = (self.h[1 - f, core].astype(F32) + self.sh[1 - f].astype(F32)).astype(BF)
            self.twin_copy().start()
            return
        for side in range(2):
            self.th[side] = (self.h[side, core].astype(F32) + self.sh[side].astype(F32)).astype(BF)

        @pl.when(jnp.logical_not(self.home))
        def _():
            self.twin_copy().start()

    def third(self):
        f, core = self.f, self.core
        self.direct = []
        self.inner[1].wait_recv()
        for i in range(8):
            t = (self.chip + i + 1) % 8
            at = f * 8 + t
            self.crossed[i].wait_recv()
            total = self.g[at, core].astype(F32) + self.sb[at].astype(F32) + self.xb[t].astype(F32)
            if i < 7:
                self.ut[t] = total.astype(BF)
                self.direct.append(
                    self.send(self.ut.at[t], self.out.at[self.chip], self.ps.at[i], self.pr.at[i], self.peers[i])
                )
            else:
                self.out[self.chip] = total.astype(BF)
        if not self.crosses_near:
            self.twin_copy().wait_recv()
            self.oh[...] = self.h[f, core].astype(F32) + self.sh[f].astype(F32) + self.xh[...].astype(F32)
            return

        @pl.when(self.home)
        def _():
            self.twin_copy().wait_recv()
            y = self.y
            self.oh[...] = self.th[y].astype(F32) + self.xh[y].astype(F32)
            self.yt[...] = (self.th[1 - y].astype(F32) + self.xh[1 - y].astype(F32)).astype(BF)
            self.near_copy().start()

    def finish(self):
        if self.crosses_near:

            @pl.when(self.home)
            def _():
                self.near_copy().wait_send()

            @pl.when(jnp.logical_not(self.home))
            def _():
                self.near_copy().wait_recv()
                self.oh[...] = self.yo[...].astype(F32)
                self.twin_copy().wait_send()
        else:
            self.twin_copy().wait_send()
        for copy in self.direct:
            copy.wait_recv()
        for copy in self.sent:
            copy.wait_send()


def collect_shapes(rows, wide, block, width, crosses_near):
    results = [((8, rows, wide), BF), ((block, width), F32)]
    buffers = [(16, rows, wide), (8, rows, wide), (8, rows, wide), (8, rows, wide), (2, block, width)]
    if crosses_near:
        buffers += [(2, block, width), (2, block, width), (block, width), (block, width)]
    else:
        buffers += [(block, width), (block, width)]
    counts = ((3,), (3,), (10,), (10,), (7,), (7,))
    scratch = [pltpu.VMEM(b, BF) for b in buffers] + [pltpu.SemaphoreType.DMA(n) for n in counts]
    return results, scratch


def back_kernel(gathers, row, lanes, left_ref, right_ref, grad_ref, hid_ref, gain_ref, g, gd, new_ref, *rest):
    full_ref = rest[0] if gathers else None
    c, od = rest[gathers : gathers + 2]
    scratch = rest[gathers + 2 :]

    def settle(half, total):
        at = half_rows(half)
        new = back_rows(total, grad_ref[at, :].astype(F32), hid_ref[at, :].astype(F32), gain_ref[row : row + 1, :])
        new_ref[at, :] = new.astype(new_ref.dtype)
        return new.astype(BF)

    def extra(place):
        return Collect(place, (g, gd), (c, od), scratch[14 + 5 * gathers :])

    product = make_product(left_ref, right_ref, True, lanes)
    exchange(plane_place(), product, settle, full_ref, scratch, extra)


def head_lanes(head):
    lane = lax.broadcasted_iota(jnp.int32, (1, 128), 1)
    return lane // 64 == head


def swap_halves(values):
    lane = lax.broadcasted_iota(jnp.int32, (1, 128), 1)
    return jnp.where(lane % 64 < 32, pltpu.roll(values, 96, 1), pltpu.roll(values, 32, 1))


NT = (((1,), (1,)), ((), ()))
TN = (((0,), (0,)), ((), ()))


def two_blocks(ref, tile, half):
    first = pl.multiple_of(2 * tile * ROWS + half * HALF, HALF)
    second = pl.multiple_of((2 * tile + 1) * ROWS + half * HALF, HALF)
    return jnp.concatenate([ref[pl.ds(first, HALF), :], ref[pl.ds(second, HALF), :]], axis=0)


def put_blocks(ref, tile, half, value):
    first = pl.multiple_of(2 * tile * ROWS + half * HALF, HALF)
    second = pl.multiple_of((2 * tile + 1) * ROWS + half * HALF, HALF)
    ref[pl.ds(first, HALF), :] = value[:HALF]
    ref[pl.ds(second, HALF), :] = value[HALF:]


def attend_kernel(layer, *refs):
    x_ref, w_ref, cos_ref, sin_ref, more_ref, pq_ref, pk_ref = refs[:7]
    q_ref, k_ref, v_ref, att_ref, lse_ref = refs[7:12]
    ss, sr = refs[-2:]
    f, c, _, _ = plane_place()
    sibling = (f, flip(c, 1))
    greet([sibling])
    rows_n = x_ref.shape[0]
    half_n = rows_n // 2

    def copies(i):
        here = pl.ds(pl.multiple_of(i * HALF, HALF), HALF)
        there = pl.ds(pl.multiple_of(half_n + i * HALF, HALF), HALF)
        return [
            remote(ref.at[h, here], ref.at[h, there], ss.at[4 * i + n], sr.at[4 * i + n], sibling)
            for n, (ref, h) in enumerate(((k_ref, 0), (k_ref, 1), (v_ref, 0), (v_ref, 1)))
        ]

    def step(i, carry):
        at = pl.ds(pl.multiple_of(i * ROWS, ROWS), ROWS)
        here = pl.ds(pl.multiple_of(i * HALF, HALF), HALF)
        rows = x_ref[at, :]
        if layer == 0:
            wide = rows.astype(F32)
            rows = (wide * norm_rows(wide) * more_ref[:1, :]).astype(BF)
            refs[12][at, :] = rows
        raw = jnp.dot(rows, w_ref[:, :384], preferred_element_type=F32)
        cosine, sine = cos_ref[at, :], sin_ref[at, :]
        q, k, v = raw[:, :128], raw[:, 128:256], raw[:, 256:]
        q_ref[at, :] = (q * cosine + swap_halves(q) * sine).astype(BF)
        k = (k * cosine + swap_halves(k) * sine).astype(BF)
        if layer == 0:
            refs[13][at, :] = v
        else:
            v = 0.5 * v + 0.5 * more_ref[at, :]
        v = v.astype(BF)
        for half in range(2):
            k_ref[half, here, :] = k[half * HALF : (half + 1) * HALF]
            v_ref[half, here, :] = v[half * HALF : (half + 1) * HALF]
        for copy in copies(i):
            copy.start()
        return carry

    lax.fori_loop(0, rows_n // ROWS, step, 0)
    for i in range(rows_n // ROWS):
        for copy in copies(i):
            copy.wait()

    def tile_step(tile, carry):
        for late in range(2):
            number = tile + late * (rows_n // (2 * ROWS))
            queries = two_blocks(q_ref, tile, late) * jnp.asarray(HD ** (-0.5), BF)
            allowed = pk_ref[late : late + 1, :] <= turn_row(pq_ref[pl.ds(number, 1), :])
            parts = []
            for head in range(2):
                masked = jnp.where(head_lanes(head), queries, jnp.zeros_like(queries))
                scores = lax.dot_general(masked, k_ref[late], NT, preferred_element_type=F32)
                scores = jnp.where(allowed, scores, NEG_FILL)
                top = jnp.max(scores, axis=-1, keepdims=True)
                if late:
                    early = lax.dot_general(masked, k_ref[0], NT, preferred_element_type=F32)
                    top = jnp.maximum(top, jnp.max(early, axis=-1, keepdims=True))
                shares = jnp.exp(scores - top)
                total = jnp.sum(shares, axis=-1, keepdims=True)
                mixed = jnp.dot(shares.astype(BF), v_ref[late], preferred_element_type=F32)
                if late:
                    shares = jnp.exp(early - top)
                    total += jnp.sum(shares, axis=-1, keepdims=True)
                    mixed += jnp.dot(shares.astype(BF), v_ref[0], preferred_element_type=F32)
                lse_ref[number, head : head + 1, :] = turn_column(top + jnp.log(total))
                parts.append(mixed / total)
            put_blocks(att_ref, tile, late, jnp.where(head_lanes(0), parts[0], parts[1]).astype(BF))
        return carry

    lax.fori_loop(0, rows_n // (2 * ROWS), tile_step, 0)


def attend(layer, x, w, cosine, sine, more, pos_q, pos_k):
    rows_n = x.shape[0]
    spec = pl.BlockSpec(memory_space=VMEM_SPACE)
    outs = [((rows_n, 128), BF), ((2, rows_n, 128), BF), ((2, rows_n, 128), BF), ((rows_n, 128), BF)]
    outs += [((rows_n // ROWS, 2, ROWS), F32)]
    if layer == 0:
        outs += [(x.shape, BF), ((rows_n, 128), F32)]
    count = 4 * (rows_n // ROWS)
    return pl.pallas_call(
        functools.partial(attend_kernel, layer),
        out_shape=[jax.ShapeDtypeStruct(*o) for o in outs],
        in_specs=[spec] * 7,
        out_specs=[spec] * len(outs),
        scratch_shapes=[pltpu.SemaphoreType.DMA((count,))] * 2,
        compiler_params=pltpu.CompilerParams(
            collective_id=10 + layer, has_side_effects=True, vmem_limit_bytes=16 * 1024 * 1024
        ),
        name="attend",
    )(x, w, cosine, sine, more, pos_q, pos_k)


def attend_back_kernel(layer, *refs):
    q_ref, k_ref, v_ref, full_ref, out_ref, att_ref, lse_ref, pq_ref, pk_ref, cos_ref, sin_ref, more_ref = refs[:12]
    three_ref, dw_ref = refs[12:14]
    pkc, dq, dk, dv, dw, sb, rb, ss, sr = refs[-9:]
    f, c, _, _ = plane_place()
    sibling = (f, flip(c, 1))
    greet([sibling])
    rows_n = q_ref.shape[0]
    half_n = rows_n // 2
    dk[...] = jnp.zeros_like(dk)
    dv[...] = jnp.zeros_like(dv)
    dw[...] = jnp.zeros_like(dw)
    for late in range(2):
        for i in range(rows_n // ROWS):
            at = slice(i * ROWS, (i + 1) * ROWS)
            pkc[late, at, :] = turn_row(pk_ref[late : late + 1, at])

    def tile_step(tile, carry):
        for late in range(2):
            number = tile + late * (rows_n // (2 * ROWS))
            queries = two_blocks(q_ref, tile, late) * jnp.asarray(HD ** (-0.5), BF)
            full = two_blocks(full_ref, tile, late)
            grads = lax.dot_general(full, out_ref[...], NT, preferred_element_type=F32).astype(BF)
            dw[...] += lax.dot_general(two_blocks(att_ref, tile, late), full, TN, preferred_element_type=F32)
            allowed = pkc[late] <= pq_ref[pl.ds(number, 1), :]
            parts = []
            for head in range(2):
                masked = jnp.where(head_lanes(head), queries, jnp.zeros_like(queries))
                grad_h = jnp.where(head_lanes(head), grads, jnp.zeros_like(grads))
                lse = lse_ref[number, head : head + 1, :]
                kinds = (1, 0) if late else (0,)
                shares, grad_shares = [], []
                delta = jnp.zeros((1, ROWS), F32)
                for kind in kinds:
                    part = jnp.exp(lax.dot_general(k_ref[kind], masked, NT, preferred_element_type=F32) - lse)
                    if kind == late:
                        part = jnp.where(allowed, part, 0.0)
                    grad = lax.dot_general(v_ref[kind], grad_h, NT, preferred_element_type=F32)
                    delta += jnp.sum(part * grad, axis=0, keepdims=True)
                    shares.append(part)
                    grad_shares.append(grad)
                found = jnp.zeros((ROWS, 128), F32)
                for kind, part, grad in zip(kinds, shares, grad_shares):
                    grad_scores = (part * (grad - delta)).astype(BF)
                    dv[kind] += jnp.dot(part.astype(BF), grad_h, preferred_element_type=F32)
                    dk[kind] += jnp.dot(grad_scores, masked, preferred_element_type=F32)
                    found += lax.dot_general(grad_scores, k_ref[kind], TN, preferred_element_type=F32)
                parts.append(found)
            put_blocks(dq, tile, late, jnp.where(head_lanes(0), parts[0], parts[1]) * HD ** (-0.5))
        return carry

    lax.fori_loop(0, rows_n // (2 * ROWS), tile_step, 0)
    copies = []
    for n, ref in enumerate((dk, dv)):
        sb[n] = ref[:, half_n:, :].astype(BF)
        copies.append(remote(sb.at[n], rb.at[n], ss.at[n], sr.at[n], sibling))
        copies[n].start()
    dw_ref[...] = dw[...].astype(BF)
    for copy in copies:
        copy.wait()

    def rows_of(n, ref, i):
        here = pl.ds(pl.multiple_of(i * HALF, HALF), HALF)
        return jnp.concatenate([ref[half, here, :] + rb[n, half, here, :].astype(F32) for half in range(2)], axis=0)

    def turn(i, carry):
        at = pl.ds(pl.multiple_of(i * ROWS, ROWS), ROWS)
        cosine, sine = cos_ref[at, :], sin_ref[at, :]
        for n, grad in enumerate((dq[at, :], rows_of(0, dk, i))):
            three_ref[at, 128 * n : 128 * n + 128] = (grad * cosine - swap_halves(grad) * sine).astype(BF)
        grad = rows_of(1, dv, i)
        if layer == 1:
            grad = 0.5 * grad
            refs[14][at, :] = grad
        else:
            grad = grad + more_ref[at, :]
        three_ref[at, 256:] = grad.astype(BF)
        return carry

    lax.fori_loop(0, rows_n // ROWS, turn, 0)


def attend_backward(layer, q, k, v, full, out_w, att, lse, pos_q, pos_k, cosine, sine, more):
    rows_n = q.shape[0]
    width = full.shape[1]
    spec = pl.BlockSpec(memory_space=VMEM_SPACE)
    outs = [((rows_n, 384), BF), ((128, width), BF)]
    if layer == 1:
        outs += [((rows_n, 128), F32)]
    return pl.pallas_call(
        functools.partial(attend_back_kernel, layer),
        out_shape=[jax.ShapeDtypeStruct(*o) for o in outs],
        in_specs=[spec] * 12,
        out_specs=[spec] * len(outs),
        scratch_shapes=[
            pltpu.VMEM((2, rows_n, 1), F32),
            pltpu.VMEM((rows_n, 128), F32),
            pltpu.VMEM((2, rows_n, 128), F32),
            pltpu.VMEM((2, rows_n, 128), F32),
            pltpu.VMEM((128, width), F32),
            pltpu.VMEM((2, 2, rows_n // 2, 128), BF),
            pltpu.VMEM((2, 2, rows_n // 2, 128), BF),
            pltpu.SemaphoreType.DMA((2,)),
            pltpu.SemaphoreType.DMA((2,)),
        ],
        compiler_params=pltpu.CompilerParams(
            collective_id=12 + layer, has_side_effects=True, vmem_limit_bytes=24 * 1024 * 1024
        ),
        name="attend_back",
    )(q, k, v, full, out_w, att, lse, pos_q, pos_k, cosine, sine, more)


def unpack_kernel(*refs):
    for l in range(2):
        cu, od, cq, oo, pre, query, keys, values, mid, gates, upproj = refs[11 * l : 11 * l + 11]
        g_pre, gq, gk, gv, g_out, g_mid, gg, gu, g_down = refs[22 + 9 * l : 31 + 9 * l]
        rows, units = gates.shape
        each = units // 32
        block = cu.shape[2] // 8
        total = jnp.zeros((rows, 1), F32)
        for chip in range(8):
            pair = 4 * (chip % 2) + chip // 2
            for n, (w, g) in enumerate(((query, gq), (keys, gk), (values, gv))):
                at = slice(128 * pair, 128 * pair + 128)
                part = cq[chip, :, 128 * n : 128 * n + 128].astype(F32)
                g[:, at] = part
                total += jnp.sum(part * w[:, at].astype(F32), axis=-1, keepdims=True)
        g_pre[...] = turn_column(total) / pre[...].astype(F32)
        for n, g in enumerate((gg, gu)):
            for chip in range(8):
                wide = cu[chip, :, 4 * block * n : 4 * block * (n + 1)].astype(F32)
                for i in range(4):
                    owner = 16 * (i // 2) + 2 * chip + i % 2
                    g[:, each * owner : each * owner + each] = wide[:, block * i : block * i + each]
        both = gg[...] * gates[...].astype(F32) + gu[...] * upproj[...].astype(F32)
        g_mid[...] = turn_column(jnp.sum(both, axis=-1, keepdims=True)) / mid[...].astype(F32)
        g_out[...] = oo[...]
        g_down[...] = od[: g_down.shape[0], :]


def unpack(collected, layers):
    args, outs = [], []
    for l, layer in enumerate(layers):
        pre, query, keys, values, out, mid, gates, upproj, down = layer
        args += [*collected[l], pre, query, keys, values, mid, gates, upproj]
        for w in layer:
            outs.append(w.shape)
    spec = pl.BlockSpec(memory_space=VMEM_SPACE)
    found = pl.pallas_call(
        unpack_kernel,
        out_shape=[jax.ShapeDtypeStruct(o, F32) for o in outs],
        in_specs=[spec] * len(args),
        out_specs=[spec] * len(outs),
        compiler_params=pltpu.CompilerParams(vmem_limit_bytes=60 * 1024 * 1024),
        name="unpack",
    )(*args)
    return [g[0] if g.shape[0] == 1 else g for g in found]


def fast_local(tokens, cotangent, pair_of, *shards):
    width = tokens.shape[2]
    rows_each, units = shards[6].shape
    each = units // 32
    block = (each + 2 + 31) // 32 * 32
    hidden_pad = 4 * block
    wide = 384 + 2 * hidden_pad
    core = lax.axis_index("ctx") % 2
    pos_all = storage_positions(pair_of, ROWS).reshape(8, 2, ROWS)
    own_pos = lax.dynamic_index_in_dim(pos_all, core, 1, False).reshape(-1)
    sib_pos = lax.dynamic_index_in_dim(pos_all, 1 - core, 1, False).reshape(-1)
    own_split = own_pos.reshape(8, 2, HALF).transpose(1, 0, 2)
    sib_split = sib_pos.reshape(8, 2, HALF).transpose(1, 0, 2)
    pos_q = own_split.reshape(8, ROWS).astype(F32)
    pos_k = jnp.concatenate([own_split, sib_split], axis=1).reshape(2, -1).astype(F32)
    cosine, sine = rope_tables(own_pos, HD)
    cosine = jnp.concatenate([cosine] * 4, axis=-1)
    sine = jnp.concatenate([-sine, sine, -sine, sine], axis=-1)

    shards = [s[None, :] if s.ndim == 1 else s for s in shards]
    layers = [shards[:9], shards[9:]]
    tok = tokens.reshape(ROWS, width)
    cot = cotangent.reshape(ROWS, width)

    def weights(spread):
        columns = spread[0].reshape(32 * rows_each, wide)
        return columns, spread[1].reshape(hidden_pad, width), spread[2].reshape(4 * rows_each, width), spread[3]

    full, *spread = begin_call(tok, layers[0], block)
    ready = [weights(spread), None]

    plane = 8 * ROWS
    full_type = ((plane, width), BF)
    rows_type = ((ROWS, width), F32)
    saved = []
    hidden = tok
    first_values = None
    for layer in range(2):
        all_w, down_w, out_w, gains = ready[layer]
        more = gains if layer == 0 else first_values
        q, k, v, att, lse, *kept = attend(layer, full, all_w, cosine, sine, more, pos_q, pos_k)
        x_full = full
        if layer == 0:
            x_full, first_values = kept
        args = (att, out_w, hidden, gains)
        if layer == 0:
            outs, packs, sems = spread_shapes(rows_each, width, block)
            middle, mlp_full, *spread = comm_call(
                first_middle_kernel, [rows_type, full_type] + outs, 1, args + tuple(layers[1]), True, "middle", packs + sems
            )
            ready[1] = weights(spread)
        else:
            middle, mlp_full = comm_call(
                functools.partial(forward_kernel, 1), [rows_type, full_type], 2, args, True, "middle"
            )
        both = jnp.dot(mlp_full, all_w[:, 384:], preferred_element_type=F32)
        gate, up = both[:, :hidden_pad], both[:, hidden_pad:]
        inner = (jax.nn.silu(gate) * up).astype(BF)
        saved.append((x_full, q, k, v, lse, att, mlp_full, gate, up, inner, hidden, middle))
        if layer == 0:
            hidden, full = comm_call(
                functools.partial(forward_kernel, 0), [rows_type, full_type], 3,
                (inner, down_w, middle, ready[1][3]), True, "result",
            )
        else:
            output, full = comm_call(
                turn_kernel, [((ROWS, width), BF), full_type], 4,
                (inner, down_w, middle, cot), True, "turn",
            )
    grad = cot
    passed = cosine
    collected = [None, None]
    for layer in (1, 0):
        x_full, q, k, v, lse, att, mlp_full, gate, up, inner, hidden, middle = saved[layer]
        all_w, down_w, out_w, gains = ready[layer]
        grad_down = left_product(inner, full)
        grad_inner = right_product(full, down_w)
        sigma = jax.nn.sigmoid(gate)
        grad_gate = (grad_inner * up * sigma * (1.0 + gate * (1.0 - sigma))).astype(BF)
        grad_up = (grad_inner * gate * sigma).astype(BF)
        both = jnp.concatenate([grad_gate, grad_up], axis=-1)
        grad_upw = left_product(mlp_full, both)
        results, more = collect_shapes(rows_each, 2 * hidden_pad, block, width, False)
        grad_mid, full, *got_up = comm_call(
            functools.partial(back_kernel, 1, 1, (384, wide)), [rows_type, full_type] + results, 5 + layer,
            (
                both, all_w, grad, middle, gains,
                grad_upw.astype(BF).reshape(16, 2, rows_each, 2 * hidden_pad),
                grad_down.astype(BF).reshape(2, 2, block, width),
            ),
            True, "middle_back", more,
        )
        three, grad_out, *kept = attend_backward(
            layer, q, k, v, full, out_w, att, lse, pos_q, pos_k, cosine, sine, passed
        )
        if layer == 1:
            (passed,) = kept
        grad_qkv = left_product(x_full, three)
        results, more = collect_shapes(rows_each, 384, rows_each, width, True)
        args = (
            three, all_w, grad_mid, hidden, gains,
            grad_qkv.astype(BF).reshape(16, 2, rows_each, 384),
            grad_out.reshape(2, 2, rows_each, width),
        )
        if layer == 1:
            grad, full, *got_qkv = comm_call(
                functools.partial(back_kernel, 1, 0, (0, 384)), [rows_type, full_type] + results, 7, args, True,
                "layer_back", more,
            )
        else:
            tokens_grad, *got_qkv = comm_call(
                functools.partial(back_kernel, 0, 0, (0, 384)), [((ROWS, width), BF)] + results, 8, args, False,
                "last_back", more,
            )
        collected[layer] = got_up + got_qkv
    found = unpack(collected, layers)
    return (output.reshape(1, ROWS, width), tokens_grad.reshape(1, ROWS, width), *found)


def solution(mesh):
    placed = (
        P("fsdp", "ctx", None),
        P("fsdp", "ctx", None),
        P(),
        P(("fsdp", "ctx")),
        P(("fsdp", "ctx"), None),
        P(("fsdp", "ctx"), None),
        P(("fsdp", "ctx"), None),
        P(("fsdp", "ctx"), None),
        P(("fsdp", "ctx")),
        P(("fsdp", "ctx"), None),
        P(("fsdp", "ctx"), None),
        P(("fsdp", "ctx"), None),
        P(("fsdp", "ctx")),
        P(("fsdp", "ctx"), None),
        P(("fsdp", "ctx"), None),
        P(("fsdp", "ctx"), None),
        P(("fsdp", "ctx"), None),
        P(("fsdp", "ctx")),
        P(("fsdp", "ctx"), None),
        P(("fsdp", "ctx"), None),
        P(("fsdp", "ctx"), None),
    )
    fits = mesh.shape["ctx"] == HEADS and mesh.shape["fsdp"] == 2
    return jax.shard_map(
        fast_local if fits else local,
        mesh=mesh,
        in_specs=placed,
        out_specs=(
            P("fsdp", "ctx", None),
            P("fsdp", "ctx", None),
            P(("fsdp", "ctx")),
            P(("fsdp", "ctx"), None),
            P(("fsdp", "ctx"), None),
            P(("fsdp", "ctx"), None),
            P(("fsdp", "ctx"), None),
            P(("fsdp", "ctx")),
            P(("fsdp", "ctx"), None),
            P(("fsdp", "ctx"), None),
            P(("fsdp", "ctx"), None),
            P(("fsdp", "ctx")),
            P(("fsdp", "ctx"), None),
            P(("fsdp", "ctx"), None),
            P(("fsdp", "ctx"), None),
            P(("fsdp", "ctx"), None),
            P(("fsdp", "ctx")),
            P(("fsdp", "ctx"), None),
            P(("fsdp", "ctx"), None),
            P(("fsdp", "ctx"), None),
        ),
        check_vma=False,
    )
```

```python
import functools
import math

import jax
import jax.numpy as jnp
from jax import lax
from jax.experimental import pallas as pl
from jax.experimental.pallas import tpu as pltpu
from jax.sharding import PartitionSpec as P

HEADS = 16
HD = 64


NORM_EPS = 1e-05
NEG_FILL = -1e30


def block_size(total_rows):
    size_now = 512
    while total_rows % size_now:
        size_now //= 2
    return size_now


def row_norm(hidden):
    inverse = lax.rsqrt(jnp.mean(hidden * hidden, axis=-1, keepdims=True) + NORM_EPS)
    return (hidden * inverse, inverse)


def norm_back(grad_normed, normed, inverse):
    return inverse * (grad_normed - normed * jnp.mean(grad_normed * normed, axis=-1, keepdims=True))


def rope_tables(positions, head_size):
    half_size = head_size // 2
    freqs = jnp.exp(
        jnp.arange(half_size, dtype=jnp.float32) * (-2.0 * math.log(10000.0) / head_size)
    )
    angles = positions.astype(jnp.float32)[:, None] * freqs[None, :]
    return (jnp.cos(angles), jnp.sin(angles))


def rotate(values_in, cosine, sine):
    half_size = values_in.shape[-1] // 2
    first_half = values_in[..., :half_size]
    second_half = values_in[..., half_size:]
    cos_rows = cosine[:, None, :]
    sin_rows = sine[:, None, :]
    return jnp.concatenate(
        [
            first_half * cos_rows - second_half * sin_rows,
            second_half * cos_rows + first_half * sin_rows,
        ],
        axis=-1,
    )


def unrotate(grads_in, cosine, sine):
    half_size = grads_in.shape[-1] // 2
    first_half = grads_in[..., :half_size]
    second_half = grads_in[..., half_size:]
    cos_rows = cosine[:, None, :]
    sin_rows = sine[:, None, :]
    return jnp.concatenate(
        [
            first_half * cos_rows + second_half * sin_rows,
            second_half * cos_rows - first_half * sin_rows,
        ],
        axis=-1,
    )


def left_product(left, right):
    return lax.dot_general(
        left, right, (((0,), (0,)), ((), ())), preferred_element_type=jnp.float32
    )


def right_product(left, right):
    return lax.dot_general(
        left, right, (((1,), (1,)), ((), ())), preferred_element_type=jnp.float32
    )


def storage_positions(pair_of, seq_dev):
    devices = pair_of.shape[0]
    rows_all = jnp.arange(devices * seq_dev, dtype=jnp.int32)
    owner = rows_all // seq_dev
    local_row = rows_all % seq_dev
    half_rows = seq_dev // 2
    picked = jnp.sum(
        jnp.where(
            owner[:, None] == jnp.arange(devices, dtype=jnp.int32)[None, :], pair_of[None, :], 0
        ),
        axis=1,
    )
    block_id = jnp.where(local_row < half_rows, picked, 2 * devices - 1 - picked)
    return block_id * half_rows + local_row % half_rows


def head_scores(queries, keys_flat, query_pos, key_pos):
    key_heads = keys_flat.reshape(keys_flat.shape[0], queries.shape[1], queries.shape[2])
    scores = jnp.einsum(
        "qhd,khd->hqk", queries, key_heads, preferred_element_type=jnp.float32
    ) * queries.shape[2] ** (-0.5)
    allowed = (key_pos[None, :] <= query_pos[:, None])[None]
    return (jnp.where(allowed, scores, NEG_FILL), allowed)


def make_stats_step(queries, query_pos, pos_all, state_in, key_part):
    size_now = block_size(key_part.shape[0])

    def inner_step(block_no, state_now):
        top_now, total_now = state_now
        offset = block_no * size_now
        key_block = lax.dynamic_slice_in_dim(key_part, offset, size_now, 0)
        key_pos = lax.dynamic_slice_in_dim(pos_all, offset, size_now, 0)
        scores, allowed = head_scores(queries, key_block, query_pos, key_pos)
        new_top = jnp.maximum(top_now, jnp.max(scores, axis=-1))
        total_now = total_now * jnp.exp(top_now - new_top) + jnp.sum(
            jnp.where(allowed, jnp.exp(scores - new_top[..., None]), 0.0), axis=-1
        )
        return (new_top, total_now)

    return lax.fori_loop(0, key_part.shape[0] // size_now, inner_step, state_in)


def make_value_step(queries, log_total, query_pos, pos_all, acc_in, pieces):
    key_part, value_part = pieces
    size_now = block_size(key_part.shape[0])

    def inner_step(block_no, acc_now):
        offset = block_no * size_now
        key_block = lax.dynamic_slice_in_dim(key_part, offset, size_now, 0)
        value_block = lax.dynamic_slice_in_dim(value_part, offset, size_now, 0)
        key_pos = lax.dynamic_slice_in_dim(pos_all, offset, size_now, 0)
        scores, allowed = head_scores(queries, key_block, query_pos, key_pos)
        shares = jnp.exp(scores - log_total[..., None]).astype(jnp.bfloat16)
        value_heads = value_block.reshape(size_now, queries.shape[1], queries.shape[2])
        return acc_now + jnp.einsum(
            "hqk,khd->qhd", shares, value_heads, preferred_element_type=jnp.float32
        )

    return lax.fori_loop(0, key_part.shape[0] // size_now, inner_step, acc_in)


def make_back_step(queries, grad_att, log_total, row_delta, query_pos, pos_all):
    scale_now = queries.shape[2] ** (-0.5)

    def back_step(state_in, pieces, start_row):
        key_part, value_part = pieces
        size_now = block_size(key_part.shape[0])

        def inner_step(block_no, state_now):
            offset = block_no * size_now
            key_block = lax.dynamic_slice_in_dim(key_part, offset, size_now, 0)
            value_block = lax.dynamic_slice_in_dim(value_part, offset, size_now, 0)
            key_pos = lax.dynamic_slice_in_dim(pos_all, offset, size_now, 0)
            scores, allowed = head_scores(queries, key_block, query_pos, key_pos)
            shares = jnp.exp(scores - log_total[..., None])
            value_heads = value_block.reshape(size_now, queries.shape[1], queries.shape[2])
            key_heads = key_block.reshape(size_now, queries.shape[1], queries.shape[2])
            grad_shares = jnp.einsum(
                "qhd,khd->hqk", grad_att, value_heads, preferred_element_type=jnp.float32
            )
            grad_scores = (shares * (grad_shares - row_delta[..., None]) * scale_now).astype(
                jnp.bfloat16
            )
            grad_query = state_now[0] + jnp.einsum(
                "hqk,khd->qhd", grad_scores, key_heads, preferred_element_type=jnp.float32
            )
            return (grad_query,)

        return lax.fori_loop(0, key_part.shape[0] // size_now, inner_step, state_in)

    return back_step


def make_query_step(own_keys, own_values, own_pos, stats_all, pos_all, head_count, head_size):
    scale_now = head_size ** (-0.5)
    value_heads = own_values.reshape(own_values.shape[0], head_count, head_size)

    def query_step(state_in, pieces, start_row):
        query_part, grad_part = pieces
        size_now = block_size(query_part.shape[0])

        def inner_step(block_no, state_now):
            offset = block_no * size_now
            query_block = lax.dynamic_slice_in_dim(query_part, offset, size_now, 0).reshape(
                size_now, head_count, head_size
            )
            grad_block = lax.dynamic_slice_in_dim(grad_part, offset, size_now, 0).reshape(
                size_now, head_count, head_size
            )
            query_pos = lax.dynamic_slice_in_dim(pos_all, offset, size_now, 0)
            log_block = lax.dynamic_slice_in_dim(stats_all[0], offset, size_now, 0).T
            delta_block = lax.dynamic_slice_in_dim(stats_all[1], offset, size_now, 0).T
            scores, allowed = head_scores(query_block, own_keys, query_pos, own_pos)
            shares = jnp.exp(scores - log_block[..., None])
            grad_shares = jnp.einsum(
                "qhd,khd->hqk", grad_block, value_heads, preferred_element_type=jnp.float32
            )
            grad_scores = (shares * (grad_shares - delta_block[..., None]) * scale_now).astype(
                jnp.bfloat16
            )
            key_term = jnp.einsum(
                "hqk,qhd->khd", grad_scores, query_block, preferred_element_type=jnp.float32
            )
            value_term = jnp.einsum(
                "hqk,qhd->khd",
                shares.astype(jnp.bfloat16),
                grad_block,
                preferred_element_type=jnp.float32,
            )
            return (
                state_now[0] + key_term.reshape(key_term.shape[0], -1),
                state_now[1] + value_term.reshape(value_term.shape[0], -1),
            )

        return lax.fori_loop(0, query_part.shape[0] // size_now, inner_step, state_in)

    return query_step


def gather_forward(shards):
    return (
        lax.all_gather(shards[0], ("fsdp", "ctx"), axis=0, tiled=True),
        lax.all_gather(shards[1], ("fsdp", "ctx"), axis=0, tiled=True),
        lax.all_gather(shards[2], ("fsdp", "ctx"), axis=0, tiled=True),
        lax.all_gather(shards[3], ("fsdp", "ctx"), axis=0, tiled=True),
        lax.all_gather(shards[4], ("fsdp", "ctx"), axis=0, tiled=True),
        lax.all_gather(shards[5], ("fsdp", "ctx"), axis=0, tiled=True),
        lax.all_gather(shards[6], ("fsdp", "ctx"), axis=0, tiled=True),
        lax.all_gather(shards[7], ("fsdp", "ctx"), axis=0, tiled=True),
        lax.all_gather(shards[8], ("fsdp", "ctx"), axis=0, tiled=True),
    )


def scatter_grads(grad_terms):
    return (
        lax.psum_scatter(grad_terms[0], ("fsdp", "ctx"), scatter_dimension=0, tiled=True),
        lax.psum_scatter(grad_terms[1], ("fsdp", "ctx"), scatter_dimension=0, tiled=True),
        lax.psum_scatter(grad_terms[2], ("fsdp", "ctx"), scatter_dimension=0, tiled=True),
        lax.psum_scatter(grad_terms[3], ("fsdp", "ctx"), scatter_dimension=0, tiled=True),
        lax.psum_scatter(grad_terms[4], ("fsdp", "ctx"), scatter_dimension=0, tiled=True),
        lax.psum_scatter(grad_terms[5], ("fsdp", "ctx"), scatter_dimension=0, tiled=True),
        lax.psum_scatter(grad_terms[6], ("fsdp", "ctx"), scatter_dimension=0, tiled=True),
        lax.psum_scatter(grad_terms[7], ("fsdp", "ctx"), scatter_dimension=0, tiled=True),
        lax.psum_scatter(grad_terms[8], ("fsdp", "ctx"), scatter_dimension=0, tiled=True),
    )


def forward_layer(hidden, full_layer, first_values, context):
    prenorm, query_w, keys_w, values_w, outproj, midnorm, gates_w, upproj_w, downproj_w = full_layer
    cosine, sine, own_pos, pos_all = context
    rows_n, model_width = hidden.shape
    normed, inverse_a = row_norm(hidden)
    attn_in = (normed * prenorm.astype(jnp.float32)).astype(jnp.bfloat16)
    query_raw = jnp.dot(attn_in, query_w, preferred_element_type=jnp.float32)
    keys_raw = jnp.dot(attn_in, keys_w, preferred_element_type=jnp.float32)
    values_raw = jnp.dot(attn_in, values_w, preferred_element_type=jnp.float32)
    mixed = values_raw if first_values is None else 0.5 * values_raw + 0.5 * first_values
    queries = rotate(query_raw.reshape(rows_n, HEADS, HD), cosine, sine).astype(jnp.bfloat16)
    keys_flat = (
        rotate(keys_raw.reshape(rows_n, HEADS, HD), cosine, sine)
        .reshape(rows_n, model_width)
        .astype(jnp.bfloat16)
    )
    values_flat = mixed.astype(jnp.bfloat16)
    top_start = jnp.full((HEADS, rows_n), NEG_FILL, jnp.float32)
    total_start = jnp.zeros((HEADS, rows_n), jnp.float32)
    top_now, total_now = make_stats_step(
        queries,
        own_pos,
        pos_all,
        (top_start, total_start),
        lax.all_gather(keys_flat, "ctx", axis=0, tiled=True),
    )
    log_total = top_now + jnp.log(total_now)
    att_out = make_value_step(
        queries,
        log_total,
        own_pos,
        pos_all,
        jnp.zeros((rows_n, HEADS, HD), jnp.float32),
        (
            lax.all_gather(keys_flat, "ctx", axis=0, tiled=True),
            lax.all_gather(values_flat, "ctx", axis=0, tiled=True),
        ),
    )
    att_low = att_out.reshape(rows_n, model_width).astype(jnp.bfloat16)
    middle = hidden + jnp.dot(att_low, outproj, preferred_element_type=jnp.float32)
    normed_mid, inverse_b = row_norm(middle)
    mlp_in = (normed_mid * midnorm.astype(jnp.float32)).astype(jnp.bfloat16)
    gate_raw = jnp.dot(mlp_in, gates_w, preferred_element_type=jnp.float32)
    up_proj = jnp.dot(mlp_in, upproj_w, preferred_element_type=jnp.float32)
    inner_act = (jax.nn.silu(gate_raw) * up_proj).astype(jnp.bfloat16)
    result = middle + jnp.dot(inner_act, downproj_w, preferred_element_type=jnp.float32)
    saved = (
        hidden,
        normed,
        inverse_a,
        attn_in,
        queries,
        keys_flat,
        values_flat,
        log_total,
        att_out,
        att_low,
        normed_mid,
        inverse_b,
        mlp_in,
        gate_raw,
        up_proj,
        inner_act,
    )
    return (result, values_raw, saved)


def backward_layer(grad_out, full_layer, saved, value_extra, is_second, context):
    prenorm, query_w, keys_w, values_w, outproj, midnorm, gates_w, upproj_w, downproj_w = full_layer
    (
        hidden,
        normed,
        inverse_a,
        attn_in,
        queries,
        keys_flat,
        values_flat,
        log_total,
        att_out,
        att_low,
        normed_mid,
        inverse_b,
        mlp_in,
        gate_raw,
        up_proj,
        inner_act,
    ) = saved
    cosine, sine, own_pos, pos_all = context
    rows_n, model_width = hidden.shape
    grad_low = grad_out.astype(jnp.bfloat16)
    grad_down = left_product(inner_act, grad_low)
    grad_inner = right_product(grad_low, downproj_w)
    sigma_gate = jax.nn.sigmoid(gate_raw)
    grad_gate = (grad_inner * up_proj * sigma_gate * (1.0 + gate_raw * (1.0 - sigma_gate))).astype(
        jnp.bfloat16
    )
    grad_up = (grad_inner * gate_raw * sigma_gate).astype(jnp.bfloat16)
    grad_gates = left_product(mlp_in, grad_gate)
    grad_upproj = left_product(mlp_in, grad_up)
    grad_mlp = right_product(grad_gate, gates_w) + right_product(grad_up, upproj_w)
    grad_midnorm = jnp.sum(grad_mlp * normed_mid, axis=0)
    grad_middle = grad_out + norm_back(
        grad_mlp * midnorm.astype(jnp.float32), normed_mid, inverse_b
    )
    branch_low = grad_middle.astype(jnp.bfloat16)
    grad_outproj = left_product(att_low, branch_low)
    grad_att = right_product(branch_low, outproj).astype(jnp.bfloat16).reshape(rows_n, HEADS, HD)
    row_delta = jnp.sum(grad_att.astype(jnp.float32) * att_out, axis=-1).T
    query_start = jnp.zeros((rows_n, HEADS, HD), jnp.float32)
    state_start = (query_start,)
    back_fn = make_back_step(queries, grad_att, log_total, row_delta, own_pos, pos_all)
    state_out = back_fn(
        state_start,
        (
            lax.all_gather(keys_flat, "ctx", axis=0, tiled=True),
            lax.all_gather(values_flat, "ctx", axis=0, tiled=True),
        ),
        jnp.int32(0),
    )
    grad_qr = state_out[0]
    stats_all = (
        lax.all_gather(log_total.T, "ctx", axis=0, tiled=True),
        lax.all_gather(row_delta.T, "ctx", axis=0, tiled=True),
    )
    query_fn = make_query_step(keys_flat, values_flat, own_pos, stats_all, pos_all, HEADS, HD)
    flat_start = jnp.zeros((rows_n, model_width), jnp.float32)
    grad_kr, grad_mix = query_fn(
        (flat_start, flat_start),
        (
            lax.all_gather(queries.reshape(rows_n, model_width), "ctx", axis=0, tiled=True),
            lax.all_gather(grad_att.reshape(rows_n, model_width), "ctx", axis=0, tiled=True),
        ),
        jnp.int32(0),
    )
    grad_query = unrotate(grad_qr, cosine, sine).reshape(rows_n, model_width).astype(jnp.bfloat16)
    grad_keys = (
        unrotate(grad_kr.reshape(rows_n, HEADS, HD), cosine, sine)
        .reshape(rows_n, model_width)
        .astype(jnp.bfloat16)
    )
    if is_second:
        grad_values = (0.5 * grad_mix).astype(jnp.bfloat16)
        passed_on = 0.5 * grad_mix
    else:
        grad_values = (grad_mix + value_extra).astype(jnp.bfloat16)
        passed_on = None
    grad_query_w = left_product(attn_in, grad_query)
    grad_keys_w = left_product(attn_in, grad_keys)
    grad_values_w = left_product(attn_in, grad_values)
    grad_attn = (
        right_product(grad_query, query_w)
        + right_product(grad_keys, keys_w)
        + right_product(grad_values, values_w)
    )
    grad_prenorm = jnp.sum(grad_attn * normed, axis=0)
    grad_hidden = grad_middle + norm_back(
        grad_attn * prenorm.astype(jnp.float32), normed, inverse_a
    )
    grad_terms = (
        grad_prenorm,
        grad_query_w,
        grad_keys_w,
        grad_values_w,
        grad_outproj,
        grad_midnorm,
        grad_gates,
        grad_upproj,
        grad_down,
    )
    return (grad_hidden, grad_terms, passed_on)


def local(
    tokens,
    cotangent,
    pair_of,
    prenorm_one,
    query_one,
    keys_one,
    values_one,
    outproj_one,
    midnorm_one,
    gates_one,
    upproj_one,
    downproj_one,
    prenorm_two,
    query_two,
    keys_two,
    values_two,
    outproj_two,
    midnorm_two,
    gates_two,
    upproj_two,
    downproj_two,
):
    seq_dev = tokens.shape[1]
    model_width = tokens.shape[2]
    pos_all = storage_positions(pair_of, seq_dev)
    own_pos = lax.dynamic_slice_in_dim(pos_all, lax.axis_index("ctx") * seq_dev, seq_dev, 0)
    cosine, sine = rope_tables(own_pos, HD)
    context = (cosine, sine, own_pos, pos_all)
    layer_shards = [
        (
            prenorm_one,
            query_one,
            keys_one,
            values_one,
            outproj_one,
            midnorm_one,
            gates_one,
            upproj_one,
            downproj_one,
        ),
        (
            prenorm_two,
            query_two,
            keys_two,
            values_two,
            outproj_two,
            midnorm_two,
            gates_two,
            upproj_two,
            downproj_two,
        ),
    ]
    hidden = tokens.reshape(seq_dev, model_width).astype(jnp.float32)
    first_values = None
    kept_full = []
    kept_saved = []
    for layer_no in range(2):
        full_layer = gather_forward(layer_shards[layer_no])
        hidden, values_raw, saved = forward_layer(hidden, full_layer, first_values, context)
        if layer_no == 0:
            first_values = values_raw
        kept_full.append(full_layer)
        kept_saved.append(saved)
    output = hidden.astype(jnp.bfloat16).reshape(1, seq_dev, model_width)
    grad_now = cotangent.reshape(seq_dev, model_width).astype(jnp.float32)
    value_extra = None
    layer_grads = [None, None]
    for layer_no in (1, 0):
        full_layer = kept_full[layer_no]
        grad_now, grad_terms, passed_on = backward_layer(
            grad_now, full_layer, kept_saved[layer_no], value_extra, layer_no == 1, context
        )
        if layer_no == 1:
            value_extra = passed_on
        layer_grads[layer_no] = scatter_grads(grad_terms)
    tokens_grad = grad_now.astype(jnp.bfloat16).reshape(1, seq_dev, model_width)
    first_grads = layer_grads[0]
    second_grads = layer_grads[1]
    return (
        output,
        tokens_grad,
        first_grads[0],
        first_grads[1],
        first_grads[2],
        first_grads[3],
        first_grads[4],
        first_grads[5],
        first_grads[6],
        first_grads[7],
        first_grads[8],
        second_grads[0],
        second_grads[1],
        second_grads[2],
        second_grads[3],
        second_grads[4],
        second_grads[5],
        second_grads[6],
        second_grads[7],
        second_grads[8],
    )


ROWS = 128
BF = jnp.bfloat16
F32 = jnp.float32
MESH = pl.DeviceIdType.MESH
VMEM_SPACE = pltpu.VMEM
HBM_SPACE = pltpu.HBM


def flip(value, weight):
    return value + weight * (1 - 2 * ((value // weight) % 2))


def to_device(f, c):
    return {"fsdp": f, "ctx": c}


def remote(src, dst, send_sem, recv_sem, target):
    return pltpu.make_async_remote_copy(
        src_ref=src,
        dst_ref=dst,
        send_sem=send_sem,
        recv_sem=recv_sem,
        device_id=to_device(*target),
        device_id_type=MESH,
    )


def arrived(ref, sem, target):
    remote(ref, ref, sem, sem, target).wait_recv()


def plane_place():
    f = lax.axis_index("fsdp")
    c = lax.axis_index("ctx")
    return f, c, (c // 2) % 2, c // 4


def row_peers(f, c, z):
    return [(f, c + 4 * ((z + i) % 4 - z)) for i in range(1, 4)]


HALF = ROWS // 2
ODD = 8


class Plane:
    def __init__(self, place, inner):
        f, c, y, z = place
        self.y, self.inner = y, inner
        self.mirrored = z // 2
        sign = 1 - 2 * self.mirrored
        self.own = 1 if inner else 0
        self.across = (f, flip(c, 2))
        self.chip_at = [(f, c + 4 * sign * (near - self.own)) for near in range(4)]
        self.sent = []

    def at(self, near):
        return near + self.mirrored * (3 - 2 * near)

    def slot(self, half, near):
        return 4 * half + self.at(near)

    def start(self, copy):
        copy.start()
        self.sent.append(copy)

    def finish(self):
        for copy in self.sent:
            copy.wait_send()


class Reduce(Plane):
    def __init__(self, place, inner, product, bufs, sems):
        super().__init__(place, inner)
        self.product = product
        self.sy, self.ry, self.acc, self.pb, self.su, self.sd, self.rb, self.ra = bufs
        self.ys, self.yr, self.us, self.ds, self.br, self.ar = sems

    def y_copy(self, slot):
        return remote(self.sy.at[slot], self.ry.at[slot], self.ys.at[slot], self.yr.at[slot], self.across)

    def got_y(self, slot):
        self.y_copy(slot).wait_recv()
        return self.ry[slot].astype(F32)

    def got(self, first, slot):
        buf, sem = (self.rb, self.br) if first else (self.ra, self.ar)
        arrived(buf.at[slot], sem.at[slot], self.across)
        return buf[slot].astype(F32)

    def pass_on(self, value, upward, slot, target, first, there=None):
        there = slot if there is None else there
        src, send = (self.su, self.us) if upward else (self.sd, self.ds)
        dst, sem = (self.rb, self.br) if first else (self.ra, self.ar)
        src[slot] = value.astype(BF)
        self.start(remote(src.at[slot], dst.at[there], send.at[slot], sem.at[there], self.chip_at[target]))

    def cross(self, slot, value):
        self.sy[slot] = value.astype(BF)
        self.start(self.y_copy(slot))

    def order(self, step):
        near = 3 - step
        if self.inner:
            near = jnp.where(step == 0, 3, jnp.where(step == 1, 0, 4 - step))
        return near, near + self.mirrored * (3 - 2 * near)

    def products(self):
        def other_row(step, carry):
            near, block = self.order(step)
            value = self.product(2 * block + 1 - self.y)
            self.sy[block] = value[:HALF].astype(BF)
            self.y_copy(block).start()
            self.pb[block] = value[HALF:]

            @pl.when((near == 1) | (near == 2))
            def _():
                self.sy[4 + block] = value[HALF:].astype(BF)
                self.y_copy(4 + block).start()

            return carry

        lax.fori_loop(0, 4, other_row, 0)
        for near in range(4):
            self.sent.append(self.y_copy(self.slot(0, near)))
        for near in (1, 2):
            self.sent.append(self.y_copy(self.slot(1, near)))
        if self.inner:
            self.pass_on(self.pb[self.at(3)], True, ODD, 3, True)
            self.pass_on(self.pb[self.at(0)], False, ODD, 0, False)
        else:
            self.pass_on(self.pb[self.at(3)], True, ODD, 3, False, ODD + 1)

        def own_row(step, carry):
            near, block = self.order(step)
            value = self.product(2 * block + self.y)
            self.acc[block] = value[:HALF]
            self.acc[4 + block] = value[HALF:]
            return carry

        lax.fori_loop(0, 4, own_row, 0)
        far = self.slot(1, 3)
        if self.inner:
            end = self.slot(1, 0)
            self.pass_on(self.acc[end], False, end, 0, False)
            self.pass_on(self.acc[far] + self.got(True, far), True, far, 3, True)
        else:
            self.pass_on(self.acc[far], True, far, 1, True)

    def relay(self, half, near):
        slot = self.slot(half, near)
        value = self.acc[slot] + self.got_y(slot)
        if not self.inner:
            self.pass_on(value, True, slot, 1, True)
        elif near == 0:
            self.pass_on(value, False, slot, 0, False)
        else:
            self.pass_on(value + self.got(True, slot), True, slot, near, near == 3)

    def relays(self):
        if self.inner:
            self.relay(0, 3)
            self.relay(0, 0)
            self.relay(0, 2)
            self.relay(1, 2)
            return
        self.relay(0, 3)
        self.relay(0, 2)
        self.relay(1, 2)
        odd = self.pb[self.at(0)] + self.got(False, ODD) + self.got(True, ODD) + self.got(False, ODD + 1)
        self.cross(self.slot(1, 0), odd)
        self.relay(0, 1)
        self.relay(1, 1)

    def own_sum(self, half):
        slot = self.slot(half, self.own)
        return self.acc[slot] + self.got_y(slot) + self.got(True, slot) + self.got(False, slot)


class Gather(Plane):
    def __init__(self, place, inner, full, sems):
        super().__init__(place, inner)
        self.full = full
        self.ys, self.yr, self.us, self.ds, self.zr = sems

    def rows(self, half, near, side):
        start = (self.at(near) * 2 + side) * ROWS + half * HALF
        return self.full.at[pl.ds(pl.multiple_of(start, HALF), HALF)]

    def to_row(self, part, sem, slot, target):
        self.start(remote(part, part, sem, self.zr.at[slot], self.chip_at[target]))

    def to_other_row(self, half, near):
        part = self.rows(half, near, self.y)
        slot = self.slot(half, near)
        self.start(remote(part, part, self.ys.at[slot], self.yr.at[slot], self.across))

    def send_own(self, half):
        part = self.rows(half, self.own, self.y)
        slot = self.slot(half, self.own)
        self.to_row(part, self.us.at[slot], slot, 2)
        self.to_row(part, self.ds.at[slot], slot, 0 if self.inner else 1)
        self.to_other_row(half, self.own)

    def take(self, half, near):
        part = self.rows(half, near, self.y)
        slot = self.slot(half, near)
        arrived(part, self.zr.at[slot], self.across)
        if self.inner and near in (2, 3):
            self.to_row(part, self.ds.at[slot], slot, 0)
        if half == 0 or near in (1, 2):
            self.to_other_row(half, near)

    def odd_slot(self, near):
        return ODD + self.at(near) // 3

    def take_odd(self, near):
        arrived(self.rows(1, near, 1 - self.y), self.zr.at[self.odd_slot(near)], self.across)

    def got_y(self, half, near):
        arrived(self.rows(half, near, 1 - self.y), self.yr.at[self.slot(half, near)], self.across)

    def forward(self, half):
        others = (0, 2, 3) if self.inner else (1, 2, 3)
        if half == 0:
            for near in others:
                self.take(0, near)
            return
        if not self.inner:
            self.got_y(1, 0)
            part = self.rows(1, 0, 1 - self.y)
            slot = self.odd_slot(0)
            self.to_row(part, self.us.at[8], slot, 3)
            self.to_row(part, self.us.at[9], slot, 2)
            self.to_row(part, self.ds.at[8], slot, 1)
        for near in others:
            self.take(1, near)
        if self.inner:
            self.take_odd(0)
        self.take_odd(3)
        for near in range(4):
            self.got_y(0, near)
        for near in (1, 2):
            self.got_y(1, near)


def both_kinds(place, run):
    z = place[3]

    @pl.when((z > 0) & (z < 3))
    def _():
        run(True)

    @pl.when((z == 0) | (z == 3))
    def _():
        run(False)


def exchange(place, product, settle, full, scratch, extra=None, rows=None):
    f, c, y, z = place
    if extra is None:
        greet(row_peers(f, c, z) + [(f, flip(c, 2))])
    else:
        peers, sibling, twin = chip_peers(f, c)
        greet(peers + [sibling, twin])
    own = (z * 2 + y) * ROWS
    if rows is not None:
        full[pl.ds(pl.multiple_of(own, ROWS), ROWS), :] = rows

    def run(inner):
        parts = []
        more = None if extra is None else extra(place)
        reduce = Reduce(place, inner, product, scratch[:8], scratch[8:14])
        reduce.products()
        if more is not None:
            more.first()
            more.early()
            parts.append(more)
        parts.append(reduce)
        if full is not None:
            gather = Gather(place, inner, full, scratch[14:19])
            parts.append(gather)
        reduce.relays()
        if rows is not None:
            gather.send_own(0)
            gather.send_own(1)
        if more is not None:
            more.second()
        for half in range(2):
            new = settle(half, reduce.own_sum(half))
            if full is not None and rows is None:
                full[pl.ds(pl.multiple_of(own + half * HALF, HALF), HALF), :] = new
                gather.send_own(half)
            if more is not None and half == 0:
                more.third()
        if full is not None:
            gather.forward(0)
        if more is not None:
            more.fourth()
        if full is not None:
            gather.forward(1)
        for part in parts:
            part.finish()

    both_kinds(place, run)


def half_rows(half):
    return pl.ds(half * HALF, HALF)


def norm_rows(hidden):
    return lax.rsqrt(jnp.mean(hidden * hidden, axis=-1, keepdims=True) + NORM_EPS)


def make_product(left_ref, right_ref, transposed, lanes=None):
    dims = (((1,), (1,)), ((), ())) if transposed else (((1,), (0,)), ((), ()))

    def product(block):
        rows = left_ref[pl.ds(pl.multiple_of(block * ROWS, ROWS), ROWS), :]
        right = right_ref[...] if lanes is None else right_ref[:, lanes[0] : lanes[1]]
        return lax.dot_general(rows, right, dims, preferred_element_type=F32)

    return product


def forward_kernel(row, left_ref, right_ref, res_ref, gain_ref, new_ref, full_ref, *scratch):
    def settle(half, total):
        hidden = res_ref[half_rows(half), :].astype(F32) + total
        new_ref[half_rows(half), :] = hidden
        return (hidden * norm_rows(hidden) * gain_ref[row : row + 1, :]).astype(BF)

    exchange(plane_place(), make_product(left_ref, right_ref, False), settle, full_ref, scratch)


def turn_kernel(left_ref, right_ref, res_ref, cot_ref, out_ref, full_ref, *scratch):
    def settle(half, total):
        out_ref[half_rows(half), :] = (res_ref[half_rows(half), :] + total).astype(BF)

    product = make_product(left_ref, right_ref, False)
    exchange(plane_place(), product, settle, full_ref, scratch, None, cot_ref[...])


def back_rows(total, grad, hidden, gain):
    inverse = norm_rows(hidden)
    normed = hidden * inverse
    scaled = total * gain
    mean = jnp.mean(scaled * normed, axis=-1, keepdims=True)
    return grad + inverse * (scaled - normed * mean)


def comm_call(kernel, outs, ident, args, gathers, name, more=()):
    width = 1024
    scratch = []
    for count, kind in ((8, BF), (8, BF), (8, F32), (4, F32), (9, BF), (9, BF), (9, BF), (10, BF)):
        scratch.append(pltpu.VMEM((count, HALF, width), kind))
    scratch += [pltpu.SemaphoreType.DMA((10,))] * 6
    if gathers:
        scratch += [pltpu.SemaphoreType.DMA((10,))] * 5
    scratch += list(more)
    spec = pl.BlockSpec(memory_space=VMEM_SPACE)
    return pl.pallas_call(
        kernel,
        out_shape=[jax.ShapeDtypeStruct(*o) for o in outs],
        in_specs=[spec] * len(args),
        out_specs=[spec] * len(outs),
        scratch_shapes=scratch,
        compiler_params=pltpu.CompilerParams(
            collective_id=ident, has_side_effects=True, vmem_limit_bytes=(24 if more else 14) * 1024 * 1024
        ),
        name=name,
    )(*args)


def chip_peers(f, c):
    chip, core = c // 2, c % 2
    return [(f, 2 * ((chip + i) % 8) + core) for i in range(1, 8)], (f, flip(c, 1)), (1 - f, c)


def greet(targets):
    barrier = pltpu.get_barrier_semaphore()
    for target in targets:
        pl.semaphore_signal(barrier, inc=1, device_id=to_device(*target), device_id_type=MESH)
    pl.semaphore_wait(barrier, len(targets))


class OutRows:
    def __init__(self, place, shard, out, sems):
        self.f, self.c, self.y, _ = place
        self.core = self.c % 2
        _, self.sibling, self.twin = chip_peers(self.f, self.c)
        self.near = (self.f, flip(self.c, 2))
        self.shard, self.out = shard, out
        self.ws, self.wr = sems
        self.home = self.y == self.f

    def near_copy(self):
        part = 2 * self.y + self.core
        return remote(self.shard, self.out.at[part], self.ws.at[0], self.wr.at[0], self.near)

    def pair_copies(self, first, target):
        parts = [self.out.at[self.core], self.out.at[2 + self.core]]
        return [
            remote(p, p, self.ws.at[first + n], self.wr.at[first + n], target) for n, p in enumerate(parts)
        ]

    def first(self):
        @pl.when(self.home)
        def _():
            self.out[2 * self.y + self.core] = self.shard[...]

        @pl.when(jnp.logical_not(self.home))
        def _():
            self.near_copy().start()

    def second(self):
        @pl.when(self.home)
        def _():
            self.near_copy().wait_recv()
            for copy in self.pair_copies(1, self.twin):
                copy.start()

    def third(self):
        @pl.when(jnp.logical_not(self.home))
        def _():
            for copy in self.pair_copies(1, self.twin):
                copy.wait_recv()

        for copy in self.pair_copies(3, self.sibling):
            copy.start()

    def finish(self):
        for copy in self.pair_copies(3, self.sibling):
            copy.wait()

        @pl.when(self.home)
        def _():
            for copy in self.pair_copies(1, self.twin):
                copy.wait_send()

        @pl.when(jnp.logical_not(self.home))
        def _():
            self.near_copy().wait_send()


class Sender:
    def __init__(self, place):
        self.f, self.c, self.y, _ = place
        self.chip, self.core = self.c // 2, self.c % 2
        self.peers, self.sibling, self.twin = chip_peers(self.f, self.c)
        self.sent = []

    def send(self, src, dst, send_sem, recv_sem, target):
        copy = remote(src, dst, send_sem, recv_sem, target)
        copy.start()
        self.sent.append(copy)
        return copy


class Spread(Sender):
    def __init__(self, place, a, r, sems):
        super().__init__(place)
        self.a, self.r = a, r
        self.ds, self.dr, self.xs, self.xr, self.ss, self.sr = sems
        self.direct, self.crossed, self.inner = {}, {}, []

    def forward(self, part, n):
        self.crossed[n] = self.send(part[0], part[1], self.xs.at[n], self.xr.at[n], self.twin)

    def to_sibling(self, part, n):
        self.inner.append(self.send(part[0], part[1], self.ss.at[n], self.sr.at[n], self.sibling))

    def first(self):
        mine = self.r.at[self.f, self.chip, self.core]
        own = self.a.at[self.chip]
        self.forward((own, mine), 0)
        for i in range(1, 8):
            t = (self.chip + i) % 8
            self.direct[i] = self.send(self.a.at[t], mine, self.ds.at[i], self.dr.at[i], self.peers[i - 1])
        self.r[self.f, self.chip, self.core] = self.a[self.chip]
        self.to_sibling((own, mine), 0)

    def second(self):
        for i in range(1, 8):
            self.direct[i].wait_recv()
            part = self.r.at[self.f, (self.chip + 8 - i) % 8, self.core]
            self.forward((part, part), i)
            self.to_sibling((part, part), i)

    def third(self):
        for i in range(8):
            self.crossed[i].wait_recv()
            part = self.r.at[1 - self.f, (self.chip + 8 - i) % 8, self.core]
            self.to_sibling((part, part), 8 + i)

    def finish(self):
        for copy in self.inner:
            copy.wait_recv()
        for copy in self.sent:
            copy.wait_send()


class Share(Sender):
    def __init__(self, place, tables, downs, out, sems):
        super().__init__(place)
        self.tables, self.downs = tables, downs
        self.xs, self.xr, self.ss, self.sr, *more = sems
        self.out = OutRows(place, *out, more) if out else None

    def places(self, f):
        found = [r.at[f, :, self.core] for _, r in self.tables]
        return found + [d.at[2 * f + self.core] for _, d in self.downs]

    def first(self):
        self.crossed, self.inner = [], []
        sources = [s for s, _ in self.tables] + [n for n, _ in self.downs]
        for n, (src, dst) in enumerate(zip(sources, self.places(self.f))):
            self.crossed.append(self.send(src, dst, self.xs.at[n], self.xr.at[n], self.twin))
            self.inner.append(self.send(src, dst, self.ss.at[n], self.sr.at[n], self.sibling))
        for src, r in self.tables:
            for j in range(8):
                r[self.f, j, self.core] = src[j]
        for src, d in self.downs:
            d[2 * self.f + self.core] = src[...]
        if self.out:
            self.out.first()

    def early(self):
        pass

    def second(self):
        if self.out:
            self.out.second()

    def third(self):
        pass

    def fourth(self):
        count = len(self.crossed)
        for n, part in enumerate(self.places(1 - self.f)):
            self.crossed[n].wait_recv()
            self.inner.append(
                self.send(part, part, self.ss.at[count + n], self.sr.at[count + n], self.sibling)
            )
        if self.out:
            self.out.third()

    def finish(self):
        for copy in self.inner:
            copy.wait_recv()
        for copy in self.sent:
            copy.wait_send()
        if self.out:
            self.out.finish()


def start_leg(parts, peers, chip, sends, receives):
    copies = []
    for n, (src, dst) in enumerate(parts):
        for i in range(1, 8):
            sem = 8 * n + i
            part = src.at[(chip + i) % 8]
            copies.append(remote(part, dst.at[chip], sends.at[sem], receives.at[sem], peers[i - 1]))
            copies[-1].start()
        dst[chip] = src[chip]
    return copies


def turn_row(row):
    size = row.shape[1]
    same = lax.broadcasted_iota(jnp.int32, (size, size), 0) == lax.broadcasted_iota(jnp.int32, (size, size), 1)
    return jnp.sum(jnp.where(same, row, 0.0), axis=1, keepdims=True)


def turn_column(column):
    size = column.shape[0]
    same = lax.broadcasted_iota(jnp.int32, (size, size), 0) == lax.broadcasted_iota(jnp.int32, (size, size), 1)
    return jnp.sum(jnp.where(same, column, 0.0), axis=0, keepdims=True)


def pack_heads(query, keys, values, a):
    for chip in range(8):
        pair = 4 * (chip % 2) + chip // 2
        for n, w in enumerate((query, keys, values)):
            a[chip, :, 128 * n : 128 * n + 128] = w[:, 128 * pair : 128 * pair + 128]


def pack_units(gates, upproj, block, a):
    rows, units = gates.shape
    each = units // 32
    empty = jnp.zeros((rows, block - each), F32)
    for chip in range(8):
        for n, w in enumerate((gates, upproj)):
            parts = []
            for i in range(4):
                owner = 16 * (i // 2) + 2 * chip + i % 2
                parts += [w[:, each * owner : each * owner + each].astype(F32), empty]
            at = 4 * block * n
            a[chip, :, at : at + 4 * block] = jnp.concatenate(parts, axis=-1).astype(BF)


def pack_down(down, dn):
    each = down.shape[0]
    dn[:each] = down[...]
    dn[each:] = jnp.zeros((dn.shape[0] - each, down.shape[1]), BF)


def begin_kernel(tok, *refs):
    given, (full, r, o, gains, u1, h2, u2, n1, n2), shards = refs[:18], refs[18:27], refs[27:45]
    ones, twos = shards[:9], shards[9:]
    loads, a, *sems = refs[45:]
    copies = [pltpu.make_async_copy(src, dst, loads.at[n]) for n, (src, dst) in enumerate(zip(given, shards))]
    soon = (0, 1, 2, 3, 4, 5, 9, 14)
    for n in soon:
        copies[n].start()
    for n in range(18):
        if n not in soon:
            copies[n].start()
    place = plane_place()
    f, c, y, z = place
    peers, sibling, twin = chip_peers(f, c)
    start = (z * 2 + y) * ROWS
    full[pl.ds(pl.multiple_of(start, ROWS), ROWS), :] = tok[...]
    for n in soon:
        copies[n].wait()
    pack_heads(ones[1], ones[2], ones[3], a)
    lane = lax.broadcasted_iota(jnp.int32, (tok.shape[1] // 32, 128), 1)
    riders = jnp.zeros(lane.shape, F32)
    for n, gain in enumerate((ones[0], ones[5], twos[0], twos[5])):
        riders = jnp.where(lane == n, turn_row(gain[...].astype(F32)), riders)
    for chip in range(8):
        a[chip, :, 384:] = riders.astype(BF)
    greet(peers + [sibling, twin])

    def run(inner):
        gather = Gather(place, inner, full, sems[:5])
        spread = Spread(place, a, r, sems[5:11])
        out = OutRows(place, ones[4], o, sems[11:])
        gather.send_own(0)
        spread.first()
        out.first()
        gather.send_own(1)
        for n in range(18):
            if n not in soon:
                copies[n].wait()
        pack_units(ones[6], ones[7], n1.shape[0], u1)
        pack_heads(twos[1], twos[2], twos[3], h2)
        pack_units(twos[6], twos[7], n1.shape[0], u2)
        pack_down(ones[8], n1)
        pack_down(twos[8], n2)
        gather.forward(0)
        spread.second()
        out.second()
        gather.forward(1)
        spread.third()
        out.third()
        gather.finish()
        spread.finish()
        out.finish()

    both_kinds(place, run)
    count = tok.shape[1]
    columns = r[:, :, :, :, 384:].reshape(count, 128)
    pick = lax.broadcasted_iota(jnp.int32, (8, 128), 0) == lax.broadcasted_iota(jnp.int32, (8, 128), 1)
    gains[...] = lax.dot_general(jnp.where(pick, 1.0, 0.0).astype(BF), columns, NT, preferred_element_type=F32)


def begin_call(tok, shards, block):
    rows, width = shards[1].shape
    spec = pl.BlockSpec(memory_space=VMEM_SPACE)
    wide = 8 * block
    outs = [
        ((8 * ROWS, width), BF), ((2, 8, 2, rows, 512), BF), ((4, rows, width), BF), ((8, width), F32),
        ((8, rows, wide), BF), ((8, rows, 384), BF), ((8, rows, wide), BF), ((block, width), BF), ((block, width), BF),
    ]
    counts = [(10,)] * 5 + [(8,), (8,), (8,), (8,), (16,), (16,), (5,), (5,)]
    return pl.pallas_call(
        begin_kernel,
        out_shape=[jax.ShapeDtypeStruct(*o) for o in outs],
        in_specs=[spec] + [pl.BlockSpec(memory_space=HBM_SPACE)] * 18,
        out_specs=[spec] * len(outs),
        scratch_shapes=[pltpu.VMEM(s.shape, s.dtype) for s in shards]
        + [pltpu.SemaphoreType.DMA((18,)), pltpu.VMEM((8, rows, 512), BF)]
        + [pltpu.SemaphoreType.DMA(n) for n in counts],
        compiler_params=pltpu.CompilerParams(
            collective_id=9, has_side_effects=True, vmem_limit_bytes=10 * 1024 * 1024
        ),
        name="begin",
    )(tok, *shards)


def middle_kernel(row, count, left_ref, right_ref, res_ref, gain_ref, *refs):
    given = 2 * count
    ins, refs = refs[:given], refs[given:]
    outs = 2 + count + 1 + (count == 2)
    new_ref, full_ref, *results = refs[:outs]
    scratch = refs[outs:]

    def settle(half, total):
        hidden = res_ref[half_rows(half), :].astype(F32) + total
        new_ref[half_rows(half), :] = hidden
        return (hidden * norm_rows(hidden) * gain_ref[row : row + 1, :]).astype(BF)

    def extra(place):
        tables = list(zip(ins[:count], results[:count]))
        downs = [(ins[count], results[count])]
        out = (ins[3], results[3]) if count == 2 else None
        return Share(place, tables, downs, out, scratch[19:])

    exchange(plane_place(), make_product(left_ref, right_ref, False), settle, full_ref, scratch, extra)


def share_shapes(rows, width, block, widths):
    outs = [((2, 8, 2, rows, w), BF) for w in widths] + [((4, block, width), BF)]
    if len(widths) == 2:
        outs += [((4, rows, width), BF)]
    return outs, [pltpu.SemaphoreType.DMA(n) for n in ((3,), (3,), (6,), (6,), (5,), (5,))]


class Collect:
    def __init__(self, place, ins, results, scratch, final):
        self.f, self.c, self.y, _ = place
        self.chip, self.core = self.c // 2, self.c % 2
        self.peers, self.sibling, self.twin = chip_peers(self.f, self.c)
        self.near = (self.f, flip(self.c, 2))
        self.final = final
        self.g, self.h = ins
        self.out, self.oh = results
        self.sb, self.xb, self.xt, self.ut, self.sh, self.xh, self.th, *near = scratch[:-6]
        self.ss, self.sr, self.xs, self.xr, self.ps, self.pr = scratch[-6:]
        self.crosses_near = bool(near)
        if near:
            self.yo, self.yt = near
        self.home = self.y == self.f

    def inner_copy(self, n):
        other = 1 - self.core
        if n == 2:
            src, dst = self.h.at[:, other], self.sh
        else:
            part = 8 * ((1 - self.f) if n == 0 else self.f)
            src, dst = self.g.at[pl.ds(part, 8), other], self.sb.at[pl.ds(part, 8)]
        return remote(src, dst, self.ss.at[n], self.sr.at[n], self.sibling)

    def target(self, i):
        return (self.chip + i + 1) % 8

    def cross_copy(self, i):
        t = self.target(i)
        return remote(self.xt.at[t], self.xb.at[t], self.xs.at[i], self.xr.at[i], self.twin)

    def direct_copy(self, i):
        src = self.ut.at[self.target(i)]
        return remote(src, self.out.at[self.chip], self.ps.at[i], self.pr.at[i], self.peers[i])

    def twin_copy(self):
        return remote(self.th, self.xh, self.xs.at[8], self.xr.at[8], self.twin)

    def near_copy(self):
        return remote(self.yt, self.yo, self.xs.at[9], self.xr.at[9], self.near)

    def first(self):
        for n in range(3):
            self.inner_copy(n).start()

    def early(self):
        f, core = self.f, self.core
        self.inner_copy(0).wait_recv()
        for i in range(8):
            t = self.target(i)
            at = (1 - f) * 8 + t
            self.xt[t] = (self.g[at, core].astype(F32) + self.sb[at].astype(F32)).astype(BF)
            self.cross_copy(i).start()
        self.inner_copy(2).wait_recv()
        if not self.crosses_near:
            self.th[...] = (self.h[1 - f, core].astype(F32) + self.sh[1 - f].astype(F32)).astype(BF)
            self.twin_copy().start()
            return
        for side in range(2):
            self.th[side] = (self.h[side, core].astype(F32) + self.sh[side].astype(F32)).astype(BF)

        @pl.when(jnp.logical_not(self.home))
        def _():
            self.twin_copy().start()

    def second(self):
        f, core = self.f, self.core
        self.inner_copy(1).wait_recv()
        for i in range(8):
            t = self.target(i)
            at = f * 8 + t
            self.cross_copy(i).wait_recv()
            total = self.g[at, core].astype(F32) + self.sb[at].astype(F32) + self.xb[t].astype(F32)
            if not self.final:
                self.out[t] = total.astype(BF)
            elif i < 7:
                self.ut[t] = total.astype(BF)
                self.direct_copy(i).start()
            else:
                self.out[self.chip] = total.astype(BF)
        if not self.crosses_near:
            self.twin_copy().wait_recv()
            self.oh[...] = self.h[f, core].astype(F32) + self.sh[f].astype(F32) + self.xh[...].astype(F32)
            return

        @pl.when(self.home)
        def _():
            self.twin_copy().wait_recv()
            y = self.y
            self.oh[...] = self.th[y].astype(F32) + self.xh[y].astype(F32)
            self.yt[...] = (self.th[1 - y].astype(F32) + self.xh[1 - y].astype(F32)).astype(BF)
            self.near_copy().start()

    def third(self):
        pass

    def fourth(self):
        pass

    def finish(self):
        if self.crosses_near:

            @pl.when(self.home)
            def _():
                self.near_copy().wait_send()

            @pl.when(jnp.logical_not(self.home))
            def _():
                self.near_copy().wait_recv()
                self.oh[...] = self.yo[...].astype(F32)
                self.twin_copy().wait_send()
        else:
            self.twin_copy().wait_send()
        for i in range(7 if self.final else 0):
            self.direct_copy(i).wait()
        for i in range(8):
            self.cross_copy(i).wait_send()
        for n in range(3):
            self.inner_copy(n).wait_send()


def collect_shapes(rows, wide, block, width, crosses_near):
    results = [((8, rows, wide), BF), ((block, width), F32)]
    buffers = [(16, rows, wide), (8, rows, wide), (8, rows, wide), (8, rows, wide), (2, block, width)]
    if crosses_near:
        buffers += [(2, block, width), (2, block, width), (block, width), (block, width)]
    else:
        buffers += [(block, width), (block, width)]
    counts = ((3,), (3,), (10,), (10,), (7,), (7,))
    scratch = [pltpu.VMEM(b, BF) for b in buffers] + [pltpu.SemaphoreType.DMA(n) for n in counts]
    return results, scratch


def back_kernel(gathers, row, crosses, left_ref, right_ref, grad_ref, hid_ref, gain_ref, g, h, new_ref, *refs):
    full_ref = refs[0] if gathers else None
    results, scratch = refs[gathers : gathers + 2], refs[gathers + 2 :]

    def settle(half, total):
        at = half_rows(half)
        new = back_rows(
            total, grad_ref[at, :].astype(F32), hid_ref[at, :].astype(F32), gain_ref[row : row + 1, :]
        )
        new_ref[at, :] = new.astype(new_ref.dtype)
        return new.astype(BF)

    def extra(place):
        return Collect(place, (g, h), results, scratch[14 + 5 * gathers :], not gathers)

    lanes = (0, 384) if crosses else None
    product = make_product(left_ref, right_ref, True, lanes)
    exchange(plane_place(), product, settle, full_ref, scratch, extra)


def head_lanes(head):
    lane = lax.broadcasted_iota(jnp.int32, (1, 128), 1)
    return lane // 64 == head


def swap_halves(values):
    lane = lax.broadcasted_iota(jnp.int32, (1, 128), 1)
    return jnp.where(lane % 64 < 32, pltpu.roll(values, 96, 1), pltpu.roll(values, 32, 1))


NT = (((1,), (1,)), ((), ()))
TN = (((0,), (0,)), ((), ()))


def two_blocks(ref, tile, half):
    first = pl.multiple_of(2 * tile * ROWS + half * HALF, HALF)
    second = pl.multiple_of((2 * tile + 1) * ROWS + half * HALF, HALF)
    return jnp.concatenate([ref[pl.ds(first, HALF), :], ref[pl.ds(second, HALF), :]], axis=0)


def put_blocks(ref, tile, half, value):
    first = pl.multiple_of(2 * tile * ROWS + half * HALF, HALF)
    second = pl.multiple_of((2 * tile + 1) * ROWS + half * HALF, HALF)
    ref[pl.ds(first, HALF), :] = value[:HALF]
    ref[pl.ds(second, HALF), :] = value[HALF:]


def attend_kernel(layer, *refs):
    x_ref, w_ref, cos_ref, sin_ref, more_ref, pq_ref, pk_ref = refs[:7]
    count = 2 - layer
    tables, refs = refs[7 : 7 + count], refs[7 + count :]
    q_ref, k_ref, v_ref, att_ref, lse_ref = refs[:5]
    kept = refs[5:7]
    placed = refs[-4 - count : -4]
    sends, receives, ss, sr = refs[-4:]
    f, c, _, _ = plane_place()
    peers, sibling, _ = chip_peers(f, c)
    rows_n = x_ref.shape[0]
    half_n = rows_n // 2
    greet(peers + [sibling])
    leg = start_leg(list(zip(tables, placed)), peers, c // 2, sends, receives)

    def copies(i):
        here = pl.ds(pl.multiple_of(i * HALF, HALF), HALF)
        there = pl.ds(pl.multiple_of(half_n + i * HALF, HALF), HALF)
        return [
            remote(ref.at[h, here], ref.at[h, there], ss.at[4 * i + n], sr.at[4 * i + n], sibling)
            for n, (ref, h) in enumerate(((k_ref, 0), (k_ref, 1), (v_ref, 0), (v_ref, 1)))
        ]

    def step(i, carry):
        at = pl.ds(pl.multiple_of(i * ROWS, ROWS), ROWS)
        here = pl.ds(pl.multiple_of(i * HALF, HALF), HALF)
        rows = x_ref[at, :]
        if layer == 0:
            wide = rows.astype(F32)
            rows = (wide * norm_rows(wide) * more_ref[:1, :]).astype(BF)
            kept[0][at, :] = rows
        raw = jnp.dot(rows, w_ref[:, :384], preferred_element_type=F32)
        cosine, sine = cos_ref[at, :], sin_ref[at, :]
        q, k, v = raw[:, :128], raw[:, 128:256], raw[:, 256:]
        q_ref[at, :] = (q * cosine + swap_halves(q) * sine).astype(BF)
        k = (k * cosine + swap_halves(k) * sine).astype(BF)
        if layer == 0:
            kept[1][at, :] = v
        else:
            v = 0.5 * v + 0.5 * more_ref[at, :]
        v = v.astype(BF)
        for half in range(2):
            k_ref[half, here, :] = k[half * HALF : (half + 1) * HALF]
            v_ref[half, here, :] = v[half * HALF : (half + 1) * HALF]
        for copy in copies(i):
            copy.start()
        return carry

    lax.fori_loop(0, rows_n // ROWS, step, 0)
    for i in range(rows_n // ROWS):
        for copy in copies(i):
            copy.wait()

    def tile_step(tile, carry):
        for late in range(2):
            number = tile + late * (rows_n // (2 * ROWS))
            queries = two_blocks(q_ref, tile, late) * jnp.asarray(HD ** (-0.5), BF)
            allowed = pk_ref[late : late + 1, :] <= turn_row(pq_ref[pl.ds(number, 1), :])
            parts = []
            for head in range(2):
                masked = jnp.where(head_lanes(head), queries, jnp.zeros_like(queries))
                scores = lax.dot_general(masked, k_ref[late], NT, preferred_element_type=F32)
                scores = jnp.where(allowed, scores, NEG_FILL)
                top = jnp.max(scores, axis=-1, keepdims=True)
                if late:
                    early = lax.dot_general(masked, k_ref[0], NT, preferred_element_type=F32)
                    top = jnp.maximum(top, jnp.max(early, axis=-1, keepdims=True))
                shares = jnp.exp(scores - top)
                total = jnp.sum(shares, axis=-1, keepdims=True)
                mixed = jnp.dot(shares.astype(BF), v_ref[late], preferred_element_type=F32)
                if late:
                    shares = jnp.exp(early - top)
                    total += jnp.sum(shares, axis=-1, keepdims=True)
                    mixed += jnp.dot(shares.astype(BF), v_ref[0], preferred_element_type=F32)
                lse_ref[number, head : head + 1, :] = turn_column(top + jnp.log(total))
                parts.append(mixed / total)
            put_blocks(att_ref, tile, late, jnp.where(head_lanes(0), parts[0], parts[1]).astype(BF))
        return carry

    lax.fori_loop(0, rows_n // (2 * ROWS), tile_step, 0)
    for copy in leg:
        copy.wait()


def attend(layer, *args):
    rows_n = args[0].shape[0]
    spec = pl.BlockSpec(memory_space=VMEM_SPACE)
    outs = [((rows_n, 128), BF), ((2, rows_n, 128), BF), ((2, rows_n, 128), BF), ((rows_n, 128), BF)]
    outs += [((rows_n // ROWS, 2, ROWS), F32)]
    count = 4 * (rows_n // ROWS)
    sems = [pltpu.SemaphoreType.DMA((count,))] * 2
    if layer == 0:
        outs += [(args[0].shape, BF), ((rows_n, 128), F32)]
    outs += [(p.shape, BF) for p in args[7:]]
    sems = [pltpu.SemaphoreType.DMA((16,))] * 2 + sems
    return pl.pallas_call(
        functools.partial(attend_kernel, layer),
        out_shape=[jax.ShapeDtypeStruct(*o) for o in outs],
        in_specs=[spec] * len(args),
        out_specs=[spec] * len(outs),
        scratch_shapes=sems,
        compiler_params=pltpu.CompilerParams(
            collective_id=10 + layer, has_side_effects=True, vmem_limit_bytes=16 * 1024 * 1024
        ),
        name="attend",
    )(*args)


def attend_back_kernel(layer, *refs):
    q_ref, k_ref, v_ref, full_ref, out_ref, att_ref, lse_ref, pq_ref, pk_ref, cos_ref, sin_ref, more_ref = refs[:12]
    count = 2 - layer
    tables, refs = refs[12 : 12 + count], refs[12 + count :]
    three_ref, dw_ref, *placed = refs[: 2 + count]
    pkc, dq, dk, dv, dw, sb, rb, ss, sr, sends, receives = refs[-11:]
    place = plane_place()
    f, c, _, _ = place
    peers, sibling, _ = chip_peers(f, c)
    greet(peers + [sibling])
    leg = start_leg(list(zip(tables, placed)), peers, c // 2, sends, receives)
    rows_n = q_ref.shape[0]
    half_n = rows_n // 2
    dk[...] = jnp.zeros_like(dk)
    dv[...] = jnp.zeros_like(dv)
    dw[...] = jnp.zeros_like(dw)
    for late in range(2):
        for i in range(rows_n // ROWS):
            at = slice(i * ROWS, (i + 1) * ROWS)
            pkc[late, at, :] = turn_row(pk_ref[late : late + 1, at])

    def tile_step(tile, carry):
        for late in range(2):
            number = tile + late * (rows_n // (2 * ROWS))
            queries = two_blocks(q_ref, tile, late) * jnp.asarray(HD ** (-0.5), BF)
            full = two_blocks(full_ref, tile, late)
            grads = lax.dot_general(full, out_ref[...], NT, preferred_element_type=F32).astype(BF)
            dw[...] += lax.dot_general(two_blocks(att_ref, tile, late), full, TN, preferred_element_type=F32)
            allowed = pkc[late] <= pq_ref[pl.ds(number, 1), :]
            parts = []
            for head in range(2):
                masked = jnp.where(head_lanes(head), queries, jnp.zeros_like(queries))
                grad_h = jnp.where(head_lanes(head), grads, jnp.zeros_like(grads))
                lse = lse_ref[number, head : head + 1, :]
                kinds = (1, 0) if late else (0,)
                shares, grad_shares = [], []
                delta = jnp.zeros((1, ROWS), F32)
                for kind in kinds:
                    part = jnp.exp(lax.dot_general(k_ref[kind], masked, NT, preferred_element_type=F32) - lse)
                    if kind == late:
                        part = jnp.where(allowed, part, 0.0)
                    grad = lax.dot_general(v_ref[kind], grad_h, NT, preferred_element_type=F32)
                    delta += jnp.sum(part * grad, axis=0, keepdims=True)
                    shares.append(part)
                    grad_shares.append(grad)
                found = jnp.zeros((ROWS, 128), F32)
                for kind, part, grad in zip(kinds, shares, grad_shares):
                    grad_scores = (part * (grad - delta)).astype(BF)
                    dv[kind] += jnp.dot(part.astype(BF), grad_h, preferred_element_type=F32)
                    dk[kind] += jnp.dot(grad_scores, masked, preferred_element_type=F32)
                    found += lax.dot_general(grad_scores, k_ref[kind], TN, preferred_element_type=F32)
                parts.append(found)
            put_blocks(dq, tile, late, jnp.where(head_lanes(0), parts[0], parts[1]) * HD ** (-0.5))
        return carry

    lax.fori_loop(0, rows_n // (2 * ROWS), tile_step, 0)
    copies = []
    for n, ref in enumerate((dk, dv)):
        sb[n] = ref[:, half_n:, :].astype(BF)
        copies.append(remote(sb.at[n], rb.at[n], ss.at[n], sr.at[n], sibling))
        copies[n].start()
    dw_ref[...] = dw[...].astype(BF)
    for copy in copies:
        copy.wait()

    def rows_of(n, ref, i):
        here = pl.ds(pl.multiple_of(i * HALF, HALF), HALF)
        return jnp.concatenate([ref[half, here, :] + rb[n, half, here, :].astype(F32) for half in range(2)], axis=0)

    def turn(i, carry):
        at = pl.ds(pl.multiple_of(i * ROWS, ROWS), ROWS)
        cosine, sine = cos_ref[at, :], sin_ref[at, :]
        for n, grad in enumerate((dq[at, :], rows_of(0, dk, i))):
            three_ref[at, 128 * n : 128 * n + 128] = (grad * cosine - swap_halves(grad) * sine).astype(BF)
        grad = rows_of(1, dv, i)
        if layer == 1:
            grad = 0.5 * grad
            refs[2 + count][at, :] = grad
        else:
            grad = grad + more_ref[at, :]
        three_ref[at, 256:] = grad.astype(BF)
        return carry

    lax.fori_loop(0, rows_n // ROWS, turn, 0)
    for copy in leg:
        copy.wait()


def attend_backward(layer, *args):
    rows_n, width = args[3].shape
    spec = pl.BlockSpec(memory_space=VMEM_SPACE)
    outs = [((rows_n, 384), BF), ((128, width), BF)] + [(u.shape, BF) for u in args[12:]]
    if layer == 1:
        outs += [((rows_n, 128), F32)]
    return pl.pallas_call(
        functools.partial(attend_back_kernel, layer),
        out_shape=[jax.ShapeDtypeStruct(*o) for o in outs],
        in_specs=[spec] * len(args),
        out_specs=[spec] * len(outs),
        scratch_shapes=[
            pltpu.VMEM((2, rows_n, 1), F32),
            pltpu.VMEM((rows_n, 128), F32),
            pltpu.VMEM((2, rows_n, 128), F32),
            pltpu.VMEM((2, rows_n, 128), F32),
            pltpu.VMEM((128, width), F32),
            pltpu.VMEM((2, 2, rows_n // 2, 128), BF),
            pltpu.VMEM((2, 2, rows_n // 2, 128), BF),
            pltpu.SemaphoreType.DMA((2,)),
            pltpu.SemaphoreType.DMA((2,)),
            pltpu.SemaphoreType.DMA((16,)),
            pltpu.SemaphoreType.DMA((16,)),
        ],
        compiler_params=pltpu.CompilerParams(
            collective_id=12 + layer, has_side_effects=True, vmem_limit_bytes=32 * 1024 * 1024
        ),
        name="attend_back",
    )(*args)


def unpack_kernel(*every):
    every[24][...] = every[0][...]
    every[25][...] = every[1][...]
    refs = every[2:24] + every[26:]
    for l in range(2):
        cu, od, cq, oo, pre, query, keys, values, mid, gates, upproj = refs[11 * l : 11 * l + 11]
        g_pre, gq, gk, gv, g_out, g_mid, gg, gu, g_down = refs[22 + 9 * l : 31 + 9 * l]
        rows, units = gates.shape
        each = units // 32
        block = cu.shape[2] // 8
        total = jnp.zeros((rows, 1), F32)
        for chip in range(8):
            pair = 4 * (chip % 2) + chip // 2
            for n, (w, g) in enumerate(((query, gq), (keys, gk), (values, gv))):
                at = slice(128 * pair, 128 * pair + 128)
                part = cq[chip, :, 128 * n : 128 * n + 128].astype(F32)
                g[:, at] = part
                total += jnp.sum(part * w[:, at].astype(F32), axis=-1, keepdims=True)
        g_pre[...] = turn_column(total) / pre[...].astype(F32)
        for n, g in enumerate((gg, gu)):
            for chip in range(8):
                wide = cu[chip, :, 4 * block * n : 4 * block * (n + 1)].astype(F32)
                for i in range(4):
                    owner = 16 * (i // 2) + 2 * chip + i % 2
                    g[:, each * owner : each * owner + each] = wide[:, block * i : block * i + each]
        both = gg[...] * gates[...].astype(F32) + gu[...] * upproj[...].astype(F32)
        g_mid[...] = turn_column(jnp.sum(both, axis=-1, keepdims=True)) / mid[...].astype(F32)
        g_out[...] = oo[...]
        g_down[...] = od[: g_down.shape[0], :]


def unpack(output, tokens_grad, collected, layers):
    args, outs = [output, tokens_grad], [(output.shape, BF), (tokens_grad.shape, BF)]
    for l, layer in enumerate(layers):
        pre, query, keys, values, out, mid, gates, upproj, down = layer
        args += [*collected[l], pre, query, keys, values, mid, gates, upproj]
        for w in layer:
            outs.append((w.shape, F32))
    spec = pl.BlockSpec(memory_space=VMEM_SPACE)
    found = pl.pallas_call(
        unpack_kernel,
        out_shape=[jax.ShapeDtypeStruct(*o) for o in outs],
        in_specs=[spec] * len(args),
        out_specs=[spec] * len(outs),
        compiler_params=pltpu.CompilerParams(vmem_limit_bytes=60 * 1024 * 1024),
        name="unpack",
    )(*args)
    return [g[0] if g.shape[0] == 1 else g for g in found]


def fast_local(tokens, cotangent, pair_of, *shards):
    width = tokens.shape[2]
    rows_each, units = shards[6].shape
    each = units // 32
    block = (each + 2 + 31) // 32 * 32
    hidden_pad = 4 * block
    wide = 384 + 2 * hidden_pad
    core = lax.axis_index("ctx") % 2
    pos_all = storage_positions(pair_of, ROWS).reshape(8, 2, ROWS)
    own_pos = lax.dynamic_index_in_dim(pos_all, core, 1, False).reshape(-1)
    sib_pos = lax.dynamic_index_in_dim(pos_all, 1 - core, 1, False).reshape(-1)
    own_split = own_pos.reshape(8, 2, HALF).transpose(1, 0, 2)
    sib_split = sib_pos.reshape(8, 2, HALF).transpose(1, 0, 2)
    pos_q = own_split.reshape(8, ROWS).astype(F32)
    pos_k = jnp.concatenate([own_split, sib_split], axis=1).reshape(2, -1).astype(F32)
    cosine, sine = rope_tables(own_pos, HD)
    cosine = jnp.concatenate([cosine] * 4, axis=-1)
    sine = jnp.concatenate([-sine, sine, -sine, sine], axis=-1)

    shards = [s[None, :] if s.ndim == 1 else s for s in shards]
    layers = [shards[:9], shards[9:]]
    tok = tokens.reshape(ROWS, width)
    cot = cotangent.reshape(ROWS, width)

    full, heads, out_rows, gains, units_one, heads_two, units_two, *downs = begin_call(tok, shards, block)
    heads_w = [heads.reshape(32 * rows_each, 512), None]
    units_w, down_w, out_w = [None, None], [None, None], [out_rows.reshape(4 * rows_each, width), None]

    plane = 8 * ROWS
    full_type = ((plane, width), BF)
    rows_type = ((ROWS, width), F32)
    saved = []
    hidden = tok
    first_values = None
    for layer in range(2):
        args = (full, heads_w[layer], cosine, sine, gains if layer == 0 else first_values, pos_q, pos_k)
        x_full = full
        if layer == 0:
            q, k, v, att, lse, x_full, first_values, *legs = attend(0, *args, units_one, heads_two)
            widths, more = (2 * hidden_pad, 384), (downs[0], layers[1][4])
        else:
            q, k, v, att, lse, *legs = attend(1, *args, units_two)
            widths, more = (2 * hidden_pad,), (downs[1],)
        outs, sems = share_shapes(rows_each, width, block, widths)
        middle, mlp_full, table, *found = comm_call(
            functools.partial(middle_kernel, 2 * layer + 1, len(widths)), [rows_type, full_type] + outs, 1 + layer,
            (att, out_w[layer], hidden, gains, *legs, *more), True, "middle", sems,
        )
        units_w[layer] = table.reshape(32 * rows_each, 2 * hidden_pad)
        if layer == 0:
            heads_w[1] = found[0].reshape(32 * rows_each, 384)
            down_w[0] = found[1].reshape(hidden_pad, width)
            out_w[1] = found[2].reshape(4 * rows_each, width)
        else:
            down_w[1] = found[0].reshape(hidden_pad, width)
        both = jnp.dot(mlp_full, units_w[layer], preferred_element_type=F32)
        gate, up = both[:, :hidden_pad], both[:, hidden_pad:]
        inner = (jax.nn.silu(gate) * up).astype(BF)
        saved.append((x_full, q, k, v, lse, att, mlp_full, gate, up, inner, hidden, middle))
        if layer == 0:
            hidden, full = comm_call(
                functools.partial(forward_kernel, 2), [rows_type, full_type], 3,
                (inner, down_w[layer], middle, gains), True, "result",
            )
        else:
            output, full = comm_call(
                turn_kernel, [((ROWS, width), BF), full_type], 4,
                (inner, down_w[layer], middle, cot), True, "turn",
            )
    grad = cot
    passed = cosine
    collected = [None, None]
    for layer in (1, 0):
        x_full, q, k, v, lse, att, mlp_full, gate, up, inner, hidden, middle = saved[layer]
        grad_down = left_product(inner, full)
        grad_inner = right_product(full, down_w[layer])
        sigma = jax.nn.sigmoid(gate)
        grad_gate = (grad_inner * up * sigma * (1.0 + gate * (1.0 - sigma))).astype(BF)
        grad_up = (grad_inner * gate * sigma).astype(BF)
        both = jnp.concatenate([grad_gate, grad_up], axis=-1)
        grad_upw = left_product(mlp_full, both)
        results, more = collect_shapes(rows_each, 2 * hidden_pad, block, width, False)
        grad_mid, full, units_sum, got_down = comm_call(
            functools.partial(back_kernel, 1, 2 * layer + 1, False), [rows_type, full_type] + results, 5 + layer,
            (
                both, units_w[layer], grad, middle, gains,
                grad_upw.astype(BF).reshape(16, 2, rows_each, 2 * hidden_pad),
                grad_down.astype(BF).reshape(2, 2, block, width),
            ),
            True, "middle_back", more,
        )
        legs = (units_sum,) if layer == 1 else (units_sum, heads_sum)
        three, grad_out, got_units, *kept = attend_backward(
            layer, q, k, v, full, out_w[layer], att, lse, pos_q, pos_k, cosine, sine, passed, *legs
        )
        collected[layer] = [got_units, got_down]
        if layer == 1:
            (passed,) = kept
        else:
            collected[1] += [kept[0], two_out]
        grad_qkv = left_product(x_full, three)
        results, more = collect_shapes(rows_each, 384, rows_each, width, True)
        args = (
            three, heads_w[layer], grad_mid, hidden, gains,
            grad_qkv.astype(BF).reshape(16, 2, rows_each, 384),
            grad_out.reshape(2, 2, rows_each, width),
        )
        if layer == 1:
            grad, full, heads_sum, two_out = comm_call(
                functools.partial(back_kernel, 1, 2, True), [rows_type, full_type] + results, 7, args, True,
                "layer_back", more,
            )
        else:
            tokens_grad, *got_heads = comm_call(
                functools.partial(back_kernel, 0, 0, True), [((ROWS, width), BF)] + results, 8, args, False,
                "last_back", more,
            )
            collected[0] += got_heads
    output, tokens_grad, *found = unpack(output, tokens_grad, collected, layers)
    return (output.reshape(1, ROWS, width), tokens_grad.reshape(1, ROWS, width), *found)


def solution(mesh):
    placed = (
        P("fsdp", "ctx", None),
        P("fsdp", "ctx", None),
        P(),
        P(("fsdp", "ctx")),
        P(("fsdp", "ctx"), None),
        P(("fsdp", "ctx"), None),
        P(("fsdp", "ctx"), None),
        P(("fsdp", "ctx"), None),
        P(("fsdp", "ctx")),
        P(("fsdp", "ctx"), None),
        P(("fsdp", "ctx"), None),
        P(("fsdp", "ctx"), None),
        P(("fsdp", "ctx")),
        P(("fsdp", "ctx"), None),
        P(("fsdp", "ctx"), None),
        P(("fsdp", "ctx"), None),
        P(("fsdp", "ctx"), None),
        P(("fsdp", "ctx")),
        P(("fsdp", "ctx"), None),
        P(("fsdp", "ctx"), None),
        P(("fsdp", "ctx"), None),
    )
    fits = mesh.shape["ctx"] == HEADS and mesh.shape["fsdp"] == 2
    return jax.shard_map(
        fast_local if fits else local,
        mesh=mesh,
        in_specs=placed,
        out_specs=(
            P("fsdp", "ctx", None),
            P("fsdp", "ctx", None),
            P(("fsdp", "ctx")),
            P(("fsdp", "ctx"), None),
            P(("fsdp", "ctx"), None),
            P(("fsdp", "ctx"), None),
            P(("fsdp", "ctx"), None),
            P(("fsdp", "ctx")),
            P(("fsdp", "ctx"), None),
            P(("fsdp", "ctx"), None),
            P(("fsdp", "ctx"), None),
            P(("fsdp", "ctx")),
            P(("fsdp", "ctx"), None),
            P(("fsdp", "ctx"), None),
            P(("fsdp", "ctx"), None),
            P(("fsdp", "ctx"), None),
            P(("fsdp", "ctx")),
            P(("fsdp", "ctx"), None),
            P(("fsdp", "ctx"), None),
            P(("fsdp", "ctx"), None),
        ),
        check_vma=False,
    )
```

```python
import functools
import math

import jax
import jax.numpy as jnp
from jax import lax
from jax.experimental import pallas as pl
from jax.experimental.pallas import tpu as pltpu
from jax.sharding import PartitionSpec as P

HEADS = 16
HD = 64


NORM_EPS = 1e-05
NEG_FILL = -1e30


def block_size(total_rows):
    size_now = 512
    while total_rows % size_now:
        size_now //= 2
    return size_now


def row_norm(hidden):
    inverse = lax.rsqrt(jnp.mean(hidden * hidden, axis=-1, keepdims=True) + NORM_EPS)
    return (hidden * inverse, inverse)


def norm_back(grad_normed, normed, inverse):
    return inverse * (grad_normed - normed * jnp.mean(grad_normed * normed, axis=-1, keepdims=True))


def rope_tables(positions, head_size):
    half_size = head_size // 2
    freqs = jnp.exp(
        jnp.arange(half_size, dtype=jnp.float32) * (-2.0 * math.log(10000.0) / head_size)
    )
    angles = positions.astype(jnp.float32)[:, None] * freqs[None, :]
    return (jnp.cos(angles), jnp.sin(angles))


def rotate(values_in, cosine, sine):
    half_size = values_in.shape[-1] // 2
    first_half = values_in[..., :half_size]
    second_half = values_in[..., half_size:]
    cos_rows = cosine[:, None, :]
    sin_rows = sine[:, None, :]
    return jnp.concatenate(
        [
            first_half * cos_rows - second_half * sin_rows,
            second_half * cos_rows + first_half * sin_rows,
        ],
        axis=-1,
    )


def unrotate(grads_in, cosine, sine):
    half_size = grads_in.shape[-1] // 2
    first_half = grads_in[..., :half_size]
    second_half = grads_in[..., half_size:]
    cos_rows = cosine[:, None, :]
    sin_rows = sine[:, None, :]
    return jnp.concatenate(
        [
            first_half * cos_rows + second_half * sin_rows,
            second_half * cos_rows - first_half * sin_rows,
        ],
        axis=-1,
    )


def left_product(left, right):
    return lax.dot_general(
        left, right, (((0,), (0,)), ((), ())), preferred_element_type=jnp.float32
    )


def right_product(left, right):
    return lax.dot_general(
        left, right, (((1,), (1,)), ((), ())), preferred_element_type=jnp.float32
    )


def storage_positions(pair_of, seq_dev):
    devices = pair_of.shape[0]
    rows_all = jnp.arange(devices * seq_dev, dtype=jnp.int32)
    owner = rows_all // seq_dev
    local_row = rows_all % seq_dev
    half_rows = seq_dev // 2
    picked = jnp.sum(
        jnp.where(
            owner[:, None] == jnp.arange(devices, dtype=jnp.int32)[None, :], pair_of[None, :], 0
        ),
        axis=1,
    )
    block_id = jnp.where(local_row < half_rows, picked, 2 * devices - 1 - picked)
    return block_id * half_rows + local_row % half_rows


def head_scores(queries, keys_flat, query_pos, key_pos):
    key_heads = keys_flat.reshape(keys_flat.shape[0], queries.shape[1], queries.shape[2])
    scores = jnp.einsum(
        "qhd,khd->hqk", queries, key_heads, preferred_element_type=jnp.float32
    ) * queries.shape[2] ** (-0.5)
    allowed = (key_pos[None, :] <= query_pos[:, None])[None]
    return (jnp.where(allowed, scores, NEG_FILL), allowed)


def make_stats_step(queries, query_pos, pos_all, state_in, key_part):
    size_now = block_size(key_part.shape[0])

    def inner_step(block_no, state_now):
        top_now, total_now = state_now
        offset = block_no * size_now
        key_block = lax.dynamic_slice_in_dim(key_part, offset, size_now, 0)
        key_pos = lax.dynamic_slice_in_dim(pos_all, offset, size_now, 0)
        scores, allowed = head_scores(queries, key_block, query_pos, key_pos)
        new_top = jnp.maximum(top_now, jnp.max(scores, axis=-1))
        total_now = total_now * jnp.exp(top_now - new_top) + jnp.sum(
            jnp.where(allowed, jnp.exp(scores - new_top[..., None]), 0.0), axis=-1
        )
        return (new_top, total_now)

    return lax.fori_loop(0, key_part.shape[0] // size_now, inner_step, state_in)


def make_value_step(queries, log_total, query_pos, pos_all, acc_in, pieces):
    key_part, value_part = pieces
    size_now = block_size(key_part.shape[0])

    def inner_step(block_no, acc_now):
        offset = block_no * size_now
        key_block = lax.dynamic_slice_in_dim(key_part, offset, size_now, 0)
        value_block = lax.dynamic_slice_in_dim(value_part, offset, size_now, 0)
        key_pos = lax.dynamic_slice_in_dim(pos_all, offset, size_now, 0)
        scores, allowed = head_scores(queries, key_block, query_pos, key_pos)
        shares = jnp.exp(scores - log_total[..., None]).astype(jnp.bfloat16)
        value_heads = value_block.reshape(size_now, queries.shape[1], queries.shape[2])
        return acc_now + jnp.einsum(
            "hqk,khd->qhd", shares, value_heads, preferred_element_type=jnp.float32
        )

    return lax.fori_loop(0, key_part.shape[0] // size_now, inner_step, acc_in)


def make_back_step(queries, grad_att, log_total, row_delta, query_pos, pos_all):
    scale_now = queries.shape[2] ** (-0.5)

    def back_step(state_in, pieces, start_row):
        key_part, value_part = pieces
        size_now = block_size(key_part.shape[0])

        def inner_step(block_no, state_now):
            offset = block_no * size_now
            key_block = lax.dynamic_slice_in_dim(key_part, offset, size_now, 0)
            value_block = lax.dynamic_slice_in_dim(value_part, offset, size_now, 0)
            key_pos = lax.dynamic_slice_in_dim(pos_all, offset, size_now, 0)
            scores, allowed = head_scores(queries, key_block, query_pos, key_pos)
            shares = jnp.exp(scores - log_total[..., None])
            value_heads = value_block.reshape(size_now, queries.shape[1], queries.shape[2])
            key_heads = key_block.reshape(size_now, queries.shape[1], queries.shape[2])
            grad_shares = jnp.einsum(
                "qhd,khd->hqk", grad_att, value_heads, preferred_element_type=jnp.float32
            )
            grad_scores = (shares * (grad_shares - row_delta[..., None]) * scale_now).astype(
                jnp.bfloat16
            )
            grad_query = state_now[0] + jnp.einsum(
                "hqk,khd->qhd", grad_scores, key_heads, preferred_element_type=jnp.float32
            )
            return (grad_query,)

        return lax.fori_loop(0, key_part.shape[0] // size_now, inner_step, state_in)

    return back_step


def make_query_step(own_keys, own_values, own_pos, stats_all, pos_all, head_count, head_size):
    scale_now = head_size ** (-0.5)
    value_heads = own_values.reshape(own_values.shape[0], head_count, head_size)

    def query_step(state_in, pieces, start_row):
        query_part, grad_part = pieces
        size_now = block_size(query_part.shape[0])

        def inner_step(block_no, state_now):
            offset = block_no * size_now
            query_block = lax.dynamic_slice_in_dim(query_part, offset, size_now, 0).reshape(
                size_now, head_count, head_size
            )
            grad_block = lax.dynamic_slice_in_dim(grad_part, offset, size_now, 0).reshape(
                size_now, head_count, head_size
            )
            query_pos = lax.dynamic_slice_in_dim(pos_all, offset, size_now, 0)
            log_block = lax.dynamic_slice_in_dim(stats_all[0], offset, size_now, 0).T
            delta_block = lax.dynamic_slice_in_dim(stats_all[1], offset, size_now, 0).T
            scores, allowed = head_scores(query_block, own_keys, query_pos, own_pos)
            shares = jnp.exp(scores - log_block[..., None])
            grad_shares = jnp.einsum(
                "qhd,khd->hqk", grad_block, value_heads, preferred_element_type=jnp.float32
            )
            grad_scores = (shares * (grad_shares - delta_block[..., None]) * scale_now).astype(
                jnp.bfloat16
            )
            key_term = jnp.einsum(
                "hqk,qhd->khd", grad_scores, query_block, preferred_element_type=jnp.float32
            )
            value_term = jnp.einsum(
                "hqk,qhd->khd",
                shares.astype(jnp.bfloat16),
                grad_block,
                preferred_element_type=jnp.float32,
            )
            return (
                state_now[0] + key_term.reshape(key_term.shape[0], -1),
                state_now[1] + value_term.reshape(value_term.shape[0], -1),
            )

        return lax.fori_loop(0, query_part.shape[0] // size_now, inner_step, state_in)

    return query_step


def gather_forward(shards):
    return (
        lax.all_gather(shards[0], ("fsdp", "ctx"), axis=0, tiled=True),
        lax.all_gather(shards[1], ("fsdp", "ctx"), axis=0, tiled=True),
        lax.all_gather(shards[2], ("fsdp", "ctx"), axis=0, tiled=True),
        lax.all_gather(shards[3], ("fsdp", "ctx"), axis=0, tiled=True),
        lax.all_gather(shards[4], ("fsdp", "ctx"), axis=0, tiled=True),
        lax.all_gather(shards[5], ("fsdp", "ctx"), axis=0, tiled=True),
        lax.all_gather(shards[6], ("fsdp", "ctx"), axis=0, tiled=True),
        lax.all_gather(shards[7], ("fsdp", "ctx"), axis=0, tiled=True),
        lax.all_gather(shards[8], ("fsdp", "ctx"), axis=0, tiled=True),
    )


def scatter_grads(grad_terms):
    return (
        lax.psum_scatter(grad_terms[0], ("fsdp", "ctx"), scatter_dimension=0, tiled=True),
        lax.psum_scatter(grad_terms[1], ("fsdp", "ctx"), scatter_dimension=0, tiled=True),
        lax.psum_scatter(grad_terms[2], ("fsdp", "ctx"), scatter_dimension=0, tiled=True),
        lax.psum_scatter(grad_terms[3], ("fsdp", "ctx"), scatter_dimension=0, tiled=True),
        lax.psum_scatter(grad_terms[4], ("fsdp", "ctx"), scatter_dimension=0, tiled=True),
        lax.psum_scatter(grad_terms[5], ("fsdp", "ctx"), scatter_dimension=0, tiled=True),
        lax.psum_scatter(grad_terms[6], ("fsdp", "ctx"), scatter_dimension=0, tiled=True),
        lax.psum_scatter(grad_terms[7], ("fsdp", "ctx"), scatter_dimension=0, tiled=True),
        lax.psum_scatter(grad_terms[8], ("fsdp", "ctx"), scatter_dimension=0, tiled=True),
    )


def forward_layer(hidden, full_layer, first_values, context):
    prenorm, query_w, keys_w, values_w, outproj, midnorm, gates_w, upproj_w, downproj_w = full_layer
    cosine, sine, own_pos, pos_all = context
    rows_n, model_width = hidden.shape
    normed, inverse_a = row_norm(hidden)
    attn_in = (normed * prenorm.astype(jnp.float32)).astype(jnp.bfloat16)
    query_raw = jnp.dot(attn_in, query_w, preferred_element_type=jnp.float32)
    keys_raw = jnp.dot(attn_in, keys_w, preferred_element_type=jnp.float32)
    values_raw = jnp.dot(attn_in, values_w, preferred_element_type=jnp.float32)
    mixed = values_raw if first_values is None else 0.5 * values_raw + 0.5 * first_values
    queries = rotate(query_raw.reshape(rows_n, HEADS, HD), cosine, sine).astype(jnp.bfloat16)
    keys_flat = (
        rotate(keys_raw.reshape(rows_n, HEADS, HD), cosine, sine)
        .reshape(rows_n, model_width)
        .astype(jnp.bfloat16)
    )
    values_flat = mixed.astype(jnp.bfloat16)
    top_start = jnp.full((HEADS, rows_n), NEG_FILL, jnp.float32)
    total_start = jnp.zeros((HEADS, rows_n), jnp.float32)
    top_now, total_now = make_stats_step(
        queries,
        own_pos,
        pos_all,
        (top_start, total_start),
        lax.all_gather(keys_flat, "ctx", axis=0, tiled=True),
    )
    log_total = top_now + jnp.log(total_now)
    att_out = make_value_step(
        queries,
        log_total,
        own_pos,
        pos_all,
        jnp.zeros((rows_n, HEADS, HD), jnp.float32),
        (
            lax.all_gather(keys_flat, "ctx", axis=0, tiled=True),
            lax.all_gather(values_flat, "ctx", axis=0, tiled=True),
        ),
    )
    att_low = att_out.reshape(rows_n, model_width).astype(jnp.bfloat16)
    middle = hidden + jnp.dot(att_low, outproj, preferred_element_type=jnp.float32)
    normed_mid, inverse_b = row_norm(middle)
    mlp_in = (normed_mid * midnorm.astype(jnp.float32)).astype(jnp.bfloat16)
    gate_raw = jnp.dot(mlp_in, gates_w, preferred_element_type=jnp.float32)
    up_proj = jnp.dot(mlp_in, upproj_w, preferred_element_type=jnp.float32)
    inner_act = (jax.nn.silu(gate_raw) * up_proj).astype(jnp.bfloat16)
    result = middle + jnp.dot(inner_act, downproj_w, preferred_element_type=jnp.float32)
    saved = (
        hidden,
        normed,
        inverse_a,
        attn_in,
        queries,
        keys_flat,
        values_flat,
        log_total,
        att_out,
        att_low,
        normed_mid,
        inverse_b,
        mlp_in,
        gate_raw,
        up_proj,
        inner_act,
    )
    return (result, values_raw, saved)


def backward_layer(grad_out, full_layer, saved, value_extra, is_second, context):
    prenorm, query_w, keys_w, values_w, outproj, midnorm, gates_w, upproj_w, downproj_w = full_layer
    (
        hidden,
        normed,
        inverse_a,
        attn_in,
        queries,
        keys_flat,
        values_flat,
        log_total,
        att_out,
        att_low,
        normed_mid,
        inverse_b,
        mlp_in,
        gate_raw,
        up_proj,
        inner_act,
    ) = saved
    cosine, sine, own_pos, pos_all = context
    rows_n, model_width = hidden.shape
    grad_low = grad_out.astype(jnp.bfloat16)
    grad_down = left_product(inner_act, grad_low)
    grad_inner = right_product(grad_low, downproj_w)
    sigma_gate = jax.nn.sigmoid(gate_raw)
    grad_gate = (grad_inner * up_proj * sigma_gate * (1.0 + gate_raw * (1.0 - sigma_gate))).astype(
        jnp.bfloat16
    )
    grad_up = (grad_inner * gate_raw * sigma_gate).astype(jnp.bfloat16)
    grad_gates = left_product(mlp_in, grad_gate)
    grad_upproj = left_product(mlp_in, grad_up)
    grad_mlp = right_product(grad_gate, gates_w) + right_product(grad_up, upproj_w)
    grad_midnorm = jnp.sum(grad_mlp * normed_mid, axis=0)
    grad_middle = grad_out + norm_back(
        grad_mlp * midnorm.astype(jnp.float32), normed_mid, inverse_b
    )
    branch_low = grad_middle.astype(jnp.bfloat16)
    grad_outproj = left_product(att_low, branch_low)
    grad_att = right_product(branch_low, outproj).astype(jnp.bfloat16).reshape(rows_n, HEADS, HD)
    row_delta = jnp.sum(grad_att.astype(jnp.float32) * att_out, axis=-1).T
    query_start = jnp.zeros((rows_n, HEADS, HD), jnp.float32)
    state_start = (query_start,)
    back_fn = make_back_step(queries, grad_att, log_total, row_delta, own_pos, pos_all)
    state_out = back_fn(
        state_start,
        (
            lax.all_gather(keys_flat, "ctx", axis=0, tiled=True),
            lax.all_gather(values_flat, "ctx", axis=0, tiled=True),
        ),
        jnp.int32(0),
    )
    grad_qr = state_out[0]
    stats_all = (
        lax.all_gather(log_total.T, "ctx", axis=0, tiled=True),
        lax.all_gather(row_delta.T, "ctx", axis=0, tiled=True),
    )
    query_fn = make_query_step(keys_flat, values_flat, own_pos, stats_all, pos_all, HEADS, HD)
    flat_start = jnp.zeros((rows_n, model_width), jnp.float32)
    grad_kr, grad_mix = query_fn(
        (flat_start, flat_start),
        (
            lax.all_gather(queries.reshape(rows_n, model_width), "ctx", axis=0, tiled=True),
            lax.all_gather(grad_att.reshape(rows_n, model_width), "ctx", axis=0, tiled=True),
        ),
        jnp.int32(0),
    )
    grad_query = unrotate(grad_qr, cosine, sine).reshape(rows_n, model_width).astype(jnp.bfloat16)
    grad_keys = (
        unrotate(grad_kr.reshape(rows_n, HEADS, HD), cosine, sine)
        .reshape(rows_n, model_width)
        .astype(jnp.bfloat16)
    )
    if is_second:
        grad_values = (0.5 * grad_mix).astype(jnp.bfloat16)
        passed_on = 0.5 * grad_mix
    else:
        grad_values = (grad_mix + value_extra).astype(jnp.bfloat16)
        passed_on = None
    grad_query_w = left_product(attn_in, grad_query)
    grad_keys_w = left_product(attn_in, grad_keys)
    grad_values_w = left_product(attn_in, grad_values)
    grad_attn = (
        right_product(grad_query, query_w)
        + right_product(grad_keys, keys_w)
        + right_product(grad_values, values_w)
    )
    grad_prenorm = jnp.sum(grad_attn * normed, axis=0)
    grad_hidden = grad_middle + norm_back(
        grad_attn * prenorm.astype(jnp.float32), normed, inverse_a
    )
    grad_terms = (
        grad_prenorm,
        grad_query_w,
        grad_keys_w,
        grad_values_w,
        grad_outproj,
        grad_midnorm,
        grad_gates,
        grad_upproj,
        grad_down,
    )
    return (grad_hidden, grad_terms, passed_on)


def local(
    tokens,
    cotangent,
    pair_of,
    prenorm_one,
    query_one,
    keys_one,
    values_one,
    outproj_one,
    midnorm_one,
    gates_one,
    upproj_one,
    downproj_one,
    prenorm_two,
    query_two,
    keys_two,
    values_two,
    outproj_two,
    midnorm_two,
    gates_two,
    upproj_two,
    downproj_two,
):
    seq_dev = tokens.shape[1]
    model_width = tokens.shape[2]
    pos_all = storage_positions(pair_of, seq_dev)
    own_pos = lax.dynamic_slice_in_dim(pos_all, lax.axis_index("ctx") * seq_dev, seq_dev, 0)
    cosine, sine = rope_tables(own_pos, HD)
    context = (cosine, sine, own_pos, pos_all)
    layer_shards = [
        (
            prenorm_one,
            query_one,
            keys_one,
            values_one,
            outproj_one,
            midnorm_one,
            gates_one,
            upproj_one,
            downproj_one,
        ),
        (
            prenorm_two,
            query_two,
            keys_two,
            values_two,
            outproj_two,
            midnorm_two,
            gates_two,
            upproj_two,
            downproj_two,
        ),
    ]
    hidden = tokens.reshape(seq_dev, model_width).astype(jnp.float32)
    first_values = None
    kept_full = []
    kept_saved = []
    for layer_no in range(2):
        full_layer = gather_forward(layer_shards[layer_no])
        hidden, values_raw, saved = forward_layer(hidden, full_layer, first_values, context)
        if layer_no == 0:
            first_values = values_raw
        kept_full.append(full_layer)
        kept_saved.append(saved)
    output = hidden.astype(jnp.bfloat16).reshape(1, seq_dev, model_width)
    grad_now = cotangent.reshape(seq_dev, model_width).astype(jnp.float32)
    value_extra = None
    layer_grads = [None, None]
    for layer_no in (1, 0):
        full_layer = kept_full[layer_no]
        grad_now, grad_terms, passed_on = backward_layer(
            grad_now, full_layer, kept_saved[layer_no], value_extra, layer_no == 1, context
        )
        if layer_no == 1:
            value_extra = passed_on
        layer_grads[layer_no] = scatter_grads(grad_terms)
    tokens_grad = grad_now.astype(jnp.bfloat16).reshape(1, seq_dev, model_width)
    first_grads = layer_grads[0]
    second_grads = layer_grads[1]
    return (
        output,
        tokens_grad,
        first_grads[0],
        first_grads[1],
        first_grads[2],
        first_grads[3],
        first_grads[4],
        first_grads[5],
        first_grads[6],
        first_grads[7],
        first_grads[8],
        second_grads[0],
        second_grads[1],
        second_grads[2],
        second_grads[3],
        second_grads[4],
        second_grads[5],
        second_grads[6],
        second_grads[7],
        second_grads[8],
    )


ROWS = 128
BF = jnp.bfloat16
F32 = jnp.float32
MESH = pl.DeviceIdType.MESH
VMEM_SPACE = pltpu.VMEM
HBM_SPACE = pltpu.HBM


def flip(value, weight):
    return value + weight * (1 - 2 * ((value // weight) % 2))


def to_device(f, c):
    return {"fsdp": f, "ctx": c}


def remote(src, dst, send_sem, recv_sem, target):
    return pltpu.make_async_remote_copy(
        src_ref=src,
        dst_ref=dst,
        send_sem=send_sem,
        recv_sem=recv_sem,
        device_id=to_device(*target),
        device_id_type=MESH,
    )


def arrived(ref, sem, target):
    remote(ref, ref, sem, sem, target).wait_recv()


def plane_place():
    f = lax.axis_index("fsdp")
    c = lax.axis_index("ctx")
    return f, c, (c // 2) % 2, c // 4


def row_peers(f, c, z):
    return [(f, c + 4 * ((z + i) % 4 - z)) for i in range(1, 4)]


HALF = ROWS // 2
ODD = 8


class Plane:
    def __init__(self, place):
        self.f, self.c, self.y, self.z = place
        self.mirrored = self.z // 2
        self.sign = 1 - 2 * self.mirrored
        self.own = self.z * (3 - self.z) // 2
        self.across = (self.f, flip(self.c, 2))

    def chip(self, near):
        return self.f, self.c + 4 * self.sign * (near - self.own)

    def at(self, near):
        return near + self.mirrored * (3 - 2 * near)

    def slot(self, half, near):
        return 4 * half + self.at(near)

    def both_kinds(self, run):
        @pl.when(self.own == 1)
        def _():
            run(True)

        @pl.when(self.own == 0)
        def _():
            run(False)


def emit(copy, live):
    if live:
        copy.start()
    else:
        copy.wait_send()


class Reduce(Plane):
    def __init__(self, place, product, bufs, sems):
        super().__init__(place)
        self.product = product
        self.sy, self.ry, self.acc, self.pb, self.su, self.sd, self.rb, self.ra = bufs
        self.ys, self.yr, self.us, self.ds, self.br, self.ar = sems

    def y_copy(self, slot):
        return remote(self.sy.at[slot], self.ry.at[slot], self.ys.at[slot], self.yr.at[slot], self.across)

    def got_y(self, slot):
        self.y_copy(slot).wait_recv()
        return self.ry[slot].astype(F32)

    def got(self, first, slot):
        buf, sem = (self.rb, self.br) if first else (self.ra, self.ar)
        arrived(buf.at[slot], sem.at[slot], self.across)
        return buf[slot].astype(F32)

    def pass_on(self, value, upward, slot, target, first, there=None):
        there = slot if there is None else there
        src, send = (self.su, self.us) if upward else (self.sd, self.ds)
        dst, sem = (self.rb, self.br) if first else (self.ra, self.ar)
        if value is not None:
            src[slot] = value.astype(BF)
        copy = remote(src.at[slot], dst.at[there], send.at[slot], sem.at[there], self.chip(target))
        emit(copy, value is not None)

    def order(self, step):
        inner = jnp.where(step == 0, 3, jnp.where(step == 1, 0, 4 - step))
        near = jnp.where(self.own == 1, inner, 3 - step)
        return near, near + self.mirrored * (3 - 2 * near)

    def products(self):
        def other_row(step, carry):
            near, block = self.order(step)
            value = self.product(2 * block + 1 - self.y)
            self.sy[block] = value[:HALF].astype(BF)
            self.y_copy(block).start()
            self.pb[block] = value[HALF:]

            @pl.when((near == 1) | (near == 2))
            def _():
                self.sy[4 + block] = value[HALF:].astype(BF)
                self.y_copy(4 + block).start()

            return carry

        def own_row(step, carry):
            near, block = self.order(step)
            value = self.product(2 * block + self.y)
            self.acc[block] = value[:HALF]
            self.acc[4 + block] = value[HALF:]
            return carry

        lax.fori_loop(0, 4, other_row, 0)
        self.both_kinds(lambda inner: self.odd(inner, True))
        lax.fori_loop(0, 4, own_row, 0)

    def odd(self, inner, live):
        far = self.pb[self.at(3)] if live else None
        if inner:
            self.pass_on(far, True, ODD, 3, True)
            self.pass_on(self.pb[self.at(0)] if live else None, False, ODD, 0, False)
        else:
            self.pass_on(far, True, ODD, 3, False, ODD + 1)

    def relay(self, half, near, inner, live, plain=False):
        slot = self.slot(half, near)
        upward = not inner or near != 0
        value = None
        if live:
            value = self.acc[slot]
            if not plain:
                value = value + self.got_y(slot)
            if inner and upward:
                value = value + self.got(True, slot)
        if not inner:
            self.pass_on(value, True, slot, 1, True)
        elif near == 0:
            self.pass_on(value, False, slot, 0, False)
        else:
            self.pass_on(value, True, slot, near, near == 3)

    def relays(self, inner, live):
        if inner:
            self.relay(1, 0, inner, live, True)
            self.relay(1, 3, inner, live, True)
            for half, near in ((0, 3), (0, 0), (0, 2), (1, 2)):
                self.relay(half, near, inner, live)
            return
        self.relay(1, 3, inner, live, True)
        for half, near in ((0, 3), (0, 2), (1, 2), (0, 1), (1, 1)):
            self.relay(half, near, inner, live)
        slot = self.slot(1, 0)
        if live:
            odd = self.pb[self.at(0)] + self.got(False, ODD) + self.got(True, ODD) + self.got(False, ODD + 1)
            self.sy[slot] = odd.astype(BF)
        emit(self.y_copy(slot), live)

    def own_sum(self, half):
        slot = self.slot(half, self.own)
        return self.acc[slot] + self.got_y(slot) + self.got(True, slot) + self.got(False, slot)

    def finish(self):
        for half, near in ((0, 0), (0, 1), (0, 2), (0, 3), (1, 1), (1, 2)):
            self.y_copy(self.slot(half, near)).wait_send()

        def left(inner):
            self.odd(inner, False)
            self.relays(inner, False)

        self.both_kinds(left)


class Gather(Plane):
    def __init__(self, place, full, sems):
        super().__init__(place)
        self.full = full
        self.ys, self.yr, self.us, self.ds, self.zr = sems

    def rows(self, half, near, side):
        start = (self.at(near) * 2 + side) * ROWS + half * HALF
        return self.full.at[pl.ds(pl.multiple_of(start, HALF), HALF)]

    def to_row(self, part, sem, slot, target, live):
        emit(remote(part, part, sem, self.zr.at[slot], self.chip(target)), live)

    def to_other_row(self, half, near, live):
        part = self.rows(half, near, self.y)
        slot = self.slot(half, near)
        emit(remote(part, part, self.ys.at[slot], self.yr.at[slot], self.across), live)

    def send_own(self, half, live=True):
        part = self.rows(half, self.own, self.y)
        slot = self.slot(half, self.own)
        self.to_other_row(half, self.own, live)
        self.to_row(part, self.ds.at[slot], slot, 1 - self.own, live)
        self.to_row(part, self.us.at[slot], slot, 2, live)

    def take(self, half, near, inner, live):
        part = self.rows(half, near, self.y)
        slot = self.slot(half, near)
        if live:
            arrived(part, self.zr.at[slot], self.across)
        if half == 0 or near in (1, 2):
            self.to_other_row(half, near, live)
        if inner and near in (2, 3):
            self.to_row(part, self.ds.at[slot], slot, 0, live)

    def odd_slot(self, near):
        return ODD + self.at(near) // 3

    def take_odd(self, near):
        arrived(self.rows(1, near, 1 - self.y), self.zr.at[self.odd_slot(near)], self.across)

    def got_y(self, half, near):
        arrived(self.rows(half, near, 1 - self.y), self.yr.at[self.slot(half, near)], self.across)

    def forward(self, half, inner, live):
        others = (2, 3, 0) if inner else (1, 2, 3)
        if half == 1 and not inner:
            part = self.rows(1, 0, 1 - self.y)
            slot = self.odd_slot(0)
            if live:
                self.got_y(1, 0)
            self.to_row(part, self.us.at[8], slot, 3, live)
            self.to_row(part, self.us.at[9], slot, 2, live)
            self.to_row(part, self.ds.at[8], slot, 1, live)
        for near in others:
            self.take(half, near, inner, live)
        if half == 1 and inner and live:
            self.take_odd(0)

    def pass_half(self, half):
        self.both_kinds(lambda inner: self.forward(half, inner, True))
        if half == 1:
            self.take_odd(3)
            for near in range(4):
                self.got_y(0, near)
            for near in (1, 2):
                self.got_y(1, near)

    def finish(self):
        self.send_own(0, False)
        self.send_own(1, False)

        def left(inner):
            self.forward(0, inner, False)
            self.forward(1, inner, False)

        self.both_kinds(left)


def exchange(place, product, settle, full, scratch, more=None, rows=None):
    f, c, y, z = place
    if more is None:
        greet(row_peers(f, c, z) + [(f, flip(c, 2))])
    else:
        peers, sibling, twin = chip_peers(f, c)
        greet(peers + [sibling, twin])
    own = (z * 2 + y) * ROWS
    reduce = Reduce(place, product, scratch[:8], scratch[8:14])
    gather = None if full is None else Gather(place, full, scratch[14:19])
    if rows is not None:
        full[pl.ds(pl.multiple_of(own, ROWS), ROWS), :] = rows
    reduce.products()
    if more is not None:
        more.first()
        more.early()
    reduce.both_kinds(lambda inner: reduce.relays(inner, True))
    if rows is not None:
        gather.send_own(0)
        gather.send_own(1)
    if more is not None:
        more.second()
    for half in range(2):
        new = settle(half, reduce.own_sum(half))
        if gather is not None and rows is None:
            full[pl.ds(pl.multiple_of(own + half * HALF, HALF), HALF), :] = new
            gather.send_own(half)
        if more is not None and half == 0:
            more.third()
    if gather is not None:
        gather.pass_half(0)
    if more is not None:
        more.fourth()
    if gather is not None:
        gather.pass_half(1)
        gather.finish()
    reduce.finish()
    if more is not None:
        more.finish()


def half_rows(half):
    return pl.ds(half * HALF, HALF)


def norm_rows(hidden):
    return lax.rsqrt(jnp.mean(hidden * hidden, axis=-1, keepdims=True) + NORM_EPS)


def make_product(left_ref, right_ref, transposed, lanes=None):
    dims = (((1,), (1,)), ((), ())) if transposed else (((1,), (0,)), ((), ()))

    def product(block):
        rows = left_ref[pl.ds(pl.multiple_of(block * ROWS, ROWS), ROWS), :]
        right = right_ref[...] if lanes is None else right_ref[:, lanes[0] : lanes[1]]
        return lax.dot_general(rows, right, dims, preferred_element_type=F32)

    return product


def forward_kernel(row, left_ref, right_ref, res_ref, gain_ref, new_ref, full_ref, *scratch):
    def settle(half, total):
        hidden = res_ref[half_rows(half), :].astype(F32) + total
        new_ref[half_rows(half), :] = hidden
        return (hidden * norm_rows(hidden) * gain_ref[row : row + 1, :]).astype(BF)

    exchange(plane_place(), make_product(left_ref, right_ref, False), settle, full_ref, scratch)


def turn_kernel(left_ref, right_ref, res_ref, cot_ref, out_ref, full_ref, *scratch):
    def settle(half, total):
        out_ref[half_rows(half), :] = (res_ref[half_rows(half), :] + total).astype(BF)

    product = make_product(left_ref, right_ref, False)
    exchange(plane_place(), product, settle, full_ref, scratch, None, cot_ref[...])


def back_rows(total, grad, hidden, gain):
    inverse = norm_rows(hidden)
    normed = hidden * inverse
    scaled = total * gain
    mean = jnp.mean(scaled * normed, axis=-1, keepdims=True)
    return grad + inverse * (scaled - normed * mean)


def comm_call(kernel, outs, ident, args, gathers, name, more=()):
    width = 1024
    scratch = []
    for count, kind in ((8, BF), (8, BF), (8, F32), (4, F32), (9, BF), (9, BF), (9, BF), (10, BF)):
        scratch.append(pltpu.VMEM((count, HALF, width), kind))
    scratch += [pltpu.SemaphoreType.DMA((10,))] * 6
    if gathers:
        scratch += [pltpu.SemaphoreType.DMA((10,))] * 5
    scratch += list(more)
    spec = pl.BlockSpec(memory_space=VMEM_SPACE)
    return pl.pallas_call(
        kernel,
        out_shape=[jax.ShapeDtypeStruct(*o) for o in outs],
        in_specs=[spec] * len(args),
        out_specs=[spec] * len(outs),
        scratch_shapes=scratch,
        compiler_params=pltpu.CompilerParams(
            collective_id=ident, has_side_effects=True, vmem_limit_bytes=(24 if more else 14) * 1024 * 1024
        ),
        name=name,
    )(*args)


def chip_peers(f, c):
    chip, core = c // 2, c % 2
    return [(f, 2 * ((chip + i) % 8) + core) for i in range(1, 8)], (f, flip(c, 1)), (1 - f, c)


def greet(targets):
    barrier = pltpu.get_barrier_semaphore()
    for target in targets:
        pl.semaphore_signal(barrier, inc=1, device_id=to_device(*target), device_id_type=MESH)
    pl.semaphore_wait(barrier, len(targets))


class OutRows:
    def __init__(self, place, shard, out, sems):
        self.f, self.c, self.y, _ = place
        self.core = self.c % 2
        _, self.sibling, self.twin = chip_peers(self.f, self.c)
        self.near = (self.f, flip(self.c, 2))
        self.shard, self.out = shard, out
        self.ws, self.wr = sems
        self.home = self.y == self.f

    def near_copy(self):
        part = 2 * self.y + self.core
        return remote(self.shard, self.out.at[part], self.ws.at[0], self.wr.at[0], self.near)

    def pair_copies(self, first, target):
        parts = [self.out.at[self.core], self.out.at[2 + self.core]]
        return [
            remote(p, p, self.ws.at[first + n], self.wr.at[first + n], target) for n, p in enumerate(parts)
        ]

    def first(self):
        @pl.when(self.home)
        def _():
            self.out[2 * self.y + self.core] = self.shard[...]

        @pl.when(jnp.logical_not(self.home))
        def _():
            self.near_copy().start()

    def second(self):
        @pl.when(self.home)
        def _():
            self.near_copy().wait_recv()
            for copy in self.pair_copies(1, self.twin):
                copy.start()

    def third(self):
        @pl.when(jnp.logical_not(self.home))
        def _():
            for copy in self.pair_copies(1, self.twin):
                copy.wait_recv()

        for copy in self.pair_copies(3, self.sibling):
            copy.start()

    def finish(self):
        for copy in self.pair_copies(3, self.sibling):
            copy.wait()

        @pl.when(self.home)
        def _():
            for copy in self.pair_copies(1, self.twin):
                copy.wait_send()

        @pl.when(jnp.logical_not(self.home))
        def _():
            self.near_copy().wait_send()


class Sender:
    def __init__(self, place):
        self.f, self.c, self.y, _ = place
        self.chip, self.core = self.c // 2, self.c % 2
        self.peers, self.sibling, self.twin = chip_peers(self.f, self.c)
        self.sent = []

    def send(self, src, dst, send_sem, recv_sem, target):
        copy = remote(src, dst, send_sem, recv_sem, target)
        copy.start()
        self.sent.append(copy)
        return copy


class Spread(Sender):
    def __init__(self, place, a, r, sems):
        super().__init__(place)
        self.a, self.r = a, r
        self.ds, self.dr, self.xs, self.xr, self.ss, self.sr = sems
        self.direct, self.crossed, self.inner = {}, {}, []

    def forward(self, part, n):
        self.crossed[n] = self.send(part[0], part[1], self.xs.at[n], self.xr.at[n], self.twin)

    def to_sibling(self, part, n):
        self.inner.append(self.send(part[0], part[1], self.ss.at[n], self.sr.at[n], self.sibling))

    def first(self):
        mine = self.r.at[self.f, self.chip, self.core]
        own = self.a.at[self.chip]
        self.forward((own, mine), 0)
        for i in range(1, 8):
            t = (self.chip + i) % 8
            self.direct[i] = self.send(self.a.at[t], mine, self.ds.at[i], self.dr.at[i], self.peers[i - 1])
        self.r[self.f, self.chip, self.core] = self.a[self.chip]
        self.to_sibling((own, mine), 0)

    def second(self):
        for i in range(1, 8):
            self.direct[i].wait_recv()
            part = self.r.at[self.f, (self.chip + 8 - i) % 8, self.core]
            self.forward((part, part), i)
            self.to_sibling((part, part), i)

    def third(self):
        for i in range(8):
            self.crossed[i].wait_recv()
            part = self.r.at[1 - self.f, (self.chip + 8 - i) % 8, self.core]
            self.to_sibling((part, part), 8 + i)

    def finish(self):
        for copy in self.inner:
            copy.wait_recv()
        for copy in self.sent:
            copy.wait_send()


class Share(Sender):
    def __init__(self, place, tables, downs, out, sems):
        super().__init__(place)
        self.tables, self.downs = tables, downs
        self.xs, self.xr, self.ss, self.sr, *more = sems
        self.out = OutRows(place, *out, more) if out else None

    def places(self, f):
        found = [r.at[f, :, self.core] for _, r in self.tables]
        return found + [d.at[2 * f + self.core] for _, d in self.downs]

    def first(self):
        self.crossed, self.inner = [], []
        sources = [s for s, _ in self.tables] + [n for n, _ in self.downs]
        for n, (src, dst) in enumerate(zip(sources, self.places(self.f))):
            self.crossed.append(self.send(src, dst, self.xs.at[n], self.xr.at[n], self.twin))
            self.inner.append(self.send(src, dst, self.ss.at[n], self.sr.at[n], self.sibling))
        if self.out:
            self.out.first()

    def early(self):
        pass

    def second(self):
        if self.out:
            self.out.second()

    def third(self):
        pass

    def fourth(self):
        for src, r in self.tables:
            for j in range(8):
                r[self.f, j, self.core] = src[j]
        for src, d in self.downs:
            d[2 * self.f + self.core] = src[...]
        count = len(self.crossed)
        for n, part in enumerate(self.places(1 - self.f)):
            self.crossed[n].wait_recv()
            self.inner.append(
                self.send(part, part, self.ss.at[count + n], self.sr.at[count + n], self.sibling)
            )
        if self.out:
            self.out.third()

    def finish(self):
        for copy in self.inner:
            copy.wait_recv()
        for copy in self.sent:
            copy.wait_send()
        if self.out:
            self.out.finish()


def start_leg(parts, peers, chip, sends, receives):
    copies = []
    for n, (src, dst) in enumerate(parts):
        for i in range(1, 8):
            sem = 8 * n + i
            part = src.at[(chip + i) % 8]
            copies.append(remote(part, dst.at[chip], sends.at[sem], receives.at[sem], peers[i - 1]))
            copies[-1].start()
        dst[chip] = src[chip]
    return copies


def turn_row(row):
    size = row.shape[1]
    same = lax.broadcasted_iota(jnp.int32, (size, size), 0) == lax.broadcasted_iota(jnp.int32, (size, size), 1)
    return jnp.sum(jnp.where(same, row, 0.0), axis=1, keepdims=True)


def turn_column(column):
    size = column.shape[0]
    same = lax.broadcasted_iota(jnp.int32, (size, size), 0) == lax.broadcasted_iota(jnp.int32, (size, size), 1)
    return jnp.sum(jnp.where(same, column, 0.0), axis=0, keepdims=True)


def pack_heads(query, keys, values, a):
    for chip in range(8):
        pair = 4 * (chip % 2) + chip // 2
        for n, w in enumerate((query, keys, values)):
            a[chip, :, 128 * n : 128 * n + 128] = w[:, 128 * pair : 128 * pair + 128]


def pack_units(gates, upproj, block, a):
    rows, units = gates.shape
    each = units // 32
    empty = jnp.zeros((rows, block - each), F32)
    for chip in range(8):
        for n, w in enumerate((gates, upproj)):
            parts = []
            for i in range(4):
                owner = 16 * (i // 2) + 2 * chip + i % 2
                parts += [w[:, each * owner : each * owner + each].astype(F32), empty]
            at = 4 * block * n
            a[chip, :, at : at + 4 * block] = jnp.concatenate(parts, axis=-1).astype(BF)


def pack_down(down, dn):
    each = down.shape[0]
    dn[:each] = down[...]
    dn[each:] = jnp.zeros((dn.shape[0] - each, down.shape[1]), BF)


def begin_kernel(tok, *refs):
    given, (full, r, o, gains, u1, h2, u2, n1, n2), shards = refs[:18], refs[18:27], refs[27:45]
    ones, twos = shards[:9], shards[9:]
    loads, a, *sems = refs[45:]
    copies = [pltpu.make_async_copy(src, dst, loads.at[n]) for n, (src, dst) in enumerate(zip(given, shards))]
    soon = (0, 1, 2, 3, 4, 5, 9, 14)
    for n in soon:
        copies[n].start()
    for n in range(18):
        if n not in soon:
            copies[n].start()
    place = plane_place()
    f, c, y, z = place
    peers, sibling, twin = chip_peers(f, c)
    start = (z * 2 + y) * ROWS
    full[pl.ds(pl.multiple_of(start, ROWS), ROWS), :] = tok[...]
    for n in soon:
        copies[n].wait()
    pack_heads(ones[1], ones[2], ones[3], a)
    lane = lax.broadcasted_iota(jnp.int32, (tok.shape[1] // 32, 128), 1)
    riders = jnp.zeros(lane.shape, F32)
    for n, gain in enumerate((ones[0], ones[5], twos[0], twos[5])):
        riders = jnp.where(lane == n, turn_row(gain[...].astype(F32)), riders)
    for chip in range(8):
        a[chip, :, 384:] = riders.astype(BF)
    greet(peers + [sibling, twin])

    gather = Gather(place, full, sems[:5])
    spread = Spread(place, a, r, sems[5:11])
    out = OutRows(place, ones[4], o, sems[11:])
    gather.send_own(0)
    spread.first()
    out.first()
    gather.send_own(1)
    for n in range(18):
        if n not in soon:
            copies[n].wait()
    pack_units(ones[6], ones[7], n1.shape[0], u1)
    gather.pass_half(0)
    spread.second()
    out.second()
    pack_heads(twos[1], twos[2], twos[3], h2)
    pack_units(twos[6], twos[7], n1.shape[0], u2)
    pack_down(ones[8], n1)
    pack_down(twos[8], n2)
    gather.pass_half(1)
    spread.third()
    out.third()
    gather.finish()
    spread.finish()
    out.finish()
    count = tok.shape[1]
    columns = r[:, :, :, :, 384:].reshape(count, 128)
    pick = lax.broadcasted_iota(jnp.int32, (8, 128), 0) == lax.broadcasted_iota(jnp.int32, (8, 128), 1)
    gains[...] = lax.dot_general(jnp.where(pick, 1.0, 0.0).astype(BF), columns, NT, preferred_element_type=F32)


def begin_call(tok, shards, block):
    rows, width = shards[1].shape
    spec = pl.BlockSpec(memory_space=VMEM_SPACE)
    wide = 8 * block
    outs = [
        ((8 * ROWS, width), BF), ((2, 8, 2, rows, 512), BF), ((4, rows, width), BF), ((8, width), F32),
        ((8, rows, wide), BF), ((8, rows, 384), BF), ((8, rows, wide), BF), ((block, width), BF), ((block, width), BF),
    ]
    counts = [(10,)] * 5 + [(8,), (8,), (8,), (8,), (16,), (16,), (5,), (5,)]
    return pl.pallas_call(
        begin_kernel,
        out_shape=[jax.ShapeDtypeStruct(*o) for o in outs],
        in_specs=[spec] + [pl.BlockSpec(memory_space=HBM_SPACE)] * 18,
        out_specs=[spec] * len(outs),
        scratch_shapes=[pltpu.VMEM(s.shape, s.dtype) for s in shards]
        + [pltpu.SemaphoreType.DMA((18,)), pltpu.VMEM((8, rows, 512), BF)]
        + [pltpu.SemaphoreType.DMA(n) for n in counts],
        compiler_params=pltpu.CompilerParams(
            collective_id=9, has_side_effects=True, vmem_limit_bytes=10 * 1024 * 1024
        ),
        name="begin",
    )(tok, *shards)


def middle_kernel(row, count, left_ref, right_ref, res_ref, gain_ref, *refs):
    given = 2 * count
    ins, refs = refs[:given], refs[given:]
    outs = 2 + count + 1 + (count == 2)
    new_ref, full_ref, *results = refs[:outs]
    scratch = refs[outs:]

    def settle(half, total):
        hidden = res_ref[half_rows(half), :].astype(F32) + total
        new_ref[half_rows(half), :] = hidden
        return (hidden * norm_rows(hidden) * gain_ref[row : row + 1, :]).astype(BF)

    tables = list(zip(ins[:count], results[:count]))
    downs = [(ins[count], results[count])]
    out = (ins[3], results[3]) if count == 2 else None
    place = plane_place()
    share = Share(place, tables, downs, out, scratch[19:])
    exchange(place, make_product(left_ref, right_ref, False), settle, full_ref, scratch, share)


def share_shapes(rows, width, block, widths):
    outs = [((2, 8, 2, rows, w), BF) for w in widths] + [((4, block, width), BF)]
    if len(widths) == 2:
        outs += [((4, rows, width), BF)]
    return outs, [pltpu.SemaphoreType.DMA(n) for n in ((3,), (3,), (6,), (6,), (5,), (5,))]


class Collect:
    def __init__(self, place, ins, results, scratch, final):
        self.f, self.c, self.y, _ = place
        self.chip, self.core = self.c // 2, self.c % 2
        self.peers, self.sibling, self.twin = chip_peers(self.f, self.c)
        self.near = (self.f, flip(self.c, 2))
        self.final = final
        self.g, self.h = ins
        self.out, self.oh = results
        self.sb, self.xb, self.xt, self.ut, self.sh, self.xh, self.th, *near = scratch[:-6]
        self.ss, self.sr, self.xs, self.xr, self.ps, self.pr = scratch[-6:]
        self.crosses_near = bool(near)
        if near:
            self.yo, self.yt = near
        self.home = self.y == self.f

    def inner_copy(self, n):
        other = 1 - self.core
        if n == 2:
            src, dst = self.h.at[:, other], self.sh
        else:
            part = 8 * ((1 - self.f) if n == 0 else self.f)
            src, dst = self.g.at[pl.ds(part, 8), other], self.sb.at[pl.ds(part, 8)]
        return remote(src, dst, self.ss.at[n], self.sr.at[n], self.sibling)

    def target(self, i):
        return (self.chip + i + 1) % 8

    def cross_copy(self, i):
        t = self.target(i)
        return remote(self.xt.at[t], self.xb.at[t], self.xs.at[i], self.xr.at[i], self.twin)

    def direct_copy(self, i):
        src = self.ut.at[self.target(i)]
        return remote(src, self.out.at[self.chip], self.ps.at[i], self.pr.at[i], self.peers[i])

    def twin_copy(self):
        return remote(self.th, self.xh, self.xs.at[8], self.xr.at[8], self.twin)

    def near_copy(self):
        return remote(self.yt, self.yo, self.xs.at[9], self.xr.at[9], self.near)

    def first(self):
        for n in range(3):
            self.inner_copy(n).start()

    def cross(self):
        f, core = self.f, self.core
        self.inner_copy(0).wait_recv()
        for i in range(8):
            t = self.target(i)
            at = (1 - f) * 8 + t
            self.xt[t] = (self.g[at, core].astype(F32) + self.sb[at].astype(F32)).astype(BF)
            self.cross_copy(i).start()
        self.inner_copy(2).wait_recv()
        if not self.crosses_near:
            self.th[...] = (self.h[1 - f, core].astype(F32) + self.sh[1 - f].astype(F32)).astype(BF)
            self.twin_copy().start()
            return
        for side in range(2):
            self.th[side] = (self.h[side, core].astype(F32) + self.sh[side].astype(F32)).astype(BF)

        @pl.when(jnp.logical_not(self.home))
        def _():
            self.twin_copy().start()

    def add_up(self):
        f, core = self.f, self.core
        self.inner_copy(1).wait_recv()
        for i in range(8):
            t = self.target(i)
            at = f * 8 + t
            self.cross_copy(i).wait_recv()
            total = self.g[at, core].astype(F32) + self.sb[at].astype(F32) + self.xb[t].astype(F32)
            if not self.final:
                self.out[t] = total.astype(BF)
            elif i < 7:
                self.ut[t] = total.astype(BF)
                self.direct_copy(i).start()
            else:
                self.out[self.chip] = total.astype(BF)
        if not self.crosses_near:
            self.twin_copy().wait_recv()
            self.oh[...] = self.h[f, core].astype(F32) + self.sh[f].astype(F32) + self.xh[...].astype(F32)
            return

        @pl.when(self.home)
        def _():
            self.twin_copy().wait_recv()
            y = self.y
            self.oh[...] = self.th[y].astype(F32) + self.xh[y].astype(F32)
            self.yt[...] = (self.th[1 - y].astype(F32) + self.xh[1 - y].astype(F32)).astype(BF)
            self.near_copy().start()

    def early(self):
        if self.final:
            self.cross()

    def second(self):
        if self.final:
            self.add_up()
        else:
            self.cross()

    def third(self):
        pass

    def fourth(self):
        if not self.final:
            self.add_up()

    def finish(self):
        if self.crosses_near:

            @pl.when(self.home)
            def _():
                self.near_copy().wait_send()

            @pl.when(jnp.logical_not(self.home))
            def _():
                self.near_copy().wait_recv()
                self.oh[...] = self.yo[...].astype(F32)
                self.twin_copy().wait_send()
        else:
            self.twin_copy().wait_send()
        for i in range(7 if self.final else 0):
            self.direct_copy(i).wait()
        for i in range(8):
            self.cross_copy(i).wait_send()
        for n in range(3):
            self.inner_copy(n).wait_send()


def collect_shapes(rows, wide, block, width, crosses_near):
    results = [((8, rows, wide), BF), ((block, width), F32)]
    buffers = [(16, rows, wide), (8, rows, wide), (8, rows, wide), (8, rows, wide), (2, block, width)]
    if crosses_near:
        buffers += [(2, block, width), (2, block, width), (block, width), (block, width)]
    else:
        buffers += [(block, width), (block, width)]
    counts = ((3,), (3,), (10,), (10,), (7,), (7,))
    scratch = [pltpu.VMEM(b, BF) for b in buffers] + [pltpu.SemaphoreType.DMA(n) for n in counts]
    return results, scratch


def back_kernel(gathers, row, crosses, left_ref, right_ref, grad_ref, hid_ref, gain_ref, g, h, new_ref, *refs):
    full_ref = refs[0] if gathers else None
    results, scratch = refs[gathers : gathers + 2], refs[gathers + 2 :]

    def settle(half, total):
        at = half_rows(half)
        new = back_rows(
            total, grad_ref[at, :].astype(F32), hid_ref[at, :].astype(F32), gain_ref[row : row + 1, :]
        )
        new_ref[at, :] = new.astype(new_ref.dtype)
        return new.astype(BF)

    place = plane_place()
    collect = Collect(place, (g, h), results, scratch[14 + 5 * gathers :], not gathers)
    lanes = (0, 384) if crosses else None
    product = make_product(left_ref, right_ref, True, lanes)
    exchange(place, product, settle, full_ref, scratch, collect)


def head_lanes(head):
    lane = lax.broadcasted_iota(jnp.int32, (1, 128), 1)
    return lane // 64 == head


def swap_halves(values):
    lane = lax.broadcasted_iota(jnp.int32, (1, 128), 1)
    return jnp.where(lane % 64 < 32, pltpu.roll(values, 96, 1), pltpu.roll(values, 32, 1))


NT = (((1,), (1,)), ((), ()))
TN = (((0,), (0,)), ((), ()))


def two_blocks(ref, tile, half):
    first = pl.multiple_of(2 * tile * ROWS + half * HALF, HALF)
    second = pl.multiple_of((2 * tile + 1) * ROWS + half * HALF, HALF)
    return jnp.concatenate([ref[pl.ds(first, HALF), :], ref[pl.ds(second, HALF), :]], axis=0)


def put_blocks(ref, tile, half, value):
    first = pl.multiple_of(2 * tile * ROWS + half * HALF, HALF)
    second = pl.multiple_of((2 * tile + 1) * ROWS + half * HALF, HALF)
    ref[pl.ds(first, HALF), :] = value[:HALF]
    ref[pl.ds(second, HALF), :] = value[HALF:]


def attend_kernel(layer, *refs):
    x_ref, w_ref, cos_ref, sin_ref, more_ref, pq_ref, pk_ref = refs[:7]
    count = 2 - layer
    tables, refs = refs[7 : 7 + count], refs[7 + count :]
    q_ref, k_ref, v_ref, att_ref, lse_ref = refs[:5]
    kept = refs[5:7]
    placed = refs[-4 - count : -4]
    sends, receives, ss, sr = refs[-4:]
    f, c, _, _ = plane_place()
    peers, sibling, _ = chip_peers(f, c)
    rows_n = x_ref.shape[0]
    half_n = rows_n // 2
    greet(peers + [sibling])
    leg = start_leg(list(zip(tables, placed)), peers, c // 2, sends, receives)

    def copies(i):
        here = pl.ds(pl.multiple_of(i * HALF, HALF), HALF)
        there = pl.ds(pl.multiple_of(half_n + i * HALF, HALF), HALF)
        return [
            remote(ref.at[h, here], ref.at[h, there], ss.at[4 * i + n], sr.at[4 * i + n], sibling)
            for n, (ref, h) in enumerate(((k_ref, 0), (k_ref, 1), (v_ref, 0), (v_ref, 1)))
        ]

    def step(i, carry):
        at = pl.ds(pl.multiple_of(i * ROWS, ROWS), ROWS)
        here = pl.ds(pl.multiple_of(i * HALF, HALF), HALF)
        rows = x_ref[at, :]
        if layer == 0:
            wide = rows.astype(F32)
            rows = (wide * norm_rows(wide) * more_ref[:1, :]).astype(BF)
            kept[0][at, :] = rows
        raw = jnp.dot(rows, w_ref[:, :384], preferred_element_type=F32)
        cosine, sine = cos_ref[at, :], sin_ref[at, :]
        q, k, v = raw[:, :128], raw[:, 128:256], raw[:, 256:]
        q_ref[at, :] = (q * cosine + swap_halves(q) * sine).astype(BF)
        k = (k * cosine + swap_halves(k) * sine).astype(BF)
        if layer == 0:
            kept[1][at, :] = v
        else:
            v = 0.5 * v + 0.5 * more_ref[at, :]
        v = v.astype(BF)
        for half in range(2):
            k_ref[half, here, :] = k[half * HALF : (half + 1) * HALF]
            v_ref[half, here, :] = v[half * HALF : (half + 1) * HALF]
        for copy in copies(i):
            copy.start()
        return carry

    lax.fori_loop(0, rows_n // ROWS, step, 0)
    for i in range(rows_n // ROWS):
        for copy in copies(i):
            copy.wait()

    def tile_step(tile, carry):
        for late in range(2):
            number = tile + late * (rows_n // (2 * ROWS))
            queries = two_blocks(q_ref, tile, late) * jnp.asarray(HD ** (-0.5), BF)
            allowed = pk_ref[late : late + 1, :] <= turn_row(pq_ref[pl.ds(number, 1), :])
            parts = []
            for head in range(2):
                masked = jnp.where(head_lanes(head), queries, jnp.zeros_like(queries))
                scores = lax.dot_general(masked, k_ref[late], NT, preferred_element_type=F32)
                scores = jnp.where(allowed, scores, NEG_FILL)
                top = jnp.max(scores, axis=-1, keepdims=True)
                if late:
                    early = lax.dot_general(masked, k_ref[0], NT, preferred_element_type=F32)
                    top = jnp.maximum(top, jnp.max(early, axis=-1, keepdims=True))
                shares = jnp.exp(scores - top)
                total = jnp.sum(shares, axis=-1, keepdims=True)
                mixed = jnp.dot(shares.astype(BF), v_ref[late], preferred_element_type=F32)
                if late:
                    shares = jnp.exp(early - top)
                    total += jnp.sum(shares, axis=-1, keepdims=True)
                    mixed += jnp.dot(shares.astype(BF), v_ref[0], preferred_element_type=F32)
                lse_ref[number, head : head + 1, :] = turn_column(top + jnp.log(total))
                parts.append(mixed / total)
            put_blocks(att_ref, tile, late, jnp.where(head_lanes(0), parts[0], parts[1]).astype(BF))
        return carry

    lax.fori_loop(0, rows_n // (2 * ROWS), tile_step, 0)
    for copy in leg:
        copy.wait()


def attend(layer, *args):
    rows_n = args[0].shape[0]
    spec = pl.BlockSpec(memory_space=VMEM_SPACE)
    outs = [((rows_n, 128), BF), ((2, rows_n, 128), BF), ((2, rows_n, 128), BF), ((rows_n, 128), BF)]
    outs += [((rows_n // ROWS, 2, ROWS), F32)]
    count = 4 * (rows_n // ROWS)
    sems = [pltpu.SemaphoreType.DMA((count,))] * 2
    if layer == 0:
        outs += [(args[0].shape, BF), ((rows_n, 128), F32)]
    outs += [(p.shape, BF) for p in args[7:]]
    sems = [pltpu.SemaphoreType.DMA((16,))] * 2 + sems
    return pl.pallas_call(
        functools.partial(attend_kernel, layer),
        out_shape=[jax.ShapeDtypeStruct(*o) for o in outs],
        in_specs=[spec] * len(args),
        out_specs=[spec] * len(outs),
        scratch_shapes=sems,
        compiler_params=pltpu.CompilerParams(
            collective_id=10 + layer, has_side_effects=True, vmem_limit_bytes=16 * 1024 * 1024
        ),
        name="attend",
    )(*args)


def attend_back_kernel(layer, *refs):
    q_ref, k_ref, v_ref, full_ref, out_ref, att_ref, lse_ref, pq_ref, pk_ref, cos_ref, sin_ref, more_ref = refs[:12]
    count = 2 - layer
    tables, refs = refs[12 : 12 + count], refs[12 + count :]
    three_ref, dw_ref, *placed = refs[: 2 + count]
    pkc, dq, dk, dv, dw, sb, rb, ss, sr, sends, receives = refs[-11:]
    place = plane_place()
    f, c, _, _ = place
    peers, sibling, _ = chip_peers(f, c)
    greet(peers + [sibling])
    leg = start_leg(list(zip(tables, placed)), peers, c // 2, sends, receives)
    rows_n = q_ref.shape[0]
    half_n = rows_n // 2
    dk[...] = jnp.zeros_like(dk)
    dv[...] = jnp.zeros_like(dv)
    dw[...] = jnp.zeros_like(dw)
    for late in range(2):
        for i in range(rows_n // ROWS):
            at = slice(i * ROWS, (i + 1) * ROWS)
            pkc[late, at, :] = turn_row(pk_ref[late : late + 1, at])

    def tile_step(tile, carry):
        for late in range(2):
            number = tile + late * (rows_n // (2 * ROWS))
            queries = two_blocks(q_ref, tile, late) * jnp.asarray(HD ** (-0.5), BF)
            full = two_blocks(full_ref, tile, late)
            grads = lax.dot_general(full, out_ref[...], NT, preferred_element_type=F32).astype(BF)
            dw[...] += lax.dot_general(two_blocks(att_ref, tile, late), full, TN, preferred_element_type=F32)
            allowed = pkc[late] <= pq_ref[pl.ds(number, 1), :]
            parts = []
            for head in range(2):
                masked = jnp.where(head_lanes(head), queries, jnp.zeros_like(queries))
                grad_h = jnp.where(head_lanes(head), grads, jnp.zeros_like(grads))
                lse = lse_ref[number, head : head + 1, :]
                kinds = (1, 0) if late else (0,)
                shares, grad_shares = [], []
                delta = jnp.zeros((1, ROWS), F32)
                for kind in kinds:
                    part = jnp.exp(lax.dot_general(k_ref[kind], masked, NT, preferred_element_type=F32) - lse)
                    if kind == late:
                        part = jnp.where(allowed, part, 0.0)
                    grad = lax.dot_general(v_ref[kind], grad_h, NT, preferred_element_type=F32)
                    delta += jnp.sum(part * grad, axis=0, keepdims=True)
                    shares.append(part)
                    grad_shares.append(grad)
                found = jnp.zeros((ROWS, 128), F32)
                for kind, part, grad in zip(kinds, shares, grad_shares):
                    grad_scores = (part * (grad - delta)).astype(BF)
                    dv[kind] += jnp.dot(part.astype(BF), grad_h, preferred_element_type=F32)
                    dk[kind] += jnp.dot(grad_scores, masked, preferred_element_type=F32)
                    found += lax.dot_general(grad_scores, k_ref[kind], TN, preferred_element_type=F32)
                parts.append(found)
            put_blocks(dq, tile, late, jnp.where(head_lanes(0), parts[0], parts[1]) * HD ** (-0.5))
        return carry

    lax.fori_loop(0, rows_n // (2 * ROWS), tile_step, 0)
    copies = []
    for n, ref in enumerate((dk, dv)):
        sb[n] = ref[:, half_n:, :].astype(BF)
        copies.append(remote(sb.at[n], rb.at[n], ss.at[n], sr.at[n], sibling))
        copies[n].start()
    dw_ref[...] = dw[...].astype(BF)
    for copy in copies:
        copy.wait()

    def rows_of(n, ref, i):
        here = pl.ds(pl.multiple_of(i * HALF, HALF), HALF)
        return jnp.concatenate([ref[half, here, :] + rb[n, half, here, :].astype(F32) for half in range(2)], axis=0)

    def turn(i, carry):
        at = pl.ds(pl.multiple_of(i * ROWS, ROWS), ROWS)
        cosine, sine = cos_ref[at, :], sin_ref[at, :]
        for n, grad in enumerate((dq[at, :], rows_of(0, dk, i))):
            three_ref[at, 128 * n : 128 * n + 128] = (grad * cosine - swap_halves(grad) * sine).astype(BF)
        grad = rows_of(1, dv, i)
        if layer == 1:
            grad = 0.5 * grad
            refs[2 + count][at, :] = grad
        else:
            grad = grad + more_ref[at, :]
        three_ref[at, 256:] = grad.astype(BF)
        return carry

    lax.fori_loop(0, rows_n // ROWS, turn, 0)
    for copy in leg:
        copy.wait()


def attend_backward(layer, *args):
    rows_n, width = args[3].shape
    spec = pl.BlockSpec(memory_space=VMEM_SPACE)
    outs = [((rows_n, 384), BF), ((128, width), BF)] + [(u.shape, BF) for u in args[12:]]
    if layer == 1:
        outs += [((rows_n, 128), F32)]
    return pl.pallas_call(
        functools.partial(attend_back_kernel, layer),
        out_shape=[jax.ShapeDtypeStruct(*o) for o in outs],
        in_specs=[spec] * len(args),
        out_specs=[spec] * len(outs),
        scratch_shapes=[
            pltpu.VMEM((2, rows_n, 1), F32),
            pltpu.VMEM((rows_n, 128), F32),
            pltpu.VMEM((2, rows_n, 128), F32),
            pltpu.VMEM((2, rows_n, 128), F32),
            pltpu.VMEM((128, width), F32),
            pltpu.VMEM((2, 2, rows_n // 2, 128), BF),
            pltpu.VMEM((2, 2, rows_n // 2, 128), BF),
            pltpu.SemaphoreType.DMA((2,)),
            pltpu.SemaphoreType.DMA((2,)),
            pltpu.SemaphoreType.DMA((16,)),
            pltpu.SemaphoreType.DMA((16,)),
        ],
        compiler_params=pltpu.CompilerParams(
            collective_id=12 + layer, has_side_effects=True, vmem_limit_bytes=32 * 1024 * 1024
        ),
        name="attend_back",
    )(*args)


def unpack_kernel(*every):
    every[24][...] = every[0][...]
    every[25][...] = every[1][...]
    refs = every[2:24] + every[26:]
    for l in range(2):
        cu, od, cq, oo, pre, query, keys, values, mid, gates, upproj = refs[11 * l : 11 * l + 11]
        g_pre, gq, gk, gv, g_out, g_mid, gg, gu, g_down = refs[22 + 9 * l : 31 + 9 * l]
        rows, units = gates.shape
        each = units // 32
        block = cu.shape[2] // 8
        total = jnp.zeros((rows, 1), F32)
        for chip in range(8):
            pair = 4 * (chip % 2) + chip // 2
            for n, (w, g) in enumerate(((query, gq), (keys, gk), (values, gv))):
                at = slice(128 * pair, 128 * pair + 128)
                part = cq[chip, :, 128 * n : 128 * n + 128].astype(F32)
                g[:, at] = part
                total += jnp.sum(part * w[:, at].astype(F32), axis=-1, keepdims=True)
        g_pre[...] = turn_column(total) / pre[...].astype(F32)
        for n, g in enumerate((gg, gu)):
            for chip in range(8):
                wide = cu[chip, :, 4 * block * n : 4 * block * (n + 1)].astype(F32)
                for i in range(4):
                    owner = 16 * (i // 2) + 2 * chip + i % 2
                    g[:, each * owner : each * owner + each] = wide[:, block * i : block * i + each]
        both = gg[...] * gates[...].astype(F32) + gu[...] * upproj[...].astype(F32)
        g_mid[...] = turn_column(jnp.sum(both, axis=-1, keepdims=True)) / mid[...].astype(F32)
        g_out[...] = oo[...]
        g_down[...] = od[: g_down.shape[0], :]


def unpack(output, tokens_grad, collected, layers):
    args, outs = [output, tokens_grad], [(output.shape, BF), (tokens_grad.shape, BF)]
    for l, layer in enumerate(layers):
        pre, query, keys, values, out, mid, gates, upproj, down = layer
        args += [*collected[l], pre, query, keys, values, mid, gates, upproj]
        for w in layer:
            outs.append((w.shape, F32))
    spec = pl.BlockSpec(memory_space=VMEM_SPACE)
    found = pl.pallas_call(
        unpack_kernel,
        out_shape=[jax.ShapeDtypeStruct(*o) for o in outs],
        in_specs=[spec] * len(args),
        out_specs=[spec] * len(outs),
        compiler_params=pltpu.CompilerParams(vmem_limit_bytes=60 * 1024 * 1024),
        name="unpack",
    )(*args)
    return [g[0] if g.shape[0] == 1 else g for g in found]


def fast_local(tokens, cotangent, pair_of, *shards):
    width = tokens.shape[2]
    rows_each, units = shards[6].shape
    each = units // 32
    block = (each + 2 + 31) // 32 * 32
    hidden_pad = 4 * block
    wide = 384 + 2 * hidden_pad
    core = lax.axis_index("ctx") % 2
    pos_all = storage_positions(pair_of, ROWS).reshape(8, 2, ROWS)
    own_pos = lax.dynamic_index_in_dim(pos_all, core, 1, False).reshape(-1)
    sib_pos = lax.dynamic_index_in_dim(pos_all, 1 - core, 1, False).reshape(-1)
    own_split = own_pos.reshape(8, 2, HALF).transpose(1, 0, 2)
    sib_split = sib_pos.reshape(8, 2, HALF).transpose(1, 0, 2)
    pos_q = own_split.reshape(8, ROWS).astype(F32)
    pos_k = jnp.concatenate([own_split, sib_split], axis=1).reshape(2, -1).astype(F32)
    cosine, sine = rope_tables(own_pos, HD)
    cosine = jnp.concatenate([cosine] * 4, axis=-1)
    sine = jnp.concatenate([-sine, sine, -sine, sine], axis=-1)

    shards = [s[None, :] if s.ndim == 1 else s for s in shards]
    layers = [shards[:9], shards[9:]]
    tok = tokens.reshape(ROWS, width)
    cot = cotangent.reshape(ROWS, width)

    full, heads, out_rows, gains, units_one, heads_two, units_two, *downs = begin_call(tok, shards, block)
    heads_w = [heads.reshape(32 * rows_each, 512), None]
    units_w, down_w, out_w = [None, None], [None, None], [out_rows.reshape(4 * rows_each, width), None]

    plane = 8 * ROWS
    full_type = ((plane, width), BF)
    rows_type = ((ROWS, width), F32)
    saved = []
    hidden = tok
    first_values = None
    for layer in range(2):
        args = (full, heads_w[layer], cosine, sine, gains if layer == 0 else first_values, pos_q, pos_k)
        x_full = full
        if layer == 0:
            q, k, v, att, lse, x_full, first_values, *legs = attend(0, *args, units_one, heads_two)
            widths, more = (2 * hidden_pad, 384), (downs[0], layers[1][4])
        else:
            q, k, v, att, lse, *legs = attend(1, *args, units_two)
            widths, more = (2 * hidden_pad,), (downs[1],)
        outs, sems = share_shapes(rows_each, width, block, widths)
        middle, mlp_full, table, *found = comm_call(
            functools.partial(middle_kernel, 2 * layer + 1, len(widths)), [rows_type, full_type] + outs, 1 + layer,
            (att, out_w[layer], hidden, gains, *legs, *more), True, "middle", sems,
        )
        units_w[layer] = table.reshape(32 * rows_each, 2 * hidden_pad)
        if layer == 0:
            heads_w[1] = found[0].reshape(32 * rows_each, 384)
            down_w[0] = found[1].reshape(hidden_pad, width)
            out_w[1] = found[2].reshape(4 * rows_each, width)
        else:
            down_w[1] = found[0].reshape(hidden_pad, width)
        both = jnp.dot(mlp_full, units_w[layer], preferred_element_type=F32)
        gate, up = both[:, :hidden_pad], both[:, hidden_pad:]
        inner = (jax.nn.silu(gate) * up).astype(BF)
        saved.append((x_full, q, k, v, lse, att, mlp_full, gate, up, inner, hidden, middle))
        if layer == 0:
            hidden, full = comm_call(
                functools.partial(forward_kernel, 2), [rows_type, full_type], 3,
                (inner, down_w[layer], middle, gains), True, "result",
            )
        else:
            output, full = comm_call(
                turn_kernel, [((ROWS, width), BF), full_type], 4,
                (inner, down_w[layer], middle, cot), True, "turn",
            )
    grad = cot
    passed = cosine
    collected = [None, None]
    for layer in (1, 0):
        x_full, q, k, v, lse, att, mlp_full, gate, up, inner, hidden, middle = saved[layer]
        grad_down = left_product(inner, full)
        grad_inner = right_product(full, down_w[layer])
        sigma = jax.nn.sigmoid(gate)
        grad_gate = (grad_inner * up * sigma * (1.0 + gate * (1.0 - sigma))).astype(BF)
        grad_up = (grad_inner * gate * sigma).astype(BF)
        both = jnp.concatenate([grad_gate, grad_up], axis=-1)
        grad_upw = left_product(mlp_full, both)
        results, more = collect_shapes(rows_each, 2 * hidden_pad, block, width, False)
        grad_mid, full, units_sum, got_down = comm_call(
            functools.partial(back_kernel, 1, 2 * layer + 1, False), [rows_type, full_type] + results, 5 + layer,
            (
                both, units_w[layer], grad, middle, gains,
                grad_upw.astype(BF).reshape(16, 2, rows_each, 2 * hidden_pad),
                grad_down.astype(BF).reshape(2, 2, block, width),
            ),
            True, "middle_back", more,
        )
        legs = (units_sum,) if layer == 1 else (units_sum, heads_sum)
        three, grad_out, got_units, *kept = attend_backward(
            layer, q, k, v, full, out_w[layer], att, lse, pos_q, pos_k, cosine, sine, passed, *legs
        )
        collected[layer] = [got_units, got_down]
        if layer == 1:
            (passed,) = kept
        else:
            collected[1] += [kept[0], two_out]
        grad_qkv = left_product(x_full, three)
        results, more = collect_shapes(rows_each, 384, rows_each, width, True)
        args = (
            three, heads_w[layer], grad_mid, hidden, gains,
            grad_qkv.astype(BF).reshape(16, 2, rows_each, 384),
            grad_out.reshape(2, 2, rows_each, width),
        )
        if layer == 1:
            grad, full, heads_sum, two_out = comm_call(
                functools.partial(back_kernel, 1, 2, True), [rows_type, full_type] + results, 7, args, True,
                "layer_back", more,
            )
        else:
            tokens_grad, *got_heads = comm_call(
                functools.partial(back_kernel, 0, 0, True), [((ROWS, width), BF)] + results, 8, args, False,
                "last_back", more,
            )
            collected[0] += got_heads
    output, tokens_grad, *found = unpack(output, tokens_grad, collected, layers)
    return (output.reshape(1, ROWS, width), tokens_grad.reshape(1, ROWS, width), *found)


def solution(mesh):
    placed = (
        P("fsdp", "ctx", None),
        P("fsdp", "ctx", None),
        P(),
        P(("fsdp", "ctx")),
        P(("fsdp", "ctx"), None),
        P(("fsdp", "ctx"), None),
        P(("fsdp", "ctx"), None),
        P(("fsdp", "ctx"), None),
        P(("fsdp", "ctx")),
        P(("fsdp", "ctx"), None),
        P(("fsdp", "ctx"), None),
        P(("fsdp", "ctx"), None),
        P(("fsdp", "ctx")),
        P(("fsdp", "ctx"), None),
        P(("fsdp", "ctx"), None),
        P(("fsdp", "ctx"), None),
        P(("fsdp", "ctx"), None),
        P(("fsdp", "ctx")),
        P(("fsdp", "ctx"), None),
        P(("fsdp", "ctx"), None),
        P(("fsdp", "ctx"), None),
    )
    fits = mesh.shape["ctx"] == HEADS and mesh.shape["fsdp"] == 2
    return jax.shard_map(
        fast_local if fits else local,
        mesh=mesh,
        in_specs=placed,
        out_specs=(
            P("fsdp", "ctx", None),
            P("fsdp", "ctx", None),
            P(("fsdp", "ctx")),
            P(("fsdp", "ctx"), None),
            P(("fsdp", "ctx"), None),
            P(("fsdp", "ctx"), None),
            P(("fsdp", "ctx"), None),
            P(("fsdp", "ctx")),
            P(("fsdp", "ctx"), None),
            P(("fsdp", "ctx"), None),
            P(("fsdp", "ctx"), None),
            P(("fsdp", "ctx")),
            P(("fsdp", "ctx"), None),
            P(("fsdp", "ctx"), None),
            P(("fsdp", "ctx"), None),
            P(("fsdp", "ctx"), None),
            P(("fsdp", "ctx")),
            P(("fsdp", "ctx"), None),
            P(("fsdp", "ctx"), None),
            P(("fsdp", "ctx"), None),
        ),
        check_vma=False,
    )
```

```python
import functools
import math

import jax
import jax.numpy as jnp
from jax import lax
from jax.experimental import pallas as pl
from jax.experimental.pallas import tpu as pltpu
from jax.sharding import PartitionSpec as P

HEADS = 16
HD = 64


NORM_EPS = 1e-05
NEG_FILL = -1e30


def block_size(total_rows):
    size_now = 512
    while total_rows % size_now:
        size_now //= 2
    return size_now


def row_norm(hidden):
    inverse = lax.rsqrt(jnp.mean(hidden * hidden, axis=-1, keepdims=True) + NORM_EPS)
    return (hidden * inverse, inverse)


def norm_back(grad_normed, normed, inverse):
    return inverse * (grad_normed - normed * jnp.mean(grad_normed * normed, axis=-1, keepdims=True))


def rope_tables(positions, head_size):
    half_size = head_size // 2
    freqs = jnp.exp(
        jnp.arange(half_size, dtype=jnp.float32) * (-2.0 * math.log(10000.0) / head_size)
    )
    angles = positions.astype(jnp.float32)[:, None] * freqs[None, :]
    return (jnp.cos(angles), jnp.sin(angles))


def rotate(values_in, cosine, sine):
    half_size = values_in.shape[-1] // 2
    first_half = values_in[..., :half_size]
    second_half = values_in[..., half_size:]
    cos_rows = cosine[:, None, :]
    sin_rows = sine[:, None, :]
    return jnp.concatenate(
        [
            first_half * cos_rows - second_half * sin_rows,
            second_half * cos_rows + first_half * sin_rows,
        ],
        axis=-1,
    )


def unrotate(grads_in, cosine, sine):
    half_size = grads_in.shape[-1] // 2
    first_half = grads_in[..., :half_size]
    second_half = grads_in[..., half_size:]
    cos_rows = cosine[:, None, :]
    sin_rows = sine[:, None, :]
    return jnp.concatenate(
        [
            first_half * cos_rows + second_half * sin_rows,
            second_half * cos_rows - first_half * sin_rows,
        ],
        axis=-1,
    )


def left_product(left, right):
    return lax.dot_general(
        left, right, (((0,), (0,)), ((), ())), preferred_element_type=jnp.float32
    )


def right_product(left, right):
    return lax.dot_general(
        left, right, (((1,), (1,)), ((), ())), preferred_element_type=jnp.float32
    )


def storage_positions(pair_of, seq_dev):
    devices = pair_of.shape[0]
    rows_all = jnp.arange(devices * seq_dev, dtype=jnp.int32)
    owner = rows_all // seq_dev
    local_row = rows_all % seq_dev
    half_rows = seq_dev // 2
    picked = jnp.sum(
        jnp.where(
            owner[:, None] == jnp.arange(devices, dtype=jnp.int32)[None, :], pair_of[None, :], 0
        ),
        axis=1,
    )
    block_id = jnp.where(local_row < half_rows, picked, 2 * devices - 1 - picked)
    return block_id * half_rows + local_row % half_rows


def head_scores(queries, keys_flat, query_pos, key_pos):
    key_heads = keys_flat.reshape(keys_flat.shape[0], queries.shape[1], queries.shape[2])
    scores = jnp.einsum(
        "qhd,khd->hqk", queries, key_heads, preferred_element_type=jnp.float32
    ) * queries.shape[2] ** (-0.5)
    allowed = (key_pos[None, :] <= query_pos[:, None])[None]
    return (jnp.where(allowed, scores, NEG_FILL), allowed)


def make_stats_step(queries, query_pos, pos_all, state_in, key_part):
    size_now = block_size(key_part.shape[0])

    def inner_step(block_no, state_now):
        top_now, total_now = state_now
        offset = block_no * size_now
        key_block = lax.dynamic_slice_in_dim(key_part, offset, size_now, 0)
        key_pos = lax.dynamic_slice_in_dim(pos_all, offset, size_now, 0)
        scores, allowed = head_scores(queries, key_block, query_pos, key_pos)
        new_top = jnp.maximum(top_now, jnp.max(scores, axis=-1))
        total_now = total_now * jnp.exp(top_now - new_top) + jnp.sum(
            jnp.where(allowed, jnp.exp(scores - new_top[..., None]), 0.0), axis=-1
        )
        return (new_top, total_now)

    return lax.fori_loop(0, key_part.shape[0] // size_now, inner_step, state_in)


def make_value_step(queries, log_total, query_pos, pos_all, acc_in, pieces):
    key_part, value_part = pieces
    size_now = block_size(key_part.shape[0])

    def inner_step(block_no, acc_now):
        offset = block_no * size_now
        key_block = lax.dynamic_slice_in_dim(key_part, offset, size_now, 0)
        value_block = lax.dynamic_slice_in_dim(value_part, offset, size_now, 0)
        key_pos = lax.dynamic_slice_in_dim(pos_all, offset, size_now, 0)
        scores, allowed = head_scores(queries, key_block, query_pos, key_pos)
        shares = jnp.exp(scores - log_total[..., None]).astype(jnp.bfloat16)
        value_heads = value_block.reshape(size_now, queries.shape[1], queries.shape[2])
        return acc_now + jnp.einsum(
            "hqk,khd->qhd", shares, value_heads, preferred_element_type=jnp.float32
        )

    return lax.fori_loop(0, key_part.shape[0] // size_now, inner_step, acc_in)


def make_back_step(queries, grad_att, log_total, row_delta, query_pos, pos_all):
    scale_now = queries.shape[2] ** (-0.5)

    def back_step(state_in, pieces, start_row):
        key_part, value_part = pieces
        size_now = block_size(key_part.shape[0])

        def inner_step(block_no, state_now):
            offset = block_no * size_now
            key_block = lax.dynamic_slice_in_dim(key_part, offset, size_now, 0)
            value_block = lax.dynamic_slice_in_dim(value_part, offset, size_now, 0)
            key_pos = lax.dynamic_slice_in_dim(pos_all, offset, size_now, 0)
            scores, allowed = head_scores(queries, key_block, query_pos, key_pos)
            shares = jnp.exp(scores - log_total[..., None])
            value_heads = value_block.reshape(size_now, queries.shape[1], queries.shape[2])
            key_heads = key_block.reshape(size_now, queries.shape[1], queries.shape[2])
            grad_shares = jnp.einsum(
                "qhd,khd->hqk", grad_att, value_heads, preferred_element_type=jnp.float32
            )
            grad_scores = (shares * (grad_shares - row_delta[..., None]) * scale_now).astype(
                jnp.bfloat16
            )
            grad_query = state_now[0] + jnp.einsum(
                "hqk,khd->qhd", grad_scores, key_heads, preferred_element_type=jnp.float32
            )
            return (grad_query,)

        return lax.fori_loop(0, key_part.shape[0] // size_now, inner_step, state_in)

    return back_step


def make_query_step(own_keys, own_values, own_pos, stats_all, pos_all, head_count, head_size):
    scale_now = head_size ** (-0.5)
    value_heads = own_values.reshape(own_values.shape[0], head_count, head_size)

    def query_step(state_in, pieces, start_row):
        query_part, grad_part = pieces
        size_now = block_size(query_part.shape[0])

        def inner_step(block_no, state_now):
            offset = block_no * size_now
            query_block = lax.dynamic_slice_in_dim(query_part, offset, size_now, 0).reshape(
                size_now, head_count, head_size
            )
            grad_block = lax.dynamic_slice_in_dim(grad_part, offset, size_now, 0).reshape(
                size_now, head_count, head_size
            )
            query_pos = lax.dynamic_slice_in_dim(pos_all, offset, size_now, 0)
            log_block = lax.dynamic_slice_in_dim(stats_all[0], offset, size_now, 0).T
            delta_block = lax.dynamic_slice_in_dim(stats_all[1], offset, size_now, 0).T
            scores, allowed = head_scores(query_block, own_keys, query_pos, own_pos)
            shares = jnp.exp(scores - log_block[..., None])
            grad_shares = jnp.einsum(
                "qhd,khd->hqk", grad_block, value_heads, preferred_element_type=jnp.float32
            )
            grad_scores = (shares * (grad_shares - delta_block[..., None]) * scale_now).astype(
                jnp.bfloat16
            )
            key_term = jnp.einsum(
                "hqk,qhd->khd", grad_scores, query_block, preferred_element_type=jnp.float32
            )
            value_term = jnp.einsum(
                "hqk,qhd->khd",
                shares.astype(jnp.bfloat16),
                grad_block,
                preferred_element_type=jnp.float32,
            )
            return (
                state_now[0] + key_term.reshape(key_term.shape[0], -1),
                state_now[1] + value_term.reshape(value_term.shape[0], -1),
            )

        return lax.fori_loop(0, query_part.shape[0] // size_now, inner_step, state_in)

    return query_step


def gather_forward(shards):
    return (
        lax.all_gather(shards[0], ("fsdp", "ctx"), axis=0, tiled=True),
        lax.all_gather(shards[1], ("fsdp", "ctx"), axis=0, tiled=True),
        lax.all_gather(shards[2], ("fsdp", "ctx"), axis=0, tiled=True),
        lax.all_gather(shards[3], ("fsdp", "ctx"), axis=0, tiled=True),
        lax.all_gather(shards[4], ("fsdp", "ctx"), axis=0, tiled=True),
        lax.all_gather(shards[5], ("fsdp", "ctx"), axis=0, tiled=True),
        lax.all_gather(shards[6], ("fsdp", "ctx"), axis=0, tiled=True),
        lax.all_gather(shards[7], ("fsdp", "ctx"), axis=0, tiled=True),
        lax.all_gather(shards[8], ("fsdp", "ctx"), axis=0, tiled=True),
    )


def scatter_grads(grad_terms):
    return (
        lax.psum_scatter(grad_terms[0], ("fsdp", "ctx"), scatter_dimension=0, tiled=True),
        lax.psum_scatter(grad_terms[1], ("fsdp", "ctx"), scatter_dimension=0, tiled=True),
        lax.psum_scatter(grad_terms[2], ("fsdp", "ctx"), scatter_dimension=0, tiled=True),
        lax.psum_scatter(grad_terms[3], ("fsdp", "ctx"), scatter_dimension=0, tiled=True),
        lax.psum_scatter(grad_terms[4], ("fsdp", "ctx"), scatter_dimension=0, tiled=True),
        lax.psum_scatter(grad_terms[5], ("fsdp", "ctx"), scatter_dimension=0, tiled=True),
        lax.psum_scatter(grad_terms[6], ("fsdp", "ctx"), scatter_dimension=0, tiled=True),
        lax.psum_scatter(grad_terms[7], ("fsdp", "ctx"), scatter_dimension=0, tiled=True),
        lax.psum_scatter(grad_terms[8], ("fsdp", "ctx"), scatter_dimension=0, tiled=True),
    )


def forward_layer(hidden, full_layer, first_values, context):
    prenorm, query_w, keys_w, values_w, outproj, midnorm, gates_w, upproj_w, downproj_w = full_layer
    cosine, sine, own_pos, pos_all = context
    rows_n, model_width = hidden.shape
    normed, inverse_a = row_norm(hidden)
    attn_in = (normed * prenorm.astype(jnp.float32)).astype(jnp.bfloat16)
    query_raw = jnp.dot(attn_in, query_w, preferred_element_type=jnp.float32)
    keys_raw = jnp.dot(attn_in, keys_w, preferred_element_type=jnp.float32)
    values_raw = jnp.dot(attn_in, values_w, preferred_element_type=jnp.float32)
    mixed = values_raw if first_values is None else 0.5 * values_raw + 0.5 * first_values
    queries = rotate(query_raw.reshape(rows_n, HEADS, HD), cosine, sine).astype(jnp.bfloat16)
    keys_flat = (
        rotate(keys_raw.reshape(rows_n, HEADS, HD), cosine, sine)
        .reshape(rows_n, model_width)
        .astype(jnp.bfloat16)
    )
    values_flat = mixed.astype(jnp.bfloat16)
    top_start = jnp.full((HEADS, rows_n), NEG_FILL, jnp.float32)
    total_start = jnp.zeros((HEADS, rows_n), jnp.float32)
    top_now, total_now = make_stats_step(
        queries,
        own_pos,
        pos_all,
        (top_start, total_start),
        lax.all_gather(keys_flat, "ctx", axis=0, tiled=True),
    )
    log_total = top_now + jnp.log(total_now)
    att_out = make_value_step(
        queries,
        log_total,
        own_pos,
        pos_all,
        jnp.zeros((rows_n, HEADS, HD), jnp.float32),
        (
            lax.all_gather(keys_flat, "ctx", axis=0, tiled=True),
            lax.all_gather(values_flat, "ctx", axis=0, tiled=True),
        ),
    )
    att_low = att_out.reshape(rows_n, model_width).astype(jnp.bfloat16)
    middle = hidden + jnp.dot(att_low, outproj, preferred_element_type=jnp.float32)
    normed_mid, inverse_b = row_norm(middle)
    mlp_in = (normed_mid * midnorm.astype(jnp.float32)).astype(jnp.bfloat16)
    gate_raw = jnp.dot(mlp_in, gates_w, preferred_element_type=jnp.float32)
    up_proj = jnp.dot(mlp_in, upproj_w, preferred_element_type=jnp.float32)
    inner_act = (jax.nn.silu(gate_raw) * up_proj).astype(jnp.bfloat16)
    result = middle + jnp.dot(inner_act, downproj_w, preferred_element_type=jnp.float32)
    saved = (
        hidden,
        normed,
        inverse_a,
        attn_in,
        queries,
        keys_flat,
        values_flat,
        log_total,
        att_out,
        att_low,
        normed_mid,
        inverse_b,
        mlp_in,
        gate_raw,
        up_proj,
        inner_act,
    )
    return (result, values_raw, saved)


def backward_layer(grad_out, full_layer, saved, value_extra, is_second, context):
    prenorm, query_w, keys_w, values_w, outproj, midnorm, gates_w, upproj_w, downproj_w = full_layer
    (
        hidden,
        normed,
        inverse_a,
        attn_in,
        queries,
        keys_flat,
        values_flat,
        log_total,
        att_out,
        att_low,
        normed_mid,
        inverse_b,
        mlp_in,
        gate_raw,
        up_proj,
        inner_act,
    ) = saved
    cosine, sine, own_pos, pos_all = context
    rows_n, model_width = hidden.shape
    grad_low = grad_out.astype(jnp.bfloat16)
    grad_down = left_product(inner_act, grad_low)
    grad_inner = right_product(grad_low, downproj_w)
    sigma_gate = jax.nn.sigmoid(gate_raw)
    grad_gate = (grad_inner * up_proj * sigma_gate * (1.0 + gate_raw * (1.0 - sigma_gate))).astype(
        jnp.bfloat16
    )
    grad_up = (grad_inner * gate_raw * sigma_gate).astype(jnp.bfloat16)
    grad_gates = left_product(mlp_in, grad_gate)
    grad_upproj = left_product(mlp_in, grad_up)
    grad_mlp = right_product(grad_gate, gates_w) + right_product(grad_up, upproj_w)
    grad_midnorm = jnp.sum(grad_mlp * normed_mid, axis=0)
    grad_middle = grad_out + norm_back(
        grad_mlp * midnorm.astype(jnp.float32), normed_mid, inverse_b
    )
    branch_low = grad_middle.astype(jnp.bfloat16)
    grad_outproj = left_product(att_low, branch_low)
    grad_att = right_product(branch_low, outproj).astype(jnp.bfloat16).reshape(rows_n, HEADS, HD)
    row_delta = jnp.sum(grad_att.astype(jnp.float32) * att_out, axis=-1).T
    query_start = jnp.zeros((rows_n, HEADS, HD), jnp.float32)
    state_start = (query_start,)
    back_fn = make_back_step(queries, grad_att, log_total, row_delta, own_pos, pos_all)
    state_out = back_fn(
        state_start,
        (
            lax.all_gather(keys_flat, "ctx", axis=0, tiled=True),
            lax.all_gather(values_flat, "ctx", axis=0, tiled=True),
        ),
        jnp.int32(0),
    )
    grad_qr = state_out[0]
    stats_all = (
        lax.all_gather(log_total.T, "ctx", axis=0, tiled=True),
        lax.all_gather(row_delta.T, "ctx", axis=0, tiled=True),
    )
    query_fn = make_query_step(keys_flat, values_flat, own_pos, stats_all, pos_all, HEADS, HD)
    flat_start = jnp.zeros((rows_n, model_width), jnp.float32)
    grad_kr, grad_mix = query_fn(
        (flat_start, flat_start),
        (
            lax.all_gather(queries.reshape(rows_n, model_width), "ctx", axis=0, tiled=True),
            lax.all_gather(grad_att.reshape(rows_n, model_width), "ctx", axis=0, tiled=True),
        ),
        jnp.int32(0),
    )
    grad_query = unrotate(grad_qr, cosine, sine).reshape(rows_n, model_width).astype(jnp.bfloat16)
    grad_keys = (
        unrotate(grad_kr.reshape(rows_n, HEADS, HD), cosine, sine)
        .reshape(rows_n, model_width)
        .astype(jnp.bfloat16)
    )
    if is_second:
        grad_values = (0.5 * grad_mix).astype(jnp.bfloat16)
        passed_on = 0.5 * grad_mix
    else:
        grad_values = (grad_mix + value_extra).astype(jnp.bfloat16)
        passed_on = None
    grad_query_w = left_product(attn_in, grad_query)
    grad_keys_w = left_product(attn_in, grad_keys)
    grad_values_w = left_product(attn_in, grad_values)
    grad_attn = (
        right_product(grad_query, query_w)
        + right_product(grad_keys, keys_w)
        + right_product(grad_values, values_w)
    )
    grad_prenorm = jnp.sum(grad_attn * normed, axis=0)
    grad_hidden = grad_middle + norm_back(
        grad_attn * prenorm.astype(jnp.float32), normed, inverse_a
    )
    grad_terms = (
        grad_prenorm,
        grad_query_w,
        grad_keys_w,
        grad_values_w,
        grad_outproj,
        grad_midnorm,
        grad_gates,
        grad_upproj,
        grad_down,
    )
    return (grad_hidden, grad_terms, passed_on)


def local(
    tokens,
    cotangent,
    pair_of,
    prenorm_one,
    query_one,
    keys_one,
    values_one,
    outproj_one,
    midnorm_one,
    gates_one,
    upproj_one,
    downproj_one,
    prenorm_two,
    query_two,
    keys_two,
    values_two,
    outproj_two,
    midnorm_two,
    gates_two,
    upproj_two,
    downproj_two,
):
    seq_dev = tokens.shape[1]
    model_width = tokens.shape[2]
    pos_all = storage_positions(pair_of, seq_dev)
    own_pos = lax.dynamic_slice_in_dim(pos_all, lax.axis_index("ctx") * seq_dev, seq_dev, 0)
    cosine, sine = rope_tables(own_pos, HD)
    context = (cosine, sine, own_pos, pos_all)
    layer_shards = [
        (
            prenorm_one,
            query_one,
            keys_one,
            values_one,
            outproj_one,
            midnorm_one,
            gates_one,
            upproj_one,
            downproj_one,
        ),
        (
            prenorm_two,
            query_two,
            keys_two,
            values_two,
            outproj_two,
            midnorm_two,
            gates_two,
            upproj_two,
            downproj_two,
        ),
    ]
    hidden = tokens.reshape(seq_dev, model_width).astype(jnp.float32)
    first_values = None
    kept_full = []
    kept_saved = []
    for layer_no in range(2):
        full_layer = gather_forward(layer_shards[layer_no])
        hidden, values_raw, saved = forward_layer(hidden, full_layer, first_values, context)
        if layer_no == 0:
            first_values = values_raw
        kept_full.append(full_layer)
        kept_saved.append(saved)
    output = hidden.astype(jnp.bfloat16).reshape(1, seq_dev, model_width)
    grad_now = cotangent.reshape(seq_dev, model_width).astype(jnp.float32)
    value_extra = None
    layer_grads = [None, None]
    for layer_no in (1, 0):
        full_layer = kept_full[layer_no]
        grad_now, grad_terms, passed_on = backward_layer(
            grad_now, full_layer, kept_saved[layer_no], value_extra, layer_no == 1, context
        )
        if layer_no == 1:
            value_extra = passed_on
        layer_grads[layer_no] = scatter_grads(grad_terms)
    tokens_grad = grad_now.astype(jnp.bfloat16).reshape(1, seq_dev, model_width)
    first_grads = layer_grads[0]
    second_grads = layer_grads[1]
    return (
        output,
        tokens_grad,
        first_grads[0],
        first_grads[1],
        first_grads[2],
        first_grads[3],
        first_grads[4],
        first_grads[5],
        first_grads[6],
        first_grads[7],
        first_grads[8],
        second_grads[0],
        second_grads[1],
        second_grads[2],
        second_grads[3],
        second_grads[4],
        second_grads[5],
        second_grads[6],
        second_grads[7],
        second_grads[8],
    )


ROWS = 128
BF = jnp.bfloat16
F32 = jnp.float32
MESH = pl.DeviceIdType.MESH
VMEM_SPACE = pltpu.VMEM
HBM_SPACE = pltpu.HBM


def flip(value, weight):
    return value + weight * (1 - 2 * ((value // weight) % 2))


def to_device(f, c):
    return {"fsdp": f, "ctx": c}


def remote(src, dst, send_sem, recv_sem, target):
    return pltpu.make_async_remote_copy(
        src_ref=src,
        dst_ref=dst,
        send_sem=send_sem,
        recv_sem=recv_sem,
        device_id=to_device(*target),
        device_id_type=MESH,
    )


def arrived(ref, sem, target):
    remote(ref, ref, sem, sem, target).wait_recv()


def plane_place():
    f = lax.axis_index("fsdp")
    c = lax.axis_index("ctx")
    return f, c, (c // 2) % 2, c // 4


def row_peers(f, c, z):
    return [(f, c + 4 * ((z + i) % 4 - z)) for i in range(1, 4)]


HALF = ROWS // 2
ODD = 8


class Plane:
    def __init__(self, place):
        self.f, self.c, self.y, self.z = place
        self.mirrored = self.z // 2
        self.sign = 1 - 2 * self.mirrored
        self.own = self.z * (3 - self.z) // 2
        self.across = (self.f, flip(self.c, 2))

    def chip(self, near):
        return self.f, self.c + 4 * self.sign * (near - self.own)

    def at(self, near):
        return near + self.mirrored * (3 - 2 * near)

    def slot(self, half, near):
        return 4 * half + self.at(near)

    def both_kinds(self, run):
        @pl.when(self.own == 1)
        def _():
            run(True)

        @pl.when(self.own == 0)
        def _():
            run(False)


def emit(copy, live):
    if live:
        copy.start()
    else:
        copy.wait_send()


class Reduce(Plane):
    def __init__(self, place, product, bufs, sems):
        super().__init__(place)
        self.product = product
        self.sy, self.ry, self.acc, self.pb, self.su, self.sd, self.rb, self.ra = bufs
        self.ys, self.yr, self.us, self.ds, self.br, self.ar = sems

    def y_copy(self, slot):
        return remote(self.sy.at[slot], self.ry.at[slot], self.ys.at[slot], self.yr.at[slot], self.across)

    def got_y(self, slot):
        self.y_copy(slot).wait_recv()
        return self.ry[slot].astype(F32)

    def got(self, first, slot):
        buf, sem = (self.rb, self.br) if first else (self.ra, self.ar)
        arrived(buf.at[slot], sem.at[slot], self.across)
        return buf[slot].astype(F32)

    def pass_on(self, value, upward, slot, target, first, there=None):
        there = slot if there is None else there
        src, send = (self.su, self.us) if upward else (self.sd, self.ds)
        dst, sem = (self.rb, self.br) if first else (self.ra, self.ar)
        if value is not None:
            src[slot] = value.astype(BF)
        copy = remote(src.at[slot], dst.at[there], send.at[slot], sem.at[there], self.chip(target))
        emit(copy, value is not None)

    def order(self, step):
        inner = jnp.where(step == 0, 3, jnp.where(step == 1, 0, 4 - step))
        near = jnp.where(self.own == 1, inner, 3 - step)
        return near, near + self.mirrored * (3 - 2 * near)

    def products(self):
        def other_row(step, carry):
            near, block = self.order(step)
            value = self.product(2 * block + 1 - self.y)
            self.sy[block] = value[:HALF].astype(BF)
            self.y_copy(block).start()
            self.pb[block] = value[HALF:]

            @pl.when((near == 1) | (near == 2))
            def _():
                self.sy[4 + block] = value[HALF:].astype(BF)
                self.y_copy(4 + block).start()

            return carry

        def own_row(step, carry):
            near, block = self.order(step)
            value = self.product(2 * block + self.y)
            self.acc[block] = value[:HALF]
            self.acc[4 + block] = value[HALF:]

            @pl.when((self.own == 0) & (near == 3))
            def _():
                self.pass_on(value[HALF:], True, 4 + block, 1, True)

            @pl.when((self.own == 1) & (near == 0))
            def _():
                self.pass_on(value[HALF:], False, 4 + block, 0, False)

            return carry

        lax.fori_loop(0, 4, other_row, 0)
        self.both_kinds(lambda inner: self.odd(inner, True))
        lax.fori_loop(0, 4, own_row, 0)

    def odd(self, inner, live):
        far = self.pb[self.at(3)] if live else None
        if inner:
            self.pass_on(far, True, ODD, 3, True)
            self.pass_on(self.pb[self.at(0)] if live else None, False, ODD, 0, False)
        else:
            self.pass_on(far, True, ODD, 3, False, ODD + 1)

    def relay(self, half, near, inner, live, plain=False):
        slot = self.slot(half, near)
        upward = not inner or near != 0
        value = None
        if live:
            value = self.acc[slot]
            if not plain:
                value = value + self.got_y(slot)
            if inner and upward:
                value = value + self.got(True, slot)
        if not inner:
            self.pass_on(value, True, slot, 1, True)
        elif near == 0:
            self.pass_on(value, False, slot, 0, False)
        else:
            self.pass_on(value, True, slot, near, near == 3)

    def relays(self, inner, live):
        if inner:
            if not live:
                self.relay(1, 0, inner, live, True)
            self.relay(1, 3, inner, live, True)
            for half, near in ((0, 3), (0, 0), (0, 2), (1, 2)):
                self.relay(half, near, inner, live)
            return
        if not live:
            self.relay(1, 3, inner, live, True)
        for half, near in ((0, 3), (0, 2), (1, 2), (0, 1), (1, 1)):
            self.relay(half, near, inner, live)
        slot = self.slot(1, 0)
        if live:
            odd = self.pb[self.at(0)] + self.got(False, ODD) + self.got(True, ODD) + self.got(False, ODD + 1)
            self.sy[slot] = odd.astype(BF)
        emit(self.y_copy(slot), live)

    def own_sum(self, half):
        slot = self.slot(half, self.own)
        return self.acc[slot] + self.got_y(slot) + self.got(True, slot) + self.got(False, slot)

    def finish(self):
        for half, near in ((0, 0), (0, 1), (0, 2), (0, 3), (1, 1), (1, 2)):
            self.y_copy(self.slot(half, near)).wait_send()

        def left(inner):
            self.odd(inner, False)
            self.relays(inner, False)

        self.both_kinds(left)


class Gather(Plane):
    def __init__(self, place, full, sems):
        super().__init__(place)
        self.full = full
        self.ys, self.yr, self.us, self.ds, self.zr = sems

    def rows(self, half, near, side):
        start = (self.at(near) * 2 + side) * ROWS + half * HALF
        return self.full.at[pl.ds(pl.multiple_of(start, HALF), HALF)]

    def to_row(self, part, sem, slot, target, live):
        emit(remote(part, part, sem, self.zr.at[slot], self.chip(target)), live)

    def to_other_row(self, half, near, live):
        part = self.rows(half, near, self.y)
        slot = self.slot(half, near)
        emit(remote(part, part, self.ys.at[slot], self.yr.at[slot], self.across), live)

    def send_own(self, half, live=True):
        part = self.rows(half, self.own, self.y)
        slot = self.slot(half, self.own)
        self.to_other_row(half, self.own, live)
        self.to_row(part, self.ds.at[slot], slot, 1 - self.own, live)
        self.to_row(part, self.us.at[slot], slot, 2, live)

    def take(self, half, near, inner, live):
        part = self.rows(half, near, self.y)
        slot = self.slot(half, near)
        if live:
            arrived(part, self.zr.at[slot], self.across)
        if half == 0 or near in (1, 2):
            self.to_other_row(half, near, live)
        if inner and near in (2, 3):
            self.to_row(part, self.ds.at[slot], slot, 0, live)

    def odd_slot(self, near):
        return ODD + self.at(near) // 3

    def take_odd(self, near):
        arrived(self.rows(1, near, 1 - self.y), self.zr.at[self.odd_slot(near)], self.across)

    def got_y(self, half, near):
        arrived(self.rows(half, near, 1 - self.y), self.yr.at[self.slot(half, near)], self.across)

    def forward(self, half, inner, live):
        others = (2, 3, 0) if inner else (1, 2, 3)
        if half == 1 and not inner:
            part = self.rows(1, 0, 1 - self.y)
            slot = self.odd_slot(0)
            if live:
                self.got_y(1, 0)
            self.to_row(part, self.us.at[8], slot, 3, live)
            self.to_row(part, self.us.at[9], slot, 2, live)
            self.to_row(part, self.ds.at[8], slot, 1, live)
        for near in others:
            self.take(half, near, inner, live)
        if half == 1 and inner and live:
            self.take_odd(0)

    def pass_half(self, half):
        self.both_kinds(lambda inner: self.forward(half, inner, True))
        if half == 1:
            self.take_odd(3)
            for near in range(4):
                self.got_y(0, near)
            for near in (1, 2):
                self.got_y(1, near)

    def finish(self):
        self.send_own(0, False)
        self.send_own(1, False)

        def left(inner):
            self.forward(0, inner, False)
            self.forward(1, inner, False)

        self.both_kinds(left)


def exchange(place, product, settle, full, scratch, more=None, rows=None):
    f, c, y, z = place
    if more is None:
        greet(row_peers(f, c, z) + [(f, flip(c, 2))])
    else:
        peers, sibling, twin = chip_peers(f, c)
        greet(peers + [sibling, twin])
    own = (z * 2 + y) * ROWS
    reduce = Reduce(place, product, scratch[:8], scratch[8:14])
    gather = None if full is None else Gather(place, full, scratch[14:19])
    if rows is not None:
        full[pl.ds(pl.multiple_of(own, ROWS), ROWS), :] = rows
    reduce.products()
    if more is not None:
        more.first()
        more.early()
    reduce.both_kinds(lambda inner: reduce.relays(inner, True))
    if rows is not None:
        gather.send_own(0)
        gather.send_own(1)
    if more is not None:
        more.second()
    for half in range(2):
        new = settle(half, reduce.own_sum(half))
        if gather is not None and rows is None:
            full[pl.ds(pl.multiple_of(own + half * HALF, HALF), HALF), :] = new
            gather.send_own(half)
        if more is not None and half == 0:
            more.third()
    if gather is not None:
        gather.pass_half(0)
    if more is not None:
        more.fourth()
    if gather is not None:
        gather.pass_half(1)
        gather.finish()
    reduce.finish()
    if more is not None:
        more.finish()


def half_rows(half):
    return pl.ds(half * HALF, HALF)


def norm_rows(hidden):
    return lax.rsqrt(jnp.mean(hidden * hidden, axis=-1, keepdims=True) + NORM_EPS)


def make_product(left_ref, right_ref, transposed, lanes=None):
    dims = (((1,), (1,)), ((), ())) if transposed else (((1,), (0,)), ((), ()))

    def product(block):
        rows = left_ref[pl.ds(pl.multiple_of(block * ROWS, ROWS), ROWS), :]
        right = right_ref[...] if lanes is None else right_ref[:, lanes[0] : lanes[1]]
        return lax.dot_general(rows, right, dims, preferred_element_type=F32)

    return product


def forward_kernel(row, left_ref, right_ref, res_ref, gain_ref, new_ref, full_ref, *scratch):
    def settle(half, total):
        hidden = res_ref[half_rows(half), :].astype(F32) + total
        new_ref[half_rows(half), :] = hidden
        return (hidden * norm_rows(hidden) * gain_ref[row : row + 1, :]).astype(BF)

    exchange(plane_place(), make_product(left_ref, right_ref, False), settle, full_ref, scratch)


def turn_kernel(left_ref, right_ref, res_ref, cot_ref, out_ref, full_ref, *scratch):
    def settle(half, total):
        out_ref[half_rows(half), :] = (res_ref[half_rows(half), :] + total).astype(BF)
        return cot_ref[half_rows(half), :]

    product = make_product(left_ref, right_ref, False)
    exchange(plane_place(), product, settle, full_ref, scratch)


def back_rows(total, grad, hidden, gain):
    inverse = norm_rows(hidden)
    normed = hidden * inverse
    scaled = total * gain
    mean = jnp.mean(scaled * normed, axis=-1, keepdims=True)
    return grad + inverse * (scaled - normed * mean)


def comm_call(kernel, outs, ident, args, gathers, name, more=()):
    width = 1024
    scratch = []
    for count, kind in ((8, BF), (8, BF), (8, F32), (4, F32), (9, BF), (9, BF), (9, BF), (10, BF)):
        scratch.append(pltpu.VMEM((count, HALF, width), kind))
    scratch += [pltpu.SemaphoreType.DMA((10,))] * 6
    if gathers:
        scratch += [pltpu.SemaphoreType.DMA((10,))] * 5
    scratch += list(more)
    spec = pl.BlockSpec(memory_space=VMEM_SPACE)
    return pl.pallas_call(
        kernel,
        out_shape=[jax.ShapeDtypeStruct(*o) for o in outs],
        in_specs=[spec] * len(args),
        out_specs=[spec] * len(outs),
        scratch_shapes=scratch,
        compiler_params=pltpu.CompilerParams(
            collective_id=ident, has_side_effects=True, vmem_limit_bytes=(24 if more else 14) * 1024 * 1024
        ),
        name=name,
    )(*args)


def chip_peers(f, c):
    chip, core = c // 2, c % 2
    return [(f, 2 * ((chip + i) % 8) + core) for i in range(1, 8)], (f, flip(c, 1)), (1 - f, c)


def greet(targets):
    barrier = pltpu.get_barrier_semaphore()
    for target in targets:
        pl.semaphore_signal(barrier, inc=1, device_id=to_device(*target), device_id_type=MESH)
    pl.semaphore_wait(barrier, len(targets))


class OutRows:
    def __init__(self, place, shard, out, sems):
        self.f, self.c, self.y, _ = place
        self.core = self.c % 2
        _, self.sibling, self.twin = chip_peers(self.f, self.c)
        self.near = (self.f, flip(self.c, 2))
        self.shard, self.out = shard, out
        self.ws, self.wr = sems
        self.home = self.y == self.f

    def near_copy(self):
        part = 2 * self.y + self.core
        return remote(self.shard, self.out.at[part], self.ws.at[0], self.wr.at[0], self.near)

    def pair_copies(self, first, target):
        parts = [self.out.at[self.core], self.out.at[2 + self.core]]
        return [
            remote(p, p, self.ws.at[first + n], self.wr.at[first + n], target) for n, p in enumerate(parts)
        ]

    def first(self):
        @pl.when(self.home)
        def _():
            self.out[2 * self.y + self.core] = self.shard[...]

        @pl.when(jnp.logical_not(self.home))
        def _():
            self.near_copy().start()

    def second(self):
        @pl.when(self.home)
        def _():
            self.near_copy().wait_recv()
            for copy in self.pair_copies(1, self.twin):
                copy.start()

    def third(self):
        @pl.when(jnp.logical_not(self.home))
        def _():
            for copy in self.pair_copies(1, self.twin):
                copy.wait_recv()

        for copy in self.pair_copies(3, self.sibling):
            copy.start()

    def finish(self):
        for copy in self.pair_copies(3, self.sibling):
            copy.wait()

        @pl.when(self.home)
        def _():
            for copy in self.pair_copies(1, self.twin):
                copy.wait_send()

        @pl.when(jnp.logical_not(self.home))
        def _():
            self.near_copy().wait_send()


class Sender:
    def __init__(self, place):
        self.f, self.c, self.y, _ = place
        self.chip, self.core = self.c // 2, self.c % 2
        self.peers, self.sibling, self.twin = chip_peers(self.f, self.c)
        self.sent = []

    def send(self, src, dst, send_sem, recv_sem, target):
        copy = remote(src, dst, send_sem, recv_sem, target)
        copy.start()
        self.sent.append(copy)
        return copy


class Spread(Sender):
    def __init__(self, place, a, r, sems):
        super().__init__(place)
        self.a, self.r = a, r
        self.ds, self.dr, self.xs, self.xr, self.ss, self.sr = sems
        self.direct, self.crossed, self.inner = {}, {}, []

    def forward(self, part, n):
        self.crossed[n] = self.send(part[0], part[1], self.xs.at[n], self.xr.at[n], self.twin)

    def to_sibling(self, part, n):
        self.inner.append(self.send(part[0], part[1], self.ss.at[n], self.sr.at[n], self.sibling))

    def first(self):
        mine = self.r.at[self.f, self.chip, self.core]
        own = self.a.at[self.chip]
        self.forward((own, mine), 0)
        for i in range(1, 8):
            t = (self.chip + i) % 8
            self.direct[i] = self.send(self.a.at[t], mine, self.ds.at[i], self.dr.at[i], self.peers[i - 1])
        self.r[self.f, self.chip, self.core] = self.a[self.chip]
        self.to_sibling((own, mine), 0)

    def second(self):
        for i in range(1, 8):
            self.direct[i].wait_recv()
            part = self.r.at[self.f, (self.chip + 8 - i) % 8, self.core]
            self.forward((part, part), i)
            self.to_sibling((part, part), i)

    def third(self):
        for i in range(8):
            self.crossed[i].wait_recv()
            part = self.r.at[1 - self.f, (self.chip + 8 - i) % 8, self.core]
            self.to_sibling((part, part), 8 + i)

    def finish(self):
        for copy in self.inner:
            copy.wait_recv()
        for copy in self.sent:
            copy.wait_send()


class Share(Sender):
    def __init__(self, place, tables, downs, out, sems):
        super().__init__(place)
        self.tables, self.downs = tables, downs
        self.xs, self.xr, self.ss, self.sr, *more = sems
        self.out = OutRows(place, *out, more) if out else None

    def places(self, f):
        found = [r.at[f, :, self.core] for _, r in self.tables]
        return found + [d.at[2 * f + self.core] for _, d in self.downs]

    def first(self):
        self.crossed, self.inner = [], []
        sources = [s for s, _ in self.tables] + [n for n, _ in self.downs]
        for n, (src, dst) in enumerate(zip(sources, self.places(self.f))):
            self.crossed.append(self.send(src, dst, self.xs.at[n], self.xr.at[n], self.twin))
            self.inner.append(self.send(src, dst, self.ss.at[n], self.sr.at[n], self.sibling))
        if self.out:
            self.out.first()

    def early(self):
        pass

    def second(self):
        if self.out:
            self.out.second()

    def third(self):
        pass

    def fourth(self):
        for src, r in self.tables:
            for j in range(8):
                r[self.f, j, self.core] = src[j]
        for src, d in self.downs:
            d[2 * self.f + self.core] = src[...]
        count = len(self.crossed)
        for n, part in enumerate(self.places(1 - self.f)):
            self.crossed[n].wait_recv()
            self.inner.append(
                self.send(part, part, self.ss.at[count + n], self.sr.at[count + n], self.sibling)
            )
        if self.out:
            self.out.third()

    def finish(self):
        for copy in self.inner:
            copy.wait_recv()
        for copy in self.sent:
            copy.wait_send()
        if self.out:
            self.out.finish()


def start_leg(parts, peers, chip, sends, receives):
    copies = []
    for n, (src, dst) in enumerate(parts):
        for i in range(1, 8):
            sem = 8 * n + i
            part = src.at[(chip + i) % 8]
            copies.append(remote(part, dst.at[chip], sends.at[sem], receives.at[sem], peers[i - 1]))
            copies[-1].start()
        dst[chip] = src[chip]
    return copies


def turn_row(row):
    size = row.shape[1]
    same = lax.broadcasted_iota(jnp.int32, (size, size), 0) == lax.broadcasted_iota(jnp.int32, (size, size), 1)
    return jnp.sum(jnp.where(same, row, 0.0), axis=1, keepdims=True)


def turn_column(column):
    size = column.shape[0]
    same = lax.broadcasted_iota(jnp.int32, (size, size), 0) == lax.broadcasted_iota(jnp.int32, (size, size), 1)
    return jnp.sum(jnp.where(same, column, 0.0), axis=0, keepdims=True)


def pack_heads(query, keys, values, a):
    for chip in range(8):
        pair = 4 * (chip % 2) + chip // 2
        for n, w in enumerate((query, keys, values)):
            a[chip, :, 128 * n : 128 * n + 128] = w[:, 128 * pair : 128 * pair + 128]


def pack_units(gates, upproj, block, a):
    rows, units = gates.shape
    each = units // 32
    empty = jnp.zeros((rows, block - each), F32)
    for chip in range(8):
        for n, w in enumerate((gates, upproj)):
            parts = []
            for i in range(4):
                owner = 16 * (i // 2) + 2 * chip + i % 2
                parts += [w[:, each * owner : each * owner + each].astype(F32), empty]
            at = 4 * block * n
            a[chip, :, at : at + 4 * block] = jnp.concatenate(parts, axis=-1).astype(BF)


def pack_down(down, dn):
    each = down.shape[0]
    dn[:each] = down[...]
    dn[each:] = jnp.zeros((dn.shape[0] - each, down.shape[1]), BF)


def begin_kernel(tok, *refs):
    given, (full, r, o, gains, u1, h2, u2, n1, n2), shards = refs[:18], refs[18:27], refs[27:45]
    ones, twos = shards[:9], shards[9:]
    loads, a, *sems = refs[45:]
    copies = [pltpu.make_async_copy(src, dst, loads.at[n]) for n, (src, dst) in enumerate(zip(given, shards))]
    soon = (0, 1, 2, 3, 4, 5, 9, 14)
    for n in soon:
        copies[n].start()
    for n in range(18):
        if n not in soon:
            copies[n].start()
    place = plane_place()
    f, c, y, z = place
    peers, sibling, twin = chip_peers(f, c)
    start = (z * 2 + y) * ROWS
    full[pl.ds(pl.multiple_of(start, ROWS), ROWS), :] = tok[...]
    for n in soon:
        copies[n].wait()
    pack_heads(ones[1], ones[2], ones[3], a)
    lane = lax.broadcasted_iota(jnp.int32, (tok.shape[1] // 32, 128), 1)
    riders = jnp.zeros(lane.shape, F32)
    for n, gain in enumerate((ones[0], ones[5], twos[0], twos[5])):
        riders = jnp.where(lane == n, turn_row(gain[...].astype(F32)), riders)
    for chip in range(8):
        a[chip, :, 384:] = riders.astype(BF)
    greet(peers + [sibling, twin])

    gather = Gather(place, full, sems[:5])
    spread = Spread(place, a, r, sems[5:11])
    out = OutRows(place, ones[4], o, sems[11:])
    gather.send_own(0)
    spread.first()
    out.first()
    gather.send_own(1)
    for n in range(18):
        if n not in soon:
            copies[n].wait()
    pack_units(ones[6], ones[7], n1.shape[0], u1)
    gather.pass_half(0)
    spread.second()
    out.second()
    pack_heads(twos[1], twos[2], twos[3], h2)
    pack_units(twos[6], twos[7], n1.shape[0], u2)
    pack_down(ones[8], n1)
    pack_down(twos[8], n2)
    gather.pass_half(1)
    spread.third()
    out.third()
    gather.finish()
    spread.finish()
    out.finish()
    count = tok.shape[1]
    columns = r[:, :, :, :, 384:].reshape(count, 128)
    pick = lax.broadcasted_iota(jnp.int32, (8, 128), 0) == lax.broadcasted_iota(jnp.int32, (8, 128), 1)
    gains[...] = lax.dot_general(jnp.where(pick, 1.0, 0.0).astype(BF), columns, NT, preferred_element_type=F32)


def begin_call(tok, shards, block):
    rows, width = shards[1].shape
    spec = pl.BlockSpec(memory_space=VMEM_SPACE)
    wide = 8 * block
    outs = [
        ((8 * ROWS, width), BF), ((2, 8, 2, rows, 512), BF), ((4, rows, width), BF), ((8, width), F32),
        ((8, rows, wide), BF), ((8, rows, 384), BF), ((8, rows, wide), BF), ((block, width), BF), ((block, width), BF),
    ]
    counts = [(10,)] * 5 + [(8,), (8,), (8,), (8,), (16,), (16,), (5,), (5,)]
    return pl.pallas_call(
        begin_kernel,
        out_shape=[jax.ShapeDtypeStruct(*o) for o in outs],
        in_specs=[spec] + [pl.BlockSpec(memory_space=HBM_SPACE)] * 18,
        out_specs=[spec] * len(outs),
        scratch_shapes=[pltpu.VMEM(s.shape, s.dtype) for s in shards]
        + [pltpu.SemaphoreType.DMA((18,)), pltpu.VMEM((8, rows, 512), BF)]
        + [pltpu.SemaphoreType.DMA(n) for n in counts],
        compiler_params=pltpu.CompilerParams(
            collective_id=9, has_side_effects=True, vmem_limit_bytes=10 * 1024 * 1024
        ),
        name="begin",
    )(tok, *shards)


def middle_kernel(row, count, left_ref, right_ref, res_ref, gain_ref, *refs):
    given = 2 * count
    ins, refs = refs[:given], refs[given:]
    outs = 2 + count + 1 + (count == 2)
    new_ref, full_ref, *results = refs[:outs]
    scratch = refs[outs:]

    def settle(half, total):
        hidden = res_ref[half_rows(half), :].astype(F32) + total
        new_ref[half_rows(half), :] = hidden
        return (hidden * norm_rows(hidden) * gain_ref[row : row + 1, :]).astype(BF)

    tables = list(zip(ins[:count], results[:count]))
    downs = [(ins[count], results[count])]
    out = (ins[3], results[3]) if count == 2 else None
    place = plane_place()
    share = Share(place, tables, downs, out, scratch[19:])
    exchange(place, make_product(left_ref, right_ref, False), settle, full_ref, scratch, share)


def share_shapes(rows, width, block, widths):
    outs = [((2, 8, 2, rows, w), BF) for w in widths] + [((4, block, width), BF)]
    if len(widths) == 2:
        outs += [((4, rows, width), BF)]
    return outs, [pltpu.SemaphoreType.DMA(n) for n in ((3,), (3,), (6,), (6,), (5,), (5,))]


class Collect:
    def __init__(self, place, ins, results, scratch, final):
        self.f, self.c, self.y, _ = place
        self.chip, self.core = self.c // 2, self.c % 2
        self.peers, self.sibling, self.twin = chip_peers(self.f, self.c)
        self.near = (self.f, flip(self.c, 2))
        self.final = final
        self.g, self.h = ins
        self.out, self.oh = results
        self.sb, self.xb, self.xt, self.ut, self.sh, self.xh, self.th, *near = scratch[:-6]
        self.ss, self.sr, self.xs, self.xr, self.ps, self.pr = scratch[-6:]
        self.crosses_near = bool(near)
        if near:
            self.yo, self.yt = near
        self.home = self.y == self.f

    def inner_copy(self, n):
        other = 1 - self.core
        if n == 2:
            src, dst = self.h.at[:, other], self.sh
        else:
            part = 8 * ((1 - self.f) if n == 0 else self.f)
            src, dst = self.g.at[pl.ds(part, 8), other], self.sb.at[pl.ds(part, 8)]
        return remote(src, dst, self.ss.at[n], self.sr.at[n], self.sibling)

    def target(self, i):
        return (self.chip + i + 1) % 8

    def cross_copy(self, i):
        t = self.target(i)
        return remote(self.xt.at[t], self.xb.at[t], self.xs.at[i], self.xr.at[i], self.twin)

    def direct_copy(self, i):
        src = self.ut.at[self.target(i)]
        return remote(src, self.out.at[self.chip], self.ps.at[i], self.pr.at[i], self.peers[i])

    def twin_copy(self):
        return remote(self.th, self.xh, self.xs.at[8], self.xr.at[8], self.twin)

    def near_copy(self):
        return remote(self.yt, self.yo, self.xs.at[9], self.xr.at[9], self.near)

    def first(self):
        for n in range(3):
            self.inner_copy(n).start()

    def cross(self):
        f, core = self.f, self.core
        self.inner_copy(0).wait_recv()
        for i in range(8):
            t = self.target(i)
            at = (1 - f) * 8 + t
            self.xt[t] = (self.g[at, core].astype(F32) + self.sb[at].astype(F32)).astype(BF)
            self.cross_copy(i).start()
        self.inner_copy(2).wait_recv()
        if not self.crosses_near:
            self.th[...] = (self.h[1 - f, core].astype(F32) + self.sh[1 - f].astype(F32)).astype(BF)
            self.twin_copy().start()
            return
        for side in range(2):
            self.th[side] = (self.h[side, core].astype(F32) + self.sh[side].astype(F32)).astype(BF)

        @pl.when(jnp.logical_not(self.home))
        def _():
            self.twin_copy().start()

    def add_up(self):
        f, core = self.f, self.core
        self.inner_copy(1).wait_recv()
        for i in range(8):
            t = self.target(i)
            at = f * 8 + t
            self.cross_copy(i).wait_recv()
            total = self.g[at, core].astype(F32) + self.sb[at].astype(F32) + self.xb[t].astype(F32)
            if not self.final:
                self.out[t] = total.astype(BF)
            elif i < 7:
                self.ut[t] = total.astype(BF)
                self.direct_copy(i).start()
            else:
                self.out[self.chip] = total.astype(BF)
        if not self.crosses_near:
            self.twin_copy().wait_recv()
            self.oh[...] = self.h[f, core].astype(F32) + self.sh[f].astype(F32) + self.xh[...].astype(F32)
            return

        @pl.when(self.home)
        def _():
            self.twin_copy().wait_recv()
            y = self.y
            self.oh[...] = self.th[y].astype(F32) + self.xh[y].astype(F32)
            self.yt[...] = (self.th[1 - y].astype(F32) + self.xh[1 - y].astype(F32)).astype(BF)
            self.near_copy().start()

    def early(self):
        if self.final:
            self.cross()

    def second(self):
        if self.final:
            self.add_up()
        else:
            self.cross()

    def third(self):
        pass

    def fourth(self):
        if not self.final:
            self.add_up()

    def finish(self):
        if self.crosses_near:

            @pl.when(self.home)
            def _():
                self.near_copy().wait_send()

            @pl.when(jnp.logical_not(self.home))
            def _():
                self.near_copy().wait_recv()
                self.oh[...] = self.yo[...].astype(F32)
                self.twin_copy().wait_send()
        else:
            self.twin_copy().wait_send()
        for i in range(7 if self.final else 0):
            self.direct_copy(i).wait()
        for i in range(8):
            self.cross_copy(i).wait_send()
        for n in range(3):
            self.inner_copy(n).wait_send()


def collect_shapes(rows, wide, block, width, crosses_near):
    results = [((8, rows, wide), BF), ((block, width), F32)]
    buffers = [(16, rows, wide), (8, rows, wide), (8, rows, wide), (8, rows, wide), (2, block, width)]
    if crosses_near:
        buffers += [(2, block, width), (2, block, width), (block, width), (block, width)]
    else:
        buffers += [(block, width), (block, width)]
    counts = ((3,), (3,), (10,), (10,), (7,), (7,))
    scratch = [pltpu.VMEM(b, BF) for b in buffers] + [pltpu.SemaphoreType.DMA(n) for n in counts]
    return results, scratch


def back_kernel(gathers, row, crosses, left_ref, right_ref, grad_ref, hid_ref, gain_ref, g, h, new_ref, *refs):
    full_ref = refs[0] if gathers else None
    results, scratch = refs[gathers : gathers + 2], refs[gathers + 2 :]

    def settle(half, total):
        at = half_rows(half)
        new = back_rows(
            total, grad_ref[at, :].astype(F32), hid_ref[at, :].astype(F32), gain_ref[row : row + 1, :]
        )
        new_ref[at, :] = new.astype(new_ref.dtype)
        return new.astype(BF)

    place = plane_place()
    collect = Collect(place, (g, h), results, scratch[14 + 5 * gathers :], not gathers)
    lanes = (0, 384) if crosses else None
    product = make_product(left_ref, right_ref, True, lanes)
    exchange(place, product, settle, full_ref, scratch, collect)


def head_lanes(head):
    lane = lax.broadcasted_iota(jnp.int32, (1, 128), 1)
    return lane // 64 == head


def swap_halves(values):
    lane = lax.broadcasted_iota(jnp.int32, (1, 128), 1)
    return jnp.where(lane % 64 < 32, pltpu.roll(values, 96, 1), pltpu.roll(values, 32, 1))


NT = (((1,), (1,)), ((), ()))
TN = (((0,), (0,)), ((), ()))


def two_blocks(ref, tile, half):
    first = pl.multiple_of(2 * tile * ROWS + half * HALF, HALF)
    second = pl.multiple_of((2 * tile + 1) * ROWS + half * HALF, HALF)
    return jnp.concatenate([ref[pl.ds(first, HALF), :], ref[pl.ds(second, HALF), :]], axis=0)


def put_blocks(ref, tile, half, value):
    first = pl.multiple_of(2 * tile * ROWS + half * HALF, HALF)
    second = pl.multiple_of((2 * tile + 1) * ROWS + half * HALF, HALF)
    ref[pl.ds(first, HALF), :] = value[:HALF]
    ref[pl.ds(second, HALF), :] = value[HALF:]


def attend_kernel(layer, *refs):
    x_ref, w_ref, cos_ref, sin_ref, more_ref, pq_ref, pk_ref = refs[:7]
    count = 2 - layer
    tables, refs = refs[7 : 7 + count], refs[7 + count :]
    q_ref, k_ref, v_ref, att_ref, lse_ref = refs[:5]
    kept = refs[5:7]
    placed = refs[-4 - count : -4]
    sends, receives, ss, sr = refs[-4:]
    f, c, _, _ = plane_place()
    peers, sibling, _ = chip_peers(f, c)
    rows_n = x_ref.shape[0]
    half_n = rows_n // 2
    greet(peers + [sibling])
    leg = start_leg(list(zip(tables, placed)), peers, c // 2, sends, receives)

    def copies(i):
        here = pl.ds(pl.multiple_of(i * HALF, HALF), HALF)
        there = pl.ds(pl.multiple_of(half_n + i * HALF, HALF), HALF)
        return [
            remote(ref.at[h, here], ref.at[h, there], ss.at[4 * i + n], sr.at[4 * i + n], sibling)
            for n, (ref, h) in enumerate(((k_ref, 0), (k_ref, 1), (v_ref, 0), (v_ref, 1)))
        ]

    def step(i, carry):
        at = pl.ds(pl.multiple_of(i * ROWS, ROWS), ROWS)
        here = pl.ds(pl.multiple_of(i * HALF, HALF), HALF)
        rows = x_ref[at, :]
        if layer == 0:
            wide = rows.astype(F32)
            rows = (wide * norm_rows(wide) * more_ref[:1, :]).astype(BF)
            kept[0][at, :] = rows
        raw = jnp.dot(rows, w_ref[:, :384], preferred_element_type=F32)
        cosine, sine = cos_ref[at, :], sin_ref[at, :]
        q, k, v = raw[:, :128], raw[:, 128:256], raw[:, 256:]
        q_ref[at, :] = (q * cosine + swap_halves(q) * sine).astype(BF)
        k = (k * cosine + swap_halves(k) * sine).astype(BF)
        if layer == 0:
            kept[1][at, :] = v
        else:
            v = 0.5 * v + 0.5 * more_ref[at, :]
        v = v.astype(BF)
        for half in range(2):
            k_ref[half, here, :] = k[half * HALF : (half + 1) * HALF]
            v_ref[half, here, :] = v[half * HALF : (half + 1) * HALF]
        for copy in copies(i):
            copy.start()
        return carry

    lax.fori_loop(0, rows_n // ROWS, step, 0)
    for i in range(rows_n // ROWS):
        for copy in copies(i):
            copy.wait()

    def tile_step(tile, carry):
        for late in range(2):
            number = tile + late * (rows_n // (2 * ROWS))
            queries = two_blocks(q_ref, tile, late) * jnp.asarray(HD ** (-0.5), BF)
            allowed = pk_ref[late : late + 1, :] <= turn_row(pq_ref[pl.ds(number, 1), :])
            parts = []
            for head in range(2):
                masked = jnp.where(head_lanes(head), queries, jnp.zeros_like(queries))
                scores = lax.dot_general(masked, k_ref[late], NT, preferred_element_type=F32)
                scores = jnp.where(allowed, scores, NEG_FILL)
                top = jnp.max(scores, axis=-1, keepdims=True)
                if late:
                    early = lax.dot_general(masked, k_ref[0], NT, preferred_element_type=F32)
                    top = jnp.maximum(top, jnp.max(early, axis=-1, keepdims=True))
                shares = jnp.exp(scores - top)
                total = jnp.sum(shares, axis=-1, keepdims=True)
                mixed = jnp.dot(shares.astype(BF), v_ref[late], preferred_element_type=F32)
                if late:
                    shares = jnp.exp(early - top)
                    total += jnp.sum(shares, axis=-1, keepdims=True)
                    mixed += jnp.dot(shares.astype(BF), v_ref[0], preferred_element_type=F32)
                lse_ref[number, head : head + 1, :] = turn_column(top + jnp.log(total))
                parts.append(mixed / total)
            put_blocks(att_ref, tile, late, jnp.where(head_lanes(0), parts[0], parts[1]).astype(BF))
        return carry

    lax.fori_loop(0, rows_n // (2 * ROWS), tile_step, 0)
    for copy in leg:
        copy.wait()


def attend(layer, *args):
    rows_n = args[0].shape[0]
    spec = pl.BlockSpec(memory_space=VMEM_SPACE)
    outs = [((rows_n, 128), BF), ((2, rows_n, 128), BF), ((2, rows_n, 128), BF), ((rows_n, 128), BF)]
    outs += [((rows_n // ROWS, 2, ROWS), F32)]
    count = 4 * (rows_n // ROWS)
    sems = [pltpu.SemaphoreType.DMA((count,))] * 2
    if layer == 0:
        outs += [(args[0].shape, BF), ((rows_n, 128), F32)]
    outs += [(p.shape, BF) for p in args[7:]]
    sems = [pltpu.SemaphoreType.DMA((16,))] * 2 + sems
    return pl.pallas_call(
        functools.partial(attend_kernel, layer),
        out_shape=[jax.ShapeDtypeStruct(*o) for o in outs],
        in_specs=[spec] * len(args),
        out_specs=[spec] * len(outs),
        scratch_shapes=sems,
        compiler_params=pltpu.CompilerParams(
            collective_id=10 + layer, has_side_effects=True, vmem_limit_bytes=16 * 1024 * 1024
        ),
        name="attend",
    )(*args)


def attend_back_kernel(layer, *refs):
    q_ref, k_ref, v_ref, full_ref, out_ref, att_ref, lse_ref, pq_ref, pk_ref, cos_ref, sin_ref, more_ref = refs[:12]
    count = 2 - layer
    tables, refs = refs[12 : 12 + count], refs[12 + count :]
    three_ref, dw_ref, *placed = refs[: 2 + count]
    pkc, dq, dk, dv, dw, sb, rb, ss, sr, sends, receives = refs[-11:]
    place = plane_place()
    f, c, _, _ = place
    peers, sibling, _ = chip_peers(f, c)
    greet(peers + [sibling])
    leg = start_leg(list(zip(tables, placed)), peers, c // 2, sends, receives)
    rows_n = q_ref.shape[0]
    half_n = rows_n // 2
    dk[...] = jnp.zeros_like(dk)
    dv[...] = jnp.zeros_like(dv)
    dw[...] = jnp.zeros_like(dw)
    for late in range(2):
        for i in range(rows_n // ROWS):
            at = slice(i * ROWS, (i + 1) * ROWS)
            pkc[late, at, :] = turn_row(pk_ref[late : late + 1, at])

    def tile_step(tile, carry):
        for late in range(2):
            number = tile + late * (rows_n // (2 * ROWS))
            queries = two_blocks(q_ref, tile, late) * jnp.asarray(HD ** (-0.5), BF)
            full = two_blocks(full_ref, tile, late)
            grads = lax.dot_general(full, out_ref[...], NT, preferred_element_type=F32).astype(BF)
            dw[...] += lax.dot_general(two_blocks(att_ref, tile, late), full, TN, preferred_element_type=F32)
            allowed = pkc[late] <= pq_ref[pl.ds(number, 1), :]
            parts = []
            for head in range(2):
                masked = jnp.where(head_lanes(head), queries, jnp.zeros_like(queries))
                grad_h = jnp.where(head_lanes(head), grads, jnp.zeros_like(grads))
                lse = lse_ref[number, head : head + 1, :]
                kinds = (1, 0) if late else (0,)
                shares, grad_shares = [], []
                delta = jnp.zeros((1, ROWS), F32)
                for kind in kinds:
                    part = jnp.exp(lax.dot_general(k_ref[kind], masked, NT, preferred_element_type=F32) - lse)
                    if kind == late:
                        part = jnp.where(allowed, part, 0.0)
                    grad = lax.dot_general(v_ref[kind], grad_h, NT, preferred_element_type=F32)
                    delta += jnp.sum(part * grad, axis=0, keepdims=True)
                    shares.append(part)
                    grad_shares.append(grad)
                found = jnp.zeros((ROWS, 128), F32)
                for kind, part, grad in zip(kinds, shares, grad_shares):
                    grad_scores = (part * (grad - delta)).astype(BF)
                    dv[kind] += jnp.dot(part.astype(BF), grad_h, preferred_element_type=F32)
                    dk[kind] += jnp.dot(grad_scores, masked, preferred_element_type=F32)
                    found += lax.dot_general(grad_scores, k_ref[kind], TN, preferred_element_type=F32)
                parts.append(found)
            put_blocks(dq, tile, late, jnp.where(head_lanes(0), parts[0], parts[1]) * HD ** (-0.5))
        return carry

    lax.fori_loop(0, rows_n // (2 * ROWS), tile_step, 0)
    copies = []
    for n, ref in enumerate((dk, dv)):
        sb[n] = ref[:, half_n:, :].astype(BF)
        copies.append(remote(sb.at[n], rb.at[n], ss.at[n], sr.at[n], sibling))
        copies[n].start()
    dw_ref[...] = dw[...].astype(BF)
    for copy in copies:
        copy.wait()

    def rows_of(n, ref, i):
        here = pl.ds(pl.multiple_of(i * HALF, HALF), HALF)
        return jnp.concatenate([ref[half, here, :] + rb[n, half, here, :].astype(F32) for half in range(2)], axis=0)

    def turn(i, carry):
        at = pl.ds(pl.multiple_of(i * ROWS, ROWS), ROWS)
        cosine, sine = cos_ref[at, :], sin_ref[at, :]
        for n, grad in enumerate((dq[at, :], rows_of(0, dk, i))):
            three_ref[at, 128 * n : 128 * n + 128] = (grad * cosine - swap_halves(grad) * sine).astype(BF)
        grad = rows_of(1, dv, i)
        if layer == 1:
            grad = 0.5 * grad
            refs[2 + count][at, :] = grad
        else:
            grad = grad + more_ref[at, :]
        three_ref[at, 256:] = grad.astype(BF)
        return carry

    lax.fori_loop(0, rows_n // ROWS, turn, 0)
    for copy in leg:
        copy.wait()


def attend_backward(layer, *args):
    rows_n, width = args[3].shape
    spec = pl.BlockSpec(memory_space=VMEM_SPACE)
    outs = [((rows_n, 384), BF), ((128, width), BF)] + [(u.shape, BF) for u in args[12:]]
    if layer == 1:
        outs += [((rows_n, 128), F32)]
    return pl.pallas_call(
        functools.partial(attend_back_kernel, layer),
        out_shape=[jax.ShapeDtypeStruct(*o) for o in outs],
        in_specs=[spec] * len(args),
        out_specs=[spec] * len(outs),
        scratch_shapes=[
            pltpu.VMEM((2, rows_n, 1), F32),
            pltpu.VMEM((rows_n, 128), F32),
            pltpu.VMEM((2, rows_n, 128), F32),
            pltpu.VMEM((2, rows_n, 128), F32),
            pltpu.VMEM((128, width), F32),
            pltpu.VMEM((2, 2, rows_n // 2, 128), BF),
            pltpu.VMEM((2, 2, rows_n // 2, 128), BF),
            pltpu.SemaphoreType.DMA((2,)),
            pltpu.SemaphoreType.DMA((2,)),
            pltpu.SemaphoreType.DMA((16,)),
            pltpu.SemaphoreType.DMA((16,)),
        ],
        compiler_params=pltpu.CompilerParams(
            collective_id=12 + layer, has_side_effects=True, vmem_limit_bytes=32 * 1024 * 1024
        ),
        name="attend_back",
    )(*args)


def unpack_kernel(*every):
    every[24][...] = every[0][...]
    every[25][...] = every[1][...]
    refs = every[2:24] + every[26:]
    for l in range(2):
        cu, od, cq, oo, pre, query, keys, values, mid, gates, upproj = refs[11 * l : 11 * l + 11]
        g_pre, gq, gk, gv, g_out, g_mid, gg, gu, g_down = refs[22 + 9 * l : 31 + 9 * l]
        rows, units = gates.shape
        each = units // 32
        block = cu.shape[2] // 8
        total = jnp.zeros((rows, 1), F32)
        for chip in range(8):
            pair = 4 * (chip % 2) + chip // 2
            for n, (w, g) in enumerate(((query, gq), (keys, gk), (values, gv))):
                at = slice(128 * pair, 128 * pair + 128)
                part = cq[chip, :, 128 * n : 128 * n + 128].astype(F32)
                g[:, at] = part
                total += jnp.sum(part * w[:, at].astype(F32), axis=-1, keepdims=True)
        g_pre[...] = turn_column(total) / pre[...].astype(F32)
        for n, g in enumerate((gg, gu)):
            for chip in range(8):
                wide = cu[chip, :, 4 * block * n : 4 * block * (n + 1)].astype(F32)
                for i in range(4):
                    owner = 16 * (i // 2) + 2 * chip + i % 2
                    g[:, each * owner : each * owner + each] = wide[:, block * i : block * i + each]
        both = gg[...] * gates[...].astype(F32) + gu[...] * upproj[...].astype(F32)
        g_mid[...] = turn_column(jnp.sum(both, axis=-1, keepdims=True)) / mid[...].astype(F32)
        g_out[...] = oo[...]
        g_down[...] = od[: g_down.shape[0], :]


def unpack(output, tokens_grad, collected, layers):
    args, outs = [output, tokens_grad], [(output.shape, BF), (tokens_grad.shape, BF)]
    for l, layer in enumerate(layers):
        pre, query, keys, values, out, mid, gates, upproj, down = layer
        args += [*collected[l], pre, query, keys, values, mid, gates, upproj]
        for w in layer:
            outs.append((w.shape, F32))
    spec = pl.BlockSpec(memory_space=VMEM_SPACE)
    found = pl.pallas_call(
        unpack_kernel,
        out_shape=[jax.ShapeDtypeStruct(*o) for o in outs],
        in_specs=[spec] * len(args),
        out_specs=[spec] * len(outs),
        compiler_params=pltpu.CompilerParams(vmem_limit_bytes=60 * 1024 * 1024),
        name="unpack",
    )(*args)
    return [g[0] if g.shape[0] == 1 else g for g in found]


def fast_local(tokens, cotangent, pair_of, *shards):
    width = tokens.shape[2]
    rows_each, units = shards[6].shape
    each = units // 32
    block = (each + 2 + 31) // 32 * 32
    hidden_pad = 4 * block
    wide = 384 + 2 * hidden_pad
    core = lax.axis_index("ctx") % 2
    pos_all = storage_positions(pair_of, ROWS).reshape(8, 2, ROWS)
    own_pos = lax.dynamic_index_in_dim(pos_all, core, 1, False).reshape(-1)
    sib_pos = lax.dynamic_index_in_dim(pos_all, 1 - core, 1, False).reshape(-1)
    own_split = own_pos.reshape(8, 2, HALF).transpose(1, 0, 2)
    sib_split = sib_pos.reshape(8, 2, HALF).transpose(1, 0, 2)
    pos_q = own_split.reshape(8, ROWS).astype(F32)
    pos_k = jnp.concatenate([own_split, sib_split], axis=1).reshape(2, -1).astype(F32)
    cosine, sine = rope_tables(own_pos, HD)
    cosine = jnp.concatenate([cosine] * 4, axis=-1)
    sine = jnp.concatenate([-sine, sine, -sine, sine], axis=-1)

    shards = [s[None, :] if s.ndim == 1 else s for s in shards]
    layers = [shards[:9], shards[9:]]
    tok = tokens.reshape(ROWS, width)
    cot = cotangent.reshape(ROWS, width)

    full, heads, out_rows, gains, units_one, heads_two, units_two, *downs = begin_call(tok, shards, block)
    heads_w = [heads.reshape(32 * rows_each, 512), None]
    units_w, down_w, out_w = [None, None], [None, None], [out_rows.reshape(4 * rows_each, width), None]

    plane = 8 * ROWS
    full_type = ((plane, width), BF)
    rows_type = ((ROWS, width), F32)
    saved = []
    hidden = tok
    first_values = None
    for layer in range(2):
        args = (full, heads_w[layer], cosine, sine, gains if layer == 0 else first_values, pos_q, pos_k)
        x_full = full
        if layer == 0:
            q, k, v, att, lse, x_full, first_values, *legs = attend(0, *args, units_one, heads_two)
            widths, more = (2 * hidden_pad, 384), (downs[0], layers[1][4])
        else:
            q, k, v, att, lse, *legs = attend(1, *args, units_two)
            widths, more = (2 * hidden_pad,), (downs[1],)
        outs, sems = share_shapes(rows_each, width, block, widths)
        middle, mlp_full, table, *found = comm_call(
            functools.partial(middle_kernel, 2 * layer + 1, len(widths)), [rows_type, full_type] + outs, 1 + layer,
            (att, out_w[layer], hidden, gains, *legs, *more), True, "middle", sems,
        )
        units_w[layer] = table.reshape(32 * rows_each, 2 * hidden_pad)
        if layer == 0:
            heads_w[1] = found[0].reshape(32 * rows_each, 384)
            down_w[0] = found[1].reshape(hidden_pad, width)
            out_w[1] = found[2].reshape(4 * rows_each, width)
        else:
            down_w[1] = found[0].reshape(hidden_pad, width)
        both = jnp.dot(mlp_full, units_w[layer], preferred_element_type=F32)
        gate, up = both[:, :hidden_pad], both[:, hidden_pad:]
        inner = (jax.nn.silu(gate) * up).astype(BF)
        saved.append((x_full, q, k, v, lse, att, mlp_full, gate, up, inner, hidden, middle))
        if layer == 0:
            hidden, full = comm_call(
                functools.partial(forward_kernel, 2), [rows_type, full_type], 3,
                (inner, down_w[layer], middle, gains), True, "result",
            )
        else:
            output, full = comm_call(
                turn_kernel, [((ROWS, width), BF), full_type], 4,
                (inner, down_w[layer], middle, cot), True, "turn",
            )
    grad = cot
    passed = cosine
    collected = [None, None]
    for layer in (1, 0):
        x_full, q, k, v, lse, att, mlp_full, gate, up, inner, hidden, middle = saved[layer]
        grad_down = left_product(inner, full)
        grad_inner = right_product(full, down_w[layer])
        sigma = jax.nn.sigmoid(gate)
        grad_gate = (grad_inner * up * sigma * (1.0 + gate * (1.0 - sigma))).astype(BF)
        grad_up = (grad_inner * gate * sigma).astype(BF)
        both = jnp.concatenate([grad_gate, grad_up], axis=-1)
        grad_upw = left_product(mlp_full, both)
        results, more = collect_shapes(rows_each, 2 * hidden_pad, block, width, False)
        grad_mid, full, units_sum, got_down = comm_call(
            functools.partial(back_kernel, 1, 2 * layer + 1, False), [rows_type, full_type] + results, 5 + layer,
            (
                both, units_w[layer], grad, middle, gains,
                grad_upw.astype(BF).reshape(16, 2, rows_each, 2 * hidden_pad),
                grad_down.astype(BF).reshape(2, 2, block, width),
            ),
            True, "middle_back", more,
        )
        legs = (units_sum,) if layer == 1 else (units_sum, heads_sum)
        three, grad_out, got_units, *kept = attend_backward(
            layer, q, k, v, full, out_w[layer], att, lse, pos_q, pos_k, cosine, sine, passed, *legs
        )
        collected[layer] = [got_units, got_down]
        if layer == 1:
            (passed,) = kept
        else:
            collected[1] += [kept[0], two_out]
        grad_qkv = left_product(x_full, three)
        results, more = collect_shapes(rows_each, 384, rows_each, width, True)
        args = (
            three, heads_w[layer], grad_mid, hidden, gains,
            grad_qkv.astype(BF).reshape(16, 2, rows_each, 384),
            grad_out.reshape(2, 2, rows_each, width),
        )
        if layer == 1:
            grad, full, heads_sum, two_out = comm_call(
                functools.partial(back_kernel, 1, 2, True), [rows_type, full_type] + results, 7, args, True,
                "layer_back", more,
            )
        else:
            tokens_grad, *got_heads = comm_call(
                functools.partial(back_kernel, 0, 0, True), [((ROWS, width), BF)] + results, 8, args, False,
                "last_back", more,
            )
            collected[0] += got_heads
    output, tokens_grad, *found = unpack(output, tokens_grad, collected, layers)
    return (output.reshape(1, ROWS, width), tokens_grad.reshape(1, ROWS, width), *found)


def solution(mesh):
    placed = (
        P("fsdp", "ctx", None),
        P("fsdp", "ctx", None),
        P(),
        P(("fsdp", "ctx")),
        P(("fsdp", "ctx"), None),
        P(("fsdp", "ctx"), None),
        P(("fsdp", "ctx"), None),
        P(("fsdp", "ctx"), None),
        P(("fsdp", "ctx")),
        P(("fsdp", "ctx"), None),
        P(("fsdp", "ctx"), None),
        P(("fsdp", "ctx"), None),
        P(("fsdp", "ctx")),
        P(("fsdp", "ctx"), None),
        P(("fsdp", "ctx"), None),
        P(("fsdp", "ctx"), None),
        P(("fsdp", "ctx"), None),
        P(("fsdp", "ctx")),
        P(("fsdp", "ctx"), None),
        P(("fsdp", "ctx"), None),
        P(("fsdp", "ctx"), None),
    )
    fits = mesh.shape["ctx"] == HEADS and mesh.shape["fsdp"] == 2
    return jax.shard_map(
        fast_local if fits else local,
        mesh=mesh,
        in_specs=placed,
        out_specs=(
            P("fsdp", "ctx", None),
            P("fsdp", "ctx", None),
            P(("fsdp", "ctx")),
            P(("fsdp", "ctx"), None),
            P(("fsdp", "ctx"), None),
            P(("fsdp", "ctx"), None),
            P(("fsdp", "ctx"), None),
            P(("fsdp", "ctx")),
            P(("fsdp", "ctx"), None),
            P(("fsdp", "ctx"), None),
            P(("fsdp", "ctx"), None),
            P(("fsdp", "ctx")),
            P(("fsdp", "ctx"), None),
            P(("fsdp", "ctx"), None),
            P(("fsdp", "ctx"), None),
            P(("fsdp", "ctx"), None),
            P(("fsdp", "ctx")),
            P(("fsdp", "ctx"), None),
            P(("fsdp", "ctx"), None),
            P(("fsdp", "ctx"), None),
        ),
        check_vma=False,
    )
```
